32 devices in a mesh: ctx: 16 (over z, y, core), wt: 2 (over x).
Axes of the slice: x: 2, y: 2, z: 4, core: 2. Of those that a mesh axis runs over, the one named last changes fastest.
Arguments:
- hidden_in: bfloat16 [2, 2048, 1024], P('wt', 'ctx'), may hold values from -6 to 6
- doc_start: int32 [2, 2048], P('wt', 'ctx'), may hold values from 0 to 1, as said below
- qkv_master: float32 [1024, 3072], P(('ctx', 'wt')), may hold values from -0.25 to 0.25
- out_master: float32 [1024, 1024], P(('ctx', 'wt')), may hold values from -0.75 to 0.75
- up_master: float32 [1024, 4096], P(('ctx', 'wt')), may hold values from -0.1875 to 0.1875
- down_master: float32 [4096, 1024], P(('ctx', 'wt')), may hold values from -0.125 to 0.125
- norm1_gain: float32 [1024], replicated, may hold values from 0.5 to 1.5
- norm1_bias: float32 [1024], replicated, may hold values from -3 to 3
- norm2_gain: float32 [1024], replicated, may hold values from 0.5 to 1.5
- norm2_bias: float32 [1024], replicated, may hold values from -3 to 3
- grad_out: bfloat16 [2, 2048, 1024], P('wt', 'ctx'), may hold values from -6 to 6
Outputs:
- layer_out: bfloat16 [2, 2048, 1024], P('wt', 'ctx')
- grad_in: bfloat16 [2, 2048, 1024], P('wt', 'ctx')
- qkv_grad: float32 [1024, 3072], P(('ctx', 'wt'))
- out_grad: float32 [1024, 1024], P(('ctx', 'wt'))
- up_grad: float32 [1024, 4096], P(('ctx', 'wt'))
- down_grad: float32 [4096, 1024], P(('ctx', 'wt'))
- norm1_gain_grad: float32 [1024], P(('ctx', 'wt'))
- norm1_bias_grad: float32 [1024], P(('ctx', 'wt'))
- norm2_gain_grad: float32 [1024], P(('ctx', 'wt'))
- norm2_bias_grad: float32 [1024], P(('ctx', 'wt'))
The draws below stay inside these ranges and needn't reach their ends.
Inputs may be any that keep to these rules, and one draw needn't show every extreme that they name: `doc_start`: 1 marks the first token of a document, rows in storage order; position 0 of every stream starts a document; every document has 1 to 1024 tokens, and each stream has one of exactly 1024.
All inputs are finite; a program needn't handle non-finite values.
Results may differ from the reference program's by a relative error of at most 0.017.
Values may be sent and summed in bfloat16 or wider, within the bound.
No kernel may reach another device: no remote copies, remote signals or barrier semaphores. Data moves between devices by JAX's collectives and lax.ppermute only.
A program may use at most 192 MiB of HBM per device.

```python
import jax
import jax.numpy as jnp
from jax import lax

D = 1024
HEADS = 16
HD = 64
FF = 4096
BLK = 64
SEQ = 2048
STREAMS = 2
MAXDOC = 1024
N_CTX = 16


def draw_doc_start(key, part):
    key_first, key_rest = jax.random.split(key)
    opening = jax.random.randint(key_first, (STREAMS, 1), 1, BLK)
    extra = jax.random.randint(key_rest, (STREAMS, SEQ), 0, 400)
    positions = jnp.arange(SEQ, dtype=jnp.int32)[None, :]
    closing = opening + MAXDOC
    marked = (positions == 0) | (positions == opening)
    marked = marked | (positions >= closing) & ((positions - closing) % MAXDOC == 0)
    marked = marked | (positions > closing) & (extra == 0)
    flags = marked.astype(jnp.int32)
    blocks = flags.reshape(STREAMS, 2, SEQ // (2 * BLK), BLK)
    first = blocks[:, 0]
    second = blocks[:, 1][:, ::-1]
    return jnp.stack([first, second], axis=2).reshape(STREAMS, SEQ)


def steps_of(rng, shape, pieces, least, high):
    def one(position, blocks):
        steps = jax.random.uniform(jax.random.fold_in(jax.random.fold_in(rng, 6), position), (blocks,), jnp.float32, least / len(pieces), high / len(pieces))
        return jnp.repeat(jnp.exp(steps), shape[position] // blocks).reshape((-1,) + (1,) * (len(shape) - position - 1))

    level = one(*pieces[0])
    for cut in pieces[1:]:
        level = level * one(*cut)
    return level


def gaussian(key, shape, width, limit, shards=(), held_as=jnp.bfloat16):
    level = steps_of(key, shape, shards, -0.22, 0.18) if shards else 1.0
    result = jax.random.normal(key, shape, jnp.float32) * width * level
    return jnp.minimum(jnp.maximum(result, -limit), limit).astype(held_as)


def setup_inputs(seed: int = 0) -> dict:
    key_list = jax.random.split(jax.random.key(seed), 12)
    hidden_in = gaussian(key_list[0], (STREAMS, SEQ, D), 1.0, 6.0, ((0, 2), (1, 16)))
    doc_start = draw_doc_start(jax.random.fold_in(key_list[11], 71), 0)
    qkv_master = gaussian(key_list[2], (D, 3 * D), (D // 2) ** -0.5, 0.25, ((0, 32),), jnp.float32)
    out_master = gaussian(key_list[3], (D, D), (D // 16) ** -0.5, 0.75, ((0, 32),), jnp.float32)
    up_master = gaussian(key_list[4], (D, FF), D ** -0.5, 0.1875, ((0, 32),), jnp.float32)
    down_master = gaussian(key_list[5], (FF, D), (FF // 2) ** -0.5, 0.125, ((0, 32),), jnp.float32)
    norm1_gain = jnp.clip(1.0 + 0.1 * jax.random.normal(key_list[6], (D,), jnp.float32), 0.5, 1.5)
    norm1_bias = gaussian(key_list[7], (D,), 0.5, 3.0, (), jnp.float32)
    norm2_gain = jnp.clip(1.0 + 0.1 * jax.random.normal(key_list[8], (D,), jnp.float32), 0.5, 1.5)
    norm2_bias = gaussian(key_list[9], (D,), 0.5, 3.0, (), jnp.float32)
    grad_out = gaussian(key_list[10], (STREAMS, SEQ, D), 1.0, 6.0, ((0, 2), (1, 16)))
    return dict(hidden_in=hidden_in, doc_start=doc_start, qkv_master=qkv_master, out_master=out_master, up_master=up_master, down_master=down_master, norm1_gain=norm1_gain, norm1_bias=norm1_bias, norm2_gain=norm2_gain, norm2_bias=norm2_bias, grad_out=grad_out)


@jax.custom_vjp
def low(v):
    return lax.optimization_barrier(v.astype(jnp.bfloat16)).astype(jnp.float32)

@jax.custom_vjp
def low_back(v):
    return v

def low_keep(v):
    return (low(v), None)

def low_pass(kept, grad):
    return (grad,)

def back_keep(v):
    return (v, None)

def back_low(kept, grad):
    return (low(grad),)
low.defvjp(low_keep, low_pass)
low_back.defvjp(back_keep, back_low)
EPS = 1e-05
FAR = -1e+30
HIGHEST = lax.Precision.HIGHEST

def gelu(values):
    return 0.5 * values * (1.0 + jnp.tanh(0.7978845608028654 * (values + 0.044715 * values * values * values)))

def to_position(array):
    shaped = array.reshape((array.shape[0], N_CTX, 2, BLK) + array.shape[2:])
    first = shaped[:, :, 0]
    second = shaped[:, ::-1, 1]
    return jnp.concatenate([first, second], axis=1).reshape(array.shape)

def to_storage(array):
    shaped = array.reshape((array.shape[0], 2, N_CTX, BLK) + array.shape[2:])
    first = shaped[:, 0]
    second = shaped[:, 1][:, ::-1]
    return jnp.stack([first, second], axis=2).reshape(array.shape)

def layer_norm(rows, gain, bias):
    centre = lax.optimization_barrier(jnp.mean(rows, axis=-1, keepdims=True))
    centred = rows - centre
    spread = lax.rsqrt(lax.optimization_barrier(jnp.mean(centred * centred, axis=-1, keepdims=True)) + EPS)
    return centred * spread * gain + bias

def attend(query, keys, values, begin):
    qblock = min(512, SEQ // 2)
    window = min(SEQ, MAXDOC + qblock)
    scaling = HD ** (-0.5)

    def one_block(index):
        first = (index * qblock).astype(jnp.int32)
        key_first = jnp.clip(first + qblock - window, 0, SEQ - window).astype(jnp.int32)
        query_rows = lax.dynamic_slice_in_dim(query, first, qblock, 0)
        key_rows = lax.dynamic_slice_in_dim(keys, key_first, window, 0)
        value_rows = lax.dynamic_slice_in_dim(values, key_first, window, 0)
        query_pos = first + jnp.arange(qblock, dtype=jnp.int32)
        key_pos = key_first + jnp.arange(window, dtype=jnp.int32)
        query_begin = lax.dynamic_slice_in_dim(begin, first, qblock, 0)
        allowed = (key_pos[None, :] <= query_pos[:, None]) & (key_pos[None, :] >= query_begin[:, None])
        scores = low_back(jnp.einsum('qhd,khd->hqk', query_rows, key_rows, precision=HIGHEST) * scaling)
        scores = jnp.where(allowed[None], scores, FAR)
        top = lax.optimization_barrier(jnp.max(scores, axis=-1, keepdims=True))
        weights = jnp.exp(scores - top)
        probs = weights / lax.optimization_barrier(jnp.sum(weights, axis=-1, keepdims=True))
        return jnp.einsum('hqk,khd->qhd', low(probs), value_rows, precision=HIGHEST)
    blocks = lax.map(jax.checkpoint(one_block), jnp.arange(SEQ // qblock, dtype=jnp.int32))
    return blocks.reshape(SEQ, HEADS, HD)

def layer(stream, begin, w_qkv, w_out, w_up, w_down, gain1, bias1, gain2, bias2):
    norm_in = low(layer_norm(stream, gain1, bias1))
    qkv = low(low_back(jnp.dot(norm_in, w_qkv, precision=HIGHEST, preferred_element_type=jnp.float32)))
    query = qkv[:, :D].reshape(SEQ, HEADS, HD)
    keys = qkv[:, D:2 * D].reshape(SEQ, HEADS, HD)
    values = qkv[:, 2 * D:].reshape(SEQ, HEADS, HD)
    attended = low(low_back(attend(query, keys, values, begin).reshape(SEQ, D)))
    branch = low_back(jnp.dot(attended, w_out, precision=HIGHEST, preferred_element_type=jnp.float32))
    mid = stream + branch
    norm_mid = low(layer_norm(mid, gain2, bias2))
    up = low_back(jnp.dot(norm_mid, w_up, precision=HIGHEST, preferred_element_type=jnp.float32))
    act_b = low(gelu(up))
    return mid + jnp.dot(act_b, w_down, precision=HIGHEST, preferred_element_type=jnp.float32)

def reference(hidden_in, doc_start, qkv_master, out_master, up_master, down_master, norm1_gain, norm1_bias, norm2_gain, norm2_bias, grad_out):
    inputs = to_position(hidden_in.astype(jnp.float32))
    flags = to_position(doc_start)
    positions = jnp.arange(SEQ, dtype=jnp.int32)
    begin = lax.cummax(jnp.where(flags == 1, positions[None, :], 0), axis=1)

    def whole(inputs, w_qkv, w_out, w_up, w_down, gain1, bias1, gain2, bias2):
        round_qkv = low(w_qkv)
        round_out = low(w_out)
        round_up = low(w_up)
        round_down = low(w_down)

        def one_stream(stream, stream_begin):
            return layer(stream, stream_begin, round_qkv, round_out, round_up, round_down, gain1, bias1, gain2, bias2)
        return jax.vmap(one_stream)(inputs, begin)
    outputs, pullback = jax.vjp(whole, inputs, qkv_master, out_master, up_master, down_master, norm1_gain, norm1_bias, norm2_gain, norm2_bias)
    grads = pullback(to_position(grad_out.astype(jnp.float32)))
    return (to_storage(outputs).astype(jnp.bfloat16), to_storage(grads[0]).astype(jnp.bfloat16), grads[1], grads[2], grads[3], grads[4], grads[5], grads[6], grads[7], grads[8])
```

```python
from functools import partial

import jax
import jax.numpy as jnp
from jax import lax
from jax.experimental import pallas as pl
from jax.experimental.pallas import tpu as pltpu
from jax.sharding import Mesh
from jax.sharding import PartitionSpec as P

HEADS = 16
HD = 64
EPS = 1e-05
FAR = -1e30
TILE = 256
BF = jnp.bfloat16
F32 = jnp.float32
CTX = ("r", "z", "y", "c")
PART = ("z", "y", "c")
SLAB = ("y", "c", "x")
ZZ = ("r", "z")
ALL = ("r", "z", "y", "c", "x")
SWAP = [(0, 1), (1, 0)]


def dot(one, two, dims):
    return lax.dot_general(one, two, ((dims[0], dims[1]), ((), ())), preferred_element_type=F32)


def layer_norm(rows, gain, bias):
    centre = jnp.mean(rows, axis=-1, keepdims=True)
    centred = rows - centre
    spread = lax.rsqrt(jnp.mean(centred * centred, axis=-1, keepdims=True) + EPS)
    normed = centred * spread
    return (normed * gain + bias, normed, spread)


def norm_back(grad, normed, spread, gain):
    scaled = grad * gain
    inner = (
        scaled
        - jnp.mean(scaled, axis=-1, keepdims=True)
        - normed * jnp.mean(scaled * normed, axis=-1, keepdims=True)
    )
    return inner * spread


def gelu_both(up):
    root = 0.7978845608028654
    square = up * up
    inner = jnp.tanh(root * up * (1.0 + 0.044715 * square))
    value = 0.5 * up * (1.0 + inner)
    slope = 0.5 * (1.0 + inner) + 0.5 * up * (1.0 - inner * inner) * root * (
        1.0 + 3.0 * 0.044715 * square
    )
    return value, slope


def block_home(block, shards):
    return (block, 0) if block < shards else (2 * shards - 1 - block, 1)


def forward_kernel(
    lo_ref, core_ref, own_ref, oth_ref, w_ref, begin_ref,
    att_ref, ot_ref, lse_ref, q_ref, k_ref, v_ref, vt_ref,
):
    shards, rows, _ = att_ref.shape
    half = rows // 2
    total = shards * rows
    core = core_ref[0]
    for chip in range(shards // 2):
        for which, ref in ((0, own_ref), (1, oth_ref)):
            made = dot(ref[chip], w_ref[...], ((1,), (0,))).astype(BF)
            shard = 2 * chip + (core if which == 0 else 1 - core)
            one = pl.multiple_of(shard * half, half)
            two = pl.multiple_of((2 * shards - 1 - shard) * half, half)
            scaled = made[:, :HD] * BF(HD**-0.5)
            for at, part in ((one, slice(0, half)), (two, slice(half, rows))):
                q_ref[pl.ds(at, half), :] = scaled[part]
                k_ref[pl.ds(at, half), :] = made[part, HD : 2 * HD]
                v_ref[pl.ds(at, half), :] = made[part, 2 * HD :]
    for at in range(0, total, 128):
        vt_ref[:, at : at + 128] = v_ref[at : at + 128, :].astype(F32).T.astype(BF)
    for tile in range(total // TILE):
        query = q_ref[tile * TILE : (tile + 1) * TILE, :]
        begin = begin_ref[tile : tile + 1, :]
        query_pos = tile * TILE + lax.broadcasted_iota(jnp.int32, (TILE, TILE), 1)

        def step(at, state):
            top, sums, accum = state
            first = pl.multiple_of(at * TILE, TILE)
            scores = dot(k_ref[pl.ds(first, TILE), :], query, ((1,), (1,)))
            key_pos = first + lax.broadcasted_iota(jnp.int32, (TILE, TILE), 0)
            scores = jnp.where((key_pos >= begin) & (key_pos <= query_pos), scores, FAR)
            higher = jnp.maximum(top, jnp.max(scores, axis=0, keepdims=True))
            weights = jnp.exp(scores - higher)
            factor = jnp.exp(top - higher)
            sums = sums * factor + jnp.sum(weights, axis=0, keepdims=True)
            accum = accum * factor + dot(
                vt_ref[:, pl.ds(first, TILE)], weights.astype(BF), ((1,), (0,))
            )
            return higher, sums, accum

        top, sums, accum = lax.fori_loop(
            lo_ref[tile],
            tile + 1,
            step,
            (
                jnp.full((1, TILE), FAR, F32),
                jnp.zeros((1, TILE), F32),
                jnp.zeros((HD, TILE), F32),
            ),
        )
        out = accum / sums
        ot_ref[:, tile * TILE : (tile + 1) * TILE] = out
        lse_ref[tile : tile + 1, :] = top + jnp.log(sums)
        turned = out.T.astype(BF)
        for piece in range(TILE // half):
            shard, side = block_home(tile * (TILE // half) + piece, shards)
            att_ref[shard, side * half : (side + 1) * half, :] = turned[
                piece * half : (piece + 1) * half
            ]


def backward_kernel(
    lo_ref, core_ref, q_ref, k_ref, v_ref, ot_ref, lse_ref, begin_ref, do_ref,
    da_ref, dn_ref, sum_ref, dop_ref, kt_ref, dq_ref, dk_ref, dv_ref,
):
    shards, rows, _ = do_ref.shape
    half = rows // 2
    total = shards * rows
    core = core_ref[0]
    for block in range(2 * shards):
        shard, side = block_home(block, shards)
        dop_ref[block * half : (block + 1) * half, :] = do_ref[
            shard, side * half : (side + 1) * half, :
        ]
    for at in range(0, total, 128):
        kt_ref[:, at : at + 128] = k_ref[at : at + 128, :].astype(F32).T.astype(BF)
    dk_ref[...] = jnp.zeros_like(dk_ref)
    dv_ref[...] = jnp.zeros_like(dv_ref)
    for tile in range(total // TILE):
        here = slice(tile * TILE, (tile + 1) * TILE)
        query = q_ref[here, :]
        dout = dop_ref[here, :]
        begin = begin_ref[tile : tile + 1, :]
        lse = lse_ref[tile : tile + 1, :]
        row_dot = jnp.sum(dout.astype(F32).T * ot_ref[:, here], axis=0, keepdims=True)
        query_pos = tile * TILE + lax.broadcasted_iota(jnp.int32, (TILE, TILE), 1)

        def step(at, accum):
            first = pl.multiple_of(at * TILE, TILE)
            there = pl.ds(first, TILE)
            scores = dot(k_ref[there, :], query, ((1,), (1,)))
            key_pos = first + lax.broadcasted_iota(jnp.int32, (TILE, TILE), 0)
            allowed = (key_pos >= begin) & (key_pos <= query_pos)
            probs = jnp.where(allowed, jnp.exp(scores - lse), 0.0)
            dprobs = dot(v_ref[there, :], dout, ((1,), (1,)))
            delta = (probs * (dprobs - row_dot)).astype(BF)
            dv_ref[there, :] += dot(probs.astype(BF), dout, ((1,), (0,)))
            dk_ref[there, :] += dot(delta, query, ((1,), (0,)))
            return accum + dot(kt_ref[:, there], delta, ((1,), (0,)))

        accum = lax.fori_loop(lo_ref[tile], tile + 1, step, jnp.zeros((HD, TILE), F32))
        dq_ref[here, :] = (accum * HD**-0.5).T
    sums = jnp.zeros((1, 3 * HD), F32)
    for block in range(2 * shards):
        shard, side = block_home(block, shards)
        at = slice(block * half, (block + 1) * half)
        joined = jnp.concatenate([dq_ref[at, :], dk_ref[at, :], dv_ref[at, :]], axis=1).astype(BF)
        to = slice(side * half, (side + 1) * half)
        da_ref[shard, to, :] = joined
        place = (core + shard) % 2
        dn_ref[place, shard // 2, to, :] = joined
        sums = sums + jnp.sum(joined.astype(F32), axis=0, keepdims=True)
    sum_ref[...] = sums


def kernel_call(body, scalars, arrays, outs, scratch, flops):
    vmem = pl.BlockSpec(memory_space=pltpu.VMEM)
    smem = pl.BlockSpec(memory_space=pltpu.SMEM)
    return pl.pallas_call(
        body,
        out_shape=outs,
        in_specs=[smem] * len(scalars) + [vmem] * len(arrays),
        out_specs=[vmem] * len(outs),
        scratch_shapes=scratch,
        compiler_params=pltpu.CompilerParams(vmem_limit_bytes=40 << 20),
        cost_estimate=pl.CostEstimate(flops=flops, bytes_accessed=8 << 20, transcendentals=4 << 20),
    )(*scalars, *arrays)


def ring_gather(rows, steps_axes, long):
    count = 2 * long
    order = [2 * at for at in range(long)] + [2 * at + 1 for at in reversed(range(long))]
    right = [(order[at], order[(at + 1) % count]) for at in range(count)]
    left = [(two, one) for one, two in right]
    chip = lax.axis_index(steps_axes)
    along, side = chip // 2, chip % 2
    spot = jnp.where(side == 0, along, count - 1 - along)

    def chip_at(place):
        place = place % count
        return jnp.where(place < long, 2 * place, 2 * (count - 1 - place) + 1)

    held = jnp.zeros((count,) + rows.shape, rows.dtype)
    held = lax.dynamic_update_index_in_dim(held, rows, chip, 0)
    ahead = behind = rows
    for hop in range(1, long + 1):
        ahead = lax.ppermute(ahead, steps_axes, right)
        if hop < long:
            behind = lax.ppermute(behind, steps_axes, left)
        held = lax.dynamic_update_index_in_dim(held, ahead, chip_at(spot - hop), 0)
        if hop < long:
            held = lax.dynamic_update_index_in_dim(held, behind, chip_at(spot + hop), 0)
    return held


def slab_gather(rows, wide):
    if wide != 2:
        return lax.all_gather(rows, SLAB, axis=0, tiled=False)
    half = rows.shape[0] // 2
    by_x = lax.ppermute(rows, "x", SWAP)
    by_y = lax.ppermute(rows, "y", SWAP)
    both_one = lax.ppermute(by_y[:half], "x", SWAP)
    both_two = lax.ppermute(by_x[half:], "y", SWAP)
    chip = jnp.stack([rows, by_x, by_y, jnp.concatenate([both_one, both_two])])
    return jnp.concatenate([chip, lax.ppermute(chip, "c", SWAP)])


def slab_scatter(parts, wide):
    if wide != 2:
        got = lax.all_to_all(parts.astype(BF), SLAB, 0, 0, tiled=True)
        return jnp.sum(got.astype(F32), axis=0)
    half = parts.shape[1] // 2
    four = parts[:4] + lax.ppermute(parts[4:].astype(BF), "c", SWAP).astype(F32)
    top, low = four[:, :half], four[:, half:]
    got_x = lax.ppermute(top[1::2].astype(BF), "x", SWAP).astype(F32)
    got_y = lax.ppermute(low[2:].astype(BF), "y", SWAP).astype(F32)
    top = top[0::2] + got_x
    low = low[:2] + got_y
    end_top = top[0] + lax.ppermute(top[1].astype(BF), "y", SWAP).astype(F32)
    end_low = low[0] + lax.ppermute(low[1].astype(BF), "x", SWAP).astype(F32)
    return jnp.concatenate([end_top, end_low])


def line_reduce(parts, along):
    me = lax.axis_index(ZZ)
    total = lax.dynamic_index_in_dim(parts, me, 0, keepdims=False)
    narrow = parts.astype(BF)
    for hop in range(1, along):
        piece = lax.dynamic_index_in_dim(narrow, (me + hop) % along, 0, keepdims=False)
        moves = [(at, (at + hop) % along) for at in range(along)]
        total = total + lax.ppermute(piece, ZZ, moves).astype(F32)
    return total


def split_two(values):
    high = values.astype(BF)
    return high, (values - high.astype(F32)).astype(BF)


def local(
    hidden_in,
    doc_start,
    qkv_master,
    out_master,
    up_master,
    down_master,
    norm1_gain,
    norm1_bias,
    norm2_gain,
    norm2_bias,
    grad_out,
    sizes,
):
    repeats, along_part, wide = sizes
    rows, width = hidden_in.shape[1:]
    shards = repeats * HEADS
    along = repeats * along_part
    slab = 4 * wide
    devices = shards * wide
    total = shards * rows
    half = rows // 2
    wrows = qkv_master.shape[0]
    triple = 3 * HD
    part = lax.axis_index("r")
    core = lax.axis_index("c").astype(jnp.int32)[None]
    flat = lax.axis_index(ALL)

    residual = hidden_in[0].astype(F32)
    norm_in, normed_one, spread_one = layer_norm(residual, norm1_gain, norm1_bias)
    norm_own = ring_gather(norm_in.astype(BF), ("r", "z", "y"), along)
    norm_oth = lax.ppermute(norm_own, "c", SWAP)

    w_qkv_own = qkv_master.astype(BF)
    by_head = w_qkv_own.reshape(wrows, 3, HEADS, HD).transpose(2, 0, 1, 3).reshape(HEADS, wrows * triple)
    by_head = jnp.concatenate(
        [by_head, jnp.broadcast_to(doc_start.astype(BF), (HEADS, rows))], axis=1
    )
    to_all = jnp.broadcast_to(
        by_head[None, :, None], (repeats, HEADS, wide, by_head.shape[1])
    ).reshape(devices, -1)
    from_all = lax.all_to_all(to_all, ALL, 0, 0, tiled=True)
    w_head = from_all[:, : wrows * triple].reshape(width, triple)
    flags = lax.dynamic_index_in_dim(
        from_all[:, wrows * triple :].reshape(shards, wide, rows), lax.axis_index("x"), 1, False
    )
    flags = jnp.concatenate([flags[:, :half], flags[::-1, half:]])
    marks = jnp.where(
        flags > 0.5, jnp.arange(total, dtype=jnp.int32).reshape(2 * shards, half), -1
    )
    inner = jnp.arange(half)
    within = jnp.max(
        jnp.where(inner[None, :, None] >= inner[None, None, :], marks[:, None, :], -1), axis=-1
    )
    outer = jnp.arange(2 * shards)
    before = jnp.max(
        jnp.where(outer[:, None] > outer[None, :], jnp.max(marks, axis=-1)[None, :], -1), axis=-1
    )
    begin = jnp.maximum(within, before[:, None]).reshape(total // TILE, TILE)
    low = begin[:, 0] // TILE

    w_out = lax.all_gather(out_master.astype(BF), ALL, axis=0, tiled=True)
    up_own = up_master.astype(BF)
    ffn = up_master.shape[1] // devices
    w_up = up_own.reshape(wrows, along, slab, ffn).transpose(2, 0, 1, 3).reshape(slab, wrows, along * ffn)
    w_up = lax.all_to_all(w_up, SLAB, 0, 0, tiled=True).reshape(slab * wrows, along * ffn)
    w_up = lax.all_gather(w_up, ZZ, axis=0, tiled=True)
    w_down = lax.all_gather(down_master.astype(BF), ZZ, axis=0, tiled=True)
    w_qkv = lax.all_gather(w_qkv_own, ALL, axis=0, tiled=True)
    grad_b = grad_out[0]
    grad_slab = slab_gather(grad_b, wide).reshape(slab * rows, width)

    tokens = jax.ShapeDtypeStruct((total, HD), BF)
    att, out_t, lse, query, keys, values = kernel_call(
        forward_kernel,
        (low, core),
        (norm_own, norm_oth, w_head, begin),
        [
            jax.ShapeDtypeStruct((shards, rows, HD), BF),
            jax.ShapeDtypeStruct((HD, total), F32),
            jax.ShapeDtypeStruct((total // TILE, TILE), F32),
            tokens,
            tokens,
            tokens,
        ],
        [pltpu.VMEM((HD, total), BF)],
        2 * total * width * triple,
    )

    def to_tokens(array):
        mine = lax.dynamic_slice_in_dim(array, part * HEADS, HEADS, 0) if repeats > 1 else array
        return lax.all_to_all(mine, PART, 0, 0, tiled=True)

    attended_b = to_tokens(att).transpose(1, 0, 2).reshape(rows, width)
    mid = residual + jnp.dot(attended_b, w_out, preferred_element_type=F32)
    norm_mid, normed_two, spread_two = layer_norm(mid, norm2_gain, norm2_bias)
    mid_slab = slab_gather(norm_mid.astype(BF), wide).reshape(slab * rows, width)

    up = jnp.dot(mid_slab, w_up, preferred_element_type=F32)
    value, slope = gelu_both(up)
    act_b = value.astype(BF)
    act_delta = dot(grad_slab, w_down, ((1,), (1,)))
    up_delta = (act_delta * slope).astype(BF)
    mid_norm_delta = slab_scatter(
        dot(up_delta, w_up, ((1,), (1,))).reshape(slab, rows, width), wide
    )
    layer_out = mid + slab_scatter(
        jnp.dot(act_b, w_down, preferred_element_type=F32).reshape(slab, rows, width), wide
    )
    down_part = dot(act_b, grad_slab, ((0,), (0,)))
    up_part = dot(mid_slab, up_delta, ((0,), (0,)))
    up_sum = jnp.sum(up_delta.astype(F32), axis=0)

    mid_delta = grad_b.astype(F32) + norm_back(mid_norm_delta, normed_two, spread_two, norm2_gain)
    mid_delta_b = mid_delta.astype(BF)
    attended_delta = dot(mid_delta_b, w_out, ((1,), (1,))).astype(BF)
    dout = lax.all_to_all(
        attended_delta.reshape(rows, HEADS, HD).transpose(1, 0, 2), PART, 0, 0, tiled=True
    )
    if repeats > 1:
        dout = lax.all_gather(dout, "r", axis=0, tiled=True)
    out_part = dot(attended_b, mid_delta_b, ((0,), (0,)))
    out_grad = lax.psum_scatter(
        out_part.astype(BF), ALL, scatter_dimension=0, tiled=True
    ).astype(F32)

    down_grad = line_reduce(down_part.reshape(along, ffn, width), along)

    def with_sums(array, sums):
        high, low_ = split_two(sums)
        shape = array.shape[:-2] + (1, array.shape[-1])
        return jnp.concatenate(
            [array, jnp.broadcast_to(high.astype(F32), shape), jnp.broadcast_to(low_.astype(F32), shape)],
            axis=-2,
        )

    up_ext = line_reduce(
        with_sums(up_part.reshape(along, slab, wrows, along * ffn), up_sum), along
    )
    up_sum = up_ext[0, wrows] + up_ext[0, wrows + 1]
    up_ext = with_sums(up_ext[:, :wrows], up_sum)
    up_ext = lax.all_to_all(up_ext.astype(BF), SLAB, 0, 0, tiled=True).astype(F32)
    up_ext = up_ext.reshape(slab, wrows + 2, along, ffn).transpose(1, 2, 0, 3).reshape(wrows + 2, -1)

    def owner_rows(array):
        return lax.dynamic_slice_in_dim(array, flat * wrows, wrows, 0)

    def norm_grads(own, ext, gain, bias):
        wide_own = own.astype(F32)
        grad = ext[:wrows]
        sums = ext[wrows] + ext[wrows + 1]
        bias_grad = jnp.sum(wide_own * sums[None], axis=1)
        gain_grad = (jnp.sum(wide_own * grad, axis=1) - owner_rows(bias) * bias_grad) / owner_rows(gain)
        return grad, gain_grad, bias_grad

    up_grad, gain_two, bias_two = norm_grads(up_own, up_ext, norm2_gain, norm2_bias)

    to_shards, to_norm, sums_one = kernel_call(
        backward_kernel,
        (low, core),
        (query, keys, values, out_t, lse, begin, dout),
        [
            jax.ShapeDtypeStruct((shards, rows, triple), BF),
            jax.ShapeDtypeStruct((2, shards // 2, rows, triple), BF),
            jax.ShapeDtypeStruct((1, triple), F32),
        ],
        [
            pltpu.VMEM((total, HD), BF),
            pltpu.VMEM((HD, total), BF),
            pltpu.VMEM((total, HD), F32),
            pltpu.VMEM((total, HD), F32),
            pltpu.VMEM((total, HD), F32),
        ],
        10 * total * total * HD // 2,
    )
    delta = to_tokens(to_shards).reshape(HEADS, rows, 3, HD).transpose(1, 2, 0, 3).reshape(rows, 3 * width)
    in_norm_delta = dot(delta, w_qkv, ((1,), (1,)))
    grad_in = (
        mid_delta + norm_back(in_norm_delta, normed_one, spread_one, norm1_gain)
    ).astype(BF)

    flat_rows = (total // 2, width)
    qkv_part = dot(norm_own.reshape(flat_rows), to_norm[0].reshape(total // 2, triple), ((0,), (0,)))
    qkv_part += dot(norm_oth.reshape(flat_rows), to_norm[1].reshape(total // 2, triple), ((0,), (0,)))
    qkv_part = qkv_part.reshape(repeats, HEADS, wide, wrows, triple)
    qkv_part = lax.dynamic_index_in_dim(qkv_part, part, 0, False)
    ext = with_sums(qkv_part, sums_one[0])
    if wide == 2:
        side = lax.axis_index("x")
        mine = lax.dynamic_index_in_dim(ext, side, 1, False)
        other = lax.dynamic_index_in_dim(ext, 1 - side, 1, False)
        ext = mine + lax.ppermute(other.astype(BF), "x", SWAP).astype(F32)
    else:
        ext = jnp.sum(lax.all_to_all(ext.astype(BF), "x", 1, 1, tiled=True).astype(F32), axis=1)
    ext = with_sums(ext[:, :wrows], ext[0, wrows] + ext[0, wrows + 1])
    ext = lax.all_to_all(ext.astype(BF), PART, 0, 0, tiled=True).astype(F32)
    ext = ext.reshape(HEADS, wrows + 2, 3, HD).transpose(1, 2, 0, 3).reshape(wrows + 2, -1)
    qkv_grad, gain_one, bias_one = norm_grads(w_qkv_own, ext, norm1_gain, norm1_bias)

    return (
        layer_out.astype(BF)[None],
        grad_in[None],
        qkv_grad,
        out_grad,
        up_grad,
        down_grad,
        gain_one,
        bias_one,
        gain_two,
        bias_two,
    )


def solution(mesh):
    ctx, wide = mesh.shape["ctx"], mesh.shape["wt"]
    repeats, along = ctx // HEADS, HEADS // 4
    grid = Mesh(mesh.devices.reshape(repeats, along, 2, 2, wide), ALL)
    tokens, weights = P("x", CTX, None), P(ALL, None)
    return jax.shard_map(
        partial(local, sizes=(repeats, along, wide)),
        mesh=grid,
        in_specs=(tokens, P("x", CTX)) + (weights,) * 4 + (P(),) * 4 + (tokens,),
        out_specs=(tokens, tokens) + (weights,) * 4 + (P(ALL),) * 4,
        check_vma=False,
    )
```

```python
from functools import partial

import jax
import jax.numpy as jnp
import numpy as np
from jax import lax
from jax.experimental import pallas as pl
from jax.experimental.pallas import tpu as pltpu
from jax.sharding import Mesh
from jax.sharding import PartitionSpec as P

HEADS = 16
HD = 64
TRIPLE = 3 * HD
EPS = 1e-05
FAR = -1e30
TILE = 256
TEAM = 8
BF = jnp.bfloat16
F32 = jnp.float32
ALL = ("r", "zh", "zl", "y", "c", "x")
CTX = ("r", "zh", "zl", "y", "c")
PART = ("zh", "zl", "y", "c")
CHIPS = ("r", "zh", "zl", "y")
TP = ("zl", "y", "c")
GROUP = ("r", "zh", "x")
SWAP = [(0, 1), (1, 0)]
NN = ((1,), (0,))
NT = ((1,), (1,))
TN = ((0,), (0,))


def dot(one, two, dims):
    return lax.dot_general(one, two, (dims, ((), ())), preferred_element_type=F32)


def normalise(rows):
    centred = rows - jnp.mean(rows, axis=-1, keepdims=True)
    spread = lax.rsqrt(jnp.mean(centred * centred, axis=-1, keepdims=True) + EPS)
    return centred * spread, spread


def norm_back(grad, normed, spread, gain):
    scaled = grad * gain
    inner = (
        scaled
        - jnp.mean(scaled, axis=-1, keepdims=True)
        - normed * jnp.mean(scaled * normed, axis=-1, keepdims=True)
    )
    return inner * spread


def gelu_both(up):
    root = 0.7978845608028654
    square = up * up
    inner = jnp.tanh(root * up * (1.0 + 0.044715 * square))
    plus = 0.5 * (1.0 + inner)
    slope = plus + 0.5 * up * (1.0 - inner * inner) * root * (1.0 + 3.0 * 0.044715 * square)
    return up * plus, slope


def block_home(block, shards):
    return (block, 0) if block < shards else (2 * shards - 1 - block, 1)


def split_two(values):
    high = values.astype(BF)
    return high, (values - high.astype(F32)).astype(BF)


def after(array, *others):
    return lax.optimization_barrier((array, *others))[0]


def call(
    body, arrays, outs, scratch=(), smem=0, smem_outs=(), flops=1 << 24, moved=1 << 21, limit=12, free=False
):
    vector = pl.BlockSpec() if free else pl.BlockSpec(memory_space=pltpu.VMEM)
    scalar = pl.BlockSpec(memory_space=pltpu.SMEM)
    return pl.pallas_call(
        body,
        out_shape=[jax.ShapeDtypeStruct(shape, kind) for shape, kind in outs],
        in_specs=[scalar] * smem + [vector] * (len(arrays) - smem),
        out_specs=[scalar if at in smem_outs else vector for at in range(len(outs))],
        scratch_shapes=[pltpu.VMEM(shape, kind) for shape, kind in scratch],
        compiler_params=pltpu.CompilerParams(vmem_limit_bytes=limit << 20),
        cost_estimate=pl.CostEstimate(flops=flops, bytes_accessed=moved, transcendentals=0),
    )(*arrays)


def first_norm_kernel(hidden_ref, gain_ref, bias_ref, out_ref):
    normed, _ = normalise(hidden_ref[...].astype(F32))
    out_ref[...] = (normed * gain_ref[...] + bias_ref[...]).astype(BF)


def cast_kernel(qkv_ref, out_ref, up_ref, down_ref, qkv_b, out_b, up_b, down_b, *, runs):
    qkv_b[...] = qkv_ref[...].astype(BF)
    out_b[...] = out_ref[...].astype(BF)
    piece = up_b.shape[2] // runs
    for mate in range(TEAM):
        for at in range(runs):
            first = (at * TEAM + mate) * piece
            up_b[mate, :, at * piece : (at + 1) * piece] = up_ref[:, first : first + piece].astype(BF)
    rows, half = down_ref.shape[0], down_ref.shape[1] // 2
    down_b[:rows] = down_ref[:, :half].astype(BF)
    down_b[rows:] = down_ref[:, half:].astype(BF)


def heads_kernel(qkv_ref, start_ref, out_ref):
    rows = qkv_ref.shape[0]
    half = rows // 2
    width = HEADS * HD
    starts = start_ref[...].astype(F32).astype(BF)
    spare = out_ref.shape[1] - rows - half
    for head in range(HEADS):
        parts = [qkv_ref[:, at * width + head * HD : at * width + (head + 1) * HD] for at in range(3)]
        out_ref[head, :rows] = jnp.concatenate(parts[:2], axis=1)
        out_ref[head, rows : rows + half] = jnp.concatenate([parts[2][:half], parts[2][half:]], axis=1)
        out_ref[head, rows + half :] = jnp.broadcast_to(starts, (spare, 2 * HD))


def forward_kernel(
    core_ref, own_ref, oth_ref, packed_ref,
    att_ref, ot_ref, lse_ref, begin_ref, lo_ref, q_ref, k_ref, v_ref,
    vt_ref, w_ref,
    *, wrows,
):
    shards, half, _ = att_ref.shape
    rows = 2 * half
    total = shards * rows
    blocks = 2 * shards
    core = core_ref[0]
    whalf = wrows // 2
    for at in range(shards):
        w_ref[at * wrows : (at + 1) * wrows, : 2 * HD] = packed_ref[at, :wrows]
        pair = packed_ref[at, wrows : wrows + whalf]
        w_ref[at * wrows : (at + 1) * wrows, 2 * HD :] = jnp.concatenate(
            [pair[:, :HD], pair[:, HD:]], axis=0
        )
    flags = []
    for block in range(blocks):
        shard, side = block_home(block, shards)
        row = packed_ref[shard, wrows + whalf : wrows + whalf + 1].astype(F32)
        flags.append(row[:, side * half : (side + 1) * half])
    flags = jnp.concatenate(flags, axis=0)
    spots = half * lax.broadcasted_iota(jnp.int32, flags.shape, 0) + lax.broadcasted_iota(
        jnp.int32, flags.shape, 1
    )
    marks = jnp.where(flags > 0.5, spots.astype(F32), -1.0)
    lane = lax.broadcasted_iota(jnp.int32, marks.shape, 1)
    hop = 1
    while hop < half:
        moved = jnp.concatenate([marks[:, half - hop :], marks[:, : half - hop]], axis=1)
        marks = jnp.maximum(marks, jnp.where(lane >= hop, moved, -1.0))
        hop *= 2
    last = jnp.broadcast_to(marks[:, half - 1 :], marks.shape)
    line = lax.broadcasted_iota(jnp.int32, marks.shape, 0)
    hop = 1
    while hop < blocks:
        moved = jnp.concatenate([last[blocks - hop :], last[: blocks - hop]], axis=0)
        last = jnp.maximum(last, jnp.where(line >= hop, moved, -1.0))
        hop *= 2
    moved = jnp.concatenate([last[blocks - 1 :], last[: blocks - 1]], axis=0)
    begins = jnp.maximum(marks, jnp.where(line >= 1, moved, -1.0))
    group = TILE // half
    for tile in range(total // TILE):
        row = jnp.concatenate([begins[tile * group + at : tile * group + at + 1] for at in range(group)], axis=1)
        begin_ref[tile : tile + 1, :] = row.astype(jnp.int32)
        lo_ref[tile] = jnp.min(row).astype(jnp.int32) // TILE
    for which, ref in ((0, own_ref), (1, oth_ref)):
        all_made = dot(ref[...].reshape(total // 2, -1), w_ref[...], NN).astype(BF)
        for chip in range(shards // 2):
            made = all_made[chip * rows : (chip + 1) * rows]
            shard = 2 * chip + (core if which == 0 else 1 - core)
            one = pl.multiple_of(shard * half, half)
            two = pl.multiple_of((blocks - 1 - shard) * half, half)
            scaled = made[:, :HD] * BF(HD**-0.5)
            for at, part in ((one, slice(0, half)), (two, slice(half, rows))):
                q_ref[pl.ds(at, half), :] = scaled[part]
                k_ref[pl.ds(at, half), :] = made[part, HD : 2 * HD]
                v_ref[pl.ds(at, half), :] = made[part, 2 * HD :]
    for at in range(0, total, 128):
        vt_ref[:, at : at + 128] = v_ref[at : at + 128, :].astype(F32).T.astype(BF)
    for tile in range(total // TILE):
        query = q_ref[tile * TILE : (tile + 1) * TILE, :]
        begin = begin_ref[tile : tile + 1, :]
        query_pos = tile * TILE + lax.broadcasted_iota(jnp.int32, (TILE, TILE), 1)

        def step(at, state):
            top, sums, accum = state
            first = pl.multiple_of(at * TILE, TILE)
            scores = dot(k_ref[pl.ds(first, TILE), :], query, NT)
            key_pos = first + lax.broadcasted_iota(jnp.int32, (TILE, TILE), 0)
            scores = jnp.where((key_pos >= begin) & (key_pos <= query_pos), scores, FAR)
            higher = jnp.maximum(top, jnp.max(scores, axis=0, keepdims=True))
            weights = jnp.exp(scores - higher)
            factor = jnp.exp(top - higher)
            sums = sums * factor + jnp.sum(weights, axis=0, keepdims=True)
            accum = accum * factor + dot(vt_ref[:, pl.ds(first, TILE)], weights.astype(BF), NN)
            return higher, sums, accum

        top, sums, accum = lax.fori_loop(
            lo_ref[tile],
            tile + 1,
            step,
            (jnp.full((1, TILE), FAR, F32), jnp.zeros((1, TILE), F32), jnp.zeros((HD, TILE), F32)),
        )
        out = accum / sums
        ot_ref[:, tile * TILE : (tile + 1) * TILE] = out
        lse_ref[tile : tile + 1, :] = top + jnp.log(sums)
        turned = out.T.astype(BF)
        for piece in range(group):
            shard, side = block_home(tile * group + piece, shards)
            att_ref[shard, :, side * HD : (side + 1) * HD] = turned[piece * half : (piece + 1) * half]


def place_rows(spots_ref, pieces_ref, out_ref):
    count, rows, _ = pieces_ref.shape
    for at in range(count):
        first = spots_ref[at] * rows
        out_ref[pl.ds(pl.multiple_of(first, rows), rows), :] = pieces_ref[at]


def middle_kernel(*refs, placed):
    if placed:
        att_ref, hidden_ref, w_ref, gain_ref, bias_ref, att_out, mid_out, norm_out = refs
    else:
        spots_ref, att_ref, hidden_ref, pieces_ref, gain_ref, bias_ref, att_out, mid_out, norm_out, w_ref = refs
        place_rows(spots_ref, pieces_ref, w_ref)
    half = att_ref.shape[1]
    for head in range(0, HEADS, 2):
        for side in range(2):
            lanes = slice(side * HD, (side + 1) * HD)
            att_out[side * half : (side + 1) * half, head * HD : (head + 2) * HD] = jnp.concatenate(
                [att_ref[head, :, lanes], att_ref[head + 1, :, lanes]], axis=1
            )
    mid = hidden_ref[...].astype(F32) + dot(att_out[...], w_ref[...], NN)
    mid_out[...] = mid
    normed, _ = normalise(mid)
    norm_out[...] = (normed * gain_ref[...] + bias_ref[...]).astype(BF)


def feed_kernel(*refs, count, wide):
    groups_ref, *refs = refs
    mids, grads = refs[:count], refs[count : 2 * count]
    (weights_ref, lay_keep, lay_send, mnd_keep, mnd_send, mid_out, act_out, delta_out, up_ref, down_ref) = refs[
        2 * count :
    ]
    groups, packed, _ = weights_ref.shape
    mine = packed // 2
    own = mine // TEAM
    ffn = mine // 2
    width = mid_out.shape[1]
    for at in range(groups):
        if own % 16 == 0:
            group = groups_ref[at]
            high, x = group // wide, group % wide
        else:
            group, high, x = at, at // wide, at % wide
        for mate in range(TEAM):
            first = ((high * TEAM + mate) * wide + x) * own
            if own % 16 == 0:
                first = pl.multiple_of(first, own)
            up_ref[pl.ds(first, own), :] = weights_ref[at, mate * own : (mate + 1) * own, :]
        first = group * ffn
        if own % 16 == 0:
            first = pl.multiple_of(first, ffn)
        down_ref[pl.ds(first, ffn), : width // 2] = weights_ref[at, mine : mine + ffn, :]
        down_ref[pl.ds(first, ffn), width // 2 :] = weights_ref[at, mine + ffn :, :]
    at = 0
    for ref in mids:
        mid_out[at : at + ref.shape[0], :] = ref[...]
        at += ref.shape[0]
    total = at
    run = 256 if total % 256 == 0 else total
    at = 0
    spots = []
    for ref in grads:
        spots.append((at, ref))
        at += ref.shape[0]
    half = total // 2
    for first in range(0, total, run):
        here = slice(first, first + run)
        up = dot(mid_out[here, :], up_ref[...], NN)
        value, slope = gelu_both(up)
        act = value.astype(BF)
        act_out[here, :] = act
        inside = [
            ref[max(first - spot, 0) : min(first + run - spot, ref.shape[0]), :]
            for spot, ref in spots
            if spot < first + run and spot + ref.shape[0] > first
        ]
        grad = inside[0] if len(inside) == 1 else jnp.concatenate(inside, axis=0)
        delta = (dot(grad, down_ref[...], NT) * slope).astype(BF)
        delta_out[here, :] = delta
        back = dot(delta, up_ref[...], NT)
        fore = dot(act, down_ref[...], NN)
        if first < half:
            mnd_keep[here, :] = back
            lay_keep[here, :] = fore
        else:
            there = slice(first - half, first - half + run)
            mnd_send[there, :] = back.astype(BF)
            lay_send[there, :] = fore.astype(BF)


def turn_kernel(
    keep_top, got_top, keep_low, got_low, grad_ref, mid_ref, w_ref, gain_ref, delta_out, bf_out, packed_out
):
    mnd = jnp.concatenate(
        [keep_top[...] + got_top[...].astype(F32), keep_low[...] + got_low[...].astype(F32)], axis=0
    )
    normed, spread = normalise(mid_ref[...])
    delta = grad_ref[...].astype(F32) + norm_back(mnd, normed, spread, gain_ref[...])
    delta_out[...] = delta
    narrow = delta.astype(BF)
    bf_out[...] = narrow
    back = dot(narrow, w_ref[...], NT).astype(BF)
    half = packed_out.shape[1]
    for head in range(HEADS):
        cols = slice(head * HD, (head + 1) * HD)
        packed_out[head] = jnp.concatenate([back[:half, cols], back[half:, cols]], axis=1)


def out_grad_kernel(att_ref, delta_ref, out_ref, *, wide):
    _, _, _, _, highs, rows, _ = out_ref.shape
    turned = att_ref[...].astype(F32).T.astype(BF)
    part = dot(turned, delta_ref[...], NN).astype(BF)
    for high in range(highs):
        for mate in range(TEAM):
            first = (high * TEAM + mate) * 2 * rows
            for side in range(2):
                out_ref[mate % 2, side, mate // 4, mate // 2 % 2, high] = part[
                    first + side * rows : first + (side + 1) * rows
                ]


def up_pack_kernel(part_ref, delta_ref, out_ref, sum_ref):
    wide, highs, _, tall, cols = out_ref.shape
    rows = tall - 8
    sums = jnp.sum(delta_ref[...].astype(F32), axis=0, keepdims=True)
    sum_ref[...] = sums
    tail = sum_lines(sums)
    for x in range(wide):
        for high in range(highs):
            for mate in range(TEAM):
                first = ((high * TEAM + mate) * wide + x) * rows
                out_ref[x, high, mate, :rows] = part_ref[first : first + rows, :].astype(BF)
                out_ref[x, high, mate, rows:] = tail


def sum_lines(sums):
    high, low = split_two(sums)
    line = lax.broadcasted_iota(jnp.int32, (8, sums.shape[1]), 0)
    return jnp.where(line == 0, high.astype(F32), jnp.where(line == 1, low.astype(F32), 0.0)).astype(BF)


def add_sums_kernel(own_ref, got_ref, out_ref):
    rows = out_ref.shape[-2] - 8
    for at in range(out_ref.shape[0]):
        total = own_ref[at].astype(F32) + got_ref[at].astype(F32)
        out_ref[at, :rows] = total[:rows].astype(BF)
        out_ref[at, rows:] = sum_lines(total[rows : rows + 1] + total[rows + 1 : rows + 2])


def norm_grads(own, grad, sums, gain, bias):
    bias_grad = jnp.sum(own * sums, axis=1, keepdims=True)
    gain_grad = (jnp.sum(own * grad, axis=1, keepdims=True) - bias * bias_grad) / gain
    return gain_grad, bias_grad


def up_end_kernel(parts_ref, own_ref, gain_ref, bias_ref, grad_out, gain_out, bias_out, *, runs):
    rows = own_ref.shape[0]
    piece = parts_ref.shape[2] // runs
    lines = []
    for at in range(runs):
        for mate in range(TEAM):
            first = (at * TEAM + mate) * piece
            part = parts_ref[mate, :, at * piece : (at + 1) * piece].astype(F32)
            grad_out[:, first : first + piece] = part[:rows]
            lines.append(part[rows : rows + 1] + part[rows + 1 : rows + 2])
    own = own_ref[...].astype(BF).astype(F32)
    gain_out[...], bias_out[...] = norm_grads(
        own, grad_out[...], jnp.concatenate(lines, axis=1), gain_ref[...], bias_ref[...]
    )


def qkv_end_kernel(parts_ref, own_ref, gain_ref, bias_ref, grad_out, gain_out, bias_out):
    rows = own_ref.shape[0]
    half = rows // 2
    width = HEADS * HD
    body = rows + half
    for head in range(0, HEADS, 2):
        for at in range(2):
            lanes = slice(at * HD, (at + 1) * HD)
            grad_out[:, at * width + head * HD : at * width + (head + 2) * HD] = jnp.concatenate(
                [parts_ref[head, :rows, lanes], parts_ref[head + 1, :rows, lanes]], axis=1
            ).astype(F32)
        for side in range(2):
            lanes = slice(side * HD, (side + 1) * HD)
            grad_out[side * half : (side + 1) * half, 2 * width + head * HD : 2 * width + (head + 2) * HD] = (
                jnp.concatenate(
                    [parts_ref[head, rows:body, lanes], parts_ref[head + 1, rows:body, lanes]], axis=1
                ).astype(F32)
            )
    lines = [[], [], []]
    for head in range(HEADS):
        tail = parts_ref[head, body:, :].astype(F32)
        pair = tail[0:1] + tail[1:2]
        lines[0].append(pair[:, :HD])
        lines[1].append(pair[:, HD:])
        lines[2].append(tail[2:3, :HD] + tail[2:3, HD:])
    own = own_ref[...].astype(BF).astype(F32)
    gain_out[...], bias_out[...] = norm_grads(
        own, grad_out[...], jnp.concatenate(lines[0] + lines[1] + lines[2], axis=1), gain_ref[...], bias_ref[...]
    )


def backward_kernel(
    core_ref, lo_ref, q_ref, k_ref, v_ref, ot_ref, lse_ref, begin_ref, do_ref,
    da_ref, dn_ref, sum_ref,
    dop_ref, kt_ref, dq_ref, dk_ref, dv_ref,
):
    shards, half, _ = do_ref.shape
    rows = 2 * half
    total = shards * rows
    core = core_ref[0]
    for block in range(2 * shards):
        shard, side = block_home(block, shards)
        dop_ref[block * half : (block + 1) * half, :] = do_ref[shard, :, side * HD : (side + 1) * HD]
    for at in range(0, total, 128):
        kt_ref[:, at : at + 128] = k_ref[at : at + 128, :].astype(F32).T.astype(BF)
    dk_ref[...] = jnp.zeros_like(dk_ref)
    dv_ref[...] = jnp.zeros_like(dv_ref)
    for tile in range(total // TILE):
        here = slice(tile * TILE, (tile + 1) * TILE)
        query = q_ref[here, :]
        dout = dop_ref[here, :]
        begin = begin_ref[tile : tile + 1, :]
        lse = lse_ref[tile : tile + 1, :]
        row_dot = jnp.sum(dout.astype(F32).T * ot_ref[:, here], axis=0, keepdims=True)
        query_pos = tile * TILE + lax.broadcasted_iota(jnp.int32, (TILE, TILE), 1)

        def step(at, accum):
            first = pl.multiple_of(at * TILE, TILE)
            there = pl.ds(first, TILE)
            scores = dot(k_ref[there, :], query, NT)
            key_pos = first + lax.broadcasted_iota(jnp.int32, (TILE, TILE), 0)
            allowed = (key_pos >= begin) & (key_pos <= query_pos)
            probs = jnp.where(allowed, jnp.exp(scores - lse), 0.0)
            dprobs = dot(v_ref[there, :], dout, NT)
            delta = (probs * (dprobs - row_dot)).astype(BF)
            dv_ref[there, :] += dot(probs.astype(BF), dout, NN)
            dk_ref[there, :] += dot(delta, query, NN)
            return accum + dot(kt_ref[:, there], delta, NN)

        accum = lax.fori_loop(lo_ref[tile], tile + 1, step, jnp.zeros((HD, TILE), F32))
        dq_ref[here, :] = (accum * HD**-0.5).T
    sums = jnp.zeros((1, TRIPLE), F32)
    for block in range(2 * shards):
        shard, side = block_home(block, shards)
        at = slice(block * half, (block + 1) * half)
        pair = jnp.concatenate([dq_ref[at, :], dk_ref[at, :]], axis=1).astype(BF)
        last = dv_ref[at, :].astype(BF)
        da_ref[shard, side * half : (side + 1) * half, :] = pair
        da_ref[shard, rows : rows + half, side * HD : (side + 1) * HD] = last
        place = (core + shard) % 2
        to = slice(side * half, (side + 1) * half)
        joined = jnp.concatenate([pair, last], axis=1)
        dn_ref[place, shard // 2, to, :] = joined
        sums = sums + jnp.sum(joined.astype(F32), axis=0, keepdims=True)
    sum_ref[...] = sums


def qkv_lines(pair, last):
    line = lax.broadcasted_iota(jnp.int32, (8, 2 * HD), 0)
    high, low = split_two(pair)
    both = jnp.concatenate(split_two(last), axis=1)
    lines = jnp.where(line == 0, high.astype(F32), jnp.where(line == 1, low.astype(F32), both.astype(F32)))
    return lines.astype(BF)


def qkv_grad_kernel(part_ref, own_ref, oth_ref, dn_ref, sum_ref, out_ref, acc_ref, *, repeats):
    chips = own_ref.shape[0]
    total = None
    for which, ref in ((0, own_ref), (1, oth_ref)):
        for chip in range(chips):
            turned = dn_ref[which, chip].astype(F32).T.astype(BF)
            step = dot(turned, ref[chip], NN)
            total = step if total is None else total + step
    acc_ref[...] = total.T
    wide, owners, tall, _ = out_ref.shape
    rows = (tall - 8) * 2 // 3
    half = rows // 2
    sums = sum_ref[...]
    lines = qkv_lines(sums[:, : 2 * HD], sums[:, 2 * HD :])

    def write(base):
        for owner in range(owners):
            for x in range(wide):
                first = base + (owner * wide + x) * rows
                grad = acc_ref[first : first + rows, :]
                out_ref[x, owner, :rows] = grad[:, : 2 * HD].astype(BF)
                out_ref[x, owner, rows : rows + half] = jnp.concatenate(
                    [grad[:half, 2 * HD :], grad[half:, 2 * HD :]], axis=1
                ).astype(BF)
                out_ref[x, owner, rows + half :] = lines

    if repeats == 1:
        write(0)
    else:
        for at in range(repeats):
            pl.when(part_ref[0] == at)(partial(write, at * owners * wide * rows))


def qkv_add_kernel(own_ref, got_ref, out_ref):
    body = out_ref.shape[1] - 8
    for at in range(out_ref.shape[0]):
        total = own_ref[at].astype(F32) + got_ref[at].astype(F32)
        out_ref[at, :body] = total[:body].astype(BF)
        tail = total[body:]
        out_ref[at, body:] = qkv_lines(tail[0:1] + tail[1:2], tail[2:3, :HD] + tail[2:3, HD:])


def last_kernel(*refs, placed):
    if placed:
        delta_ref, mid_delta_ref, hidden_ref, w_ref, gain_ref, out_ref, all_ref = refs
    else:
        spots_ref, delta_ref, mid_delta_ref, hidden_ref, pieces_ref, gain_ref, out_ref, all_ref, w_ref = refs
        place_rows(spots_ref, pieces_ref, w_ref)
    rows, width = hidden_ref.shape
    half = rows // 2
    for head in range(0, HEADS, 2):
        for at in range(2):
            lanes = slice(at * HD, (at + 1) * HD)
            all_ref[:, at * width + head * HD : at * width + (head + 2) * HD] = jnp.concatenate(
                [delta_ref[head, :rows, lanes], delta_ref[head + 1, :rows, lanes]], axis=1
            )
        for side in range(2):
            lanes = slice(side * HD, (side + 1) * HD)
            all_ref[side * half : (side + 1) * half, 2 * width + head * HD : 2 * width + (head + 2) * HD] = (
                jnp.concatenate([delta_ref[head, rows:, lanes], delta_ref[head + 1, rows:, lanes]], axis=1)
            )
    grad = dot(all_ref[...], w_ref[...], NT)
    normed, spread = normalise(hidden_ref[...].astype(F32))
    out_ref[...] = (mid_delta_ref[...] + norm_back(grad, normed, spread, gain_ref[...])).astype(BF)


def ring_gather(rows, long):
    count = 2 * long
    order = [2 * at for at in range(long)] + [2 * at + 1 for at in reversed(range(long))]
    right = [(order[at], order[(at + 1) % count]) for at in range(count)]
    left = [(two, one) for one, two in right]
    chip = lax.axis_index(CHIPS)
    along, side = chip // 2, chip % 2
    spot = jnp.where(side == 0, along, count - 1 - along)

    def chip_at(place):
        place = place % count
        return jnp.where(place < long, 2 * place, 2 * (count - 1 - place) + 1)

    def put(buffer, piece, place):
        return lax.dynamic_update_index_in_dim(buffer, piece, place, 0)

    own = put(jnp.zeros((count,) + rows.shape, rows.dtype), rows, chip)
    oth = put(jnp.zeros((count,) + rows.shape, rows.dtype), lax.ppermute(rows, "c", SWAP), chip)
    ahead = behind = rows
    hops = []
    for hop in range(1, long + 1):
        ahead = lax.ppermute(ahead, CHIPS, right)
        own = put(own, ahead, chip_at(spot - hop))
        oth = put(oth, lax.ppermute(ahead, "c", SWAP), chip_at(spot - hop))
        if hop < long:
            behind = lax.ppermute(behind, CHIPS, left)
            own = put(own, behind, chip_at(spot + hop))
            oth = put(oth, lax.ppermute(behind, "c", SWAP), chip_at(spot + hop))
        hops.append(ahead)
    return own, oth, hops


def cube_spots(order, axes, sizes):
    if any(sizes[axis] != 2 for axis in axes):
        return jnp.arange(int(np.prod([sizes[axis] for axis in axes])), dtype=jnp.int32)
    masks = [0]
    for axis in order:
        bit = 1 << (len(axes) - 1 - axes.index(axis))
        masks = masks + [mask | bit for mask in masks]
    return lax.axis_index(axes).astype(jnp.int32) ^ jnp.array(masks, jnp.int32)


def cube_gather(own, axes, order, sizes, gates=()):
    if any(sizes[axis] != 2 for axis in axes):
        return lax.all_gather(own, axes, axis=0, tiled=False)
    own = own[None]
    for at, axis in enumerate(order):
        if at < len(gates) and gates[at] is not None:
            own = after(own, gates[at])
        own = jnp.concatenate([own, lax.ppermute(own, axis, SWAP)])
    return own


def team_gather(rows):
    half = rows.shape[0] // 2
    by_z = lax.ppermute(rows, "zl", SWAP)
    by_y = lax.ppermute(rows, "y", SWAP)
    both_one = lax.ppermute(by_y[:half], "zl", SWAP)
    both_two = lax.ppermute(by_z[half:], "y", SWAP)
    chip = [rows, by_z, by_y, both_one, both_two]
    return chip + [lax.ppermute(piece, "c", SWAP) for piece in chip]


def team_scatter(keep, send):
    rows = keep.shape[0] // 4
    half = rows // 2
    got = lax.ppermute(send, "c", SWAP)
    four = (keep + got.astype(F32)).reshape(4, rows, -1)
    top, low = four[:, :half], four[:, half:]
    got_z = lax.ppermute(top[1::2].astype(BF), "zl", SWAP)
    got_y = lax.ppermute(low[2:].astype(BF), "y", SWAP)
    top = top[0::2] + got_z.astype(F32)
    low = low[:2] + got_y.astype(F32)
    end_top = lax.ppermute(top[1].astype(BF), "y", SWAP)
    end_low = lax.ppermute(low[1].astype(BF), "zl", SWAP)
    return (top[0], end_top, low[0], end_low), (got, got_z)


def pick(array, place, axis):
    return lax.dynamic_index_in_dim(array, place, axis, keepdims=False)


def halve(array, axis_name, axis):
    me = lax.axis_index(axis_name)
    got = lax.ppermute(pick(array, 1 - me, axis).astype(BF), axis_name, SWAP)
    return pick(array, me, axis).astype(F32) + got.astype(F32)


def group_reduce(array, sizes):
    if sizes["r"] == 1 and sizes["zh"] == 2 and sizes["x"] == 2:
        return halve(halve(array[0], "x", 1), "zh", 0)
    flat = array.reshape((-1,) + array.shape[3:]).astype(BF)
    return jnp.sum(lax.all_to_all(flat, GROUP, 0, 0, tiled=True).astype(F32), axis=0)


def local(
    hidden_in,
    doc_start,
    qkv_master,
    out_master,
    up_master,
    down_master,
    norm1_gain,
    norm1_bias,
    norm2_gain,
    norm2_bias,
    grad_out,
    sizes,
):
    repeats, wide = sizes["r"], sizes["x"]
    rows, width = hidden_in.shape[1:]
    half = rows // 2
    shards = repeats * HEADS
    total = shards * rows
    wrows = qkv_master.shape[0]
    ffn = down_master.shape[0]
    highs = repeats * sizes["zh"]
    cols = highs * wide * ffn
    cube = repeats == 1 and wide == 2
    every = ALL[1:] if cube else ALL
    group = GROUP[1:] if cube else GROUP
    part = lax.axis_index("r").astype(jnp.int32)
    core = lax.axis_index("c").astype(jnp.int32)[None]
    flat = lax.axis_index(ALL)
    hidden, grad_b = hidden_in[0], grad_out[0]
    gain1, bias1, gain2, bias2 = (a[None] for a in (norm1_gain, norm1_bias, norm2_gain, norm2_bias))

    def owner_rows(array):
        return lax.dynamic_slice_in_dim(array, flat * wrows, wrows, 0)[:, None]

    (norm_in,) = call(first_norm_kernel, (hidden, gain1, bias1), [((rows, width), BF)], free=True)
    qkv_b, out_b, up_b, down_b = call(
        partial(cast_kernel, runs=highs),
        (after(qkv_master, norm_in), out_master, up_master, down_master),
        [
            ((wrows, 3 * width), BF),
            ((wrows, width), BF),
            ((TEAM, wrows, cols), BF),
            ((2 * ffn, width // 2), BF),
        ],
        free=True,
    )
    norm_own, norm_oth, hops = ring_gather(norm_in, repeats * 4)

    if wide == 2:
        qkv_x = lax.ppermute(qkv_b, "x", SWAP)
        qkv_x = jnp.where(lax.axis_index("x") == 0, jnp.stack([qkv_b, qkv_x]), jnp.stack([qkv_x, qkv_b]))
    else:
        qkv_x = lax.all_gather(qkv_b, "x", axis=0, tiled=False)
    prows = wide * wrows
    (by_head,) = call(
        heads_kernel,
        (qkv_x.reshape(prows, 3 * width), doc_start),
        [((HEADS, prows * 3 // 2 + 8, 2 * HD), BF)],
    )
    packed = lax.all_to_all(by_head, PART, 0, 0, tiled=True)
    if repeats > 1:
        packed = lax.all_gather(packed, "r", axis=0, tiled=True)

    order = ("zh", "zl", "y", "x", "c")
    w_out = cube_gather(out_b, every, order, sizes, (hops[0], hops[1], hops[2], hops[3]))
    spots = cube_spots(order, every, sizes)
    up_team = lax.all_to_all(after(up_b, hops[1]), TP, 0, 0, tiled=True).reshape(TEAM * wrows, cols)
    ffn_own = jnp.concatenate([up_team, down_b.reshape(-1, cols)])

    tokens = ((total, HD), BF)
    tiles = (total // TILE, TILE)
    att, out_t, lse, begin, low, query, keys, values = call(
        partial(forward_kernel, wrows=prows),
        (core, norm_own, norm_oth, packed),
        [
            ((shards, half, 2 * HD), BF),
            ((HD, total), F32),
            (tiles, F32),
            (tiles, jnp.int32),
            (tiles[:1], jnp.int32),
            tokens,
            tokens,
            tokens,
        ],
        [((HD, total), BF), ((width, TRIPLE), BF)],
        smem=1,
        smem_outs=(4,),
        limit=12 * repeats,
        flops=2 * total * width * TRIPLE * 4,
        moved=32 << 20,
    )
    ring_end = hops[-1]
    grad_team = team_gather(after(grad_b, ring_end))
    w_ffn = cube_gather(ffn_own, group, ("zh", "x"), sizes, (ring_end, att))

    def to_tokens(array):
        mine = lax.dynamic_slice_in_dim(array, part * HEADS, HEADS, 0) if repeats > 1 else array
        return lax.all_to_all(mine, PART, 0, 0, tiled=True)

    middle_outs = [((rows, width), BF), ((rows, width), F32), ((rows, width), BF)]
    if cube:
        attended_b, mid, norm_mid, w_out = call(
            partial(middle_kernel, placed=False),
            (spots, to_tokens(att), hidden, w_out, gain2, bias2),
            middle_outs + [((width, width), BF)],
            smem=1,
        )
    else:
        w_out = w_out.reshape(width, width)
        attended_b, mid, norm_mid = call(
            partial(middle_kernel, placed=True), (to_tokens(att), hidden, w_out, gain2, bias2), middle_outs
        )

    mid_team = team_gather(norm_mid)
    many = TEAM * rows
    lay_keep, lay_send, mnd_keep, mnd_send, mid_all, act_b, up_delta = call(
        partial(feed_kernel, count=len(mid_team), wide=wide),
        (cube_spots(("zh", "x"), group, sizes), *mid_team, *grad_team, w_ffn),
        [
            ((many // 2, width), F32),
            ((many // 2, width), BF),
            ((many // 2, width), F32),
            ((many // 2, width), BF),
            ((many, width), BF),
            ((many, cols), BF),
            ((many, cols), BF),
        ],
        [((width, cols), BF), ((cols, width), BF)],
        smem=1,
        flops=8 * many * width * cols,
        moved=24 << 20,
    )
    ends, stages = team_scatter(mnd_keep, mnd_send)
    mid_delta, mid_delta_b, packed_delta = call(
        turn_kernel,
        (*ends, grad_b, mid, w_out, gain2),
        [((rows, width), F32), ((rows, width), BF), ((HEADS, half, 2 * HD), BF)],
    )
    dout = lax.all_to_all(packed_delta, PART, 0, 0, tiled=True)
    if repeats > 1:
        dout = lax.all_gather(dout, "r", axis=0, tiled=True)

    up_part = dot(mid_all, after(up_delta, stages[0]), TN)
    tall = wrows + 8
    up_part, _ = call(
        up_pack_kernel,
        (up_part, up_delta),
        [((wide, highs, TEAM, tall, cols), BF), ((1, cols), F32)],
    )
    grad_all = jnp.concatenate(grad_team)
    down_part = dot(after(act_b, stages[1]), grad_all, TN).astype(BF)
    down_part = down_part.reshape(highs, wide, ffn, width)

    if cube:
        up_own, up_got = swap_part(up_part, "x", 0)
        up_shape = (highs * TEAM, tall, cols)
        (up_mid,) = call(add_sums_kernel, (up_own.reshape(up_shape), up_got.reshape(up_shape)), [(up_shape, BF)])
        down_mid = halve(down_part, "x", 1)
        up_mid = after(up_mid.reshape(highs, TEAM, tall, cols), mid_delta)
        up_own, up_got = swap_part(up_mid, "zh", 0)
        (up_end,) = call(add_sums_kernel, (up_own, up_got), [((TEAM, tall, cols), BF)])
        down_grad = halve(after(down_mid, mid_delta), "zh", 0)
    else:
        flat_up = up_part.transpose(1, 0, 2, 3, 4).reshape(highs * wide, TEAM, tall, cols)
        up_end = jnp.sum(lax.all_to_all(flat_up, GROUP, 0, 0, tiled=True).astype(F32), axis=0).astype(BF)
        flat_down = down_part.reshape(highs * wide, ffn, width)
        down_grad = jnp.sum(lax.all_to_all(flat_down, GROUP, 0, 0, tiled=True).astype(F32), axis=0)
    up_end = lax.all_to_all(up_end, TP, 0, 0, tiled=True)
    column = ((wrows, 1), F32)
    up_grad, gain_two, bias_two = call(
        partial(up_end_kernel, runs=highs),
        (up_end, up_master, owner_rows(norm2_gain), owner_rows(norm2_bias)),
        [(up_master.shape, F32), column, column],
    )

    ends, lay_stages = team_scatter(after(lay_keep, mid_delta), after(lay_send, mid_delta))
    top, got_top, bottom, got_bottom = ends
    layer_out = mid + jnp.concatenate([top + got_top.astype(F32), bottom + got_bottom.astype(F32)])

    (out_part,) = call(
        partial(out_grad_kernel, wide=wide),
        (attended_b, mid_delta_b),
        [((2, 2, 2, 2, highs, prows // 2, width), BF)],
    )
    out_grad = reduce_out(out_part, wrows, sizes, lay_stages[0])

    w_qkv = cube_gather(qkv_b, every, order, sizes, (ring_end, att, norm_mid, stages[0], mid_delta))

    to_shards, to_norm, sums_one = call(
        backward_kernel,
        (core, low, query, keys, values, out_t, lse, begin, dout),
        [
            ((shards, rows + half, 2 * HD), BF),
            ((2, shards // 2, rows, TRIPLE), BF),
            ((1, TRIPLE), F32),
        ],
        [
            ((total, HD), BF),
            ((HD, total), BF),
            ((total, HD), F32),
            ((total, HD), F32),
            ((total, HD), F32),
        ],
        smem=2,
        limit=12 * repeats,
        flops=10 * total * total * HD,
        moved=32 << 20,
    )
    delta_heads = to_tokens(to_shards)
    if cube:
        (grad_in,) = call(
            partial(last_kernel, placed=False),
            (spots, delta_heads, mid_delta, hidden, w_qkv, gain1),
            [((rows, width), BF)],
            [((rows, 3 * width), BF), ((width, 3 * width), BF)],
            smem=1,
            limit=16,
        )
    else:
        (grad_in,) = call(
            partial(last_kernel, placed=True),
            (delta_heads, mid_delta, hidden, w_qkv.reshape(width, 3 * width), gain1),
            [((rows, width), BF)],
            [((rows, 3 * width), BF)],
        )

    tall = wrows * 3 // 2 + 8
    (qkv_part,) = call(
        partial(qkv_grad_kernel, repeats=repeats),
        (part[None], norm_own, norm_oth, to_norm, sums_one),
        [((wide, HEADS, tall, 2 * HD), BF)],
        [((width, TRIPLE), F32)],
        smem=1,
    )
    if wide == 2:
        own, got = swap_part(qkv_part, "x", 0)
        (ext,) = call(qkv_add_kernel, (own, got), [((HEADS, tall, 2 * HD), BF)])
    else:
        got = lax.all_to_all(qkv_part, "x", 0, 0, tiled=True)
        ext = got[0]
        for at in range(1, wide):
            (ext,) = call(qkv_add_kernel, (ext, got[at]), [((HEADS, tall, 2 * HD), BF)])
    ext = lax.all_to_all(ext, PART, 0, 0, tiled=True)
    qkv_grad, gain_one, bias_one = call(
        qkv_end_kernel,
        (ext, qkv_master, owner_rows(norm1_gain), owner_rows(norm1_bias)),
        [(qkv_master.shape, F32), column, column],
    )

    return (
        layer_out.astype(BF)[None],
        grad_in[None],
        qkv_grad,
        out_grad,
        up_grad,
        down_grad,
        gain_one[:, 0],
        bias_one[:, 0],
        gain_two[:, 0],
        bias_two[:, 0],
    )


def swap_part(array, axis_name, axis):
    me = lax.axis_index(axis_name)
    got = lax.ppermute(pick(array, 1 - me, axis), axis_name, SWAP)
    return pick(array, me, axis), got


def reduce_out(part, wrows, sizes, gate):
    array = halve(part, "c", 0)
    array = after(array, gate)
    top = halve(halve(array[0], "zl", 0), "y", 0)
    low = halve(halve(array[1], "y", 1), "zl", 0)
    array = jnp.stack([top, low], axis=1)
    shape = (sizes["r"], sizes["zh"], sizes["x"], wrows, part.shape[-1])
    return group_reduce(array.reshape(shape), sizes)


def solution(mesh):
    ctx, wide = mesh.shape["ctx"], mesh.shape["wt"]
    sizes = {"r": ctx // HEADS, "zh": HEADS // 8, "zl": 2, "y": 2, "c": 2, "x": wide}
    grid = Mesh(mesh.devices.reshape(tuple(sizes.values())), ALL)
    tokens, weights = P("x", CTX, None), P(ALL, None)
    return jax.shard_map(
        partial(local, sizes=sizes),
        mesh=grid,
        in_specs=(tokens, P("x", CTX)) + (weights,) * 4 + (P(),) * 4 + (tokens,),
        out_specs=(tokens, tokens) + (weights,) * 4 + (P(ALL),) * 4,
        check_vma=False,
    )
```

```python
from functools import partial

import jax
import jax.numpy as jnp
from jax import lax
from jax.experimental import pallas as pl
from jax.experimental.pallas import tpu as pltpu
from jax.sharding import Mesh
from jax.sharding import PartitionSpec as P

HEADS = 16
HD = 64
TRIPLE = 3 * HD
EPS = 1e-05
FAR = -1e30
TILE = 256
TEAM = 8
TAIL = 8
BF = jnp.bfloat16
F32 = jnp.float32
ALL = ("r", "zh", "zl", "y", "c", "x")
CTX = ("r", "zh", "zl", "y", "c")
PART = ("zh", "zl", "y", "c")
CHIPS = ("r", "zh", "zl", "y")
TP = ("zl", "y", "c")
GROUP = ("r", "zh", "x")
SWAP = [(0, 1), (1, 0)]
MASKS = [
    z * 8 + y * 4 + c * 2 + x for c in range(2) for y in range(2) for x in range(2) for z in range(4)
]
NN = ((1,), (0,))
NT = ((1,), (1,))
TN = ((0,), (0,))


def dot(one, two, dims):
    return lax.dot_general(one, two, (dims, ((), ())), preferred_element_type=F32)


def normalise(rows):
    centred = rows - jnp.mean(rows, axis=-1, keepdims=True)
    spread = lax.rsqrt(jnp.mean(centred * centred, axis=-1, keepdims=True) + EPS)
    return centred * spread, spread


def norm_back(grad, normed, spread, gain):
    scaled = grad * gain
    inner = (
        scaled
        - jnp.mean(scaled, axis=-1, keepdims=True)
        - normed * jnp.mean(scaled * normed, axis=-1, keepdims=True)
    )
    return inner * spread


def gelu_both(up):
    root = 0.7978845608028654
    square = up * up
    inner = jnp.tanh(root * up * (1.0 + 0.044715 * square))
    plus = 0.5 * (1.0 + inner)
    slope = plus + 0.5 * up * (1.0 - inner * inner) * root * (1.0 + 3.0 * 0.044715 * square)
    return up * plus, slope


def block_home(block, shards):
    return (block, 0) if block < shards else (2 * shards - 1 - block, 1)


def split_two(values):
    high = values.astype(BF)
    return high, (values - high.astype(F32)).astype(BF)


def after(array, *others):
    return lax.optimization_barrier((array, *others))[0]


class Place:
    def __init__(self, table):
        self.r, self.zh, self.zl, self.y, self.c, self.x = (table[at] for at in range(6))
        self.mate = self.zl * 4 + self.y * 2 + self.c
        self.ctx = self.zh * TEAM + self.mate

    def flat(self, wide):
        return (self.r * HEADS + self.ctx) * wide + self.x


def call(body, arrays, outs, scratch=(), smem=1, smem_outs=(), far=0, sems=0, limit=12, micros=0):
    vector = pl.BlockSpec(memory_space=pltpu.VMEM)
    scalar = pl.BlockSpec(memory_space=pltpu.SMEM)
    there = pl.BlockSpec(memory_space=pl.ANY)
    scratch = [pltpu.VMEM(shape, kind) for shape, kind in scratch]
    if sems:
        scratch.append(pltpu.SemaphoreType.DMA((sems,)))
    return pl.pallas_call(
        body,
        out_shape=[jax.ShapeDtypeStruct(shape, kind) for shape, kind in outs],
        in_specs=[scalar] * smem + [there] * far + [vector] * (len(arrays) - smem - far),
        out_specs=[scalar if at in smem_outs else vector for at in range(len(outs))],
        scratch_shapes=scratch,
        compiler_params=pltpu.CompilerParams(vmem_limit_bytes=limit << 20),
        cost_estimate=pl.CostEstimate(flops=micros * 10**9 + 1000, bytes_accessed=1 << 10, transcendentals=0),
    )(*arrays)


def start_copies(pairs, sems):
    copies = [pltpu.make_async_copy(source, target, sems.at[at]) for at, (source, target) in enumerate(pairs)]
    for copy in copies:
        copy.start()
    return copies


def first_kernel(table, hidden_ref, gain_ref, bias_ref, qkv_ref, out_ref, up_ref, down_ref, start_ref, *refs, runs):
    (
        norm_out, *heads, out_b, one_ref, two_ref, three_ref, four_ref, down_b,
        hidden_at, gain_at, bias_at, qkv_at, out_at, up_at, down_at, start_at, made_ref, sems,
    ) = refs
    ups = one_ref, two_ref, three_ref, four_ref
    place = Place(table)
    copies = start_copies(
        (
            (hidden_ref, hidden_at), (gain_ref, gain_at), (bias_ref, bias_at), (start_ref, start_at), (qkv_ref, qkv_at),
            (out_ref, out_at), (up_ref, up_at), (down_ref, down_at),
        ),
        sems,
    )
    for copy in copies[:3]:
        copy.wait()
    normed, _ = normalise(hidden_at[...].astype(F32))
    norm_out[...] = (normed * gain_at[...] + bias_at[...]).astype(BF)
    for copy in copies[3:]:
        copy.wait()
    rows = qkv_at.shape[0]
    half = rows // 2
    width = HEADS * HD
    starts = start_at[...].astype(F32).astype(BF)
    for head in range(HEADS):
        part = [qkv_at[:, at * width + head * HD : at * width + (head + 1) * HD].astype(BF) for at in range(3)]
        made_ref[head, :rows] = jnp.concatenate(part[:2], axis=1)
        made_ref[head, rows : rows + half] = jnp.concatenate([part[2][:half], part[2][half:]], axis=1)
        made_ref[head, rows + half :] = jnp.broadcast_to(starts, (TAIL, 2 * HD))
    for near in range(4):
        for far in range(4):
            heads[near][far] = made_ref[place.ctx ^ (far * 4 + near)]
    out_b[...] = out_at[...].astype(BF)
    piece = ups[0].shape[2] // runs
    for near in range(4):
        for high in range(2):
            mate = place.mate ^ (high * 4 + near)
            for at in range(runs):
                first = pl.multiple_of((at * TEAM + mate) * piece, piece)
                ups[near][high, :, at * piece : (at + 1) * piece] = up_at[:, pl.ds(first, piece)].astype(BF)
    rows, half = down_at.shape[0], down_at.shape[1] // 2
    down_b[:rows] = down_at[:, :half].astype(BF)
    down_b[rows:] = down_at[:, half:].astype(BF)


def settle_kernel(table, *refs):
    place = Place(table)
    for far in range(4):
        for near in range(4):
            refs[4][place.ctx ^ (far * 4 + near)] = refs[far][near]


def head_weights(packs, w_ref, wrows, wide):
    whalf = wrows // 2
    for x in range(wide):
        for at in range(packs[x].shape[0]):
            first = (at * wide + x) * wrows
            w_ref[first : first + wrows, : 2 * HD] = packs[x][at, :wrows]
            pair = packs[x][at, wrows : wrows + whalf]
            w_ref[first : first + whalf, 2 * HD :] = pair[:, :HD]
            w_ref[first + whalf : first + wrows, 2 * HD :] = pair[:, HD:]


def unstacked(refs):
    return [ref.at[at] for ref in refs for at in range(ref.shape[0])]


def in_order(place, packs, one_ref, two_ref):
    for at in range(packs[0].shape[0]):
        one_ref[at] = jnp.where(place.x == 0, packs[0][at], packs[1][at])
        two_ref[at] = jnp.where(place.x == 0, packs[1][at], packs[0][at])


def join_kernel(table, one_ref, two_ref, _, out_ref):
    place = Place(table)
    rows = one_ref.shape[1]
    for at in range(TEAM):
        mate = place.mate ^ at
        part = (one_ref if at < 4 else two_ref)[at % 4]
        if rows % 16 == 0:
            out_ref[pl.ds(pl.multiple_of(mate * rows, rows), rows), :] = part
        else:
            for to in range(TEAM):

                @pl.when(mate == to)
                def _(to=to, part=part):
                    out_ref[to * rows : (to + 1) * rows, :] = part


def mix_kernel(*refs):
    count = len(refs) - refs[0].shape[0]
    for near in range(count):
        for far, out in enumerate(refs[count:]):
            out[near] = refs[near][far]


def ring_shifts(chips):
    shifts = [0]
    for hop in range(1, chips // 2 + 1):
        shifts += [-hop, hop] if hop < chips // 2 else [-hop]
    return shifts


def ring_order(chips, place):
    long = chips // 2
    along = (place.r * 2 + place.zh) * 2 + place.zl
    spot = jnp.where(place.y == 0, along, chips - 1 - along)
    order = []
    for shift in ring_shifts(chips):
        at = lax.rem(spot + shift + chips, chips)
        order.append(jnp.where(at < long, 2 * at, 2 * (chips - 1 - at) + 1))
    return order


def forward_kernel(table, *refs, wrows, chips, others, wide):
    pieces, others, refs = refs[:chips], refs[chips : chips + others], refs[chips + others :]
    pieces = list(pieces) + unstacked(others)
    own_ref, *refs = refs
    packs, refs = ([own_ref, refs[0]], refs[1:]) if wide == 2 else (refs[:wide], refs[wide:])
    outs, seconds = refs[:4], refs[16:]
    lse_ref, begin_ref, lo_ref, w_top, w_low, q_ref, k_ref, v_ref, ot_ref, vt_ref, att_ref, w_ref = refs[4:16]
    place = Place(table)
    if wide == 2:
        in_order(place, packs, *seconds)
        packs = seconds
    head_weights(packs, w_ref, wrows, wide)
    w_top[...] = w_ref[: w_top.shape[0], :]
    w_low[...] = w_ref[w_top.shape[0] :, :]
    shards, half, _ = att_ref.shape
    rows = 2 * half
    total = shards * rows
    blocks = 2 * shards
    order = ring_order(chips, place)
    whalf = wrows // 2
    flags = []
    for block in range(blocks):
        shard, side = block_home(block, shards)
        row = own_ref[shard, wrows + whalf : wrows + whalf + 1].astype(F32)
        flags.append(row[:, side * half : (side + 1) * half])
    flags = jnp.concatenate(flags, axis=0)
    spots = half * lax.broadcasted_iota(jnp.int32, flags.shape, 0) + lax.broadcasted_iota(
        jnp.int32, flags.shape, 1
    )
    marks = jnp.where(flags > 0.5, spots.astype(F32), -1.0)
    lane = lax.broadcasted_iota(jnp.int32, marks.shape, 1)
    hop = 1
    while hop < half:
        moved = jnp.concatenate([marks[:, half - hop :], marks[:, : half - hop]], axis=1)
        marks = jnp.maximum(marks, jnp.where(lane >= hop, moved, -1.0))
        hop *= 2
    last = jnp.broadcast_to(marks[:, half - 1 :], marks.shape)
    line = lax.broadcasted_iota(jnp.int32, marks.shape, 0)
    hop = 1
    while hop < blocks:
        moved = jnp.concatenate([last[blocks - hop :], last[: blocks - hop]], axis=0)
        last = jnp.maximum(last, jnp.where(line >= hop, moved, -1.0))
        hop *= 2
    moved = jnp.concatenate([last[blocks - 1 :], last[: blocks - 1]], axis=0)
    begins = jnp.maximum(marks, jnp.where(line >= 1, moved, -1.0))
    group = TILE // half
    for tile in range(total // TILE):
        row = jnp.concatenate([begins[tile * group + at : tile * group + at + 1] for at in range(group)], axis=1)
        begin_ref[tile : tile + 1, :] = row.astype(jnp.int32)
        lo_ref[tile] = jnp.min(row).astype(jnp.int32) // TILE
    for which in range(2):
        for at in range(chips):
            made = dot(pieces[which * chips + at][...], w_ref[...], NN).astype(BF)
            shard = 2 * order[at] + (place.c if which == 0 else 1 - place.c)
            one = pl.multiple_of(shard * half, half)
            two = pl.multiple_of((blocks - 1 - shard) * half, half)
            scaled = made[:, :HD] * BF(HD**-0.5)
            for first, part in ((one, slice(0, half)), (two, slice(half, rows))):
                q_ref[pl.ds(first, half), :] = scaled[part]
                k_ref[pl.ds(first, half), :] = made[part, HD : 2 * HD]
                v_ref[pl.ds(first, half), :] = made[part, 2 * HD :]
    for at in range(0, total, 128):
        vt_ref[:, at : at + 128] = v_ref[at : at + 128, :].astype(F32).T.astype(BF)
    for tile in range(total // TILE):
        query = q_ref[tile * TILE : (tile + 1) * TILE, :]
        begin = begin_ref[tile : tile + 1, :]
        query_pos = tile * TILE + lax.broadcasted_iota(jnp.int32, (TILE, TILE), 1)

        def step(at, state):
            top, sums, accum = state
            first = pl.multiple_of(at * TILE, TILE)
            scores = dot(k_ref[pl.ds(first, TILE), :], query, NT)
            key_pos = first + lax.broadcasted_iota(jnp.int32, (TILE, TILE), 0)
            scores = jnp.where((key_pos >= begin) & (key_pos <= query_pos), scores, FAR)
            higher = jnp.maximum(top, jnp.max(scores, axis=0, keepdims=True))
            weights = jnp.exp(scores - higher)
            factor = jnp.exp(top - higher)
            sums = sums * factor + jnp.sum(weights, axis=0, keepdims=True)
            accum = accum * factor + dot(vt_ref[:, pl.ds(first, TILE)], weights.astype(BF), NN)
            return higher, sums, accum

        top, sums, accum = lax.fori_loop(
            lo_ref[tile],
            tile + 1,
            step,
            (jnp.full((1, TILE), FAR, F32), jnp.zeros((1, TILE), F32), jnp.zeros((HD, TILE), F32)),
        )
        out = accum / sums
        ot_ref[:, tile * TILE : (tile + 1) * TILE] = out
        lse_ref[tile : tile + 1, :] = top + jnp.log(sums)
        turned = out.T.astype(BF)
        for piece in range(group):
            shard, side = block_home(tile * group + piece, shards)
            att_ref[shard, :, side * HD : (side + 1) * HD] = turned[piece * half : (piece + 1) * half]
    for near in range(4):
        for far in range(4):
            outs[near][far] = att_ref[place.r * HEADS + (place.ctx ^ (far * 4 + near))]


def middle_kernel(table, *refs, count):
    weights, atts, refs = refs[:count], refs[count : count + 4], refs[count + 4 :]
    hidden_ref, gain_ref, bias_ref, att_out, mid_out, norm_out, w_ref, heads_ref = refs
    place = Place(table)
    if count > 1:
        for at, ref in enumerate(unstacked(weights)):
            rows = ref.shape[0]
            first = (place.flat(2) ^ MASKS[at]) * rows
            w_ref[pl.ds(pl.multiple_of(first, rows), rows), :] = ref[...]
    else:
        w_ref[...] = weights[0][...]
    for far in range(4):
        for near in range(4):
            heads_ref[place.ctx ^ (far * 4 + near)] = atts[far][near]
    half = heads_ref.shape[1]
    for head in range(0, HEADS, 2):
        for side in range(2):
            lanes = slice(side * HD, (side + 1) * HD)
            att_out[side * half : (side + 1) * half, head * HD : (head + 2) * HD] = jnp.concatenate(
                [heads_ref[head, :, lanes], heads_ref[head + 1, :, lanes]], axis=1
            )
    mid = hidden_ref[...].astype(F32) + dot(att_out[...], w_ref[...], NN)
    mid_out[...] = mid
    normed, _ = normalise(mid)
    norm_out[...] = (normed * gain_ref[...] + bias_ref[...]).astype(BF)


def feed_kernel(table, *refs, grads, mids, wide, groups):
    grads, mids, refs = refs[:grads], refs[grads : grads + mids], refs[grads + mids :]
    *weights, lay_keep, lay_send, mnd_keep, mnd_send, mid_out, act_out, delta_out, grad_out, up_ref, down_ref = refs
    place = Place(table)
    for out, arrays in ((grad_out, grads), (mid_out, mids)):
        first = 0
        for ref in arrays:
            for part in unstacked([ref]) if len(ref.shape) == 3 else [ref]:
                out[first : first + part.shape[0], :] = part[...]
                first += part.shape[0]
    width = mid_out.shape[1]
    own = width // (TEAM * groups)
    ffn = down_ref.shape[0] // groups
    moving = len(weights) > 2
    count = len(weights) // 2
    ups, downs = weights[:count], weights[count:]
    if not moving:
        ups, downs = unstacked(ups), unstacked(downs)
    for at in range(groups):
        if moving:
            high, x = place.zh ^ (at & 1), place.x ^ (at >> 1)
        else:
            high, x = at // wide, at % wide
        for mate in range(TEAM):
            first = ((high * TEAM + mate) * wide + x) * own
            if moving:
                first = pl.multiple_of(first, own)
            up_ref[pl.ds(first, own), :] = ups[at][mate * own : (mate + 1) * own, :]
        first = (high * wide + x) * ffn
        if moving:
            first = pl.multiple_of(first, ffn)
        down_ref[pl.ds(first, ffn), : width // 2] = downs[at][:ffn, :]
        down_ref[pl.ds(first, ffn), width // 2 :] = downs[at][ffn:, :]
    total = mid_out.shape[0]
    run = 256
    half = total // 2
    for first in list(range(half, total, run)) + list(range(0, half, run)):
        here = slice(first, first + run)
        up = dot(mid_out[here, :], up_ref[...], NN)
        value, slope = gelu_both(up)
        act = value.astype(BF)
        act_out[here, :] = act
        delta = (dot(grad_out[here, :], down_ref[...], NT) * slope).astype(BF)
        delta_out[here, :] = delta
        back = dot(delta, up_ref[...], NT)
        fore = dot(act, down_ref[...], NN)
        if first < half:
            mnd_keep[here, :] = back
            lay_keep[here, :] = fore.astype(BF)
        else:
            there = slice(first - half, first - half + run)
            mnd_send[there, :] = back.astype(BF)
            lay_send[there, :] = fore.astype(BF)


def turn_kernel(
    table, grad_ref, mid_ref, w_ref, keep_top, got_top, keep_low, got_low, gain_ref, delta_out, bf_out, *refs
):
    *outs, made_ref = refs
    mnd = jnp.concatenate(
        [keep_top[...] + got_top[...].astype(F32), keep_low[...] + got_low[...].astype(F32)], axis=0
    )
    normed, spread = normalise(mid_ref[...])
    delta = grad_ref[...].astype(F32) + norm_back(mnd, normed, spread, gain_ref[...])
    delta_out[...] = delta
    narrow = delta.astype(BF)
    bf_out[...] = narrow
    back = dot(narrow, w_ref[...], NT).astype(BF)
    half = made_ref.shape[1]
    for head in range(HEADS):
        cols = slice(head * HD, (head + 1) * HD)
        made_ref[head] = jnp.concatenate([back[:half, cols], back[half:, cols]], axis=1)
    place = Place(table)
    for near in range(4):
        for far in range(4):
            outs[near][far] = made_ref[place.ctx ^ (far * 4 + near)]


TEAM_ORDER = (0, 4, 2, 6, 1, 5, 3, 7)


def out_grad_kernel(table, lay_keep, lay_send, att_ref, delta_ref, keep_out, send_out, part_ref, *, wide, wrows):
    turned = att_ref[...].astype(F32).T.astype(BF)
    part_ref[...] = dot(turned, delta_ref[...], NN).astype(BF).reshape(part_ref.shape)
    place = Place(table)
    rows = lay_keep.shape[0] // 4
    highs = part_ref.shape[0] // (TEAM * wide)
    for at in range(TEAM):
        mate = place.mate ^ TEAM_ORDER[at]
        out, lay = (keep_out, lay_keep) if at < 4 else (send_out, lay_send)
        first = (at % 4) * 2 * rows
        out[first : first + rows, :] = lay[(at % 4) * rows : (at % 4 + 1) * rows, :]
        first += rows
        for x in range(wide):
            for high in range(highs):
                out[first : first + wrows, :] = part_ref[(high * TEAM + mate) * wide + x]
                first += wrows


def up_pack_kernel(table, part_ref, delta_ref, *outs, wide):
    _, tall, _ = outs[0].shape
    rows = tall - TAIL
    tail = sum_lines(jnp.sum(delta_ref[...].astype(F32), axis=0, keepdims=True))
    place = Place(table)
    highs = len(outs) // wide
    for at, out in enumerate(outs):
        if wide == 2:
            x, high = place.x ^ (at >> 1), place.zh ^ (at & 1)
        else:
            x, high = at // highs, at % highs
        for mate in range(TEAM):
            first = ((high * TEAM + mate) * wide + x) * rows
            if wide == 2:
                first = pl.multiple_of(first, rows)
            out[mate, :rows] = part_ref[pl.ds(first, rows), :].astype(BF)
            out[mate, rows:] = tail


def down_pack_kernel(table, part_ref, *outs, wide):
    rows = outs[0].shape[0]
    place = Place(table)
    highs = len(outs) // wide
    for at, out in enumerate(outs):
        if wide == 2:
            x, high = place.x ^ (at >> 1), place.zh ^ (at & 1)
        else:
            x, high = at // highs, at % highs
        first = (high * wide + x) * rows
        if wide == 2:
            first = pl.multiple_of(first, rows)
        out[...] = part_ref[pl.ds(first, rows), :].astype(BF)


def up_add_kernel(own_ref, got_ref, out_ref):
    rows = out_ref.shape[1] - TAIL
    for mate in range(TEAM):
        out_ref[mate, :rows], out_ref[mate, rows:] = add_lines(own_ref[mate], got_ref[mate])


def sum_kernel(own_ref, got_ref, out_ref):
    out_ref[...] = (own_ref[...].astype(F32) + got_ref[...].astype(F32)).astype(out_ref.dtype)


def up_share_kernel(table, own_ref, got_ref, *outs):
    place = Place(table)
    rows = own_ref.shape[1] - TAIL
    for near in range(4):
        for high in range(2):
            mate = place.mate ^ (high * 4 + near)
            out = outs[near]
            out[high, :rows], out[high, rows:] = add_lines(own_ref[mate], got_ref[mate])


def sum_lines(sums):
    high, low = split_two(sums)
    line = lax.broadcasted_iota(jnp.int32, (8, sums.shape[1]), 0)
    return jnp.where(line == 0, high.astype(F32), jnp.where(line == 1, low.astype(F32), 0.0)).astype(BF)


def add_lines(own, got):
    rows = own.shape[0] - TAIL
    total = own.astype(F32) + got.astype(F32)
    return total[:rows].astype(BF), sum_lines(total[rows : rows + 1] + total[rows + 1 : rows + 2])


def owner_column(row_ref, first, rows):
    shape = (rows, row_ref.shape[1])
    hit = lax.broadcasted_iota(jnp.int32, shape, 1) == first + lax.broadcasted_iota(jnp.int32, shape, 0)
    return jnp.sum(jnp.where(hit, row_ref[...], 0.0), axis=1, keepdims=True)


def as_row(column):
    shape = (column.shape[0],) * 2
    hit = lax.broadcasted_iota(jnp.int32, shape, 0) == lax.broadcasted_iota(jnp.int32, shape, 1)
    return jnp.sum(jnp.where(hit, column, 0.0), axis=0, keepdims=True)


def norm_grads(place, master_ref, grad_ref, sums, gain_ref, bias_ref, gain_out, bias_out, wide):
    rows = master_ref.shape[0]
    first = place.flat(wide) * rows
    own = master_ref[...].astype(BF).astype(F32)
    bias_grad = jnp.sum(own * sums, axis=1, keepdims=True)
    bias_out[...] = as_row(bias_grad)
    gain_grad = jnp.sum(own * grad_ref[...], axis=1, keepdims=True) - owner_column(bias_ref, first, rows) * bias_grad
    gain_out[...] = as_row(gain_grad / owner_column(gain_ref, first, rows))


def up_end_kernel(table, one_ref, two_ref, own_ref, gain_ref, bias_ref, grad_out, gain_out, bias_out, sum_ref, *, runs, wide):
    place = Place(table)
    rows = own_ref.shape[0]
    piece = one_ref.shape[2] // runs
    for high, ref in ((0, one_ref), (1, two_ref)):
        for near in range(4):
            mate = place.mate ^ (high * 4 + near)
            for at in range(runs):
                there = pl.ds(pl.multiple_of((at * TEAM + mate) * piece, piece), piece)
                part = ref[near, :, at * piece : (at + 1) * piece].astype(F32)
                grad_out[:, there] = part[:rows]
                sum_ref[:, there] = part[rows : rows + 1] + part[rows + 1 : rows + 2]
    norm_grads(place, own_ref, grad_out, sum_ref[...], gain_ref, bias_ref, gain_out, bias_out, wide)


def qkv_end_kernel(table, *refs, wide):
    parts, (own_ref, gain_ref, bias_ref, grad_out, gain_out, bias_out, all_ref) = refs[:4], refs[4:]
    place = Place(table)
    for far in range(4):
        for near in range(4):
            all_ref[place.ctx ^ (far * 4 + near)] = parts[far][near]
    rows = own_ref.shape[0]
    half = rows // 2
    width = HEADS * HD
    body = rows + half
    for head in range(0, HEADS, 2):
        for at in range(2):
            lanes = slice(at * HD, (at + 1) * HD)
            grad_out[:, at * width + head * HD : at * width + (head + 2) * HD] = jnp.concatenate(
                [all_ref[head, :rows, lanes], all_ref[head + 1, :rows, lanes]], axis=1
            ).astype(F32)
        for side in range(2):
            lanes = slice(side * HD, (side + 1) * HD)
            grad_out[side * half : (side + 1) * half, 2 * width + head * HD : 2 * width + (head + 2) * HD] = (
                jnp.concatenate([all_ref[head, rows:body, lanes], all_ref[head + 1, rows:body, lanes]], axis=1).astype(
                    F32
                )
            )
    lines = [[], [], []]
    for head in range(HEADS):
        tail = all_ref[head, body:, :].astype(F32)
        pair = tail[0:1] + tail[1:2]
        lines[0].append(pair[:, :HD])
        lines[1].append(pair[:, HD:])
        lines[2].append(tail[2:3, :HD] + tail[2:3, HD:])
    sums = jnp.concatenate(lines[0] + lines[1] + lines[2], axis=1)
    norm_grads(place, own_ref, grad_out, sums, gain_ref, bias_ref, gain_out, bias_out, wide)


def backward_kernel(table, lo_ref, *refs):
    douts, refs = refs[:4], refs[4:]
    (
        q_ref, k_ref, v_ref, ot_ref, lse_ref, begin_ref, own_out, mate_out, dn_ref, sum_ref,
        do_ref, dop_ref, kt_ref, dq_ref, dk_ref, dv_ref, da_ref,
    ) = refs
    place = Place(table)
    for part in range(douts[0].shape[0]):
        for far in range(4):
            for near in range(4):
                do_ref[part * HEADS + (place.ctx ^ (far * 4 + near))] = douts[far][part, near]
    shards, half, _ = do_ref.shape
    rows = 2 * half
    total = shards * rows
    for block in range(2 * shards):
        shard, side = block_home(block, shards)
        dop_ref[block * half : (block + 1) * half, :] = do_ref[shard, :, side * HD : (side + 1) * HD]
    for at in range(0, total, 128):
        kt_ref[:, at : at + 128] = k_ref[at : at + 128, :].astype(F32).T.astype(BF)
    dk_ref[...] = jnp.zeros_like(dk_ref)
    dv_ref[...] = jnp.zeros_like(dv_ref)
    for tile in range(total // TILE):
        here = slice(tile * TILE, (tile + 1) * TILE)
        query = q_ref[here, :]
        dout = dop_ref[here, :]
        begin = begin_ref[tile : tile + 1, :]
        lse = lse_ref[tile : tile + 1, :]
        row_dot = jnp.sum(dout.astype(F32).T * ot_ref[:, here], axis=0, keepdims=True)
        query_pos = tile * TILE + lax.broadcasted_iota(jnp.int32, (TILE, TILE), 1)

        def step(at, accum):
            first = pl.multiple_of(at * TILE, TILE)
            there = pl.ds(first, TILE)
            scores = dot(k_ref[there, :], query, NT)
            key_pos = first + lax.broadcasted_iota(jnp.int32, (TILE, TILE), 0)
            allowed = (key_pos >= begin) & (key_pos <= query_pos)
            probs = jnp.where(allowed, jnp.exp(scores - lse), 0.0)
            dprobs = dot(v_ref[there, :], dout, NT)
            delta = (probs * (dprobs - row_dot)).astype(BF)
            dv_ref[there, :] += dot(probs.astype(BF), dout, NN)
            dk_ref[there, :] += dot(delta, query, NN)
            return accum + dot(kt_ref[:, there], delta, NN)

        accum = lax.fori_loop(lo_ref[tile], tile + 1, step, jnp.zeros((HD, TILE), F32))
        dq_ref[here, :] = (accum * HD**-0.5).T
    sums = jnp.zeros((1, TRIPLE), F32)
    for block in range(2 * shards):
        shard, side = block_home(block, shards)
        at = slice(block * half, (block + 1) * half)
        pair = jnp.concatenate([dq_ref[at, :], dk_ref[at, :]], axis=1).astype(BF)
        last = dv_ref[at, :].astype(BF)
        da_ref[shard, side * half : (side + 1) * half, :] = pair
        da_ref[shard, rows : rows + half, side * HD : (side + 1) * HD] = last
        to = slice(side * half, (side + 1) * half)
        joined = jnp.concatenate([pair, last], axis=1)
        dn_ref[shard, to, :] = joined
        sums = sums + jnp.sum(joined.astype(F32), axis=0, keepdims=True)
    sum_ref[...] = sums
    base = place.r * HEADS
    for at in range(TEAM):
        own_out[at] = da_ref[base + place.zh * TEAM + at]
        mate_out[at] = da_ref[base + (1 - place.zh) * TEAM + at]


def qkv_lines(pair, last):
    line = lax.broadcasted_iota(jnp.int32, (8, 2 * HD), 0)
    high, low = split_two(pair)
    both = jnp.concatenate(split_two(last), axis=1)
    lines = jnp.where(line == 0, high.astype(F32), jnp.where(line == 1, low.astype(F32), both.astype(F32)))
    return lines.astype(BF)


def qkv_grad_kernel(table, *refs, repeats, chips, others, wide):
    pieces, stacks, (dn_ref, sum_ref, *outs, acc_ref) = refs[:chips], refs[chips : chips + others], refs[chips + others :]
    pieces = list(pieces) + unstacked(stacks)
    place = Place(table)
    order = ring_order(chips, place)
    total = None
    for which in range(2):
        for at in range(chips):
            shard = 2 * order[at] + (place.c if which == 0 else 1 - place.c)
            turned = dn_ref[shard].astype(F32).T.astype(BF)
            step = dot(turned, pieces[which * chips + at][...], NN)
            total = step if total is None else total + step
    acc_ref[...] = total.T
    owners, tall, _ = outs[0].shape
    rows = (tall - TAIL) * 2 // 3
    half = rows // 2
    sums = sum_ref[...]
    lines = qkv_lines(sums[:, : 2 * HD], sums[:, 2 * HD :])

    def write(base):
        for at, out in enumerate(outs):
            x = place.x ^ at if wide == 2 else at
            for owner in range(owners):
                first = base + (owner * wide + x) * rows
                if wide == 2:
                    first = pl.multiple_of(first, rows)
                grad = acc_ref[pl.ds(first, rows), :]
                out[owner, :rows] = grad[:, : 2 * HD].astype(BF)
                out[owner, rows : rows + half] = jnp.concatenate(
                    [grad[:half, 2 * HD :], grad[half:, 2 * HD :]], axis=1
                ).astype(BF)
                out[owner, rows + half :] = lines

    if repeats == 1:
        write(0)
    else:
        for at in range(repeats):
            pl.when(place.r == at)(partial(write, at * owners * wide * rows))


def qkv_add_kernel(table, own_ref, got_ref, *outs):
    place = Place(table)
    body = own_ref.shape[1] - TAIL
    for near in range(4):
        for far in range(4):
            at = place.ctx ^ (far * 4 + near)
            total = own_ref[at].astype(F32) + got_ref[at].astype(F32)
            outs[near][far, :body] = total[:body].astype(BF)
            tail = total[body:]
            outs[near][far, body:] = qkv_lines(tail[0:1] + tail[1:2], tail[2:3, :HD] + tail[2:3, HD:])


def spread_kernel(_, keep_ref, got_ref, send_z, send_y, top_out, low_out):
    rows = keep_ref.shape[0] // 4
    half = rows // 2
    for at in range(4):
        for side in range(2):
            here = slice(at * rows + side * half, at * rows + (side + 1) * half)
            total = keep_ref[here, :].astype(F32) + got_ref[here, :].astype(F32)
            if side == 0:
                if at % 2 == 0:
                    top_out[at // 2] = total
                else:
                    send_z[at // 2] = total.astype(BF)
            elif at < 2:
                low_out[at] = total
            else:
                send_y[at - 2] = total.astype(BF)


def narrow_kernel(_, top_ref, got_z, low_ref, got_y, send_y, send_z, top_out, low_out):
    top_out[...] = top_ref[0] + got_z[0].astype(F32)
    low_out[...] = low_ref[0] + got_y[0].astype(F32)
    send_y[...] = (top_ref[1] + got_z[1].astype(F32)).astype(BF)
    send_z[...] = (low_ref[1] + got_y[1].astype(F32)).astype(BF)


def input_kernel(table, own_ref, got_ref, *refs):
    tall = own_ref.shape[1]
    rows = tall * 2 // 3
    half = rows // 2
    place = Place(table)
    *weights, keep_out, send_out, lhs_ref, rhs_ref = refs
    first = 0
    for w_own, w_got in zip(weights[:2], weights[2:], strict=True):
        here = slice(first, first + w_got.shape[0])
        rhs_ref[here, : 2 * HD] = w_own[:, : 2 * HD]
        rhs_ref[here, 2 * HD : 3 * HD] = w_own[:, 2 * HD :]
        rhs_ref[here, 3 * HD : 4 * HD] = w_got[:, 2 * HD :]
        rhs_ref[here, 4 * HD :] = w_got[:, : 2 * HD]
        first += w_got.shape[0]
    for at in range(TEAM):
        mate = place.mate ^ TEAM_ORDER[at]
        first = at * rows
        one, two = own_ref[mate], got_ref[mate]
        lhs_ref[first : first + rows, : 2 * HD] = one[:rows]
        lhs_ref[first : first + rows, 4 * HD :] = two[:rows]
        for side in range(2):
            lanes = slice(side * HD, (side + 1) * HD)
            lhs_ref[first + side * half : first + (side + 1) * half, 2 * HD : 4 * HD] = jnp.concatenate(
                [one[rows:, lanes], two[rows:, lanes]], axis=1
            )
    middle = TEAM * rows // 2
    send_out[...] = dot(lhs_ref[middle:, :], rhs_ref[...], NT).astype(BF)
    keep_out[...] = dot(lhs_ref[:middle, :], rhs_ref[...], NT)


def last_kernel(_, keep_top, got_top, keep_low, got_low, mid_delta_ref, hidden_ref, gain_ref, out_ref):
    grad = jnp.concatenate(
        [keep_top[...] + got_top[...].astype(F32), keep_low[...] + got_low[...].astype(F32)], axis=0
    )
    normed, spread = normalise(hidden_ref[...].astype(F32))
    out_ref[...] = (mid_delta_ref[...] + norm_back(grad, normed, spread, gain_ref[...])).astype(BF)


def outs_kernel(table, mid_ref, lay_ref, got_lay, part_ref, got_part, lay_out, *outs, wide):
    lay_out[...] = (mid_ref[...] + lay_ref[...] + got_lay[...].astype(F32)).astype(BF)
    rows = outs[0].shape[0]
    place = Place(table)
    highs = len(outs) // wide
    for at, out in enumerate(outs):
        if wide == 2:
            x, high = place.x ^ (at >> 1), place.zh ^ (at & 1)
        else:
            x, high = at // highs, at % highs
        first = (x * highs + high) * rows
        if wide == 2:
            first = pl.multiple_of(first, rows)
        out[...] = (part_ref[pl.ds(first, rows), :] + got_part[pl.ds(first, rows), :].astype(F32)).astype(BF)


def after(array, *others):
    return lax.optimization_barrier((array, *others))[0]


def apart(count, mask):
    return [(at, at ^ mask) for at in range(count)]


def stack(arrays):
    count = sum(array.shape[0] if array.ndim == 3 else 1 for array in arrays)
    return call(stack_kernel, arrays, [((count,) + arrays[0].shape[-2:], arrays[0].dtype)], smem=0)[0]


def meet(*arrays):
    return lax.optimization_barrier(arrays)


def near(arrays):
    return [lax.ppermute(arrays[at], ("y", "c"), apart(4, at)) for at in range(1, 4)]


def far(arrays):
    return [lax.ppermute(arrays[at], ("zh", "zl"), apart(4, at)) for at in range(1, 4)]


def swap(array, axis):
    return lax.ppermute(array, axis, SWAP)


def mix(arrays):
    shape = arrays[0].shape
    return call(mix_kernel, arrays, [((len(arrays),) + shape[1:], arrays[0].dtype)] * shape[0], smem=0)


def stack_kernel(*refs):
    at = 0
    for ref in refs[:-1]:
        count = ref.shape[0] if len(ref.shape) == 3 else 1
        for part in range(count):
            refs[-1][at] = ref[part] if len(ref.shape) == 3 else ref[...]
            at += 1


def spread(table, keep, got):
    shape = (keep.shape[0] // 8, keep.shape[1])
    return call(spread_kernel, (table, keep, got), [((2, *shape), BF)] * 2 + [((2, *shape), F32)] * 2)


def narrow(table, top, got_z, low, got_y):
    shape = top.shape[1:]
    return call(narrow_kernel, (table, top, got_z, low, got_y), [(shape, BF)] * 2 + [(shape, F32)] * 2)


def add(one, two, kind):
    return call(sum_kernel, (one, two), [(one.shape, kind)], smem=0)[0]


class Steps:
    def __init__(self, arrays, sizes):
        (
            self.hidden, self.start, self.qkv, self.out, self.up, self.down,
            gain1, bias1, gain2, bias2, self.grad,
        ) = arrays
        self.hidden, self.grad = self.hidden[0], self.grad[0]
        self.gain1, self.bias1, self.gain2, self.bias2 = (a[None] for a in (gain1, bias1, gain2, bias2))
        self.repeats, self.wide = sizes["r"], sizes["x"]
        self.rows, self.width = self.hidden.shape
        self.half = self.rows // 2
        self.shards = self.repeats * HEADS
        self.total = self.shards * self.rows
        self.wrows, self.ffn = self.qkv.shape[0], self.down.shape[0]
        self.highs = 2 * self.repeats
        self.cols = self.highs * self.wide * self.ffn
        self.many = TEAM * self.rows
        self.qkv_tall = self.wrows * 3 // 2 + TAIL
        self.up_tall = self.wrows + TAIL
        self.sides = self.wide * self.highs
        self.piece = ((4, self.half, 2 * HD), BF)
        self.table = jnp.stack([lax.axis_index(axis).astype(jnp.int32) for axis in ALL])

    def first(self):
        masters = (self.qkv, self.out, self.up, self.down)
        row = ((1, self.width), F32)
        outs = call(
            partial(first_kernel, runs=self.highs),
            (self.table, self.hidden, self.gain1, self.bias1, *masters, self.start),
            [
                ((self.rows, self.width), BF),
                *[((4, self.qkv_tall, 2 * HD), BF)] * 4,
                ((self.wrows, self.width), BF),
                *[((2, self.wrows, self.cols), BF)] * 4,
                ((2 * self.ffn, self.width // 2), BF),
            ],
            [
                ((self.rows, self.width), BF), row, row,
                *[(a.shape, F32) for a in masters],
                (self.start.shape, jnp.int32),
                ((HEADS, self.qkv_tall, 2 * HD), BF),
            ],
            far=8,
            sems=8,
            limit=58,
        )
        return outs[0], list(outs[1:5]), outs[5], list(outs[6:10]), outs[10]

    def forward(self, pieces, others, packs):
        tokens = ((self.total, HD), BF)
        tiles = (self.total // TILE, TILE)
        whalf = ((self.width // 2, TRIPLE), BF)
        outs = call(
            partial(forward_kernel, wrows=self.wrows, chips=len(pieces), others=len(others), wide=self.wide),
            (self.table, *pieces, *others, *packs),
            [
                *[self.piece] * 4,
                (tiles, F32), (tiles, jnp.int32), (tiles[:1], jnp.int32),
                whalf, whalf,
                tokens, tokens, tokens,
                ((HD, self.total), F32),
            ],
            [((HD, self.total), BF), ((self.shards, self.half, 2 * HD), BF), ((self.width, TRIPLE), BF)]
            + [((self.shards, self.qkv_tall, 2 * HD), BF)] * (2 if self.wide == 2 else 0),
            smem_outs=(6,),
            limit=12 * self.repeats,
            micros=14,
        )
        lse, begin, low = outs[4:7]
        return list(outs[:4]), list(outs[7:9]), (low, *outs[9:], lse, begin)

    def middle(self, weights, heads):
        return call(
            partial(middle_kernel, count=len(weights)),
            (self.table, *weights, *heads, self.hidden, self.gain2, self.bias2),
            [
                ((self.rows, self.width), BF),
                ((self.rows, self.width), F32),
                ((self.rows, self.width), BF),
                ((self.width, self.width), BF),
            ],
            [((HEADS, self.half, 2 * HD), BF)],
        )

    def feed(self, grads, mids, weights):
        half, full = (self.many // 2, self.width), (self.many, self.width)
        inner = ((self.many, self.cols), BF)
        return call(
            partial(
                feed_kernel, grads=len(grads), mids=len(mids), wide=self.wide, groups=self.highs * self.wide
            ),
            (self.table, *grads, *mids, *weights),
            [(half, BF), (half, BF), (half, F32), (half, BF), (full, BF), inner, inner, (full, BF)],
            [((self.width, self.cols), BF), ((self.cols, self.width), BF)],
            micros=6,
        )

    def up_gradient(self, mids, delta):
        return call(
            partial(up_pack_kernel, wide=self.wide),
            (self.table, dot(mids, delta, TN), delta),
            [((TEAM, self.up_tall, self.cols), BF)] * self.sides,
        )

    def down_gradient(self, acts, grads):
        return call(
            partial(down_pack_kernel, wide=self.wide),
            (self.table, dot(acts, grads, TN)),
            [((self.ffn, self.width), BF)] * self.sides,
        )

    def turn(self, mid, w_out, ends):
        outs = call(
            turn_kernel,
            (self.table, self.grad, mid, w_out, *ends, self.gain2),
            [((self.rows, self.width), F32), ((self.rows, self.width), BF), *[self.piece] * 4],
            [((HEADS, self.half, 2 * HD), BF)],
        )
        return outs[0], outs[1], list(outs[2:])

    def out_gradient(self, lay_keep, lay_send, attended, delta):
        return call(
            partial(out_grad_kernel, wide=self.wide, wrows=self.wrows),
            (self.table, lay_keep, lay_send, attended, delta),
            [((self.many, self.width), BF)] * 2,
            [((self.shards * self.wide, self.wrows, self.width), BF)],
        )

    def backward(self, kept, douts):
        low, query, keys, values, out_t, lse, begin = kept
        tall = self.rows + self.half
        total = ((self.total, HD), F32)
        return call(
            backward_kernel,
            (self.table, low, *douts, query, keys, values, out_t, lse, begin),
            [
                ((TEAM, tall, 2 * HD), BF),
                ((TEAM, tall, 2 * HD), BF),
                ((self.shards, self.rows, TRIPLE), BF),
                ((1, TRIPLE), F32),
            ],
            [
                ((self.shards, self.half, 2 * HD), BF),
                ((self.total, HD), BF),
                ((HD, self.total), BF),
                total, total, total,
                ((self.shards, tall, 2 * HD), BF),
            ],
            smem=2,
            limit=12 * self.repeats,
            micros=12,
        )

    def qkv_gradient(self, pieces, others, by_shard, sums):
        return call(
            partial(
                qkv_grad_kernel,
                repeats=self.repeats, chips=len(pieces), others=len(others), wide=self.wide,
            ),
            (self.table, *pieces, *others, by_shard, sums),
            [((HEADS, self.qkv_tall, 2 * HD), BF)] * self.wide,
            [((self.width, TRIPLE), F32)],
        )

    def up_share(self, own, got):
        return list(call(up_share_kernel, (self.table, own, got), [((2, self.up_tall, self.cols), BF)] * 4))

    def qkv_share(self, own, got):
        return list(call(qkv_add_kernel, (self.table, own, got), [((4, self.qkv_tall, 2 * HD), BF)] * 4))

    def outputs(self, mid, ends):
        return call(
            partial(outs_kernel, wide=self.wide),
            (self.table, mid, *ends),
            [((self.rows, self.width), BF)] + [((self.wrows, self.width), BF)] * self.sides,
        )

    def inputs(self, to_own, from_mate, weights, mates):
        return call(
            input_kernel,
            (self.table, to_own, from_mate, *weights, *mates),
            [((self.many // 2, self.width), F32), ((self.many // 2, self.width), BF)],
            [((self.many, 2 * TRIPLE), BF), ((self.width, 2 * TRIPLE), BF)],
        )

    def last(self, ends, mid_delta):
        return call(
            last_kernel,
            (self.table, *ends, mid_delta, self.hidden, self.gain1),
            [((self.rows, self.width), BF)],
        )[0]

    def up_end(self, ends):
        line = ((1, self.wrows), F32)
        return call(
            partial(up_end_kernel, runs=self.highs, wide=self.wide),
            (self.table, *ends, self.up, self.gain2, self.bias2),
            [(self.up.shape, F32), line, line],
            [((1, self.up.shape[1]), F32)],
        )

    def qkv_end(self, ends):
        line = ((1, self.wrows), F32)
        return call(
            partial(qkv_end_kernel, wide=self.wide),
            (self.table, *ends, self.qkv, self.gain1, self.bias1),
            [(self.qkv.shape, F32), line, line],
            [((HEADS, self.qkv_tall, 2 * HD), BF)],
        )


def ring_moves(long):
    count = 2 * long
    order = [2 * at for at in range(long)] + [2 * at + 1 for at in reversed(range(long))]
    right = [(order[at], order[(at + 1) % count]) for at in range(count)]
    return right, [(two, one) for one, two in right]


def results(layer_out, grad_in, qkv, out, up, down):
    return (
        layer_out[None], grad_in[None], qkv[0], out, up[0], down,
        qkv[1][0], qkv[2][0], up[1][0], up[2][0],
    )


def local(*arrays, sizes):
    s = Steps(arrays, sizes)
    right, left = ring_moves(4)

    def ahead(array):
        return lax.ppermute(array, CHIPS, right)

    def behind(array):
        return lax.ppermute(array, CHIPS, left)

    norm_in, by_head, out_b, up_b, down_b = s.first()
    a1, b1, *got = meet(ahead(norm_in), behind(norm_in), *near(by_head))
    packs = mix([by_head[0], *got])
    a2, b2, *got = meet(ahead(a1), behind(b1), *far(packs))
    (packed,) = call(settle_kernel, (s.table, packs[0], *got), [((HEADS, s.qkv_tall, 2 * HD), BF)])
    first = stack([norm_in, a1, b1, a2, b2])
    ups = [after(up, a2) for up in up_b]
    a3, b3, packed_x, *got = meet(ahead(a2), behind(b2), swap(packed, "x"), *near(ups))
    ups = mix([ups[0], *got])
    a4, up_z, first, down_x = meet(
        ahead(a3), swap(ups[1], "zl"), swap(after(first, a3), "c"), swap(after(down_b, a3), "x")
    )
    second = stack([a3, b3])
    (up_t,) = call(join_kernel, (s.table, ups[0], up_z, down_b), [((TEAM * s.wrows, s.cols), BF)])
    pieces = [norm_in, a1, b1, a2, b2, a3, b3, a4]
    others = [first, *meet(swap(second, "c"), swap(a4[None], "c"))]

    out = after(out_b, a4)
    out_z = [lax.ppermute(out, ("zh", "zl"), apart(4, at)) for at in range(1, 4)]
    up_z = swap(after(up_t, a4), "zh")
    grad = after(s.grad, a4)
    grad_z = swap(grad, "zl")
    att, w_head, kept = s.forward(pieces, others, [packed, packed_x])
    *att, grad_z, up_z, o1, o2, o3 = meet(*att, grad_z, up_z, *out_z)
    out_4 = stack([out, o1, o2, o3])
    grad_2 = stack([grad, grad_z])
    *got, out_x, out_y, down_z = meet(
        *near(att), swap(out_4, "x"), swap(out_4, "y"), swap(after(down_b, att[0]), "zh")
    )
    att = mix([att[0], *got])
    out_12 = stack([out_4, out_x, out_y])
    *got, o1, o2, out_12c, up_x = meet(
        *far(att),
        swap(after(out_y[:2], att[0]), "x"),
        swap(after(out_x[2:], att[0]), "y"),
        swap(out_12, "c"),
        swap(after(up_t, att[0]), "x"),
    )
    out_xy = stack([o1, o2])
    grad_2y, out_xyc = swap(after(grad_2, out_xy), "y"), swap(out_xy, "c")
    attended, mid, norm_mid, w_out = s.middle([out_12, out_xy, out_12c, out_xyc], [att[0], *got])

    half = s.half
    by_z, by_y, up_zx, grad_2y = meet(
        swap(norm_mid, "zl"), swap(norm_mid, "y"), swap(after(up_z, norm_mid), "x"), grad_2y
    )
    three = stack([norm_mid, by_z, by_y])
    grad_4 = stack([grad_2, grad_2y])
    both_one, both_two, three, down_zx, grad_4c = meet(
        swap(by_y[:half], "zl"), swap(by_z[half:], "y"), swap(three, "c"), swap(after(down_z, by_z), "x"), swap(grad_4, "c")
    )
    both = stack([both_one, both_two])
    mids = [norm_mid, by_z, by_y, both_one, both_two, three, swap(both, "c")]
    mate_1 = swap(after(w_head[0], both_one), "zh")
    lay_keep, lay_send, keep, send, mids, acts, delta, grads = s.feed(
        [grad_4, grad_4c], mids, [up_t, up_z, up_x, up_zx, down_b, down_z, down_x, down_zx]
    )
    send, mate_1 = meet(send, mate_1)
    got = swap(send, "c")
    send_z, send_y, top, low = spread(s.table, keep, got)
    up_parts = s.up_gradient(mids, after(delta, send_z))
    got_z, got_y, *up_parts = meet(swap(send_z, "zl"), swap(send_y, "y"), *up_parts)
    send_y, send_z, top, low = narrow(s.table, top, got_z, low, got_y)
    down_parts = s.down_gradient(after(acts, send_y), grads)
    end_top, end_low, up_far, *down_parts = meet(
        swap(send_y, "y"), swap(send_z, "zl"), swap(after(up_parts[3], send_y), "x"), *down_parts
    )
    mid_delta, mid_delta_b, by_head = s.turn(mid, w_out, (top, end_top, low, end_low))
    *got, up_near, mate_2 = meet(
        *near(by_head),
        swap(after(up_parts[2], mid_delta), "x"),
        swap(after(w_head[1], mid_delta), "zh"),
    )
    by_head = mix([by_head[0], *got])
    up_shape = (TEAM, s.up_tall, s.cols)
    (up_send,) = call(up_add_kernel, (up_parts[1], after(up_far, by_head[0])), [(up_shape, BF)], smem=0)
    keep, send = s.out_gradient(after(lay_keep, by_head[0]), lay_send, attended, mid_delta_b)
    *got, send, down_far, up_send = meet(
        *far(by_head), swap(send, "c"), swap(after(down_parts[3], by_head[0]), "x"), up_send
    )

    douts = [array[None] for array in (by_head[0], *got)]
    send_z, send_y, top, low = spread(s.table, keep, send)
    got_z, got_y = swap(send_z, "zl"), swap(send_y, "y")
    up_got = swap(up_send, "zh")
    down_near = swap(after(down_parts[2], send), "x")
    kept = (after(kept[0], send_z), *kept[1:])
    to_own, to_mate, by_shard, sums = s.backward(kept, douts)
    to_own, to_mate, got_z, got_y, up_got, down_near = meet(to_own, to_mate, got_z, got_y, up_got, down_near)
    send_y, send_z, top, low = narrow(s.table, top, got_z, low, got_y)
    from_mate = swap(to_mate, "zh")
    (up_keep,) = call(up_add_kernel, (up_parts[0], after(up_near, to_own)), [(up_shape, BF)], smem=0)
    ups = s.up_share(up_keep, up_got)
    qkv_own, qkv_send = s.qkv_gradient(pieces, others, after(by_shard, ups[0]), sums)
    end_top, end_low, qkv_send, *got = meet(
        swap(send_y, "y"), swap(send_z, "zl"), qkv_send, *near(ups)
    )
    ups = mix([ups[0], *got])
    layer_out, *outs = s.outputs(mid, (top, end_top, low, end_low))
    down_keep = add(down_parts[0], after(down_near, end_top), F32)
    down_send = add(down_parts[1], after(down_far, end_top), BF)
    from_mate, qkv_got, ups_z, down_send, layer_out = meet(
        from_mate, swap(after(qkv_send, end_top), "x"), swap(ups[1], "zl"), down_send, layer_out
    )
    keep, send = s.inputs(to_own, from_mate, w_head, [mate_1, mate_2])
    qkv = s.qkv_share(qkv_own, qkv_got)

    down_got = swap(after(down_send, send), "zh")
    send, out_near, out_far, *qkv = meet(
        swap(send, "c"), swap(after(outs[2], send), "x"), swap(after(outs[3], send), "x"), *qkv
    )
    send_z, send_y, top, low = spread(s.table, keep, send)
    out_keep, out_send = add(outs[0], after(out_near, send_z), F32), add(outs[1], after(out_far, send_z), BF)
    got_z, got_y, out_send, *got = meet(
        swap(send_z, "zl"), swap(send_y, "y"), out_send, *near([after(a, send_z) for a in qkv])
    )
    send_y, send_z, top, low = narrow(s.table, top, got_z, low, got_y)
    qkv = mix([after(qkv[0], send_y), *got])
    up = s.up_end((after(ups[0], send_y), ups_z))
    end_top, end_low, down_got, up_grad, *got = meet(
        swap(send_y, "y"), swap(send_z, "zl"), down_got, up[0], *far(qkv)
    )
    out_got = swap(after(out_send, end_top), "zh")
    grad_in = s.last((top, end_top, low, end_low), mid_delta)
    down = add(down_keep, down_got, F32)
    end = s.qkv_end([qkv[0], *got])
    out = add(out_keep, out_got, F32)
    return results(layer_out, grad_in, end, out, (up_grad, *up[1:]), down)


def local_any(*arrays, sizes):
    s = Steps(arrays, sizes)
    repeats, wide = s.repeats, s.wide
    long = 4 * repeats
    right, left = ring_moves(long)
    norm_in, by_head, out_b, up_b, down_b = s.first()
    one = two = norm_in
    pieces = [norm_in]
    for hop in range(1, long + 1):
        one = lax.ppermute(one, CHIPS, right)
        pieces.append(one)
        if hop < long:
            two = lax.ppermute(two, CHIPS, left)
            pieces.append(two)
    others = [swap(piece[None], "c") for piece in pieces]

    def by_parts(arrays):
        return [lax.all_gather(array, "r", axis=0, tiled=False) for array in arrays]

    def share(arrays):
        got = mix([arrays[0], *near(arrays)])
        return [got[0], *far(got)]

    def team_gather(array):
        half = array.shape[0] // 2
        by_z, by_y = swap(array, "zl"), swap(array, "y")
        chip = [array, by_z, by_y, swap(by_y[:half], "zl"), swap(by_z[half:], "y")]
        return chip + [swap(piece, "c") for piece in chip]

    def team_scatter(keep, send):
        send_z, send_y, top, low = spread(s.table, keep, swap(send, "c"))
        send_y, send_z, top, low = narrow(s.table, top, swap(send_z, "zl"), low, swap(send_y, "y"))
        return top, swap(send_y, "y"), low, swap(send_z, "zl")

    def to_owners(parts):
        array = jnp.stack(parts).reshape((wide, s.highs) + parts[0].shape).swapaxes(0, 1)
        array = array.reshape((wide * s.highs,) + parts[0].shape)
        return jnp.sum(lax.all_to_all(array, GROUP, 0, 0, tiled=True).astype(F32), axis=0)

    packs = share(by_head)
    (packed,) = call(settle_kernel, (s.table, *packs), [((HEADS, s.qkv_tall, 2 * HD), BF)])
    packed = lax.all_gather(packed, "r", axis=0, tiled=True)
    packs = [packed, *lax.all_gather(packed, "x", axis=0, tiled=False)]
    if wide == 2:
        packs = [packed, swap(packed, "x")]
    ups = mix([up_b[0], *near(up_b)])
    up_t = call(
        join_kernel, (s.table, ups[0], swap(ups[1], "zl"), down_b), [((TEAM * s.wrows, s.cols), BF)]
    )[0]
    weights = [lax.all_gather(array, GROUP, axis=0, tiled=False) for array in (up_t, down_b)]
    att, w_head, kept = s.forward(pieces, others, packs)

    def mine(arrays):
        return share(arrays)

    w_out = lax.all_gather(out_b, ALL, axis=0, tiled=True)
    attended, mid, norm_mid, w_out = s.middle([w_out], mine(att))
    lay_keep, lay_send, keep, send, mids, acts, delta, grads = s.feed(
        team_gather(s.grad), team_gather(norm_mid), weights
    )
    mid_delta, mid_delta_b, by_head = s.turn(mid, w_out, team_scatter(keep, send))
    up = to_owners(s.up_gradient(mids, delta)).astype(BF)
    down = to_owners(s.down_gradient(acts, grads))
    to_own, to_mate, by_shard, sums = s.backward(kept, by_parts(share(by_head)))
    layer_out, *outs = s.outputs(
        mid, team_scatter(*s.out_gradient(lay_keep, lay_send, attended, mid_delta_b))
    )
    keep, send = s.inputs(to_own, swap(to_mate, "zh"), w_head, [swap(array, "zh") for array in w_head])
    grad_in = s.last(team_scatter(keep, send), mid_delta)
    parts = s.qkv_gradient(pieces, others, by_shard, sums)
    own, *got = list(lax.all_to_all(jnp.stack(parts), "x", 0, 0, tiled=True))
    while len(got) > 1:
        own, got = own.astype(F32) + got[0].astype(F32), got[1:]
    ups = s.up_share(up, jnp.zeros_like(up))
    ups = mix([ups[0], *near(ups)])
    return results(
        layer_out,
        grad_in,
        s.qkv_end(share(s.qkv_share(own, got[0]))),
        to_owners(outs),
        s.up_end((ups[0], swap(ups[1], "zl"))),
        down,
    )


def solution(mesh):
    ctx, wide = mesh.shape["ctx"], mesh.shape["wt"]
    sizes = {"r": ctx // HEADS, "zh": 2, "zl": 2, "y": 2, "c": 2, "x": wide}
    grid = Mesh(mesh.devices.reshape(tuple(sizes.values())), ALL)
    tokens, weights = P("x", CTX, None), P(ALL, None)
    return jax.shard_map(
        partial(local if sizes["r"] == 1 and wide == 2 else local_any, sizes=sizes),
        mesh=grid,
        in_specs=(tokens, P("x", CTX)) + (weights,) * 4 + (P(),) * 4 + (tokens,),
        out_specs=(tokens, tokens) + (weights,) * 4 + (P(ALL),) * 4,
        check_vma=False,
    )
```

```python
from functools import partial

import jax
import jax.numpy as jnp
from jax import lax
from jax.experimental import pallas as pl
from jax.experimental.pallas import tpu as pltpu
from jax.sharding import Mesh
from jax.sharding import PartitionSpec as P

HEADS = 16
HD = 64
TRIPLE = 3 * HD
EPS = 1e-05
FAR = -1e30
TILE = 256
TEAM = 8
TAIL = 8
BF = jnp.bfloat16
F32 = jnp.float32
ALL = ("r", "zh", "zl", "y", "c", "x")
CTX = ("r", "zh", "zl", "y", "c")
PART = ("zh", "zl", "y", "c")
CHIPS = ("r", "zh", "zl", "y")
TP = ("zl", "y", "c")
GROUP = ("r", "zh", "x")
SWAP = [(0, 1), (1, 0)]
MASKS = [
    z * 8 + y * 4 + c * 2 + x for c in range(2) for y in range(2) for x in range(2) for z in range(4)
]
NN = ((1,), (0,))
NT = ((1,), (1,))
TN = ((0,), (0,))


def dot(one, two, dims):
    return lax.dot_general(one, two, (dims, ((), ())), preferred_element_type=F32)


def normalise(rows):
    centred = rows - jnp.mean(rows, axis=-1, keepdims=True)
    spread = lax.rsqrt(jnp.mean(centred * centred, axis=-1, keepdims=True) + EPS)
    return centred * spread, spread


def norm_back(grad, normed, spread, gain):
    scaled = grad * gain
    inner = (
        scaled
        - jnp.mean(scaled, axis=-1, keepdims=True)
        - normed * jnp.mean(scaled * normed, axis=-1, keepdims=True)
    )
    return inner * spread


def gelu_both(up):
    root = 0.7978845608028654
    square = up * up
    inner = jnp.tanh(root * up * (1.0 + 0.044715 * square))
    plus = 0.5 * (1.0 + inner)
    slope = plus + 0.5 * up * (1.0 - inner * inner) * root * (1.0 + 3.0 * 0.044715 * square)
    return up * plus, slope


def block_home(block, shards):
    return (block, 0) if block < shards else (2 * shards - 1 - block, 1)


def split_two(values):
    high = values.astype(BF)
    return high, (values - high.astype(F32)).astype(BF)


def after(array, *others):
    return lax.optimization_barrier((array, *others))[0]


class Place:
    def __init__(self, table):
        self.r, self.zh, self.zl, self.y, self.c, self.x = (table[at] for at in range(6))
        self.mate = self.zl * 4 + self.y * 2 + self.c
        self.ctx = self.zh * TEAM + self.mate

    def flat(self, wide):
        return (self.r * HEADS + self.ctx) * wide + self.x


def call(body, arrays, outs, scratch=(), smem=1, smem_outs=(), far=0, sems=0, limit=12, micros=0):
    vector = pl.BlockSpec(memory_space=pltpu.VMEM)
    scalar = pl.BlockSpec(memory_space=pltpu.SMEM)
    there = pl.BlockSpec(memory_space=pl.ANY)
    scratch = [pltpu.VMEM(shape, kind) for shape, kind in scratch]
    if sems:
        scratch.append(pltpu.SemaphoreType.DMA((sems,)))
    return pl.pallas_call(
        body,
        out_shape=[jax.ShapeDtypeStruct(shape, kind) for shape, kind in outs],
        in_specs=[scalar] * smem + [there] * far + [vector] * (len(arrays) - smem - far),
        out_specs=[scalar if at in smem_outs else vector for at in range(len(outs))],
        scratch_shapes=scratch,
        compiler_params=pltpu.CompilerParams(vmem_limit_bytes=limit << 20),
        cost_estimate=pl.CostEstimate(flops=micros * 10**9 + 1000, bytes_accessed=1 << 10, transcendentals=0),
    )(*arrays)


def start_copies(pairs, sems):
    copies = [pltpu.make_async_copy(source, target, sems.at[at]) for at, (source, target) in enumerate(pairs)]
    for copy in copies:
        copy.start()
    return copies


def first_kernel(table, hidden_ref, gain_ref, bias_ref, qkv_ref, out_ref, up_ref, down_ref, start_ref, *refs, runs):
    (
        norm_out, *heads, out_b, one_ref, two_ref, three_ref, four_ref, down_b,
        hidden_at, gain_at, bias_at, qkv_at, out_at, up_at, down_at, start_at, made_ref, sems,
    ) = refs
    ups = one_ref, two_ref, three_ref, four_ref
    place = Place(table)
    copies = start_copies(
        (
            (hidden_ref, hidden_at), (gain_ref, gain_at), (bias_ref, bias_at), (start_ref, start_at), (qkv_ref, qkv_at),
            (out_ref, out_at), (up_ref, up_at), (down_ref, down_at),
        ),
        sems,
    )
    for copy in copies[:3]:
        copy.wait()
    normed, _ = normalise(hidden_at[...].astype(F32))
    norm_out[...] = (normed * gain_at[...] + bias_at[...]).astype(BF)
    for copy in copies[3:]:
        copy.wait()
    rows = qkv_at.shape[0]
    half = rows // 2
    width = HEADS * HD
    starts = start_at[...].astype(F32).astype(BF)
    for head in range(HEADS):
        part = [qkv_at[:, at * width + head * HD : at * width + (head + 1) * HD].astype(BF) for at in range(3)]
        made_ref[head, :rows] = jnp.concatenate(part[:2], axis=1)
        made_ref[head, rows : rows + half] = jnp.concatenate([part[2][:half], part[2][half:]], axis=1)
        made_ref[head, rows + half :] = jnp.broadcast_to(starts, (TAIL, 2 * HD))
    for near in range(4):
        for far in range(4):
            heads[near][far] = made_ref[place.ctx ^ (far * 4 + near)]
    out_b[...] = out_at[...].astype(BF)
    piece = ups[0].shape[2] // runs
    for near in range(4):
        for high in range(2):
            mate = place.mate ^ (high * 4 + near)
            for at in range(runs):
                first = pl.multiple_of((at * TEAM + mate) * piece, piece)
                ups[near][high, :, at * piece : (at + 1) * piece] = up_at[:, pl.ds(first, piece)].astype(BF)
    rows, half = down_at.shape[0], down_at.shape[1] // 2
    down_b[:rows] = down_at[:, :half].astype(BF)
    down_b[rows:] = down_at[:, half:].astype(BF)


def settle_kernel(table, *refs):
    place = Place(table)
    for far in range(4):
        for near in range(4):
            refs[4][place.ctx ^ (far * 4 + near)] = refs[far][near]


def head_weights(packs, w_ref, wrows, wide):
    whalf = wrows // 2
    for x in range(wide):
        for at in range(packs[x].shape[0]):
            first = (at * wide + x) * wrows
            w_ref[first : first + wrows, : 2 * HD] = packs[x][at, :wrows]
            pair = packs[x][at, wrows : wrows + whalf]
            w_ref[first : first + whalf, 2 * HD :] = pair[:, :HD]
            w_ref[first + whalf : first + wrows, 2 * HD :] = pair[:, HD:]


def unstacked(refs):
    return [ref.at[at] for ref in refs for at in range(ref.shape[0])]


def in_order(place, packs, one_ref, two_ref):
    for at in range(packs[0].shape[0]):
        one_ref[at] = jnp.where(place.x == 0, packs[0][at], packs[1][at])
        two_ref[at] = jnp.where(place.x == 0, packs[1][at], packs[0][at])


def join_kernel(table, one_ref, two_ref, _, out_ref):
    place = Place(table)
    rows = one_ref.shape[1]
    for at in range(TEAM):
        mate = place.mate ^ at
        part = (one_ref if at < 4 else two_ref)[at % 4]
        if rows % 16 == 0:
            out_ref[pl.ds(pl.multiple_of(mate * rows, rows), rows), :] = part
        else:
            for to in range(TEAM):

                @pl.when(mate == to)
                def _(to=to, part=part):
                    out_ref[to * rows : (to + 1) * rows, :] = part


def mix_kernel(*refs):
    count = len(refs) - refs[0].shape[0]
    for near in range(count):
        for far, out in enumerate(refs[count:]):
            out[near] = refs[near][far]


def ring_shifts(chips):
    shifts = [0]
    for hop in range(1, chips // 2 + 1):
        shifts += [-hop, hop] if hop < chips // 2 else [-hop]
    return shifts


def ring_order(chips, place):
    long = chips // 2
    along = (place.r * 2 + place.zh) * 2 + place.zl
    spot = jnp.where(place.y == 0, along, chips - 1 - along)
    order = []
    for shift in ring_shifts(chips):
        at = lax.rem(spot + shift + chips, chips)
        order.append(jnp.where(at < long, 2 * at, 2 * (chips - 1 - at) + 1))
    return order


def forward_kernel(table, *refs, wrows, chips, others, wide):
    pieces, others, refs = refs[:chips], refs[chips : chips + others], refs[chips + others :]
    pieces = list(pieces) + unstacked(others)
    own_ref, *refs = refs
    packs, refs = ([own_ref, refs[0]], refs[1:]) if wide == 2 else (refs[:wide], refs[wide:])
    outs, seconds = refs[:4], refs[14:]
    lse_ref, begin_ref, w_ref, w_send, q_ref, k_ref, v_ref, ot_ref, vt_ref, att_ref = refs[4:14]
    place = Place(table)
    if wide == 2:
        in_order(place, packs, *seconds)
        packs = seconds
    head_weights(packs, w_ref, wrows, wide)
    count = w_send.shape[0]
    if count < w_ref.shape[0]:
        w_send[...] = w_ref[pl.ds(pl.multiple_of(place.x * count, count), count), :]
    else:
        w_send[...] = w_ref[...]
    shards, half, _ = att_ref.shape
    rows = 2 * half
    total = shards * rows
    blocks = 2 * shards
    order = ring_order(chips, place)
    whalf = wrows // 2
    flags = []
    for block in range(blocks):
        shard, side = block_home(block, shards)
        row = own_ref[shard, wrows + whalf : wrows + whalf + 1].astype(F32)
        flags.append(row[:, side * half : (side + 1) * half])
    flags = jnp.concatenate(flags, axis=0)
    spots = half * lax.broadcasted_iota(jnp.int32, flags.shape, 0) + lax.broadcasted_iota(
        jnp.int32, flags.shape, 1
    )
    marks = jnp.where(flags > 0.5, spots.astype(F32), -1.0)
    lane = lax.broadcasted_iota(jnp.int32, marks.shape, 1)
    hop = 1
    while hop < half:
        moved = jnp.concatenate([marks[:, half - hop :], marks[:, : half - hop]], axis=1)
        marks = jnp.maximum(marks, jnp.where(lane >= hop, moved, -1.0))
        hop *= 2
    last = jnp.broadcast_to(marks[:, half - 1 :], marks.shape)
    line = lax.broadcasted_iota(jnp.int32, marks.shape, 0)
    hop = 1
    while hop < blocks:
        moved = jnp.concatenate([last[blocks - hop :], last[: blocks - hop]], axis=0)
        last = jnp.maximum(last, jnp.where(line >= hop, moved, -1.0))
        hop *= 2
    moved = jnp.concatenate([last[blocks - 1 :], last[: blocks - 1]], axis=0)
    begins = jnp.maximum(marks, jnp.where(line >= 1, moved, -1.0))
    group = TILE // half
    for tile in range(total // TILE):
        row = jnp.concatenate([begins[tile * group + at : tile * group + at + 1] for at in range(group)], axis=1)
        begin_ref[tile : tile + 1, :] = row.astype(jnp.int32)
    for which in range(2):
        for at in range(chips):
            made = dot(pieces[which * chips + at][...], w_ref[...], NN).astype(BF)
            shard = 2 * order[at] + (place.c if which == 0 else 1 - place.c)
            one = pl.multiple_of(shard * half, half)
            two = pl.multiple_of((blocks - 1 - shard) * half, half)
            scaled = made[:, :HD] * BF(HD**-0.5)
            for first, part in ((one, slice(0, half)), (two, slice(half, rows))):
                q_ref[pl.ds(first, half), :] = scaled[part]
                k_ref[pl.ds(first, half), :] = made[part, HD : 2 * HD]
                v_ref[pl.ds(first, half), :] = made[part, 2 * HD :]
    for at in range(0, total, 128):
        vt_ref[:, at : at + 128] = v_ref[at : at + 128, :].astype(F32).T.astype(BF)
    wide_tile = 2 * TILE
    for tile in range(total // wide_tile):
        low = max(0, tile - total // 2 // wide_tile) * wide_tile
        high = (tile + 1) * wide_tile
        query = q_ref[high - wide_tile : high, :]
        begin = jnp.concatenate([begin_ref[2 * tile : 2 * tile + 1, :], begin_ref[2 * tile + 1 : 2 * tile + 2, :]], axis=1)
        query_pos = high - wide_tile + lax.broadcasted_iota(jnp.int32, (1, wide_tile), 1)
        scores = dot(k_ref[low:high, :], query, NT)
        key_pos = low + lax.broadcasted_iota(jnp.int32, scores.shape, 0)
        scores = jnp.where((key_pos >= begin) & (key_pos <= query_pos), scores, FAR)
        top = jnp.max(scores, axis=0, keepdims=True)
        weights = jnp.exp(scores - top)
        sums = jnp.sum(weights, axis=0, keepdims=True)
        out = dot(vt_ref[:, low:high], weights.astype(BF), NN) / sums
        ot_ref[:, high - wide_tile : high] = out
        lse = top + jnp.log(sums)
        lse_ref[2 * tile : 2 * tile + 1, :] = lse[:, :TILE]
        lse_ref[2 * tile + 1 : 2 * tile + 2, :] = lse[:, TILE:]
        turned = out.T.astype(BF)
        for piece in range(2 * group):
            shard, side = block_home(tile * 2 * group + piece, shards)
            att_ref[shard, :, side * HD : (side + 1) * HD] = turned[piece * half : (piece + 1) * half]
    for near in range(4):
        for far in range(4):
            outs[near][far] = att_ref[place.r * HEADS + (place.ctx ^ (far * 4 + near))]


def middle_kernel(table, *refs, count):
    weights, atts, refs = refs[:count], refs[count : count + 4], refs[count + 4 :]
    hidden_ref, gain_ref, bias_ref, att_out, mid_out, norm_out, w_ref, heads_ref = refs
    place = Place(table)
    if count > 1:
        for at, ref in enumerate(unstacked(weights)):
            rows = ref.shape[0]
            first = (place.flat(2) ^ MASKS[at]) * rows
            w_ref[pl.ds(pl.multiple_of(first, rows), rows), :] = ref[...]
    else:
        w_ref[...] = weights[0][...]
    for far in range(4):
        for near in range(4):
            heads_ref[place.ctx ^ (far * 4 + near)] = atts[far][near]
    half = heads_ref.shape[1]
    for head in range(0, HEADS, 2):
        for side in range(2):
            lanes = slice(side * HD, (side + 1) * HD)
            att_out[side * half : (side + 1) * half, head * HD : (head + 2) * HD] = jnp.concatenate(
                [heads_ref[head, :, lanes], heads_ref[head + 1, :, lanes]], axis=1
            )
    mid = hidden_ref[...].astype(F32) + dot(att_out[...], w_ref[...], NN)
    mid_out[...] = mid
    normed, _ = normalise(mid)
    norm_out[...] = (normed * gain_ref[...] + bias_ref[...]).astype(BF)


def feed_kernel(table, *refs, grads, mids, wide, groups):
    grads, mids, refs = refs[:grads], refs[grads : grads + mids], refs[grads + mids :]
    *weights, lay_keep, lay_send, mnd_keep, mnd_send, mid_out, act_out, delta_out, grad_out, up_ref, down_ref = refs
    place = Place(table)
    for out, arrays in ((grad_out, grads), (mid_out, mids)):
        first = 0
        for ref in arrays:
            for part in unstacked([ref]) if len(ref.shape) == 3 else [ref]:
                out[first : first + part.shape[0], :] = part[...]
                first += part.shape[0]
    width = mid_out.shape[1]
    own = width // (TEAM * groups)
    ffn = down_ref.shape[0] // groups
    moving = len(weights) > 2
    count = len(weights) // 2
    ups, downs = weights[:count], weights[count:]
    if not moving:
        ups, downs = unstacked(ups), unstacked(downs)
    for at in range(groups):
        if moving:
            high, x = place.zh ^ (at & 1), place.x ^ (at >> 1)
        else:
            high, x = at // wide, at % wide
        for mate in range(TEAM):
            first = ((high * TEAM + mate) * wide + x) * own
            if moving:
                first = pl.multiple_of(first, own)
            up_ref[pl.ds(first, own), :] = ups[at][mate * own : (mate + 1) * own, :]
        first = (high * wide + x) * ffn
        if moving:
            first = pl.multiple_of(first, ffn)
        down_ref[pl.ds(first, ffn), : width // 2] = downs[at][:ffn, :]
        down_ref[pl.ds(first, ffn), width // 2 :] = downs[at][ffn:, :]
    total = mid_out.shape[0]
    run = 256
    half = total // 2
    for first in list(range(half, total, run)) + list(range(0, half, run)):
        here = slice(first, first + run)
        up = dot(mid_out[here, :], up_ref[...], NN)
        value, slope = gelu_both(up)
        act = value.astype(BF)
        act_out[here, :] = act
        delta = (dot(grad_out[here, :], down_ref[...], NT) * slope).astype(BF)
        delta_out[here, :] = delta
        back = dot(delta, up_ref[...], NT)
        fore = dot(act, down_ref[...], NN)
        if first < half:
            mnd_keep[here, :] = back
            lay_keep[here, :] = fore.astype(BF)
        else:
            there = slice(first - half, first - half + run)
            mnd_send[there, :] = back.astype(BF)
            lay_send[there, :] = fore.astype(BF)


def turn_kernel(
    table, grad_ref, mid_ref, w_ref, keep_top, got_top, keep_low, got_low, gain_ref, delta_out, bf_out, *refs
):
    *outs, made_ref = refs
    mnd = jnp.concatenate(
        [keep_top[...] + got_top[...].astype(F32), keep_low[...] + got_low[...].astype(F32)], axis=0
    )
    normed, spread = normalise(mid_ref[...])
    delta = grad_ref[...].astype(F32) + norm_back(mnd, normed, spread, gain_ref[...])
    delta_out[...] = delta
    narrow = delta.astype(BF)
    bf_out[...] = narrow
    back = dot(narrow, w_ref[...], NT).astype(BF)
    half = made_ref.shape[1]
    for head in range(HEADS):
        cols = slice(head * HD, (head + 1) * HD)
        made_ref[head] = jnp.concatenate([back[:half, cols], back[half:, cols]], axis=1)
    place = Place(table)
    for near in range(4):
        for far in range(4):
            outs[near][far] = made_ref[place.ctx ^ (far * 4 + near)]


TEAM_ORDER = (0, 4, 2, 6, 1, 5, 3, 7)


def out_grad_kernel(table, lay_keep, lay_send, att_ref, delta_ref, keep_out, send_out, part_ref, *, wide, wrows):
    turned = att_ref[...].astype(F32).T.astype(BF)
    part_ref[...] = dot(turned, delta_ref[...], NN).astype(BF).reshape(part_ref.shape)
    place = Place(table)
    rows = lay_keep.shape[0] // 4
    highs = part_ref.shape[0] // (TEAM * wide)
    for at in range(TEAM):
        mate = place.mate ^ TEAM_ORDER[at]
        out, lay = (keep_out, lay_keep) if at < 4 else (send_out, lay_send)
        first = (at % 4) * 2 * rows
        out[first : first + rows, :] = lay[(at % 4) * rows : (at % 4 + 1) * rows, :]
        first += rows
        for x in range(wide):
            for high in range(highs):
                out[first : first + wrows, :] = part_ref[(high * TEAM + mate) * wide + x]
                first += wrows


def up_pack_kernel(table, part_ref, delta_ref, *outs, wide):
    rows = (outs[0].shape[0] - TAIL) // TEAM
    tail = sum_lines(jnp.sum(delta_ref[...].astype(F32), axis=0, keepdims=True))
    place = Place(table)
    highs = len(outs) // wide
    for at, out in enumerate(outs):
        if wide == 2:
            x, high = place.x ^ (at >> 1), place.zh ^ (at & 1)
        else:
            x, high = at // highs, at % highs
        for mate in range(TEAM):
            first = ((high * TEAM + mate) * wide + x) * rows
            if wide == 2:
                first = pl.multiple_of(first, rows)
            out[mate * rows : (mate + 1) * rows] = part_ref[pl.ds(first, rows), :].astype(BF)
        out[TEAM * rows :] = tail


def down_pack_kernel(table, part_ref, *outs, wide):
    rows = outs[0].shape[0]
    place = Place(table)
    highs = len(outs) // wide
    for at, out in enumerate(outs):
        if wide == 2:
            x, high = place.x ^ (at >> 1), place.zh ^ (at & 1)
        else:
            x, high = at // highs, at % highs
        first = (high * wide + x) * rows
        if wide == 2:
            first = pl.multiple_of(first, rows)
        out[...] = part_ref[pl.ds(first, rows), :].astype(BF)


def up_add_kernel(own_ref, got_ref, out_ref):
    body, tail = add_lines(own_ref[...], got_ref[...])
    out_ref[: body.shape[0]] = body
    out_ref[body.shape[0] :] = tail


def sum_kernel(own_ref, got_ref, out_ref):
    out_ref[...] = (own_ref[...].astype(F32) + got_ref[...].astype(F32)).astype(out_ref.dtype)


def up_share_kernel(table, own_ref, got_ref, *refs):
    *outs, all_ref = refs
    place = Place(table)
    rows = outs[0].shape[1] - TAIL
    body, tail = add_lines(own_ref[...], got_ref[...])
    for mate in range(TEAM):
        all_ref[mate] = body[mate * rows : (mate + 1) * rows]
    for near in range(4):
        for high in range(2):
            out = outs[near]
            out[high, :rows] = all_ref[place.mate ^ (high * 4 + near)]
            out[high, rows:] = tail


def sum_lines(sums):
    high, low = split_two(sums)
    line = lax.broadcasted_iota(jnp.int32, (8, sums.shape[1]), 0)
    return jnp.where(line == 0, high.astype(F32), jnp.where(line == 1, low.astype(F32), 0.0)).astype(BF)


def add_lines(own, got):
    rows = own.shape[0] - TAIL
    total = own.astype(F32) + got.astype(F32)
    return total[:rows].astype(BF), sum_lines(total[rows : rows + 1] + total[rows + 1 : rows + 2])


def owner_column(row_ref, first, rows):
    shape = (rows, row_ref.shape[1])
    hit = lax.broadcasted_iota(jnp.int32, shape, 1) == first + lax.broadcasted_iota(jnp.int32, shape, 0)
    return jnp.sum(jnp.where(hit, row_ref[...], 0.0), axis=1, keepdims=True)


def as_row(column):
    shape = (column.shape[0],) * 2
    hit = lax.broadcasted_iota(jnp.int32, shape, 0) == lax.broadcasted_iota(jnp.int32, shape, 1)
    return jnp.sum(jnp.where(hit, column, 0.0), axis=0, keepdims=True)


def norm_grads(place, master_ref, grad_ref, sums, gain_ref, bias_ref, gain_out, bias_out, wide):
    rows = master_ref.shape[0]
    first = place.flat(wide) * rows
    own = master_ref[...].astype(BF).astype(F32)
    bias_grad = jnp.sum(own * sums, axis=1, keepdims=True)
    bias_out[...] = as_row(bias_grad)
    gain_grad = jnp.sum(own * grad_ref[...], axis=1, keepdims=True) - owner_column(bias_ref, first, rows) * bias_grad
    gain_out[...] = as_row(gain_grad / owner_column(gain_ref, first, rows))


def up_end_kernel(table, one_ref, two_ref, own_ref, gain_ref, bias_ref, grad_out, gain_out, bias_out, sum_ref, *, runs, wide):
    place = Place(table)
    rows = own_ref.shape[0]
    piece = one_ref.shape[2] // runs
    for high, ref in ((0, one_ref), (1, two_ref)):
        for near in range(4):
            mate = place.mate ^ (high * 4 + near)
            for at in range(runs):
                there = pl.ds(pl.multiple_of((at * TEAM + mate) * piece, piece), piece)
                part = ref[near, :, at * piece : (at + 1) * piece].astype(F32)
                grad_out[:, there] = part[:rows]
                sum_ref[:, there] = part[rows : rows + 1] + part[rows + 1 : rows + 2]
    norm_grads(place, own_ref, grad_out, sum_ref[...], gain_ref, bias_ref, gain_out, bias_out, wide)


def qkv_end_kernel(table, *refs, wide):
    parts, (own_ref, gain_ref, bias_ref, grad_out, gain_out, bias_out, all_ref) = refs[:4], refs[4:]
    place = Place(table)
    for far in range(4):
        for near in range(4):
            all_ref[place.ctx ^ (far * 4 + near)] = parts[far][near]
    rows = own_ref.shape[0]
    half = rows // 2
    width = HEADS * HD
    body = rows + half
    for head in range(0, HEADS, 2):
        for at in range(2):
            lanes = slice(at * HD, (at + 1) * HD)
            grad_out[:, at * width + head * HD : at * width + (head + 2) * HD] = jnp.concatenate(
                [all_ref[head, :rows, lanes], all_ref[head + 1, :rows, lanes]], axis=1
            ).astype(F32)
        for side in range(2):
            lanes = slice(side * HD, (side + 1) * HD)
            grad_out[side * half : (side + 1) * half, 2 * width + head * HD : 2 * width + (head + 2) * HD] = (
                jnp.concatenate([all_ref[head, rows:body, lanes], all_ref[head + 1, rows:body, lanes]], axis=1).astype(
                    F32
                )
            )
    lines = [[], [], []]
    for head in range(HEADS):
        tail = all_ref[head, body:, :].astype(F32)
        pair = tail[0:1] + tail[1:2]
        lines[0].append(pair[:, :HD])
        lines[1].append(pair[:, HD:])
        lines[2].append(tail[2:3, :HD] + tail[2:3, HD:])
    sums = jnp.concatenate(lines[0] + lines[1] + lines[2], axis=1)
    norm_grads(place, own_ref, grad_out, sums, gain_ref, bias_ref, gain_out, bias_out, wide)


def backward_kernel(table, *refs):
    douts, refs = refs[:4], refs[4:]
    (
        q_ref, k_ref, v_ref, ot_ref, lse_ref, begin_ref, own_out, mate_out, dn_ref, sum_ref,
        do_ref, dop_ref, kt_ref, dq_ref, dk_ref, dv_ref, da_ref,
    ) = refs
    place = Place(table)
    for part in range(douts[0].shape[0]):
        for far in range(4):
            for near in range(4):
                do_ref[part * HEADS + (place.ctx ^ (far * 4 + near))] = douts[far][part, near]
    shards, half, _ = do_ref.shape
    rows = 2 * half
    total = shards * rows
    for block in range(2 * shards):
        shard, side = block_home(block, shards)
        dop_ref[block * half : (block + 1) * half, :] = do_ref[shard, :, side * HD : (side + 1) * HD]
    for at in range(0, total, 128):
        kt_ref[:, at : at + 128] = k_ref[at : at + 128, :].astype(F32).T.astype(BF)
    dk_ref[...] = jnp.zeros_like(dk_ref)
    dv_ref[...] = jnp.zeros_like(dv_ref)
    for tile in range(total // TILE):
        here = slice(tile * TILE, (tile + 1) * TILE)
        query = q_ref[here, :]
        dout = dop_ref[here, :]
        begin = begin_ref[tile : tile + 1, :]
        lse = lse_ref[tile : tile + 1, :]
        row_dot = jnp.sum(dout.astype(F32).T * ot_ref[:, here], axis=0, keepdims=True)
        query_pos = tile * TILE + lax.broadcasted_iota(jnp.int32, (1, TILE), 1)
        low = max(0, tile - total // 2 // TILE) * TILE
        there = slice(low, (tile + 1) * TILE)
        scores = dot(k_ref[there, :], query, NT)
        key_pos = low + lax.broadcasted_iota(jnp.int32, scores.shape, 0)
        allowed = (key_pos >= begin) & (key_pos <= query_pos)
        probs = jnp.where(allowed, jnp.exp(scores - lse), 0.0)
        dprobs = dot(v_ref[there, :], dout, NT)
        delta = (probs * (dprobs - row_dot)).astype(BF)
        dv_ref[there, :] += dot(probs.astype(BF), dout, NN)
        dk_ref[there, :] += dot(delta, query, NN)
        accum = dot(kt_ref[:, there], delta, NN)
        dq_ref[here, :] = (accum * HD**-0.5).T
    sums = jnp.zeros((1, TRIPLE), F32)
    for block in range(2 * shards):
        shard, side = block_home(block, shards)
        at = slice(block * half, (block + 1) * half)
        pair = jnp.concatenate([dq_ref[at, :], dk_ref[at, :]], axis=1).astype(BF)
        last = dv_ref[at, :].astype(BF)
        da_ref[shard, side * half : (side + 1) * half, :] = pair
        da_ref[shard, rows : rows + half, side * HD : (side + 1) * HD] = last
        to = slice(side * half, (side + 1) * half)
        joined = jnp.concatenate([pair, last], axis=1)
        dn_ref[shard, to, :] = joined
        sums = sums + jnp.sum(joined.astype(F32), axis=0, keepdims=True)
    sum_ref[...] = sums
    base = place.r * HEADS
    for at in range(TEAM):
        own_out[at] = da_ref[base + place.zh * TEAM + at]
        mate_out[at] = da_ref[base + (1 - place.zh) * TEAM + at]


def qkv_lines(pair, last):
    line = lax.broadcasted_iota(jnp.int32, (8, 2 * HD), 0)
    high, low = split_two(pair)
    both = jnp.concatenate(split_two(last), axis=1)
    lines = jnp.where(line == 0, high.astype(F32), jnp.where(line == 1, low.astype(F32), both.astype(F32)))
    return lines.astype(BF)


def qkv_grad_kernel(table, *refs, repeats, chips, others, wide):
    pieces, stacks, (dn_ref, sum_ref, *outs, acc_ref) = refs[:chips], refs[chips : chips + others], refs[chips + others :]
    pieces = list(pieces) + unstacked(stacks)
    place = Place(table)
    order = ring_order(chips, place)
    total = None
    for which in range(2):
        for at in range(chips):
            shard = 2 * order[at] + (place.c if which == 0 else 1 - place.c)
            turned = dn_ref[shard].astype(F32).T.astype(BF)
            step = dot(turned, pieces[which * chips + at][...], NN)
            total = step if total is None else total + step
    acc_ref[...] = total.T
    owners, tall, _ = outs[0].shape
    rows = (tall - TAIL) * 2 // 3
    half = rows // 2
    sums = sum_ref[...]
    lines = qkv_lines(sums[:, : 2 * HD], sums[:, 2 * HD :])

    def write(base):
        for at, out in enumerate(outs):
            x = place.x ^ at if wide == 2 else at
            for owner in range(owners):
                first = base + (owner * wide + x) * rows
                if wide == 2:
                    first = pl.multiple_of(first, rows)
                grad = acc_ref[pl.ds(first, rows), :]
                out[owner, :rows] = grad[:, : 2 * HD].astype(BF)
                out[owner, rows : rows + half] = jnp.concatenate(
                    [grad[:half, 2 * HD :], grad[half:, 2 * HD :]], axis=1
                ).astype(BF)
                out[owner, rows + half :] = lines

    if repeats == 1:
        write(0)
    else:
        for at in range(repeats):
            pl.when(place.r == at)(partial(write, at * owners * wide * rows))


def qkv_add_kernel(table, own_ref, got_ref, *outs):
    place = Place(table)
    body = own_ref.shape[1] - TAIL
    for near in range(4):
        for far in range(4):
            at = place.ctx ^ (far * 4 + near)
            total = own_ref[at].astype(F32) + got_ref[at].astype(F32)
            outs[near][far, :body] = total[:body].astype(BF)
            tail = total[body:]
            outs[near][far, body:] = qkv_lines(tail[0:1] + tail[1:2], tail[2:3, :HD] + tail[2:3, HD:])


def spread_kernel(_, keep_ref, got_ref, send_z, send_y, top_out, low_out):
    rows = keep_ref.shape[0] // 4
    half = rows // 2
    for at in range(4):
        for side in range(2):
            here = slice(at * rows + side * half, at * rows + (side + 1) * half)
            total = keep_ref[here, :].astype(F32) + got_ref[here, :].astype(F32)
            if side == 0:
                if at % 2 == 0:
                    top_out[at // 2] = total
                else:
                    send_z[at // 2] = total.astype(BF)
            elif at < 2:
                low_out[at] = total
            else:
                send_y[at - 2] = total.astype(BF)


def narrow_kernel(_, top_ref, got_z, low_ref, got_y, send_y, send_z, top_out, low_out):
    top_out[...] = top_ref[0] + got_z[0].astype(F32)
    low_out[...] = low_ref[0] + got_y[0].astype(F32)
    send_y[...] = (top_ref[1] + got_z[1].astype(F32)).astype(BF)
    send_z[...] = (low_ref[1] + got_y[1].astype(F32)).astype(BF)


def input_kernel(table, own_ref, got_ref, *refs):
    tall = own_ref.shape[1]
    rows = tall * 2 // 3
    half = rows // 2
    place = Place(table)
    w_own, *mates, keep_out, send_out, lhs_ref, rhs_ref = refs
    rhs_ref[:, : 2 * HD] = w_own[:, : 2 * HD]
    rhs_ref[:, 2 * HD : 3 * HD] = w_own[:, 2 * HD :]
    for at, w_got in enumerate(mates):
        count = w_got.shape[0]
        here = slice(0, count)
        if len(mates) == 2:
            here = pl.ds(pl.multiple_of((place.x ^ at) * count, count), count)
        rhs_ref[here, 3 * HD : 4 * HD] = w_got[:, 2 * HD :]
        rhs_ref[here, 4 * HD :] = w_got[:, : 2 * HD]
    for at in range(TEAM):
        mate = place.mate ^ TEAM_ORDER[at]
        first = at * rows
        one, two = own_ref[mate], got_ref[mate]
        lhs_ref[first : first + rows, : 2 * HD] = one[:rows]
        lhs_ref[first : first + rows, 4 * HD :] = two[:rows]
        for side in range(2):
            lanes = slice(side * HD, (side + 1) * HD)
            lhs_ref[first + side * half : first + (side + 1) * half, 2 * HD : 4 * HD] = jnp.concatenate(
                [one[rows:, lanes], two[rows:, lanes]], axis=1
            )
    middle = TEAM * rows // 2
    send_out[...] = dot(lhs_ref[middle:, :], rhs_ref[...], NT).astype(BF)
    keep_out[...] = dot(lhs_ref[:middle, :], rhs_ref[...], NT)


def last_kernel(_, keep_top, got_top, keep_low, got_low, mid_delta_ref, hidden_ref, gain_ref, out_ref):
    grad = jnp.concatenate(
        [keep_top[...] + got_top[...].astype(F32), keep_low[...] + got_low[...].astype(F32)], axis=0
    )
    normed, spread = normalise(hidden_ref[...].astype(F32))
    out_ref[...] = (mid_delta_ref[...] + norm_back(grad, normed, spread, gain_ref[...])).astype(BF)


def outs_kernel(table, mid_ref, lay_ref, got_lay, part_ref, got_part, lay_out, *outs, wide):
    lay_out[...] = (mid_ref[...] + lay_ref[...] + got_lay[...].astype(F32)).astype(BF)
    highs, rows, _ = outs[0].shape
    place = Place(table)
    for side, out in enumerate(outs):
        for at in range(highs):
            x, high = (place.x ^ side, place.zh ^ at) if wide == 2 else (side, at)
            first = (x * highs + high) * rows
            if wide == 2:
                first = pl.multiple_of(first, rows)
            out[at] = (part_ref[pl.ds(first, rows), :] + got_part[pl.ds(first, rows), :].astype(F32)).astype(BF)


def after(array, *others):
    return lax.optimization_barrier((array, *others))[0]


def apart(count, mask):
    return [(at, at ^ mask) for at in range(count)]


def stack(arrays):
    count = sum(array.shape[0] if array.ndim == 3 else 1 for array in arrays)
    return call(stack_kernel, arrays, [((count,) + arrays[0].shape[-2:], arrays[0].dtype)], smem=0)[0]


def meet(*arrays):
    return lax.optimization_barrier(arrays)


def near(arrays):
    return [lax.ppermute(arrays[at], ("y", "c"), apart(4, at)) for at in range(1, 4)]


def far(arrays):
    return [lax.ppermute(arrays[at], ("zh", "zl"), apart(4, at)) for at in range(1, 4)]


def swap(array, axis):
    return lax.ppermute(array, axis, SWAP)


def mix(arrays):
    shape = arrays[0].shape
    return call(mix_kernel, arrays, [((len(arrays),) + shape[1:], arrays[0].dtype)] * shape[0], smem=0)


def stack_kernel(*refs):
    at = 0
    for ref in refs[:-1]:
        count = ref.shape[0] if len(ref.shape) == 3 else 1
        for part in range(count):
            refs[-1][at] = ref[part] if len(ref.shape) == 3 else ref[...]
            at += 1


def spread(table, keep, got):
    shape = (keep.shape[0] // 8, keep.shape[1])
    return call(spread_kernel, (table, keep, got), [((2, *shape), BF)] * 2 + [((2, *shape), F32)] * 2)


def narrow(table, top, got_z, low, got_y):
    shape = top.shape[1:]
    return call(narrow_kernel, (table, top, got_z, low, got_y), [(shape, BF)] * 2 + [(shape, F32)] * 2)


def add(one, two, kind):
    return call(sum_kernel, (one, two), [(one.shape, kind)], smem=0)[0]


class Steps:
    def __init__(self, arrays, sizes):
        (
            self.hidden, self.start, self.qkv, self.out, self.up, self.down,
            gain1, bias1, gain2, bias2, self.grad,
        ) = arrays
        self.hidden, self.grad = self.hidden[0], self.grad[0]
        self.gain1, self.bias1, self.gain2, self.bias2 = (a[None] for a in (gain1, bias1, gain2, bias2))
        self.repeats, self.wide = sizes["r"], sizes["x"]
        self.rows, self.width = self.hidden.shape
        self.half = self.rows // 2
        self.shards = self.repeats * HEADS
        self.total = self.shards * self.rows
        self.wrows, self.ffn = self.qkv.shape[0], self.down.shape[0]
        self.highs = 2 * self.repeats
        self.cols = self.highs * self.wide * self.ffn
        self.many = TEAM * self.rows
        self.qkv_tall = self.wrows * 3 // 2 + TAIL
        self.up_tall = self.wrows + TAIL
        self.sides = self.wide * self.highs
        self.piece = ((4, self.half, 2 * HD), BF)
        self.table = jnp.stack([lax.axis_index(axis).astype(jnp.int32) for axis in ALL])

    def first(self):
        masters = (self.qkv, self.out, self.up, self.down)
        row = ((1, self.width), F32)
        outs = call(
            partial(first_kernel, runs=self.highs),
            (self.table, self.hidden, self.gain1, self.bias1, *masters, self.start),
            [
                ((self.rows, self.width), BF),
                *[((4, self.qkv_tall, 2 * HD), BF)] * 4,
                ((self.wrows, self.width), BF),
                *[((2, self.wrows, self.cols), BF)] * 4,
                ((2 * self.ffn, self.width // 2), BF),
            ],
            [
                ((self.rows, self.width), BF), row, row,
                *[(a.shape, F32) for a in masters],
                (self.start.shape, jnp.int32),
                ((HEADS, self.qkv_tall, 2 * HD), BF),
            ],
            far=8,
            sems=8,
            limit=58,
        )
        return outs[0], list(outs[1:5]), outs[5], list(outs[6:10]), outs[10]

    def forward(self, pieces, others, packs):
        tokens = ((self.total, HD), BF)
        tiles = (self.total // TILE, TILE)
        sent = self.width // 2 if self.repeats == 1 and self.wide == 2 else self.width
        outs = call(
            partial(forward_kernel, wrows=self.wrows, chips=len(pieces), others=len(others), wide=self.wide),
            (self.table, *pieces, *others, *packs),
            [
                *[self.piece] * 4,
                (tiles, F32), (tiles, jnp.int32),
                ((self.width, TRIPLE), BF), ((sent, TRIPLE), BF),
                tokens, tokens, tokens,
                ((HD, self.total), F32),
            ],
            [((HD, self.total), BF), ((self.shards, self.half, 2 * HD), BF)]
            + [((self.shards, self.qkv_tall, 2 * HD), BF)] * (2 if self.wide == 2 else 0),
            limit=20 * self.repeats * self.repeats,
            micros=7,
        )
        return list(outs[:4]), list(outs[6:8]), (*outs[8:], *outs[4:6])

    def middle(self, weights, heads):
        return call(
            partial(middle_kernel, count=len(weights)),
            (self.table, *weights, *heads, self.hidden, self.gain2, self.bias2),
            [
                ((self.rows, self.width), BF),
                ((self.rows, self.width), F32),
                ((self.rows, self.width), BF),
                ((self.width, self.width), BF),
            ],
            [((HEADS, self.half, 2 * HD), BF)],
        )

    def feed(self, grads, mids, weights):
        half, full = (self.many // 2, self.width), (self.many, self.width)
        inner = ((self.many, self.cols), BF)
        return call(
            partial(
                feed_kernel, grads=len(grads), mids=len(mids), wide=self.wide, groups=self.highs * self.wide
            ),
            (self.table, *grads, *mids, *weights),
            [(half, BF), (half, BF), (half, F32), (half, BF), (full, BF), inner, inner, (full, BF)],
            [((self.width, self.cols), BF), ((self.cols, self.width), BF)],
            micros=6,
        )

    def up_gradient(self, mids, delta):
        return call(
            partial(up_pack_kernel, wide=self.wide),
            (self.table, dot(mids, delta, TN), delta),
            [((self.width // (self.highs * self.wide) + TAIL, self.cols), BF)] * self.sides,
        )

    def down_gradient(self, acts, grads):
        return call(
            partial(down_pack_kernel, wide=self.wide),
            (self.table, dot(acts, grads, TN)),
            [((self.ffn, self.width), BF)] * self.sides,
        )

    def turn(self, mid, w_out, ends):
        outs = call(
            turn_kernel,
            (self.table, self.grad, mid, w_out, *ends, self.gain2),
            [((self.rows, self.width), F32), ((self.rows, self.width), BF), *[self.piece] * 4],
            [((HEADS, self.half, 2 * HD), BF)],
        )
        return outs[0], outs[1], list(outs[2:])

    def out_gradient(self, lay_keep, lay_send, attended, delta):
        return call(
            partial(out_grad_kernel, wide=self.wide, wrows=self.wrows),
            (self.table, lay_keep, lay_send, attended, delta),
            [((self.many, self.width), BF)] * 2,
            [((self.shards * self.wide, self.wrows, self.width), BF)],
        )

    def backward(self, kept, douts):
        query, keys, values, out_t, lse, begin = kept
        tall = self.rows + self.half
        total = ((self.total, HD), F32)
        return call(
            backward_kernel,
            (self.table, *douts, query, keys, values, out_t, lse, begin),
            [
                ((TEAM, tall, 2 * HD), BF),
                ((TEAM, tall, 2 * HD), BF),
                ((self.shards, self.rows, TRIPLE), BF),
                ((1, TRIPLE), F32),
            ],
            [
                ((self.shards, self.half, 2 * HD), BF),
                ((self.total, HD), BF),
                ((HD, self.total), BF),
                total, total, total,
                ((self.shards, tall, 2 * HD), BF),
            ],
            limit=14 * self.repeats * self.repeats,
            micros=8,
        )

    def qkv_gradient(self, pieces, others, by_shard, sums):
        return call(
            partial(
                qkv_grad_kernel,
                repeats=self.repeats, chips=len(pieces), others=len(others), wide=self.wide,
            ),
            (self.table, *pieces, *others, by_shard, sums),
            [((HEADS, self.qkv_tall, 2 * HD), BF)] * self.wide,
            [((self.width, TRIPLE), F32)],
        )

    def up_share(self, own, got):
        return list(
            call(
                up_share_kernel,
                (self.table, own, got),
                [((2, self.up_tall, self.cols), BF)] * 4,
                [((TEAM, self.wrows, self.cols), BF)],
            )
        )

    def qkv_share(self, own, got):
        return list(call(qkv_add_kernel, (self.table, own, got), [((4, self.qkv_tall, 2 * HD), BF)] * 4))

    def outputs(self, mid, ends):
        return call(
            partial(outs_kernel, wide=self.wide),
            (self.table, mid, *ends),
            [((self.rows, self.width), BF)] + [((self.highs, self.wrows, self.width), BF)] * self.wide,
        )

    def inputs(self, to_own, from_mate, weights, mates):
        return call(
            input_kernel,
            (self.table, to_own, from_mate, weights, *mates),
            [((self.many // 2, self.width), F32), ((self.many // 2, self.width), BF)],
            [((self.many, 2 * TRIPLE), BF), ((self.width, 2 * TRIPLE), BF)],
        )

    def last(self, ends, mid_delta):
        return call(
            last_kernel,
            (self.table, *ends, mid_delta, self.hidden, self.gain1),
            [((self.rows, self.width), BF)],
        )[0]

    def up_end(self, ends):
        line = ((1, self.wrows), F32)
        return call(
            partial(up_end_kernel, runs=self.highs, wide=self.wide),
            (self.table, *ends, self.up, self.gain2, self.bias2),
            [(self.up.shape, F32), line, line],
            [((1, self.up.shape[1]), F32)],
        )

    def qkv_end(self, ends):
        line = ((1, self.wrows), F32)
        return call(
            partial(qkv_end_kernel, wide=self.wide),
            (self.table, *ends, self.qkv, self.gain1, self.bias1),
            [(self.qkv.shape, F32), line, line],
            [((HEADS, self.qkv_tall, 2 * HD), BF)],
        )


def ring_moves(long):
    count = 2 * long
    order = [2 * at for at in range(long)] + [2 * at + 1 for at in reversed(range(long))]
    right = [(order[at], order[(at + 1) % count]) for at in range(count)]
    return right, [(two, one) for one, two in right]


def results(layer_out, grad_in, qkv, out, up, down):
    return (
        layer_out[None], grad_in[None], qkv[0], out, up[0], down,
        qkv[1][0], qkv[2][0], up[1][0], up[2][0],
    )


def local(*arrays, sizes):
    s = Steps(arrays, sizes)
    right, left = ring_moves(4)

    def ahead(array):
        return lax.ppermute(array, CHIPS, right)

    def behind(array):
        return lax.ppermute(array, CHIPS, left)

    norm_in, by_head, out_b, up_b, down_b = s.first()
    a1, b1, *got = meet(ahead(norm_in), behind(norm_in), *near(by_head))
    packs = mix([by_head[0], *got])
    a2, b2, *got = meet(ahead(a1), behind(b1), *far(packs))
    (packed,) = call(settle_kernel, (s.table, packs[0], *got), [((HEADS, s.qkv_tall, 2 * HD), BF)])
    first = stack([norm_in, a1, b1, a2, b2])
    ups = [after(up, a2) for up in up_b]
    a3, b3, packed_x, *got = meet(ahead(a2), behind(b2), swap(packed, "x"), *near(ups))
    ups = mix([ups[0], *got])
    a4, up_z, first, down_x = meet(
        ahead(a3), swap(ups[1], "zl"), swap(after(first, a3), "c"), swap(after(down_b, a3), "x")
    )
    second = stack([a3, b3])
    (up_t,) = call(join_kernel, (s.table, ups[0], up_z, down_b), [((TEAM * s.wrows, s.cols), BF)])
    pieces = [norm_in, a1, b1, a2, b2, a3, b3, a4]
    others = [first, *meet(swap(second, "c"), swap(a4[None], "c"))]

    out = after(out_b, a4)
    out_z = [lax.ppermute(out, ("zh", "zl"), apart(4, at)) for at in range(1, 4)]
    grad = after(s.grad, a4)
    grad_z = swap(grad, "zl")
    att, w_head, kept = s.forward(pieces, others, [packed, packed_x])
    *att, grad_z, o1, o2, o3 = meet(*att, grad_z, *out_z)
    out_4 = stack([out, o1, o2, o3])
    *got, out_x, up_z, grad_y = meet(
        *near(att), swap(out_4, "x"), swap(after(up_t, att[0]), "zh"), swap(after(grad, att[0]), "y")
    )
    att = mix([att[0], *got])
    out_8 = stack([out_4, out_x])
    *got, out_8y, up_x, out_8c = meet(
        *far(att), swap(out_8, "y"), swap(after(up_t, att[0]), "x"), swap(out_8, "c")
    )
    attended, mid, norm_mid, w_out = s.middle([out_8, out_8y, out_8c, swap(out_8y, "c")], [att[0], *got])

    half = s.half
    grad_3 = stack([after(grad, norm_mid), grad_z, grad_y])
    by_z, by_y, up_zx, down_z, grad_3c = meet(
        swap(norm_mid, "zl"),
        swap(norm_mid, "y"),
        swap(after(up_z, norm_mid), "x"),
        swap(after(down_b, norm_mid), "zh"),
        swap(grad_3, "c"),
    )
    three = stack([norm_mid, by_z, by_y])
    both_one, both_two, three, down_zx, grad_one, grad_two = meet(
        swap(by_y[:half], "zl"),
        swap(by_z[half:], "y"),
        swap(three, "c"),
        swap(after(down_z, by_z), "x"),
        swap(after(grad_y[:half], by_z), "zl"),
        swap(after(grad_z[half:], by_z), "y"),
    )
    both = stack([both_one, both_two])
    grad_both = stack([grad_one, grad_two])
    mids = [norm_mid, by_z, by_y, both_one, both_two, three, swap(both, "c")]
    grads = [grad, grad_z, grad_y, grad_one, grad_two, grad_3c, swap(grad_both, "c")]
    lay_keep, lay_send, keep, send, mids, acts, delta, grads = s.feed(
        grads, mids, [up_t, up_z, up_x, up_zx, down_b, down_z, down_x, down_zx]
    )
    send_z, send_y, top, low = spread(s.table, keep, swap(send, "c"))
    up_parts = s.up_gradient(mids, after(delta, send_z))
    got_z, got_y, *up_parts = meet(swap(send_z, "zl"), swap(send_y, "y"), *up_parts)
    send_y, send_z, top, low = narrow(s.table, top, got_z, low, got_y)
    down_parts = s.down_gradient(after(acts, send_y), grads)
    end_top, end_low, up_far, *down_parts = meet(
        swap(send_y, "y"), swap(send_z, "zl"), swap(after(up_parts[3], send_y), "x"), *down_parts
    )
    mid_delta, mid_delta_b, by_head = s.turn(mid, w_out, (top, end_top, low, end_low))
    *got, up_near, mate_1 = meet(
        *near(by_head),
        swap(after(up_parts[2], mid_delta), "x"),
        swap(after(w_head[1], mid_delta), "zh"),
    )
    by_head = mix([by_head[0], *got])
    up_shape = up_parts[0].shape
    (up_send,) = call(up_add_kernel, (up_parts[1], after(up_far, by_head[0])), [(up_shape, BF)], smem=0)
    keep, send = s.out_gradient(after(lay_keep, by_head[0]), lay_send, attended, mid_delta_b)
    *got, send, down_far, up_send = meet(
        *far(by_head), swap(send, "c"), swap(after(down_parts[3], by_head[0]), "x"), up_send
    )

    douts = [array[None] for array in (by_head[0], *got)]
    send_z, send_y, top, low = spread(s.table, keep, send)
    got_z, got_y = swap(send_z, "zl"), swap(send_y, "y")
    up_got = swap(up_send, "zh")
    down_near = swap(after(down_parts[2], send), "x")
    mate_2 = swap(after(mate_1, send), "x")
    kept = (after(kept[0], send_z), *kept[1:])
    to_own, to_mate, by_shard, sums = s.backward(kept, douts)
    from_mate = swap(to_mate, "zh")
    to_own, got_z, got_y, down_near, mate_2 = meet(to_own, got_z, got_y, down_near, mate_2)
    send_y, send_z, top, low = narrow(s.table, top, got_z, low, got_y)
    (up_keep,) = call(up_add_kernel, (up_parts[0], after(up_near, to_own)), [(up_shape, BF)], smem=0)
    qkv_own, qkv_send = s.qkv_gradient(pieces, others, after(by_shard, send_y), sums)
    down_send = add(down_parts[1], after(down_far, send_y), BF)
    end_top, end_low, qkv_send, up_got, down_send = meet(
        swap(send_y, "y"), swap(send_z, "zl"), qkv_send, up_got, down_send
    )
    ups = s.up_share(up_keep, up_got)
    ends = top, end_top, low, end_low
    down_keep = add(down_parts[0], after(down_near, end_top), F32)
    from_mate, qkv_got, *got = meet(from_mate, swap(after(qkv_send, end_top), "x"), *near(ups))
    keep, send = s.inputs(to_own, from_mate, w_head[0], [mate_1, mate_2])
    layer_out, *outs = s.outputs(mid, [after(array, send) for array in ends])
    qkv = s.qkv_share(qkv_own, after(qkv_got, send))
    send, layer_out, *qkv = meet(swap(send, "c"), layer_out, *qkv)

    send_z, send_y, top, low = spread(s.table, keep, send)
    down_got = swap(after(down_send, send_z), "zh")
    got_z, got_y, out_got, *more = meet(
        swap(send_z, "zl"),
        swap(send_y, "y"),
        swap(after(outs[1], send_z), "x"),
        *near([after(a, send_z) for a in qkv]),
    )
    send_y, send_z, top, low = narrow(s.table, top, got_z, low, got_y)
    ups = mix([after(ups[0], send_y), *got])
    qkv = mix([after(qkv[0], send_y), *more])
    (out_sum,) = call(sum_kernel, (outs[0], after(out_got, send_y)), [(outs[0].shape, BF)], smem=0)
    end_top, end_low, ups_z, down_got, *more = meet(
        swap(send_y, "y"), swap(send_z, "zl"), swap(ups[1], "zl"), down_got, *far(qkv)
    )
    out_got = swap(after(out_sum[1], end_top), "zh")
    grad_in = s.last((top, end_top, low, end_low), mid_delta)
    end = s.qkv_end([qkv[0], *more])
    up = s.up_end((ups[0], ups_z))
    down = add(down_keep, down_got, F32)
    out = add(out_sum[0], out_got, F32)
    return results(layer_out, grad_in, end, out, up, down)


def local_any(*arrays, sizes):
    s = Steps(arrays, sizes)
    repeats, wide = s.repeats, s.wide
    long = 4 * repeats
    right, left = ring_moves(long)
    norm_in, by_head, out_b, up_b, down_b = s.first()
    one = two = norm_in
    pieces = [norm_in]
    for hop in range(1, long + 1):
        one = lax.ppermute(one, CHIPS, right)
        pieces.append(one)
        if hop < long:
            two = lax.ppermute(two, CHIPS, left)
            pieces.append(two)
    others = [swap(piece[None], "c") for piece in pieces]

    def by_parts(arrays):
        return [lax.all_gather(array, "r", axis=0, tiled=False) for array in arrays]

    def share(arrays):
        got = mix([arrays[0], *near(arrays)])
        return [got[0], *far(got)]

    def team_gather(array):
        half = array.shape[0] // 2
        by_z, by_y = swap(array, "zl"), swap(array, "y")
        chip = [array, by_z, by_y, swap(by_y[:half], "zl"), swap(by_z[half:], "y")]
        return chip + [swap(piece, "c") for piece in chip]

    def team_scatter(keep, send):
        send_z, send_y, top, low = spread(s.table, keep, swap(send, "c"))
        send_y, send_z, top, low = narrow(s.table, top, swap(send_z, "zl"), low, swap(send_y, "y"))
        return top, swap(send_y, "y"), low, swap(send_z, "zl")

    def to_owners(parts):
        array = jnp.stack(parts).reshape((wide, s.highs) + parts[0].shape).swapaxes(0, 1)
        array = array.reshape((wide * s.highs,) + parts[0].shape)
        return jnp.sum(lax.all_to_all(array, GROUP, 0, 0, tiled=True).astype(F32), axis=0)

    packs = share(by_head)
    (packed,) = call(settle_kernel, (s.table, *packs), [((HEADS, s.qkv_tall, 2 * HD), BF)])
    packed = lax.all_gather(packed, "r", axis=0, tiled=True)
    packs = [packed, *lax.all_gather(packed, "x", axis=0, tiled=False)]
    if wide == 2:
        packs = [packed, swap(packed, "x")]
    ups = mix([up_b[0], *near(up_b)])
    up_t = call(
        join_kernel, (s.table, ups[0], swap(ups[1], "zl"), down_b), [((TEAM * s.wrows, s.cols), BF)]
    )[0]
    weights = [lax.all_gather(array, GROUP, axis=0, tiled=False) for array in (up_t, down_b)]
    att, w_head, kept = s.forward(pieces, others, packs)

    def mine(arrays):
        return share(arrays)

    w_out = lax.all_gather(out_b, ALL, axis=0, tiled=True)
    attended, mid, norm_mid, w_out = s.middle([w_out], mine(att))
    lay_keep, lay_send, keep, send, mids, acts, delta, grads = s.feed(
        team_gather(s.grad), team_gather(norm_mid), weights
    )
    mid_delta, mid_delta_b, by_head = s.turn(mid, w_out, team_scatter(keep, send))
    up = to_owners(s.up_gradient(mids, delta)).astype(BF)
    down = to_owners(s.down_gradient(acts, grads))
    to_own, to_mate, by_shard, sums = s.backward(kept, by_parts(share(by_head)))
    layer_out, *outs = s.outputs(
        mid, team_scatter(*s.out_gradient(lay_keep, lay_send, attended, mid_delta_b))
    )
    keep, send = s.inputs(to_own, swap(to_mate, "zh"), w_head[0], [swap(w_head[0], "zh")])
    grad_in = s.last(team_scatter(keep, send), mid_delta)
    parts = s.qkv_gradient(pieces, others, by_shard, sums)
    own, *got = list(lax.all_to_all(jnp.stack(parts), "x", 0, 0, tiled=True))
    while len(got) > 1:
        own, got = own.astype(F32) + got[0].astype(F32), got[1:]
    ups = s.up_share(up, jnp.zeros_like(up))
    ups = mix([ups[0], *near(ups)])
    return results(
        layer_out,
        grad_in,
        s.qkv_end(share(s.qkv_share(own, got[0]))),
        to_owners([part[at] for part in outs for at in range(s.highs)]),
        s.up_end((ups[0], swap(ups[1], "zl"))),
        down,
    )


def solution(mesh):
    ctx, wide = mesh.shape["ctx"], mesh.shape["wt"]
    sizes = {"r": ctx // HEADS, "zh": 2, "zl": 2, "y": 2, "c": 2, "x": wide}
    grid = Mesh(mesh.devices.reshape(tuple(sizes.values())), ALL)
    tokens, weights = P("x", CTX, None), P(ALL, None)
    return jax.shard_map(
        partial(local if sizes["r"] == 1 and wide == 2 else local_any, sizes=sizes),
        mesh=grid,
        in_specs=(tokens, P("x", CTX)) + (weights,) * 4 + (P(),) * 4 + (tokens,),
        out_specs=(tokens, tokens) + (weights,) * 4 + (P(ALL),) * 4,
        check_vma=False,
    )
```

```python
from functools import partial

import jax
import jax.numpy as jnp
from jax import lax
from jax.experimental import pallas as pl
from jax.experimental.pallas import tpu as pltpu
from jax.sharding import Mesh
from jax.sharding import PartitionSpec as P

HEADS = 16
HD = 64
TRIPLE = 3 * HD
EPS = 1e-05
FAR = -1e30
TILE = 256
TEAM = 8
TAIL = 8
BF = jnp.bfloat16
F32 = jnp.float32
ALL = ("r", "zh", "zl", "y", "c", "x")
CTX = ("r", "zh", "zl", "y", "c")
PART = ("zh", "zl", "y", "c")
CHIPS = ("r", "zh", "zl", "y")
TP = ("zl", "y", "c")
GROUP = ("r", "zh", "x")
SWAP = [(0, 1), (1, 0)]
MASKS = [
    z * 8 + y * 4 + c * 2 + x for c in range(2) for y in range(2) for x in range(2) for z in range(4)
]
NN = ((1,), (0,))
NT = ((1,), (1,))
TN = ((0,), (0,))


def dot(one, two, dims):
    return lax.dot_general(one, two, (dims, ((), ())), preferred_element_type=F32)


def normalise(rows):
    centred = rows - jnp.mean(rows, axis=-1, keepdims=True)
    spread = lax.rsqrt(jnp.mean(centred * centred, axis=-1, keepdims=True) + EPS)
    return centred * spread, spread


def norm_back(grad, normed, spread, gain):
    scaled = grad * gain
    inner = (
        scaled
        - jnp.mean(scaled, axis=-1, keepdims=True)
        - normed * jnp.mean(scaled * normed, axis=-1, keepdims=True)
    )
    return inner * spread


def gelu_both(up):
    root = 0.7978845608028654
    square = up * up
    inner = jnp.tanh(root * up * (1.0 + 0.044715 * square))
    plus = 0.5 * (1.0 + inner)
    slope = plus + 0.5 * up * (1.0 - inner * inner) * root * (1.0 + 3.0 * 0.044715 * square)
    return up * plus, slope


def block_home(block, shards):
    return (block, 0) if block < shards else (2 * shards - 1 - block, 1)


def split_two(values):
    high = values.astype(BF)
    return high, (values - high.astype(F32)).astype(BF)


def after(array, *others):
    return lax.optimization_barrier((array, *others))[0]


class Place:
    def __init__(self, table):
        self.r, self.zh, self.zl, self.y, self.c, self.x = (table[at] for at in range(6))
        self.mate = self.zl * 4 + self.y * 2 + self.c
        self.ctx = self.zh * TEAM + self.mate

    def flat(self, wide):
        return (self.r * HEADS + self.ctx) * wide + self.x


def call(body, arrays, outs, scratch=(), smem=1, smem_outs=(), far=0, sems=0, limit=12, micros=0):
    vector = pl.BlockSpec(memory_space=pltpu.VMEM)
    scalar = pl.BlockSpec(memory_space=pltpu.SMEM)
    there = pl.BlockSpec(memory_space=pl.ANY)
    scratch = [pltpu.VMEM(shape, kind) for shape, kind in scratch]
    if sems:
        scratch.append(pltpu.SemaphoreType.DMA((sems,)))
    return pl.pallas_call(
        body,
        out_shape=[jax.ShapeDtypeStruct(shape, kind) for shape, kind in outs],
        in_specs=[scalar] * smem + [there] * far + [vector] * (len(arrays) - smem - far),
        out_specs=[scalar if at in smem_outs else vector for at in range(len(outs))],
        scratch_shapes=scratch,
        compiler_params=pltpu.CompilerParams(vmem_limit_bytes=limit << 20),
        cost_estimate=pl.CostEstimate(flops=micros * 10**9 + 1000, bytes_accessed=1 << 10, transcendentals=0),
    )(*arrays)


def start_copies(pairs, sems):
    copies = [pltpu.make_async_copy(source, target, sems.at[at]) for at, (source, target) in enumerate(pairs)]
    for copy in copies:
        copy.start()
    return copies


def first_kernel(table, hidden_ref, gain_ref, bias_ref, qkv_ref, out_ref, up_ref, down_ref, start_ref, *refs, runs):
    (
        norm_out, *heads, out_b, one_ref, two_ref, three_ref, four_ref, down_b,
        hidden_at, gain_at, bias_at, qkv_at, out_at, up_at, down_at, start_at, made_ref, sems,
    ) = refs
    ups = one_ref, two_ref, three_ref, four_ref
    place = Place(table)
    copies = start_copies(
        (
            (hidden_ref, hidden_at), (gain_ref, gain_at), (bias_ref, bias_at), (start_ref, start_at), (qkv_ref, qkv_at),
            (out_ref, out_at), (up_ref, up_at), (down_ref, down_at),
        ),
        sems,
    )
    for copy in copies[:3]:
        copy.wait()
    normed, _ = normalise(hidden_at[...].astype(F32))
    norm_out[...] = (normed * gain_at[...] + bias_at[...]).astype(BF)
    for copy in copies[3:]:
        copy.wait()
    rows = qkv_at.shape[0]
    half = rows // 2
    width = HEADS * HD
    starts = start_at[...].astype(F32).astype(BF)
    for head in range(HEADS):
        part = [qkv_at[:, at * width + head * HD : at * width + (head + 1) * HD].astype(BF) for at in range(3)]
        made_ref[head, :rows] = jnp.concatenate(part[:2], axis=1)
        made_ref[head, rows : rows + half] = jnp.concatenate([part[2][:half], part[2][half:]], axis=1)
        made_ref[head, rows + half :] = jnp.broadcast_to(starts, (TAIL, 2 * HD))
    for near in range(4):
        for far in range(4):
            heads[near][far] = made_ref[place.ctx ^ (far * 4 + near)]
    out_b[...] = out_at[...].astype(BF)
    piece = ups[0].shape[2] // runs
    for near in range(4):
        for high in range(2):
            mate = place.mate ^ (high * 4 + near)
            for at in range(runs):
                first = pl.multiple_of((at * TEAM + mate) * piece, piece)
                ups[near][high, :, at * piece : (at + 1) * piece] = up_at[:, pl.ds(first, piece)].astype(BF)
    rows, half = down_at.shape[0], down_at.shape[1] // 2
    down_b[:rows] = down_at[:, :half].astype(BF)
    down_b[rows:] = down_at[:, half:].astype(BF)


def settle_kernel(table, *refs):
    place = Place(table)
    for far in range(4):
        for near in range(4):
            refs[4][place.ctx ^ (far * 4 + near)] = refs[far][near]


def head_weights(packs, w_ref, wrows, wide):
    whalf = wrows // 2
    for x in range(wide):
        for at in range(packs[x].shape[0]):
            first = (at * wide + x) * wrows
            w_ref[first : first + wrows, : 2 * HD] = packs[x][at, :wrows]
            pair = packs[x][at, wrows : wrows + whalf]
            w_ref[first : first + whalf, 2 * HD :] = pair[:, :HD]
            w_ref[first + whalf : first + wrows, 2 * HD :] = pair[:, HD:]


def unstacked(refs):
    return [ref.at[at] for ref in refs for at in range(ref.shape[0])]


def in_order(place, packs, one_ref, two_ref):
    for at in range(packs[0].shape[0]):
        one_ref[at] = jnp.where(place.x == 0, packs[0][at], packs[1][at])
        two_ref[at] = jnp.where(place.x == 0, packs[1][at], packs[0][at])


def join_kernel(table, one_ref, two_ref, _, out_ref):
    place = Place(table)
    rows = one_ref.shape[1]
    for at in range(TEAM):
        mate = place.mate ^ at
        part = (one_ref if at < 4 else two_ref)[at % 4]
        if rows % 16 == 0:
            out_ref[pl.ds(pl.multiple_of(mate * rows, rows), rows), :] = part
        else:
            for to in range(TEAM):

                @pl.when(mate == to)
                def _(to=to, part=part):
                    out_ref[to * rows : (to + 1) * rows, :] = part


def mix_kernel(*refs):
    count = len(refs) - refs[0].shape[0]
    for near in range(count):
        for far, out in enumerate(refs[count:]):
            out[near] = refs[near][far]


def ring_shifts(chips):
    shifts = [0]
    for hop in range(1, chips // 2 + 1):
        shifts += [-hop, hop] if hop < chips // 2 else [-hop]
    return shifts


def ring_order(chips, place):
    long = chips // 2
    along = (place.r * 2 + place.zh) * 2 + place.zl
    spot = jnp.where(place.y == 0, along, chips - 1 - along)
    order = []
    for shift in ring_shifts(chips):
        at = lax.rem(spot + shift + chips, chips)
        order.append(jnp.where(at < long, 2 * at, 2 * (chips - 1 - at) + 1))
    return order


def forward_kernel(table, *refs, wrows, chips, others, wide):
    pieces, others, refs = refs[:chips], refs[chips : chips + others], refs[chips + others :]
    pieces = list(pieces) + unstacked(others)
    own_ref, *refs = refs
    packs, refs = ([own_ref, refs[0]], refs[1:]) if wide == 2 else (refs[:wide], refs[wide:])
    outs, seconds = refs[:4], refs[14:]
    lse_ref, begin_ref, w_ref, w_send, q_ref, k_ref, v_ref, ot_ref, vt_ref, att_ref = refs[4:14]
    place = Place(table)
    if wide == 2:
        in_order(place, packs, *seconds)
        packs = seconds
    head_weights(packs, w_ref, wrows, wide)
    count = w_send.shape[0]
    if count < w_ref.shape[0]:
        w_send[...] = w_ref[pl.ds(pl.multiple_of(place.x * count, count), count), :]
    else:
        w_send[...] = w_ref[...]
    shards, half, _ = att_ref.shape
    rows = 2 * half
    total = shards * rows
    blocks = 2 * shards
    order = ring_order(chips, place)
    whalf = wrows // 2
    flags = []
    for block in range(blocks):
        shard, side = block_home(block, shards)
        row = own_ref[shard, wrows + whalf : wrows + whalf + 1].astype(F32)
        flags.append(row[:, side * half : (side + 1) * half])
    flags = jnp.concatenate(flags, axis=0)
    spots = half * lax.broadcasted_iota(jnp.int32, flags.shape, 0) + lax.broadcasted_iota(
        jnp.int32, flags.shape, 1
    )
    marks = jnp.where(flags > 0.5, spots.astype(F32), -1.0)
    lane = lax.broadcasted_iota(jnp.int32, marks.shape, 1)
    hop = 1
    while hop < half:
        moved = jnp.concatenate([marks[:, half - hop :], marks[:, : half - hop]], axis=1)
        marks = jnp.maximum(marks, jnp.where(lane >= hop, moved, -1.0))
        hop *= 2
    last = jnp.broadcast_to(marks[:, half - 1 :], marks.shape)
    line = lax.broadcasted_iota(jnp.int32, marks.shape, 0)
    hop = 1
    while hop < blocks:
        moved = jnp.concatenate([last[blocks - hop :], last[: blocks - hop]], axis=0)
        last = jnp.maximum(last, jnp.where(line >= hop, moved, -1.0))
        hop *= 2
    moved = jnp.concatenate([last[blocks - 1 :], last[: blocks - 1]], axis=0)
    begins = jnp.maximum(marks, jnp.where(line >= 1, moved, -1.0))
    group = TILE // half
    for tile in range(total // TILE):
        row = jnp.concatenate([begins[tile * group + at : tile * group + at + 1] for at in range(group)], axis=1)
        begin_ref[tile : tile + 1, :] = row.astype(jnp.int32)
    for which in range(2):
        for at in range(chips):
            made = dot(pieces[which * chips + at][...], w_ref[...], NN).astype(BF)
            shard = 2 * order[at] + (place.c if which == 0 else 1 - place.c)
            one = pl.multiple_of(shard * half, half)
            two = pl.multiple_of((blocks - 1 - shard) * half, half)
            scaled = made[:, :HD] * BF(HD**-0.5)
            for first, part in ((one, slice(0, half)), (two, slice(half, rows))):
                q_ref[pl.ds(first, half), :] = scaled[part]
                k_ref[pl.ds(first, half), :] = made[part, HD : 2 * HD]
                v_ref[pl.ds(first, half), :] = made[part, 2 * HD :]
    for at in range(0, total, 128):
        vt_ref[:, at : at + 128] = v_ref[at : at + 128, :].astype(F32).T.astype(BF)
    wide_tile = 2 * TILE
    for tile in range(total // wide_tile):
        low = max(0, tile - total // 2 // wide_tile) * wide_tile
        high = (tile + 1) * wide_tile
        query = q_ref[high - wide_tile : high, :]
        begin = jnp.concatenate([begin_ref[2 * tile : 2 * tile + 1, :], begin_ref[2 * tile + 1 : 2 * tile + 2, :]], axis=1)
        query_pos = high - wide_tile + lax.broadcasted_iota(jnp.int32, (1, wide_tile), 1)
        scores = dot(k_ref[low:high, :], query, NT)
        key_pos = low + lax.broadcasted_iota(jnp.int32, scores.shape, 0)
        scores = jnp.where((key_pos >= begin) & (key_pos <= query_pos), scores, FAR)
        top = jnp.max(scores, axis=0, keepdims=True)
        weights = jnp.exp(scores - top)
        sums = jnp.sum(weights, axis=0, keepdims=True)
        out = dot(vt_ref[:, low:high], weights.astype(BF), NN) / sums
        ot_ref[:, high - wide_tile : high] = out
        lse = top + jnp.log(sums)
        lse_ref[2 * tile : 2 * tile + 1, :] = lse[:, :TILE]
        lse_ref[2 * tile + 1 : 2 * tile + 2, :] = lse[:, TILE:]
        turned = out.T.astype(BF)
        for piece in range(2 * group):
            shard, side = block_home(tile * 2 * group + piece, shards)
            att_ref[shard, :, side * HD : (side + 1) * HD] = turned[piece * half : (piece + 1) * half]
    for near in range(4):
        for far in range(4):
            outs[near][far] = att_ref[place.r * HEADS + (place.ctx ^ (far * 4 + near))]


def middle_kernel(table, *refs, count):
    weights, atts, refs = refs[:count], refs[count : count + 4], refs[count + 4 :]
    hidden_ref, gain_ref, bias_ref, att_out, mid_out, norm_out, w_ref, heads_ref = refs
    place = Place(table)
    if count > 1:
        for at, ref in enumerate(unstacked(weights)):
            rows = ref.shape[0]
            first = (place.flat(2) ^ MASKS[at]) * rows
            w_ref[pl.ds(pl.multiple_of(first, rows), rows), :] = ref[...]
    else:
        w_ref[...] = weights[0][...]
    for far in range(4):
        for near in range(4):
            heads_ref[place.ctx ^ (far * 4 + near)] = atts[far][near]
    half = heads_ref.shape[1]
    for head in range(0, HEADS, 2):
        for side in range(2):
            lanes = slice(side * HD, (side + 1) * HD)
            att_out[side * half : (side + 1) * half, head * HD : (head + 2) * HD] = jnp.concatenate(
                [heads_ref[head, :, lanes], heads_ref[head + 1, :, lanes]], axis=1
            )
    mid = hidden_ref[...].astype(F32) + dot(att_out[...], w_ref[...], NN)
    mid_out[...] = mid
    normed, _ = normalise(mid)
    norm_out[...] = (normed * gain_ref[...] + bias_ref[...]).astype(BF)


def feed_kernel(table, *refs, grads, mids, wide, groups):
    grads, mids, refs = refs[:grads], refs[grads : grads + mids], refs[grads + mids :]
    *weights, lay_keep, lay_send, mnd_keep, mnd_send, mid_out, act_out, delta_out, grad_out, up_ref, down_ref = refs
    place = Place(table)
    for out, arrays in ((grad_out, grads), (mid_out, mids)):
        first = 0
        for ref in arrays:
            for part in unstacked([ref]) if len(ref.shape) == 3 else [ref]:
                out[first : first + part.shape[0], :] = part[...]
                first += part.shape[0]
    width = mid_out.shape[1]
    own = width // (TEAM * groups)
    ffn = down_ref.shape[0] // groups
    moving = len(weights) > 2
    count = len(weights) // 2
    ups, downs = weights[:count], weights[count:]
    if not moving:
        ups, downs = unstacked(ups), unstacked(downs)
    for at in range(groups):
        if moving:
            high, x = place.zh ^ (at & 1), place.x ^ (at >> 1)
        else:
            high, x = at // wide, at % wide
        for mate in range(TEAM):
            first = ((high * TEAM + mate) * wide + x) * own
            if moving:
                first = pl.multiple_of(first, own)
            up_ref[pl.ds(first, own), :] = ups[at][mate * own : (mate + 1) * own, :]
        first = (high * wide + x) * ffn
        if moving:
            first = pl.multiple_of(first, ffn)
        down_ref[pl.ds(first, ffn), : width // 2] = downs[at][:ffn, :]
        down_ref[pl.ds(first, ffn), width // 2 :] = downs[at][ffn:, :]
    total = mid_out.shape[0]
    run = 256
    half = total // 2
    for first in list(range(half, total, run)) + list(range(0, half, run)):
        here = slice(first, first + run)
        up = dot(mid_out[here, :], up_ref[...], NN)
        value, slope = gelu_both(up)
        act = value.astype(BF)
        act_out[here, :] = act
        delta = (dot(grad_out[here, :], down_ref[...], NT) * slope).astype(BF)
        delta_out[here, :] = delta
        back = dot(delta, up_ref[...], NT)
        fore = dot(act, down_ref[...], NN)
        if first < half:
            mnd_keep[here, :] = back
            lay_keep[here, :] = fore.astype(BF)
        else:
            there = slice(first - half, first - half + run)
            mnd_send[there, :] = back.astype(BF)
            lay_send[there, :] = fore.astype(BF)


def turn_kernel(
    table, grad_ref, mid_ref, w_ref, keep_top, got_top, keep_low, got_low, gain_ref, delta_out, bf_out, *refs
):
    *outs, made_ref = refs
    mnd = jnp.concatenate(
        [keep_top[...] + got_top[...].astype(F32), keep_low[...] + got_low[...].astype(F32)], axis=0
    )
    normed, spread = normalise(mid_ref[...])
    delta = grad_ref[...].astype(F32) + norm_back(mnd, normed, spread, gain_ref[...])
    delta_out[...] = delta
    narrow = delta.astype(BF)
    bf_out[...] = narrow
    back = dot(narrow, w_ref[...], NT).astype(BF)
    half = made_ref.shape[1]
    for head in range(HEADS):
        cols = slice(head * HD, (head + 1) * HD)
        made_ref[head] = jnp.concatenate([back[:half, cols], back[half:, cols]], axis=1)
    place = Place(table)
    for near in range(4):
        for far in range(4):
            outs[near][far] = made_ref[place.ctx ^ (far * 4 + near)]


TEAM_ORDER = (0, 4, 2, 6, 1, 5, 3, 7)


def out_grad_kernel(table, lay_keep, lay_send, att_ref, delta_ref, keep_out, send_out, part_ref, *, wide, wrows):
    turned = att_ref[...].astype(F32).T.astype(BF)
    part_ref[...] = dot(turned, delta_ref[...], NN).astype(BF).reshape(part_ref.shape)
    place = Place(table)
    rows = lay_keep.shape[0] // 4
    highs = part_ref.shape[0] // (TEAM * wide)
    for at in range(TEAM):
        mate = place.mate ^ TEAM_ORDER[at]
        out, lay = (keep_out, lay_keep) if at < 4 else (send_out, lay_send)
        first = (at % 4) * 2 * rows
        out[first : first + rows, :] = lay[(at % 4) * rows : (at % 4 + 1) * rows, :]
        first += rows
        for x in range(wide):
            for high in range(highs):
                out[first : first + wrows, :] = part_ref[(high * TEAM + mate) * wide + x]
                first += wrows


def up_pack_kernel(table, part_ref, delta_ref, *outs, wide):
    rows = (outs[0].shape[0] - TAIL) // TEAM
    tail = sum_lines(jnp.sum(delta_ref[...].astype(F32), axis=0, keepdims=True))
    place = Place(table)
    highs = len(outs) // wide
    for at, out in enumerate(outs):
        if wide == 2:
            x, high = place.x ^ (at >> 1), place.zh ^ (at & 1)
        else:
            x, high = at // highs, at % highs
        for mate in range(TEAM):
            first = ((high * TEAM + mate) * wide + x) * rows
            if wide == 2:
                first = pl.multiple_of(first, rows)
            out[mate * rows : (mate + 1) * rows] = part_ref[pl.ds(first, rows), :].astype(BF)
        out[TEAM * rows :] = tail


def down_pack_kernel(table, part_ref, *outs, wide):
    rows = outs[0].shape[0]
    place = Place(table)
    highs = len(outs) // wide
    for at, out in enumerate(outs):
        if wide == 2:
            x, high = place.x ^ (at >> 1), place.zh ^ (at & 1)
        else:
            x, high = at // highs, at % highs
        first = (high * wide + x) * rows
        if wide == 2:
            first = pl.multiple_of(first, rows)
        out[...] = part_ref[pl.ds(first, rows), :].astype(BF)


def up_add_kernel(own_ref, got_ref, out_ref):
    body, tail = add_lines(own_ref[...], got_ref[...])
    out_ref[: body.shape[0]] = body
    out_ref[body.shape[0] :] = tail


def sum_kernel(own_ref, got_ref, out_ref):
    out_ref[...] = (own_ref[...].astype(F32) + got_ref[...].astype(F32)).astype(out_ref.dtype)


def up_share_kernel(table, own_ref, got_ref, *refs):
    *outs, all_ref = refs
    place = Place(table)
    rows = outs[0].shape[1] - TAIL
    body, tail = add_lines(own_ref[...], got_ref[...])
    for mate in range(TEAM):
        all_ref[mate] = body[mate * rows : (mate + 1) * rows]
    for near in range(4):
        for high in range(2):
            out = outs[near]
            out[high, :rows] = all_ref[place.mate ^ (high * 4 + near)]
            out[high, rows:] = tail


def sum_lines(sums):
    high, low = split_two(sums)
    line = lax.broadcasted_iota(jnp.int32, (8, sums.shape[1]), 0)
    return jnp.where(line == 0, high.astype(F32), jnp.where(line == 1, low.astype(F32), 0.0)).astype(BF)


def add_lines(own, got):
    rows = own.shape[0] - TAIL
    total = own.astype(F32) + got.astype(F32)
    return total[:rows].astype(BF), sum_lines(total[rows : rows + 1] + total[rows + 1 : rows + 2])


def owner_column(row_ref, first, rows):
    shape = (rows, row_ref.shape[1])
    hit = lax.broadcasted_iota(jnp.int32, shape, 1) == first + lax.broadcasted_iota(jnp.int32, shape, 0)
    return jnp.sum(jnp.where(hit, row_ref[...], 0.0), axis=1, keepdims=True)


def as_row(column):
    shape = (column.shape[0],) * 2
    hit = lax.broadcasted_iota(jnp.int32, shape, 0) == lax.broadcasted_iota(jnp.int32, shape, 1)
    return jnp.sum(jnp.where(hit, column, 0.0), axis=0, keepdims=True)


def norm_grads(place, master_ref, grad_ref, sums, gain_ref, bias_ref, gain_out, bias_out, wide):
    rows = master_ref.shape[0]
    first = place.flat(wide) * rows
    own = master_ref[...].astype(BF).astype(F32)
    bias_grad = jnp.sum(own * sums, axis=1, keepdims=True)
    bias_out[...] = as_row(bias_grad)
    gain_grad = jnp.sum(own * grad_ref[...], axis=1, keepdims=True) - owner_column(bias_ref, first, rows) * bias_grad
    gain_out[...] = as_row(gain_grad / owner_column(gain_ref, first, rows))


def up_end_kernel(table, one_ref, two_ref, own_ref, gain_ref, bias_ref, grad_out, gain_out, bias_out, sum_ref, *, runs, wide):
    place = Place(table)
    rows = own_ref.shape[0]
    piece = one_ref.shape[2] // runs
    for high, ref in ((0, one_ref), (1, two_ref)):
        for near in range(4):
            mate = place.mate ^ (high * 4 + near)
            for at in range(runs):
                there = pl.ds(pl.multiple_of((at * TEAM + mate) * piece, piece), piece)
                part = ref[near, :, at * piece : (at + 1) * piece].astype(F32)
                grad_out[:, there] = part[:rows]
                sum_ref[:, there] = part[rows : rows + 1] + part[rows + 1 : rows + 2]
    norm_grads(place, own_ref, grad_out, sum_ref[...], gain_ref, bias_ref, gain_out, bias_out, wide)


def qkv_end_kernel(table, *refs, wide):
    parts, (own_ref, gain_ref, bias_ref, grad_out, gain_out, bias_out, all_ref) = refs[:4], refs[4:]
    place = Place(table)
    for far in range(4):
        for near in range(4):
            all_ref[place.ctx ^ (far * 4 + near)] = parts[far][near, : all_ref.shape[1]]
    rows = own_ref.shape[0]
    half = rows // 2
    width = HEADS * HD
    body = rows + half
    for head in range(0, HEADS, 2):
        for at in range(2):
            lanes = slice(at * HD, (at + 1) * HD)
            grad_out[:, at * width + head * HD : at * width + (head + 2) * HD] = jnp.concatenate(
                [all_ref[head, :rows, lanes], all_ref[head + 1, :rows, lanes]], axis=1
            ).astype(F32)
        for side in range(2):
            lanes = slice(side * HD, (side + 1) * HD)
            grad_out[side * half : (side + 1) * half, 2 * width + head * HD : 2 * width + (head + 2) * HD] = (
                jnp.concatenate([all_ref[head, rows:body, lanes], all_ref[head + 1, rows:body, lanes]], axis=1).astype(
                    F32
                )
            )
    lines = [[], [], []]
    for head in range(HEADS):
        tail = all_ref[head, body:, :].astype(F32)
        pair = tail[0:1] + tail[1:2]
        lines[0].append(pair[:, :HD])
        lines[1].append(pair[:, HD:])
        lines[2].append(tail[2:3, :HD] + tail[2:3, HD:])
    sums = jnp.concatenate(lines[0] + lines[1] + lines[2], axis=1)
    norm_grads(place, own_ref, grad_out, sums, gain_ref, bias_ref, gain_out, bias_out, wide)


def backward_kernel(table, *refs):
    douts, refs = refs[:4], refs[4:]
    (
        q_ref, k_ref, v_ref, ot_ref, lse_ref, begin_ref, own_out, mate_out, dn_ref, sum_ref,
        do_ref, dop_ref, kt_ref, dq_ref, dk_ref, dv_ref, da_ref,
    ) = refs
    place = Place(table)
    for part in range(douts[0].shape[0]):
        for far in range(4):
            for near in range(4):
                do_ref[part * HEADS + (place.ctx ^ (far * 4 + near))] = douts[far][part, near]
    shards, half, _ = do_ref.shape
    rows = 2 * half
    total = shards * rows
    for block in range(2 * shards):
        shard, side = block_home(block, shards)
        dop_ref[block * half : (block + 1) * half, :] = do_ref[shard, :, side * HD : (side + 1) * HD]
    for at in range(0, total, 128):
        kt_ref[:, at : at + 128] = k_ref[at : at + 128, :].astype(F32).T.astype(BF)
    dk_ref[...] = jnp.zeros_like(dk_ref)
    dv_ref[...] = jnp.zeros_like(dv_ref)
    for tile in range(total // TILE):
        here = slice(tile * TILE, (tile + 1) * TILE)
        query = q_ref[here, :]
        dout = dop_ref[here, :]
        begin = begin_ref[tile : tile + 1, :]
        lse = lse_ref[tile : tile + 1, :]
        row_dot = jnp.sum(dout.astype(F32).T * ot_ref[:, here], axis=0, keepdims=True)
        query_pos = tile * TILE + lax.broadcasted_iota(jnp.int32, (1, TILE), 1)
        low = max(0, tile - total // 2 // TILE) * TILE
        there = slice(low, (tile + 1) * TILE)
        scores = dot(k_ref[there, :], query, NT)
        key_pos = low + lax.broadcasted_iota(jnp.int32, scores.shape, 0)
        allowed = (key_pos >= begin) & (key_pos <= query_pos)
        probs = jnp.where(allowed, jnp.exp(scores - lse), 0.0)
        dprobs = dot(v_ref[there, :], dout, NT)
        delta = (probs * (dprobs - row_dot)).astype(BF)
        dv_ref[there, :] += dot(probs.astype(BF), dout, NN)
        dk_ref[there, :] += dot(delta, query, NN)
        accum = dot(kt_ref[:, there], delta, NN)
        dq_ref[here, :] = (accum * HD**-0.5).T
    sums = jnp.zeros((1, TRIPLE), F32)
    for block in range(2 * shards):
        shard, side = block_home(block, shards)
        at = slice(block * half, (block + 1) * half)
        pair = jnp.concatenate([dq_ref[at, :], dk_ref[at, :]], axis=1).astype(BF)
        last = dv_ref[at, :].astype(BF)
        da_ref[shard, side * half : (side + 1) * half, :] = pair
        da_ref[shard, rows : rows + half, side * HD : (side + 1) * HD] = last
        to = slice(side * half, (side + 1) * half)
        joined = jnp.concatenate([pair, last], axis=1)
        dn_ref[shard, to, :] = joined
        sums = sums + jnp.sum(joined.astype(F32), axis=0, keepdims=True)
    sum_ref[...] = sums
    base = place.r * HEADS
    for at in range(TEAM):
        own_out[at] = da_ref[base + place.zh * TEAM + at]
        mate_out[at] = da_ref[base + (1 - place.zh) * TEAM + at]


def qkv_lines(pair, last):
    line = lax.broadcasted_iota(jnp.int32, (8, 2 * HD), 0)
    high, low = split_two(pair)
    both = jnp.concatenate(split_two(last), axis=1)
    lines = jnp.where(line == 0, high.astype(F32), jnp.where(line == 1, low.astype(F32), both.astype(F32)))
    return lines.astype(BF)


def qkv_grad_kernel(table, *refs, repeats, chips, others, wide):
    pieces, stacks, (dn_ref, sum_ref, *outs, acc_ref) = refs[:chips], refs[chips : chips + others], refs[chips + others :]
    pieces = list(pieces) + unstacked(stacks)
    place = Place(table)
    order = ring_order(chips, place)
    total = None
    for which in range(2):
        for at in range(chips):
            shard = 2 * order[at] + (place.c if which == 0 else 1 - place.c)
            turned = dn_ref[shard].astype(F32).T.astype(BF)
            step = dot(turned, pieces[which * chips + at][...], NN)
            total = step if total is None else total + step
    acc_ref[...] = total.T
    owners, tall, _ = outs[0].shape
    rows = (tall - TAIL) * 2 // 3
    half = rows // 2
    sums = sum_ref[...]
    lines = qkv_lines(sums[:, : 2 * HD], sums[:, 2 * HD :])

    def write(base):
        for at, out in enumerate(outs):
            x = place.x ^ at if wide == 2 else at
            for owner in range(owners):
                first = base + (owner * wide + x) * rows
                if wide == 2:
                    first = pl.multiple_of(first, rows)
                grad = acc_ref[pl.ds(first, rows), :]
                out[owner, :rows] = grad[:, : 2 * HD].astype(BF)
                out[owner, rows : rows + half] = jnp.concatenate(
                    [grad[:half, 2 * HD :], grad[half:, 2 * HD :]], axis=1
                ).astype(BF)
                out[owner, rows + half :] = lines

    if repeats == 1:
        write(0)
    else:
        for at in range(repeats):
            pl.when(place.r == at)(partial(write, at * owners * wide * rows))


def qkv_add_kernel(table, own_ref, got_ref, *outs):
    place = Place(table)
    body = own_ref.shape[1] - TAIL
    for near in range(4):
        for far in range(4):
            at = place.ctx ^ (far * 4 + near)
            total = own_ref[at].astype(F32) + got_ref[at].astype(F32)
            outs[near][far, :body] = total[:body].astype(BF)
            tail = total[body:]
            outs[near][far, body:] = qkv_lines(tail[0:1] + tail[1:2], tail[2:3, :HD] + tail[2:3, HD:])


def spread_kernel(_, keep_ref, got_ref, send_z, send_y, top_out, low_out):
    rows = keep_ref.shape[0] // 4
    half = rows // 2
    for at in range(4):
        for side in range(2):
            here = slice(at * rows + side * half, at * rows + (side + 1) * half)
            total = keep_ref[here, :].astype(F32) + got_ref[here, :].astype(F32)
            if side == 0:
                if at % 2 == 0:
                    top_out[at // 2] = total
                else:
                    send_z[at // 2] = total.astype(BF)
            elif at < 2:
                low_out[at] = total
            else:
                send_y[at - 2] = total.astype(BF)


def narrow_kernel(_, top_ref, got_z, low_ref, got_y, send_y, send_z, top_out, low_out):
    top_out[...] = top_ref[0] + got_z[0].astype(F32)
    low_out[...] = low_ref[0] + got_y[0].astype(F32)
    send_y[...] = (top_ref[1] + got_z[1].astype(F32)).astype(BF)
    send_z[...] = (low_ref[1] + got_y[1].astype(F32)).astype(BF)


def input_kernel(table, own_ref, got_ref, *refs):
    tall = own_ref.shape[1]
    rows = tall * 2 // 3
    half = rows // 2
    place = Place(table)
    w_own, *mates, keep_out, send_out, lhs_ref, rhs_ref = refs
    rhs_ref[:, : 2 * HD] = w_own[:, : 2 * HD]
    rhs_ref[:, 2 * HD : 3 * HD] = w_own[:, 2 * HD :]
    for at, w_got in enumerate(mates):
        count = w_got.shape[0]
        here = slice(0, count)
        if len(mates) == 2:
            here = pl.ds(pl.multiple_of((place.x ^ at) * count, count), count)
        rhs_ref[here, 3 * HD : 4 * HD] = w_got[:, 2 * HD :]
        rhs_ref[here, 4 * HD :] = w_got[:, : 2 * HD]
    for at in range(TEAM):
        mate = place.mate ^ TEAM_ORDER[at]
        first = at * rows
        one, two = own_ref[mate], got_ref[mate]
        lhs_ref[first : first + rows, : 2 * HD] = one[:rows]
        lhs_ref[first : first + rows, 4 * HD :] = two[:rows]
        for side in range(2):
            lanes = slice(side * HD, (side + 1) * HD)
            lhs_ref[first + side * half : first + (side + 1) * half, 2 * HD : 4 * HD] = jnp.concatenate(
                [one[rows:, lanes], two[rows:, lanes]], axis=1
            )
    middle = TEAM * rows // 2
    send_out[...] = dot(lhs_ref[middle:, :], rhs_ref[...], NT).astype(BF)
    keep_out[...] = dot(lhs_ref[:middle, :], rhs_ref[...], NT)


def blend_kernel(*refs):
    ups, qkvs, (up_keep, *outs) = refs[:4], refs[4:8], refs[8:]
    tall = qkvs[0].shape[1]
    rows = ups[0].shape[1]
    for near in range(4):
        up_keep[near] = ups[near][0]
        for far, out in enumerate(outs):
            out[near, :tall] = qkvs[near][far]
        for at in range(ups[0].shape[2] // (2 * HD)):
            first = tall + at * rows
            outs[1][near, first : first + rows] = ups[near][1, :, at * 2 * HD : (at + 1) * 2 * HD]


def sums_kernel(one_ref, two_ref, out_own, out_got, send_out, keep_out):
    rows = one_ref.shape[0]
    send_out[:rows] = (one_ref[...].astype(F32) + two_ref[...].astype(F32)).astype(BF)
    send_out[rows:] = (out_own[1].astype(F32) + out_got[1].astype(F32)).astype(BF)
    keep_out[...] = out_own[0].astype(F32) + out_got[0].astype(F32)


def end_kernel(
    table, keep_top, got_top, keep_low, got_low, mid_delta_ref, hidden_ref, gain1_ref, bias1_ref, gain2_ref, bias2_ref,
    q0_ref, q1_ref, q2_ref, q3_ref, qkv_ref, up_one, up_ref, down_keep, out_keep, got_ref,
    grad_out, qkv_out, qkv_gain, qkv_bias, up_out, up_gain, up_bias, down_out, out_out,
    all_ref, up_two, sum_ref,
):
    last_kernel(table, keep_top, got_top, keep_low, got_low, mid_delta_ref, hidden_ref, gain1_ref, grad_out)
    tall, rows = q0_ref.shape[1], up_one.shape[1]
    for near in range(4):
        for at in range(up_one.shape[2] // (2 * HD)):
            first = tall + at * rows
            up_two[near, :, at * 2 * HD : (at + 1) * 2 * HD] = q1_ref[near, first : first + rows]
    qkv_end_kernel(
        table, q0_ref, q1_ref, q2_ref, q3_ref, qkv_ref, gain1_ref, bias1_ref, qkv_out, qkv_gain, qkv_bias, all_ref, wide=2
    )
    up_end_kernel(
        table, up_one, up_two, up_ref, gain2_ref, bias2_ref, up_out, up_gain, up_bias, sum_ref, runs=2, wide=2
    )
    rows = down_keep.shape[0]
    down_out[...] = down_keep[...] + got_ref[:rows].astype(F32)
    out_out[...] = out_keep[...] + got_ref[rows:].astype(F32)


def last_kernel(_, keep_top, got_top, keep_low, got_low, mid_delta_ref, hidden_ref, gain_ref, out_ref):
    grad = jnp.concatenate(
        [keep_top[...] + got_top[...].astype(F32), keep_low[...] + got_low[...].astype(F32)], axis=0
    )
    normed, spread = normalise(hidden_ref[...].astype(F32))
    out_ref[...] = (mid_delta_ref[...] + norm_back(grad, normed, spread, gain_ref[...])).astype(BF)


def outs_kernel(table, mid_ref, lay_ref, got_lay, part_ref, got_part, lay_out, *outs, wide):
    lay_out[...] = (mid_ref[...] + lay_ref[...] + got_lay[...].astype(F32)).astype(BF)
    highs, rows, _ = outs[0].shape
    place = Place(table)
    for side, out in enumerate(outs):
        for at in range(highs):
            x, high = (place.x ^ side, place.zh ^ at) if wide == 2 else (side, at)
            first = (x * highs + high) * rows
            if wide == 2:
                first = pl.multiple_of(first, rows)
            out[at] = (part_ref[pl.ds(first, rows), :] + got_part[pl.ds(first, rows), :].astype(F32)).astype(BF)


def after(array, *others):
    return lax.optimization_barrier((array, *others))[0]


def apart(count, mask):
    return [(at, at ^ mask) for at in range(count)]


def stack(arrays):
    count = sum(array.shape[0] if array.ndim == 3 else 1 for array in arrays)
    return call(stack_kernel, arrays, [((count,) + arrays[0].shape[-2:], arrays[0].dtype)], smem=0)[0]


def meet(*arrays):
    return lax.optimization_barrier(arrays)


def near(arrays):
    return [lax.ppermute(arrays[at], ("y", "c"), apart(4, at)) for at in range(1, 4)]


def far(arrays):
    return [lax.ppermute(arrays[at], ("zh", "zl"), apart(4, at)) for at in range(1, 4)]


def swap(array, axis):
    return lax.ppermute(array, axis, SWAP)


def mix(arrays):
    shape = arrays[0].shape
    return call(mix_kernel, arrays, [((len(arrays),) + shape[1:], arrays[0].dtype)] * shape[0], smem=0)


def stack_kernel(*refs):
    at = 0
    for ref in refs[:-1]:
        count = ref.shape[0] if len(ref.shape) == 3 else 1
        for part in range(count):
            refs[-1][at] = ref[part] if len(ref.shape) == 3 else ref[...]
            at += 1


def spread(table, keep, got):
    shape = (keep.shape[0] // 8, keep.shape[1])
    return call(spread_kernel, (table, keep, got), [((2, *shape), BF)] * 2 + [((2, *shape), F32)] * 2)


def narrow(table, top, got_z, low, got_y):
    shape = top.shape[1:]
    return call(narrow_kernel, (table, top, got_z, low, got_y), [(shape, BF)] * 2 + [(shape, F32)] * 2)


def add(one, two, kind):
    return call(sum_kernel, (one, two), [(one.shape, kind)], smem=0)[0]


class Steps:
    def __init__(self, arrays, sizes):
        (
            self.hidden, self.start, self.qkv, self.out, self.up, self.down,
            gain1, bias1, gain2, bias2, self.grad,
        ) = arrays
        self.hidden, self.grad = self.hidden[0], self.grad[0]
        self.gain1, self.bias1, self.gain2, self.bias2 = (a[None] for a in (gain1, bias1, gain2, bias2))
        self.repeats, self.wide = sizes["r"], sizes["x"]
        self.rows, self.width = self.hidden.shape
        self.half = self.rows // 2
        self.shards = self.repeats * HEADS
        self.total = self.shards * self.rows
        self.wrows, self.ffn = self.qkv.shape[0], self.down.shape[0]
        self.highs = 2 * self.repeats
        self.cols = self.highs * self.wide * self.ffn
        self.many = TEAM * self.rows
        self.qkv_tall = self.wrows * 3 // 2 + TAIL
        self.up_tall = self.wrows + TAIL
        self.sides = self.wide * self.highs
        self.piece = ((4, self.half, 2 * HD), BF)
        self.table = jnp.stack([lax.axis_index(axis).astype(jnp.int32) for axis in ALL])

    def first(self):
        masters = (self.qkv, self.out, self.up, self.down)
        row = ((1, self.width), F32)
        outs = call(
            partial(first_kernel, runs=self.highs),
            (self.table, self.hidden, self.gain1, self.bias1, *masters, self.start),
            [
                ((self.rows, self.width), BF),
                *[((4, self.qkv_tall, 2 * HD), BF)] * 4,
                ((self.wrows, self.width), BF),
                *[((2, self.wrows, self.cols), BF)] * 4,
                ((2 * self.ffn, self.width // 2), BF),
            ],
            [
                ((self.rows, self.width), BF), row, row,
                *[(a.shape, F32) for a in masters],
                (self.start.shape, jnp.int32),
                ((HEADS, self.qkv_tall, 2 * HD), BF),
            ],
            far=8,
            sems=8,
            limit=58,
        )
        return outs[0], list(outs[1:5]), outs[5], list(outs[6:10]), outs[10]

    def forward(self, pieces, others, packs):
        tokens = ((self.total, HD), BF)
        tiles = (self.total // TILE, TILE)
        sent = self.width // 2 if self.repeats == 1 and self.wide == 2 else self.width
        outs = call(
            partial(forward_kernel, wrows=self.wrows, chips=len(pieces), others=len(others), wide=self.wide),
            (self.table, *pieces, *others, *packs),
            [
                *[self.piece] * 4,
                (tiles, F32), (tiles, jnp.int32),
                ((self.width, TRIPLE), BF), ((sent, TRIPLE), BF),
                tokens, tokens, tokens,
                ((HD, self.total), F32),
            ],
            [((HD, self.total), BF), ((self.shards, self.half, 2 * HD), BF)]
            + [((self.shards, self.qkv_tall, 2 * HD), BF)] * (2 if self.wide == 2 else 0),
            limit=20 * self.repeats * self.repeats,
            micros=7,
        )
        return list(outs[:4]), list(outs[6:8]), (*outs[8:], *outs[4:6])

    def middle(self, weights, heads):
        return call(
            partial(middle_kernel, count=len(weights)),
            (self.table, *weights, *heads, self.hidden, self.gain2, self.bias2),
            [
                ((self.rows, self.width), BF),
                ((self.rows, self.width), F32),
                ((self.rows, self.width), BF),
                ((self.width, self.width), BF),
            ],
            [((HEADS, self.half, 2 * HD), BF)],
        )

    def feed(self, grads, mids, weights):
        half, full = (self.many // 2, self.width), (self.many, self.width)
        inner = ((self.many, self.cols), BF)
        return call(
            partial(
                feed_kernel, grads=len(grads), mids=len(mids), wide=self.wide, groups=self.highs * self.wide
            ),
            (self.table, *grads, *mids, *weights),
            [(half, BF), (half, BF), (half, F32), (half, BF), (full, BF), inner, inner, (full, BF)],
            [((self.width, self.cols), BF), ((self.cols, self.width), BF)],
            micros=6,
        )

    def up_gradient(self, mids, delta):
        return call(
            partial(up_pack_kernel, wide=self.wide),
            (self.table, dot(mids, delta, TN), delta),
            [((self.width // (self.highs * self.wide) + TAIL, self.cols), BF)] * self.sides,
        )

    def down_gradient(self, acts, grads):
        return call(
            partial(down_pack_kernel, wide=self.wide),
            (self.table, dot(acts, grads, TN)),
            [((self.ffn, self.width), BF)] * self.sides,
        )

    def turn(self, mid, w_out, ends):
        outs = call(
            turn_kernel,
            (self.table, self.grad, mid, w_out, *ends, self.gain2),
            [((self.rows, self.width), F32), ((self.rows, self.width), BF), *[self.piece] * 4],
            [((HEADS, self.half, 2 * HD), BF)],
        )
        return outs[0], outs[1], list(outs[2:])

    def out_gradient(self, lay_keep, lay_send, attended, delta):
        return call(
            partial(out_grad_kernel, wide=self.wide, wrows=self.wrows),
            (self.table, lay_keep, lay_send, attended, delta),
            [((self.many, self.width), BF)] * 2,
            [((self.shards * self.wide, self.wrows, self.width), BF)],
        )

    def backward(self, kept, douts):
        query, keys, values, out_t, lse, begin = kept
        tall = self.rows + self.half
        total = ((self.total, HD), F32)
        return call(
            backward_kernel,
            (self.table, *douts, query, keys, values, out_t, lse, begin),
            [
                ((TEAM, tall, 2 * HD), BF),
                ((TEAM, tall, 2 * HD), BF),
                ((self.shards, self.rows, TRIPLE), BF),
                ((1, TRIPLE), F32),
            ],
            [
                ((self.shards, self.half, 2 * HD), BF),
                ((self.total, HD), BF),
                ((HD, self.total), BF),
                total, total, total,
                ((self.shards, tall, 2 * HD), BF),
            ],
            limit=14 * self.repeats * self.repeats,
            micros=8,
        )

    def qkv_gradient(self, pieces, others, by_shard, sums):
        return call(
            partial(
                qkv_grad_kernel,
                repeats=self.repeats, chips=len(pieces), others=len(others), wide=self.wide,
            ),
            (self.table, *pieces, *others, by_shard, sums),
            [((HEADS, self.qkv_tall, 2 * HD), BF)] * self.wide,
            [((self.width, TRIPLE), F32)],
        )

    def up_share(self, own, got):
        return list(
            call(
                up_share_kernel,
                (self.table, own, got),
                [((2, self.up_tall, self.cols), BF)] * 4,
                [((TEAM, self.wrows, self.cols), BF)],
            )
        )

    def qkv_share(self, own, got):
        return list(call(qkv_add_kernel, (self.table, own, got), [((4, self.qkv_tall, 2 * HD), BF)] * 4))

    def outputs(self, mid, ends):
        return call(
            partial(outs_kernel, wide=self.wide),
            (self.table, mid, *ends),
            [((self.rows, self.width), BF)] + [((self.highs, self.wrows, self.width), BF)] * self.wide,
        )

    def inputs(self, to_own, from_mate, weights, mates):
        return call(
            input_kernel,
            (self.table, to_own, from_mate, weights, *mates),
            [((self.many // 2, self.width), F32), ((self.many // 2, self.width), BF)],
            [((self.many, 2 * TRIPLE), BF), ((self.width, 2 * TRIPLE), BF)],
        )

    def last(self, ends, mid_delta):
        return call(
            last_kernel,
            (self.table, *ends, mid_delta, self.hidden, self.gain1),
            [((self.rows, self.width), BF)],
        )[0]

    def up_end(self, ends):
        line = ((1, self.wrows), F32)
        return call(
            partial(up_end_kernel, runs=self.highs, wide=self.wide),
            (self.table, *ends, self.up, self.gain2, self.bias2),
            [(self.up.shape, F32), line, line],
            [((1, self.up.shape[1]), F32)],
        )

    def qkv_end(self, ends):
        line = ((1, self.wrows), F32)
        return call(
            partial(qkv_end_kernel, wide=self.wide),
            (self.table, *ends, self.qkv, self.gain1, self.bias1),
            [(self.qkv.shape, F32), line, line],
            [((HEADS, self.qkv_tall, 2 * HD), BF)],
        )


def ring_moves(long):
    count = 2 * long
    order = [2 * at for at in range(long)] + [2 * at + 1 for at in reversed(range(long))]
    right = [(order[at], order[(at + 1) % count]) for at in range(count)]
    return right, [(two, one) for one, two in right]


def results(layer_out, grad_in, qkv, out, up, down):
    return (
        layer_out[None], grad_in[None], qkv[0], out, up[0], down,
        qkv[1][0], qkv[2][0], up[1][0], up[2][0],
    )


def local(*arrays, sizes):
    s = Steps(arrays, sizes)
    right, left = ring_moves(4)

    def ahead(array):
        return lax.ppermute(array, CHIPS, right)

    def behind(array):
        return lax.ppermute(array, CHIPS, left)

    norm_in, by_head, out_b, up_b, down_b = s.first()
    a1, b1, *got = meet(ahead(norm_in), behind(norm_in), *near(by_head))
    packs = mix([by_head[0], *got])
    a2, b2, *got = meet(ahead(a1), behind(b1), *far(packs))
    (packed,) = call(settle_kernel, (s.table, packs[0], *got), [((HEADS, s.qkv_tall, 2 * HD), BF)])
    first = stack([norm_in, a1, b1, a2, b2])
    ups = [after(up, a2) for up in up_b]
    a3, b3, packed_x, *got = meet(ahead(a2), behind(b2), swap(packed, "x"), *near(ups))
    ups = mix([ups[0], *got])
    half = s.half
    one, two, up_z, first, down_x = meet(
        ahead(a3[:half]),
        behind(b3[half:]),
        swap(ups[1], "zl"),
        swap(after(first, a3), "c"),
        swap(after(down_b, a3), "x"),
    )
    a4 = stack([one, two]).reshape(s.rows, s.width)
    second = stack([a3, b3])
    (up_t,) = call(join_kernel, (s.table, ups[0], up_z, down_b), [((TEAM * s.wrows, s.cols), BF)])
    pieces = [norm_in, a1, b1, a2, b2, a3, b3, a4]
    others = [first, *meet(swap(second, "c"), swap(a4[None], "c"))]

    out = after(out_b, a4)
    out_z = [lax.ppermute(out, ("zh", "zl"), apart(4, at)) for at in range(1, 4)]
    grad = after(s.grad, a4)
    grad_z = swap(grad, "zl")
    att, w_head, kept = s.forward(pieces, others, [packed, packed_x])
    *att, grad_z, o1, o2, o3 = meet(*att, grad_z, *out_z)
    out_4 = stack([out, o1, o2, o3])
    *got, out_x, up_z, grad_y = meet(
        *near(att), swap(out_4, "x"), swap(after(up_t, att[0]), "zh"), swap(after(grad, att[0]), "y")
    )
    att = mix([att[0], *got])
    out_8 = stack([out_4, out_x])
    *got, out_8y, up_x, out_8c = meet(
        *far(att), swap(out_8, "y"), swap(after(up_t, att[0]), "x"), swap(out_8, "c")
    )
    attended, mid, norm_mid, w_out = s.middle([out_8, out_8y, out_8c, swap(out_8y, "c")], [att[0], *got])

    half = s.half
    grad_3 = stack([after(grad, norm_mid), grad_z, grad_y])
    by_z, by_y, up_zx, down_z, grad_3c = meet(
        swap(norm_mid, "zl"),
        swap(norm_mid, "y"),
        swap(after(up_z, norm_mid), "x"),
        swap(after(down_b, norm_mid), "zh"),
        swap(grad_3, "c"),
    )
    three = stack([norm_mid, by_z, by_y])
    both_one, both_two, three, down_zx, grad_one, grad_two = meet(
        swap(by_y[:half], "zl"),
        swap(by_z[half:], "y"),
        swap(three, "c"),
        swap(after(down_z, by_z), "x"),
        swap(after(grad_y[:half], by_z), "zl"),
        swap(after(grad_z[half:], by_z), "y"),
    )
    both = stack([both_one, both_two])
    grad_both = stack([grad_one, grad_two])
    mids = [norm_mid, by_z, by_y, both_one, both_two, three, swap(both, "c")]
    grads = [grad, grad_z, grad_y, grad_one, grad_two, grad_3c, swap(grad_both, "c")]
    lay_keep, lay_send, keep, send, mids, acts, delta, grads = s.feed(
        grads, mids, [up_t, up_z, up_x, up_zx, down_b, down_z, down_x, down_zx]
    )
    send_z, send_y, top, low = spread(s.table, keep, swap(send, "c"))
    up_parts = s.up_gradient(mids, after(delta, send_z))
    got_z, got_y, *up_parts = meet(swap(send_z, "zl"), swap(send_y, "y"), *up_parts)
    send_y, send_z, top, low = narrow(s.table, top, got_z, low, got_y)
    down_parts = s.down_gradient(after(acts, send_y), grads)
    end_top, end_low, up_far, *down_parts = meet(
        swap(send_y, "y"), swap(send_z, "zl"), swap(after(up_parts[3], send_y), "x"), *down_parts
    )
    mid_delta, mid_delta_b, by_head = s.turn(mid, w_out, (top, end_top, low, end_low))
    *got, up_near, mate_1 = meet(
        *near(by_head),
        swap(after(up_parts[2], mid_delta), "x"),
        swap(after(w_head[1], mid_delta), "zh"),
    )
    by_head = mix([by_head[0], *got])
    up_shape = up_parts[0].shape
    (up_send,) = call(up_add_kernel, (up_parts[1], after(up_far, by_head[0])), [(up_shape, BF)], smem=0)
    keep, send = s.out_gradient(after(lay_keep, by_head[0]), lay_send, attended, mid_delta_b)
    *got, send, down_far, up_send = meet(
        *far(by_head), swap(send, "c"), swap(after(down_parts[3], by_head[0]), "x"), up_send
    )

    douts = [array[None] for array in (by_head[0], *got)]
    send_z, send_y, top, low = spread(s.table, keep, send)
    got_z, got_y = swap(send_z, "zl"), swap(send_y, "y")
    up_got = swap(up_send, "zh")
    down_near = swap(after(down_parts[2], send), "x")
    mate_2 = swap(after(mate_1, send), "x")
    kept = (after(kept[0], send_z), *kept[1:])
    to_own, to_mate, by_shard, sums = s.backward(kept, douts)
    from_mate = swap(to_mate, "zh")
    to_own, got_z, got_y, down_near, mate_2 = meet(to_own, got_z, got_y, down_near, mate_2)
    send_y, send_z, top, low = narrow(s.table, top, got_z, low, got_y)
    (up_keep,) = call(up_add_kernel, (up_parts[0], after(up_near, to_own)), [(up_shape, BF)], smem=0)
    qkv_own, qkv_send = s.qkv_gradient(pieces, others, after(by_shard, send_y), sums)
    end_top, end_low, qkv_send, up_got = meet(
        swap(send_y, "y"), swap(send_z, "zl"), qkv_send, up_got
    )
    ups = s.up_share(up_keep, up_got)
    ends = top, end_top, low, end_low
    down_keep = add(down_parts[0], after(down_near, end_top), F32)
    from_mate, qkv_got, *got = meet(from_mate, swap(after(qkv_send, end_top), "x"), *near(ups))
    keep, send = s.inputs(to_own, from_mate, w_head[0], [mate_1, mate_2])
    layer_out, *outs = s.outputs(mid, ends)
    qkv = s.qkv_share(qkv_own, after(qkv_got, send))
    send, out_got, *qkv = meet(swap(send, "c"), swap(after(outs[1], send), "x"), *qkv)

    send_z, send_y, top, low = spread(s.table, keep, send)
    last_send, out_keep = call(
        sums_kernel,
        (after(down_parts[1], send_z), down_far, outs[0], out_got),
        [((s.ffn + s.wrows, s.width), BF), ((s.wrows, s.width), F32)],
        smem=0,
    )
    last_got = swap(last_send, "zh")
    got_z, got_y, *more = meet(
        swap(send_z, "zl"), swap(send_y, "y"), *near([after(a, send_z) for a in qkv])
    )
    send_y, send_z, top, low = narrow(s.table, top, got_z, low, got_y)
    piece = ((4, s.qkv_tall, 2 * HD), BF)
    tall = s.qkv_tall + s.up_tall * s.cols // (2 * HD)
    up_keep, *qkv = call(
        blend_kernel,
        (after(ups[0], send_y), *got, qkv[0], *more),
        [((4, s.up_tall, s.cols), BF), piece, ((4, tall, 2 * HD), BF), piece, piece],
        smem=0,
    )
    end_top, end_low, last_got, *more = meet(swap(send_y, "y"), swap(send_z, "zl"), last_got, *far(qkv))
    line = ((1, s.wrows), F32)
    outs = call(
        end_kernel,
        (
            s.table, top, end_top, low, end_low, mid_delta, s.hidden, s.gain1, s.bias1, s.gain2, s.bias2,
            qkv[0], *more, s.qkv, up_keep, s.up, down_keep, out_keep, last_got,
        ),
        [
            ((s.rows, s.width), BF),
            (s.qkv.shape, F32), line, line,
            (s.up.shape, F32), line, line,
            (s.down.shape, F32),
            (s.out.shape, F32),
        ],
        [
            ((HEADS, s.qkv_tall, 2 * HD), BF),
            ((4, s.up_tall, s.cols), BF),
            ((1, s.up.shape[1]), F32),
        ],
    )
    return results(layer_out, outs[0], outs[1:4], outs[8], outs[4:7], outs[7])


def local_any(*arrays, sizes):
    s = Steps(arrays, sizes)
    repeats, wide = s.repeats, s.wide
    long = 4 * repeats
    right, left = ring_moves(long)
    norm_in, by_head, out_b, up_b, down_b = s.first()
    one = two = norm_in
    pieces = [norm_in]
    for hop in range(1, long + 1):
        one = lax.ppermute(one, CHIPS, right)
        pieces.append(one)
        if hop < long:
            two = lax.ppermute(two, CHIPS, left)
            pieces.append(two)
    others = [swap(piece[None], "c") for piece in pieces]

    def by_parts(arrays):
        return [lax.all_gather(array, "r", axis=0, tiled=False) for array in arrays]

    def share(arrays):
        got = mix([arrays[0], *near(arrays)])
        return [got[0], *far(got)]

    def team_gather(array):
        half = array.shape[0] // 2
        by_z, by_y = swap(array, "zl"), swap(array, "y")
        chip = [array, by_z, by_y, swap(by_y[:half], "zl"), swap(by_z[half:], "y")]
        return chip + [swap(piece, "c") for piece in chip]

    def team_scatter(keep, send):
        send_z, send_y, top, low = spread(s.table, keep, swap(send, "c"))
        send_y, send_z, top, low = narrow(s.table, top, swap(send_z, "zl"), low, swap(send_y, "y"))
        return top, swap(send_y, "y"), low, swap(send_z, "zl")

    def to_owners(parts):
        array = jnp.stack(parts).reshape((wide, s.highs) + parts[0].shape).swapaxes(0, 1)
        array = array.reshape((wide * s.highs,) + parts[0].shape)
        return jnp.sum(lax.all_to_all(array, GROUP, 0, 0, tiled=True).astype(F32), axis=0)

    packs = share(by_head)
    (packed,) = call(settle_kernel, (s.table, *packs), [((HEADS, s.qkv_tall, 2 * HD), BF)])
    packed = lax.all_gather(packed, "r", axis=0, tiled=True)
    packs = [packed, *lax.all_gather(packed, "x", axis=0, tiled=False)]
    if wide == 2:
        packs = [packed, swap(packed, "x")]
    ups = mix([up_b[0], *near(up_b)])
    up_t = call(
        join_kernel, (s.table, ups[0], swap(ups[1], "zl"), down_b), [((TEAM * s.wrows, s.cols), BF)]
    )[0]
    weights = [lax.all_gather(array, GROUP, axis=0, tiled=False) for array in (up_t, down_b)]
    att, w_head, kept = s.forward(pieces, others, packs)

    def mine(arrays):
        return share(arrays)

    w_out = lax.all_gather(out_b, ALL, axis=0, tiled=True)
    attended, mid, norm_mid, w_out = s.middle([w_out], mine(att))
    lay_keep, lay_send, keep, send, mids, acts, delta, grads = s.feed(
        team_gather(s.grad), team_gather(norm_mid), weights
    )
    mid_delta, mid_delta_b, by_head = s.turn(mid, w_out, team_scatter(keep, send))
    up = to_owners(s.up_gradient(mids, delta)).astype(BF)
    down = to_owners(s.down_gradient(acts, grads))
    to_own, to_mate, by_shard, sums = s.backward(kept, by_parts(share(by_head)))
    layer_out, *outs = s.outputs(
        mid, team_scatter(*s.out_gradient(lay_keep, lay_send, attended, mid_delta_b))
    )
    keep, send = s.inputs(to_own, swap(to_mate, "zh"), w_head[0], [swap(w_head[0], "zh")])
    grad_in = s.last(team_scatter(keep, send), mid_delta)
    parts = s.qkv_gradient(pieces, others, by_shard, sums)
    own, *got = list(lax.all_to_all(jnp.stack(parts), "x", 0, 0, tiled=True))
    while len(got) > 1:
        own, got = own.astype(F32) + got[0].astype(F32), got[1:]
    ups = s.up_share(up, jnp.zeros_like(up))
    ups = mix([ups[0], *near(ups)])
    return results(
        layer_out,
        grad_in,
        s.qkv_end(share(s.qkv_share(own, got[0]))),
        to_owners([part[at] for part in outs for at in range(s.highs)]),
        s.up_end((ups[0], swap(ups[1], "zl"))),
        down,
    )


def solution(mesh):
    ctx, wide = mesh.shape["ctx"], mesh.shape["wt"]
    sizes = {"r": ctx // HEADS, "zh": 2, "zl": 2, "y": 2, "c": 2, "x": wide}
    grid = Mesh(mesh.devices.reshape(tuple(sizes.values())), ALL)
    tokens, weights = P("x", CTX, None), P(ALL, None)
    return jax.shard_map(
        partial(local if sizes["r"] == 1 and wide == 2 else local_any, sizes=sizes),
        mesh=grid,
        in_specs=(tokens, P("x", CTX)) + (weights,) * 4 + (P(),) * 4 + (tokens,),
        out_specs=(tokens, tokens) + (weights,) * 4 + (P(ALL),) * 4,
        check_vma=False,
    )
```

```python
from functools import partial

import jax
import jax.numpy as jnp
from jax import lax
from jax.experimental import pallas as pl
from jax.experimental.pallas import tpu as pltpu
from jax.sharding import Mesh
from jax.sharding import PartitionSpec as P

HEADS = 16
HD = 64
TRIPLE = 3 * HD
EPS = 1e-05
FAR = -1e30
TILE = 256
TEAM = 8
TAIL = 8
BF = jnp.bfloat16
F32 = jnp.float32
ALL = ("r", "zh", "zl", "y", "c", "x")
CTX = ("r", "zh", "zl", "y", "c")
PART = ("zh", "zl", "y", "c")
CHIPS = ("r", "zh", "zl", "y")
TP = ("zl", "y", "c")
GROUP = ("r", "zh", "x")
SWAP = [(0, 1), (1, 0)]
MASKS = [
    z * 8 + y * 4 + c * 2 + x for c in range(2) for y in range(2) for x in range(2) for z in range(4)
]
NN = ((1,), (0,))
NT = ((1,), (1,))
TN = ((0,), (0,))


def dot(one, two, dims):
    return lax.dot_general(one, two, (dims, ((), ())), preferred_element_type=F32)


def normalise(rows):
    centred = rows - jnp.mean(rows, axis=-1, keepdims=True)
    spread = lax.rsqrt(jnp.mean(centred * centred, axis=-1, keepdims=True) + EPS)
    return centred * spread, spread


def norm_back(grad, normed, spread, gain):
    scaled = grad * gain
    inner = (
        scaled
        - jnp.mean(scaled, axis=-1, keepdims=True)
        - normed * jnp.mean(scaled * normed, axis=-1, keepdims=True)
    )
    return inner * spread


def gelu_both(up):
    root = 0.7978845608028654
    square = up * up
    inner = jnp.tanh(root * up * (1.0 + 0.044715 * square))
    plus = 0.5 * (1.0 + inner)
    slope = plus + 0.5 * up * (1.0 - inner * inner) * root * (1.0 + 3.0 * 0.044715 * square)
    return up * plus, slope


def block_home(block, shards):
    return (block, 0) if block < shards else (2 * shards - 1 - block, 1)


def split_two(values):
    high = values.astype(BF)
    return high, (values - high.astype(F32)).astype(BF)


def after(array, *others):
    return lax.optimization_barrier((array, *others))[0]


class Place:
    def __init__(self, table):
        self.r, self.zh, self.zl, self.y, self.c, self.x = (table[at] for at in range(6))
        self.mate = self.zl * 4 + self.y * 2 + self.c
        self.ctx = self.zh * TEAM + self.mate

    def flat(self, wide):
        return (self.r * HEADS + self.ctx) * wide + self.x


def call(body, arrays, outs, scratch=(), smem=1, smem_outs=(), far=0, sems=0, limit=12, micros=0):
    vector = pl.BlockSpec(memory_space=pltpu.VMEM)
    scalar = pl.BlockSpec(memory_space=pltpu.SMEM)
    there = pl.BlockSpec(memory_space=pl.ANY)
    scratch = [pltpu.VMEM(shape, kind) for shape, kind in scratch]
    if sems:
        scratch.append(pltpu.SemaphoreType.DMA((sems,)))
    return pl.pallas_call(
        body,
        out_shape=[jax.ShapeDtypeStruct(shape, kind) for shape, kind in outs],
        in_specs=[scalar] * smem + [there] * far + [vector] * (len(arrays) - smem - far),
        out_specs=[scalar if at in smem_outs else vector for at in range(len(outs))],
        scratch_shapes=scratch,
        compiler_params=pltpu.CompilerParams(vmem_limit_bytes=limit << 20),
        cost_estimate=pl.CostEstimate(flops=micros * 10**9 + 1000, bytes_accessed=1 << 10, transcendentals=0),
    )(*arrays)


def start_copies(pairs, sems):
    copies = [pltpu.make_async_copy(source, target, sems.at[at]) for at, (source, target) in enumerate(pairs)]
    for copy in copies:
        copy.start()
    return copies


def first_kernel(table, hidden_ref, gain_ref, bias_ref, qkv_ref, out_ref, up_ref, down_ref, start_ref, *refs, runs):
    (
        norm_out, *heads, out_b, one_ref, two_ref, three_ref, four_ref, down_b,
        hidden_at, gain_at, bias_at, qkv_at, out_at, up_at, down_at, start_at, made_ref, sems,
    ) = refs
    ups = one_ref, two_ref, three_ref, four_ref
    place = Place(table)
    copies = start_copies(
        (
            (hidden_ref, hidden_at), (gain_ref, gain_at), (bias_ref, bias_at), (start_ref, start_at), (qkv_ref, qkv_at),
            (out_ref, out_at), (up_ref, up_at), (down_ref, down_at),
        ),
        sems,
    )
    for copy in copies[:3]:
        copy.wait()
    normed, _ = normalise(hidden_at[...].astype(F32))
    norm_out[...] = (normed * gain_at[...] + bias_at[...]).astype(BF)
    for copy in copies[3:]:
        copy.wait()
    rows = qkv_at.shape[0]
    half = rows // 2
    width = HEADS * HD
    starts = start_at[...].astype(F32).astype(BF)
    for head in range(HEADS):
        part = [qkv_at[:, at * width + head * HD : at * width + (head + 1) * HD].astype(BF) for at in range(3)]
        made_ref[head, :rows] = jnp.concatenate(part[:2], axis=1)
        made_ref[head, rows : rows + half] = jnp.concatenate([part[2][:half], part[2][half:]], axis=1)
        made_ref[head, rows + half :] = jnp.broadcast_to(starts, (TAIL, 2 * HD))
    for near in range(4):
        for far in range(4):
            heads[near][far] = made_ref[place.ctx ^ (far * 4 + near)]
    out_b[...] = out_at[...].astype(BF)
    piece = ups[0].shape[2] // runs
    for near in range(4):
        for high in range(2):
            mate = place.mate ^ (high * 4 + near)
            for at in range(runs):
                first = pl.multiple_of((at * TEAM + mate) * piece, piece)
                ups[near][high, :, at * piece : (at + 1) * piece] = up_at[:, pl.ds(first, piece)].astype(BF)
    rows, half = down_at.shape[0], down_at.shape[1] // 2
    down_b[:rows] = down_at[:, :half].astype(BF)
    down_b[rows:] = down_at[:, half:].astype(BF)


def settle_kernel(table, *refs):
    place = Place(table)
    for far in range(4):
        for near in range(4):
            refs[4][place.ctx ^ (far * 4 + near)] = refs[far][near]


def head_weights(packs, w_ref, wrows, wide):
    whalf = wrows // 2
    for x in range(wide):
        for at in range(packs[x].shape[0]):
            first = (at * wide + x) * wrows
            w_ref[first : first + wrows, : 2 * HD] = packs[x][at, :wrows]
            pair = packs[x][at, wrows : wrows + whalf]
            w_ref[first : first + whalf, 2 * HD :] = pair[:, :HD]
            w_ref[first + whalf : first + wrows, 2 * HD :] = pair[:, HD:]


def unstacked(refs):
    return [ref.at[at] for ref in refs for at in range(ref.shape[0])]


def in_order(place, packs, one_ref, two_ref):
    for at in range(packs[0].shape[0]):
        one_ref[at] = jnp.where(place.x == 0, packs[0][at], packs[1][at])
        two_ref[at] = jnp.where(place.x == 0, packs[1][at], packs[0][at])


def join_kernel(table, one_ref, two_ref, _, out_ref):
    place = Place(table)
    rows = one_ref.shape[1]
    for at in range(TEAM):
        mate = place.mate ^ at
        part = (one_ref if at < 4 else two_ref)[at % 4]
        if rows % 16 == 0:
            out_ref[pl.ds(pl.multiple_of(mate * rows, rows), rows), :] = part
        else:
            for to in range(TEAM):

                @pl.when(mate == to)
                def _(to=to, part=part):
                    out_ref[to * rows : (to + 1) * rows, :] = part


def mix_kernel(*refs):
    count = len(refs) - refs[0].shape[0]
    for near in range(count):
        for far, out in enumerate(refs[count:]):
            out[near] = refs[near][far]


def ring_shifts(chips):
    shifts = [0]
    for hop in range(1, chips // 2 + 1):
        shifts += [-hop, hop] if hop < chips // 2 else [-hop]
    return shifts


def ring_order(chips, place):
    long = chips // 2
    along = (place.r * 2 + place.zh) * 2 + place.zl
    spot = jnp.where(place.y == 0, along, chips - 1 - along)
    order = []
    for shift in ring_shifts(chips):
        at = lax.rem(spot + shift + chips, chips)
        order.append(jnp.where(at < long, 2 * at, 2 * (chips - 1 - at) + 1))
    return order


def forward_kernel(table, *refs, wrows, chips, others, wide):
    pieces, others, refs = refs[:chips], refs[chips : chips + others], refs[chips + others :]
    pieces = list(pieces) + unstacked(others)
    own_ref, *refs = refs
    packs, refs = ([own_ref, refs[0]], refs[1:]) if wide == 2 else (refs[:wide], refs[wide:])
    outs, seconds = refs[:4], refs[14:]
    lse_ref, begin_ref, w_ref, w_send, q_ref, k_ref, v_ref, ot_ref, vt_ref, att_ref = refs[4:14]
    place = Place(table)
    if wide == 2:
        in_order(place, packs, *seconds)
        packs = seconds
    head_weights(packs, w_ref, wrows, wide)
    count = w_send.shape[0]
    if count < w_ref.shape[0]:
        w_send[...] = w_ref[pl.ds(pl.multiple_of(place.x * count, count), count), :]
    else:
        w_send[...] = w_ref[...]
    shards, half, _ = att_ref.shape
    rows = 2 * half
    total = shards * rows
    blocks = 2 * shards
    order = ring_order(chips, place)
    whalf = wrows // 2
    flags = []
    for block in range(blocks):
        shard, side = block_home(block, shards)
        row = own_ref[shard, wrows + whalf : wrows + whalf + 1].astype(F32)
        flags.append(row[:, side * half : (side + 1) * half])
    flags = jnp.concatenate(flags, axis=0)
    spots = half * lax.broadcasted_iota(jnp.int32, flags.shape, 0) + lax.broadcasted_iota(
        jnp.int32, flags.shape, 1
    )
    marks = jnp.where(flags > 0.5, spots.astype(F32), -1.0)
    lane = lax.broadcasted_iota(jnp.int32, marks.shape, 1)
    hop = 1
    while hop < half:
        moved = jnp.concatenate([marks[:, half - hop :], marks[:, : half - hop]], axis=1)
        marks = jnp.maximum(marks, jnp.where(lane >= hop, moved, -1.0))
        hop *= 2
    last = jnp.broadcast_to(marks[:, half - 1 :], marks.shape)
    line = lax.broadcasted_iota(jnp.int32, marks.shape, 0)
    hop = 1
    while hop < blocks:
        moved = jnp.concatenate([last[blocks - hop :], last[: blocks - hop]], axis=0)
        last = jnp.maximum(last, jnp.where(line >= hop, moved, -1.0))
        hop *= 2
    moved = jnp.concatenate([last[blocks - 1 :], last[: blocks - 1]], axis=0)
    begins = jnp.maximum(marks, jnp.where(line >= 1, moved, -1.0))
    group = TILE // half
    for tile in range(total // TILE):
        row = jnp.concatenate([begins[tile * group + at : tile * group + at + 1] for at in range(group)], axis=1)
        begin_ref[tile : tile + 1, :] = row.astype(jnp.int32)
    for which in range(2):
        for at in range(chips):
            made = dot(pieces[which * chips + at][...], w_ref[...], NN).astype(BF)
            shard = 2 * order[at] + (place.c if which == 0 else 1 - place.c)
            one = pl.multiple_of(shard * half, half)
            two = pl.multiple_of((blocks - 1 - shard) * half, half)
            scaled = made[:, :HD] * BF(HD**-0.5)
            for first, part in ((one, slice(0, half)), (two, slice(half, rows))):
                q_ref[pl.ds(first, half), :] = scaled[part]
                k_ref[pl.ds(first, half), :] = made[part, HD : 2 * HD]
                v_ref[pl.ds(first, half), :] = made[part, 2 * HD :]
    for at in range(0, total, 128):
        vt_ref[:, at : at + 128] = v_ref[at : at + 128, :].astype(F32).T.astype(BF)
    wide_tile = 2 * TILE
    for tile in range(total // wide_tile):
        low = max(0, tile - total // 2 // wide_tile) * wide_tile
        high = (tile + 1) * wide_tile
        query = q_ref[high - wide_tile : high, :]
        begin = jnp.concatenate([begin_ref[2 * tile : 2 * tile + 1, :], begin_ref[2 * tile + 1 : 2 * tile + 2, :]], axis=1)
        query_pos = high - wide_tile + lax.broadcasted_iota(jnp.int32, (1, wide_tile), 1)
        scores = dot(k_ref[low:high, :], query, NT)
        key_pos = low + lax.broadcasted_iota(jnp.int32, scores.shape, 0)
        scores = jnp.where((key_pos >= begin) & (key_pos <= query_pos), scores, FAR)
        top = jnp.max(scores, axis=0, keepdims=True)
        weights = jnp.exp(scores - top)
        sums = jnp.sum(weights, axis=0, keepdims=True)
        out = dot(vt_ref[:, low:high], weights.astype(BF), NN) / sums
        ot_ref[:, high - wide_tile : high] = out
        lse = top + jnp.log(sums)
        lse_ref[2 * tile : 2 * tile + 1, :] = lse[:, :TILE]
        lse_ref[2 * tile + 1 : 2 * tile + 2, :] = lse[:, TILE:]
        turned = out.T.astype(BF)
        for piece in range(2 * group):
            shard, side = block_home(tile * 2 * group + piece, shards)
            att_ref[shard, :, side * HD : (side + 1) * HD] = turned[piece * half : (piece + 1) * half]
    for near in range(4):
        for far in range(4):
            outs[near][far] = att_ref[place.r * HEADS + (place.ctx ^ (far * 4 + near))]


def middle_kernel(table, *refs, count):
    weights, atts, refs = refs[:count], refs[count : count + 4], refs[count + 4 :]
    hidden_ref, gain_ref, bias_ref, att_out, mid_out, norm_out, w_ref, heads_ref = refs
    place = Place(table)
    if count > 1:
        for at, ref in enumerate(unstacked(weights)):
            rows = ref.shape[0]
            first = (place.flat(2) ^ MASKS[at]) * rows
            w_ref[pl.ds(pl.multiple_of(first, rows), rows), :] = ref[...]
    else:
        w_ref[...] = weights[0][...]
    for far in range(4):
        for near in range(4):
            heads_ref[place.ctx ^ (far * 4 + near)] = atts[far][near]
    half = heads_ref.shape[1]
    for head in range(0, HEADS, 2):
        for side in range(2):
            lanes = slice(side * HD, (side + 1) * HD)
            att_out[side * half : (side + 1) * half, head * HD : (head + 2) * HD] = jnp.concatenate(
                [heads_ref[head, :, lanes], heads_ref[head + 1, :, lanes]], axis=1
            )
    mid = hidden_ref[...].astype(F32) + dot(att_out[...], w_ref[...], NN)
    mid_out[...] = mid
    normed, _ = normalise(mid)
    norm_out[...] = (normed * gain_ref[...] + bias_ref[...]).astype(BF)


def feed_kernel(table, *refs, grads, mids, wide, groups):
    grads, mids, refs = refs[:grads], refs[grads : grads + mids], refs[grads + mids :]
    *weights, lay_keep, lay_send, mnd_keep, mnd_send, mid_out, act_out, delta_out, grad_out, up_ref, down_ref = refs
    place = Place(table)
    for out, arrays in ((grad_out, grads), (mid_out, mids)):
        first = 0
        for ref in arrays:
            for part in unstacked([ref]) if len(ref.shape) == 3 else [ref]:
                out[first : first + part.shape[0], :] = part[...]
                first += part.shape[0]
    width = mid_out.shape[1]
    own = width // (TEAM * groups)
    ffn = down_ref.shape[0] // groups
    moving = len(weights) > 2
    count = len(weights) // 2
    ups, downs = weights[:count], weights[count:]
    if not moving:
        ups, downs = unstacked(ups), unstacked(downs)
    for at in range(groups):
        if moving:
            high, x = place.zh ^ (at & 1), place.x ^ (at >> 1)
        else:
            high, x = at // wide, at % wide
        for mate in range(TEAM):
            first = ((high * TEAM + mate) * wide + x) * own
            if moving:
                first = pl.multiple_of(first, own)
            up_ref[pl.ds(first, own), :] = ups[at][mate * own : (mate + 1) * own, :]
        first = (high * wide + x) * ffn
        if moving:
            first = pl.multiple_of(first, ffn)
        down_ref[pl.ds(first, ffn), : width // 2] = downs[at][:ffn, :]
        down_ref[pl.ds(first, ffn), width // 2 :] = downs[at][ffn:, :]
    total = mid_out.shape[0]
    run = 256
    half = total // 2
    for first in list(range(half, total, run)) + list(range(0, half, run)):
        here = slice(first, first + run)
        up = dot(mid_out[here, :], up_ref[...], NN)
        value, slope = gelu_both(up)
        act = value.astype(BF)
        act_out[here, :] = act
        delta = (dot(grad_out[here, :], down_ref[...], NT) * slope).astype(BF)
        delta_out[here, :] = delta
        back = dot(delta, up_ref[...], NT)
        fore = dot(act, down_ref[...], NN)
        if first < half:
            mnd_keep[here, :] = back
            lay_keep[here, :] = fore.astype(BF)
        else:
            there = slice(first - half, first - half + run)
            mnd_send[there, :] = back.astype(BF)
            lay_send[there, :] = fore.astype(BF)


def turn_kernel(
    table, grad_ref, mid_ref, w_ref, keep_top, got_top, keep_low, got_low, gain_ref, delta_out, bf_out, *refs
):
    *outs, made_ref = refs
    mnd = jnp.concatenate(
        [keep_top[...] + got_top[...].astype(F32), keep_low[...] + got_low[...].astype(F32)], axis=0
    )
    normed, spread = normalise(mid_ref[...])
    delta = grad_ref[...].astype(F32) + norm_back(mnd, normed, spread, gain_ref[...])
    delta_out[...] = delta
    narrow = delta.astype(BF)
    bf_out[...] = narrow
    back = dot(narrow, w_ref[...], NT).astype(BF)
    half = made_ref.shape[1]
    for head in range(HEADS):
        cols = slice(head * HD, (head + 1) * HD)
        made_ref[head] = jnp.concatenate([back[:half, cols], back[half:, cols]], axis=1)
    place = Place(table)
    for near in range(4):
        for far in range(4):
            outs[near][far] = made_ref[place.ctx ^ (far * 4 + near)]


TEAM_ORDER = (0, 4, 2, 6, 1, 5, 3, 7)


def out_grad_kernel(table, lay_keep, lay_send, att_ref, delta_ref, keep_out, send_out, part_ref, *, wide, wrows):
    turned = att_ref[...].astype(F32).T.astype(BF)
    part_ref[...] = dot(turned, delta_ref[...], NN).astype(BF).reshape(part_ref.shape)
    place = Place(table)
    rows = lay_keep.shape[0] // 4
    highs = part_ref.shape[0] // (TEAM * wide)
    for at in range(TEAM):
        mate = place.mate ^ TEAM_ORDER[at]
        out, lay = (keep_out, lay_keep) if at < 4 else (send_out, lay_send)
        first = (at % 4) * 2 * rows
        out[first : first + rows, :] = lay[(at % 4) * rows : (at % 4 + 1) * rows, :]
        first += rows
        for x in range(wide):
            for high in range(highs):
                out[first : first + wrows, :] = part_ref[(high * TEAM + mate) * wide + x]
                first += wrows


def up_pack_kernel(table, part_ref, delta_ref, *outs, wide):
    rows = (outs[0].shape[0] - TAIL) // TEAM
    tail = sum_lines(jnp.sum(delta_ref[...].astype(F32), axis=0, keepdims=True))
    place = Place(table)
    highs = len(outs) // wide
    for at, out in enumerate(outs):
        if wide == 2:
            x, high = place.x ^ (at >> 1), place.zh ^ (at & 1)
        else:
            x, high = at // highs, at % highs
        for mate in range(TEAM):
            first = ((high * TEAM + mate) * wide + x) * rows
            if wide == 2:
                first = pl.multiple_of(first, rows)
            out[mate * rows : (mate + 1) * rows] = part_ref[pl.ds(first, rows), :].astype(BF)
        out[TEAM * rows :] = tail


def down_pack_kernel(table, part_ref, *outs, wide):
    rows = outs[0].shape[0]
    place = Place(table)
    highs = len(outs) // wide
    for at, out in enumerate(outs):
        if wide == 2:
            x, high = place.x ^ (at >> 1), place.zh ^ (at & 1)
        else:
            x, high = at // highs, at % highs
        first = (high * wide + x) * rows
        if wide == 2:
            first = pl.multiple_of(first, rows)
        out[...] = part_ref[pl.ds(first, rows), :].astype(BF)


def up_add_kernel(own_ref, got_ref, out_ref):
    body, tail = add_lines(own_ref[...], got_ref[...])
    out_ref[: body.shape[0]] = body
    out_ref[body.shape[0] :] = tail


def sum_kernel(own_ref, got_ref, out_ref):
    out_ref[...] = (own_ref[...].astype(F32) + got_ref[...].astype(F32)).astype(out_ref.dtype)


def up_share_kernel(table, own_ref, got_ref, *refs):
    *outs, all_ref = refs
    place = Place(table)
    rows = outs[0].shape[1] - TAIL
    body, tail = add_lines(own_ref[...], got_ref[...])
    for mate in range(TEAM):
        all_ref[mate] = body[mate * rows : (mate + 1) * rows]
    for near in range(4):
        for high in range(2):
            out = outs[near]
            out[high, :rows] = all_ref[place.mate ^ (high * 4 + near)]
            out[high, rows:] = tail


def sum_lines(sums):
    high, low = split_two(sums)
    line = lax.broadcasted_iota(jnp.int32, (8, sums.shape[1]), 0)
    return jnp.where(line == 0, high.astype(F32), jnp.where(line == 1, low.astype(F32), 0.0)).astype(BF)


def add_lines(own, got):
    rows = own.shape[0] - TAIL
    total = own.astype(F32) + got.astype(F32)
    return total[:rows].astype(BF), sum_lines(total[rows : rows + 1] + total[rows + 1 : rows + 2])


def owner_column(row_ref, first, rows):
    shape = (rows, row_ref.shape[1])
    hit = lax.broadcasted_iota(jnp.int32, shape, 1) == first + lax.broadcasted_iota(jnp.int32, shape, 0)
    return jnp.sum(jnp.where(hit, row_ref[...], 0.0), axis=1, keepdims=True)


def as_row(column):
    shape = (column.shape[0],) * 2
    hit = lax.broadcasted_iota(jnp.int32, shape, 0) == lax.broadcasted_iota(jnp.int32, shape, 1)
    return jnp.sum(jnp.where(hit, column, 0.0), axis=0, keepdims=True)


def norm_grads(place, master_ref, grad_ref, sums, gain_ref, bias_ref, gain_out, bias_out, wide):
    rows = master_ref.shape[0]
    first = place.flat(wide) * rows
    own = master_ref[...].astype(BF).astype(F32)
    bias_grad = jnp.sum(own * sums, axis=1, keepdims=True)
    bias_out[...] = as_row(bias_grad)
    gain_grad = jnp.sum(own * grad_ref[...], axis=1, keepdims=True) - owner_column(bias_ref, first, rows) * bias_grad
    gain_out[...] = as_row(gain_grad / owner_column(gain_ref, first, rows))


def up_end_kernel(table, one_ref, two_ref, own_ref, gain_ref, bias_ref, grad_out, gain_out, bias_out, sum_ref, *, runs, wide):
    place = Place(table)
    rows = own_ref.shape[0]
    piece = one_ref.shape[2] // runs
    for high, ref in ((0, one_ref), (1, two_ref)):
        for near in range(4):
            mate = place.mate ^ (high * 4 + near)
            for at in range(runs):
                there = pl.ds(pl.multiple_of((at * TEAM + mate) * piece, piece), piece)
                part = ref[near, :, at * piece : (at + 1) * piece].astype(F32)
                grad_out[:, there] = part[:rows]
                sum_ref[:, there] = part[rows : rows + 1] + part[rows + 1 : rows + 2]
    norm_grads(place, own_ref, grad_out, sum_ref[...], gain_ref, bias_ref, gain_out, bias_out, wide)


def qkv_end_kernel(table, *refs, wide):
    parts, (own_ref, gain_ref, bias_ref, grad_out, gain_out, bias_out, all_ref) = refs[:4], refs[4:]
    place = Place(table)
    for far in range(4):
        for near in range(4):
            all_ref[place.ctx ^ (far * 4 + near)] = parts[far][near, : all_ref.shape[1]]
    rows = own_ref.shape[0]
    half = rows // 2
    width = HEADS * HD
    body = rows + half
    for head in range(0, HEADS, 2):
        for at in range(2):
            lanes = slice(at * HD, (at + 1) * HD)
            grad_out[:, at * width + head * HD : at * width + (head + 2) * HD] = jnp.concatenate(
                [all_ref[head, :rows, lanes], all_ref[head + 1, :rows, lanes]], axis=1
            ).astype(F32)
        for side in range(2):
            lanes = slice(side * HD, (side + 1) * HD)
            grad_out[side * half : (side + 1) * half, 2 * width + head * HD : 2 * width + (head + 2) * HD] = (
                jnp.concatenate([all_ref[head, rows:body, lanes], all_ref[head + 1, rows:body, lanes]], axis=1).astype(
                    F32
                )
            )
    lines = [[], [], []]
    for head in range(HEADS):
        tail = all_ref[head, body:, :].astype(F32)
        pair = tail[0:1] + tail[1:2]
        lines[0].append(pair[:, :HD])
        lines[1].append(pair[:, HD:])
        lines[2].append(tail[2:3, :HD] + tail[2:3, HD:])
    sums = jnp.concatenate(lines[0] + lines[1] + lines[2], axis=1)
    norm_grads(place, own_ref, grad_out, sums, gain_ref, bias_ref, gain_out, bias_out, wide)


def backward_kernel(table, *refs):
    douts, refs = refs[:4], refs[4:]
    (
        q_ref, k_ref, v_ref, ot_ref, lse_ref, begin_ref, own_out, mate_out, dn_ref, sum_ref,
        do_ref, dop_ref, kt_ref, dq_ref, dk_ref, dv_ref, da_ref,
    ) = refs
    place = Place(table)
    for part in range(douts[0].shape[0]):
        for far in range(4):
            for near in range(4):
                do_ref[part * HEADS + (place.ctx ^ (far * 4 + near))] = douts[far][part, near]
    shards, half, _ = do_ref.shape
    rows = 2 * half
    total = shards * rows
    for block in range(2 * shards):
        shard, side = block_home(block, shards)
        dop_ref[block * half : (block + 1) * half, :] = do_ref[shard, :, side * HD : (side + 1) * HD]
    for at in range(0, total, 128):
        kt_ref[:, at : at + 128] = k_ref[at : at + 128, :].astype(F32).T.astype(BF)
    dk_ref[...] = jnp.zeros_like(dk_ref)
    dv_ref[...] = jnp.zeros_like(dv_ref)
    for tile in range(total // TILE):
        here = slice(tile * TILE, (tile + 1) * TILE)
        query = q_ref[here, :]
        dout = dop_ref[here, :]
        begin = begin_ref[tile : tile + 1, :]
        lse = lse_ref[tile : tile + 1, :]
        row_dot = jnp.sum(dout.astype(F32).T * ot_ref[:, here], axis=0, keepdims=True)
        query_pos = tile * TILE + lax.broadcasted_iota(jnp.int32, (1, TILE), 1)
        low = max(0, tile - total // 2 // TILE) * TILE
        there = slice(low, (tile + 1) * TILE)
        scores = dot(k_ref[there, :], query, NT)
        key_pos = low + lax.broadcasted_iota(jnp.int32, scores.shape, 0)
        allowed = (key_pos >= begin) & (key_pos <= query_pos)
        probs = jnp.where(allowed, jnp.exp(scores - lse), 0.0)
        dprobs = dot(v_ref[there, :], dout, NT)
        delta = (probs * (dprobs - row_dot)).astype(BF)
        dv_ref[there, :] += dot(probs.astype(BF), dout, NN)
        dk_ref[there, :] += dot(delta, query, NN)
        accum = dot(kt_ref[:, there], delta, NN)
        dq_ref[here, :] = (accum * HD**-0.5).T
    sums = jnp.zeros((1, TRIPLE), F32)
    for block in range(2 * shards):
        shard, side = block_home(block, shards)
        at = slice(block * half, (block + 1) * half)
        pair = jnp.concatenate([dq_ref[at, :], dk_ref[at, :]], axis=1).astype(BF)
        last = dv_ref[at, :].astype(BF)
        da_ref[shard, side * half : (side + 1) * half, :] = pair
        da_ref[shard, rows : rows + half, side * HD : (side + 1) * HD] = last
        to = slice(side * half, (side + 1) * half)
        joined = jnp.concatenate([pair, last], axis=1)
        dn_ref[shard, to, :] = joined
        sums = sums + jnp.sum(joined.astype(F32), axis=0, keepdims=True)
    sum_ref[...] = sums
    base = place.r * HEADS
    for at in range(TEAM):
        own_out[at] = da_ref[base + place.zh * TEAM + at]
        mate_out[at] = da_ref[base + (1 - place.zh) * TEAM + at]


def qkv_lines(pair, last):
    line = lax.broadcasted_iota(jnp.int32, (8, 2 * HD), 0)
    high, low = split_two(pair)
    both = jnp.concatenate(split_two(last), axis=1)
    lines = jnp.where(line == 0, high.astype(F32), jnp.where(line == 1, low.astype(F32), both.astype(F32)))
    return lines.astype(BF)


def qkv_grad_kernel(table, *refs, repeats, chips, others, wide):
    pieces, stacks, (dn_ref, sum_ref, *outs, acc_ref) = refs[:chips], refs[chips : chips + others], refs[chips + others :]
    pieces = list(pieces) + unstacked(stacks)
    place = Place(table)
    order = ring_order(chips, place)
    total = None
    for which in range(2):
        for at in range(chips):
            shard = 2 * order[at] + (place.c if which == 0 else 1 - place.c)
            turned = dn_ref[shard].astype(F32).T.astype(BF)
            step = dot(turned, pieces[which * chips + at][...], NN)
            total = step if total is None else total + step
    acc_ref[...] = total.T
    owners, tall, _ = outs[0].shape
    rows = (tall - TAIL) * 2 // 3
    half = rows // 2
    sums = sum_ref[...]
    lines = qkv_lines(sums[:, : 2 * HD], sums[:, 2 * HD :])

    def write(base):
        for at, out in enumerate(outs):
            x = place.x ^ at if wide == 2 else at
            for owner in range(owners):
                first = base + (owner * wide + x) * rows
                if wide == 2:
                    first = pl.multiple_of(first, rows)
                grad = acc_ref[pl.ds(first, rows), :]
                out[owner, :rows] = grad[:, : 2 * HD].astype(BF)
                out[owner, rows : rows + half] = jnp.concatenate(
                    [grad[:half, 2 * HD :], grad[half:, 2 * HD :]], axis=1
                ).astype(BF)
                out[owner, rows + half :] = lines

    if repeats == 1:
        write(0)
    else:
        for at in range(repeats):
            pl.when(place.r == at)(partial(write, at * owners * wide * rows))


def qkv_add_kernel(table, own_ref, got_ref, *outs):
    place = Place(table)
    body = own_ref.shape[1] - TAIL
    for near in range(4):
        for far in range(4):
            at = place.ctx ^ (far * 4 + near)
            total = own_ref[at].astype(F32) + got_ref[at].astype(F32)
            outs[near][far, :body] = total[:body].astype(BF)
            tail = total[body:]
            outs[near][far, body:] = qkv_lines(tail[0:1] + tail[1:2], tail[2:3, :HD] + tail[2:3, HD:])


def spread_kernel(_, keep_ref, got_ref, send_z, send_y, top_out, low_out):
    rows = keep_ref.shape[0] // 4
    half = rows // 2
    for at in range(4):
        for side in range(2):
            here = slice(at * rows + side * half, at * rows + (side + 1) * half)
            total = keep_ref[here, :].astype(F32) + got_ref[here, :].astype(F32)
            if side == 0:
                if at % 2 == 0:
                    top_out[at // 2] = total
                else:
                    send_z[at // 2] = total.astype(BF)
            elif at < 2:
                low_out[at] = total
            else:
                send_y[at - 2] = total.astype(BF)


def narrow_kernel(_, top_ref, got_z, low_ref, got_y, send_y, send_z, top_out, low_out):
    top_out[...] = top_ref[0] + got_z[0].astype(F32)
    low_out[...] = low_ref[0] + got_y[0].astype(F32)
    send_y[...] = (top_ref[1] + got_z[1].astype(F32)).astype(BF)
    send_z[...] = (low_ref[1] + got_y[1].astype(F32)).astype(BF)


def input_kernel(table, own_ref, got_ref, *refs):
    tall = own_ref.shape[1]
    rows = tall * 2 // 3
    half = rows // 2
    place = Place(table)
    w_own, *mates, keep_out, send_out, lhs_ref, rhs_ref = refs
    rhs_ref[:, : 2 * HD] = w_own[:, : 2 * HD]
    rhs_ref[:, 2 * HD : 3 * HD] = w_own[:, 2 * HD :]
    for at, w_got in enumerate(mates):
        count = w_got.shape[0]
        here = slice(0, count)
        if len(mates) == 2:
            here = pl.ds(pl.multiple_of((place.x ^ at) * count, count), count)
        rhs_ref[here, 3 * HD : 4 * HD] = w_got[:, 2 * HD :]
        rhs_ref[here, 4 * HD :] = w_got[:, : 2 * HD]
    for at in range(TEAM):
        mate = place.mate ^ TEAM_ORDER[at]
        first = at * rows
        one, two = own_ref[mate], got_ref[mate]
        lhs_ref[first : first + rows, : 2 * HD] = one[:rows]
        lhs_ref[first : first + rows, 4 * HD :] = two[:rows]
        for side in range(2):
            lanes = slice(side * HD, (side + 1) * HD)
            lhs_ref[first + side * half : first + (side + 1) * half, 2 * HD : 4 * HD] = jnp.concatenate(
                [one[rows:, lanes], two[rows:, lanes]], axis=1
            )
    middle = TEAM * rows // 2
    send_out[...] = dot(lhs_ref[middle:, :], rhs_ref[...], NT).astype(BF)
    keep_out[...] = dot(lhs_ref[:middle, :], rhs_ref[...], NT)


def blocks(count):
    return [(slice(at * 2 * HD, (at + 1) * 2 * HD), at * 4 // count, at % (count // 4)) for at in range(count)]


def spread_both_kernel(table, keep_ref, got_ref, share_ref, send_z, both_ref, top_out, low_out, send_y):
    spread_kernel(table, keep_ref, got_ref, send_z, send_y, top_out, low_out)
    tall, rows = share_ref.shape[1], send_y.shape[1]
    both_ref[:, :tall] = share_ref[...]
    for lanes, run, at in blocks(send_y.shape[2] // (2 * HD)):
        for high in range(2):
            first = tall + (2 * at + high) * rows
            both_ref[run, first : first + rows] = send_y[high, :, lanes]


def blend_kernel(_, top_ref, got_z, low_ref, both_ref, *refs):
    ups, qkvs, own_ref, got_ref = refs[:4], (refs[4], refs[5], both_ref, refs[6]), refs[7], refs[8]
    send_y, top_out, low_out, up_keep, *outs = refs[9:]
    tall, rows, part = refs[4].shape[1], ups[0].shape[1], own_ref.shape[1] // 4
    half = top_out.shape[0]
    top_out[...] = top_ref[0] + got_z[0].astype(F32)
    send_y[...] = (top_ref[1] + got_z[1].astype(F32)).astype(BF)
    after_ups = tall + rows * (ups[0].shape[2] // (2 * HD))
    for lanes, run, at in blocks(low_out.shape[1] // (2 * HD)):
        first = tall + 2 * at * half
        low_out[:, lanes] = low_ref[0, :, lanes] + both_ref[run, first : first + half].astype(F32)
        got = both_ref[run, first + half : first + 2 * half].astype(F32)
        to = after_ups + at * half
        outs[1][run, to : to + half] = (low_ref[1, :, lanes] + got).astype(BF)
    for near in range(4):
        up_keep[near] = ups[near][0]
        for far, out in enumerate(outs):
            out[near, :tall] = qkvs[near][far, :tall]
        for at in range(ups[0].shape[2] // (2 * HD)):
            first = tall + at * rows
            outs[1][near, first : first + rows] = ups[near][1, :, at * 2 * HD : (at + 1) * 2 * HD]
        here = slice(near * part, (near + 1) * part)
        total = (own_ref[1, here].astype(F32) + got_ref[1, here].astype(F32)).astype(BF)
        for at in range(own_ref.shape[2] // (2 * HD)):
            first = tall + at * part
            outs[2][near, first : first + part] = total[:, at * 2 * HD : (at + 1) * 2 * HD]


def end_kernel(
    table, keep_top, got_top, keep_low, mid_delta_ref, hidden_ref, gain1_ref, bias1_ref, gain2_ref, bias2_ref,
    q0_ref, q1_ref, q2_ref, q3_ref, qkv_ref, up_one, up_ref, down_ref, down_near, down_got, out_own, out_got,
    grad_out, qkv_out, qkv_gain, qkv_bias, up_out, up_gain, up_bias, down_out, out_out,
    all_ref, up_two, sum_ref, got_low,
):
    tall, rows, half = q0_ref.shape[1], up_one.shape[1], got_low.shape[0]
    after_ups = tall + rows * (up_one.shape[2] // (2 * HD))
    for lanes, run, at in blocks(got_low.shape[1] // (2 * HD)):
        first = after_ups + at * half
        got_low[:, lanes] = q1_ref[run, first : first + half]
    last_kernel(table, keep_top, got_top, keep_low, got_low, mid_delta_ref, hidden_ref, gain1_ref, grad_out)
    for near in range(4):
        for at in range(up_one.shape[2] // (2 * HD)):
            first = tall + at * rows
            up_two[near, :, at * 2 * HD : (at + 1) * 2 * HD] = q1_ref[near, first : first + rows]
    qkv_end_kernel(
        table, q0_ref, q1_ref, q2_ref, q3_ref, qkv_ref, gain1_ref, bias1_ref, qkv_out, qkv_gain, qkv_bias, all_ref, wide=2
    )
    up_end_kernel(
        table, up_one, up_two, up_ref, gain2_ref, bias2_ref, up_out, up_gain, up_bias, sum_ref, runs=2, wide=2
    )
    down_out[...] = down_ref[...].astype(F32) + down_near[...].astype(F32) + down_got[...].astype(F32)
    part = out_own.shape[1] // 4
    for near in range(4):
        rows = slice(near * part, (near + 1) * part)
        keep = out_own[0, rows].astype(F32) + out_got[0, rows].astype(F32)
        for at in range(out_own.shape[2] // (2 * HD)):
            first = tall + at * part
            lanes = slice(at * 2 * HD, (at + 1) * 2 * HD)
            out_out[rows, lanes] = keep[:, lanes] + q2_ref[near, first : first + part].astype(F32)


def last_kernel(_, keep_top, got_top, keep_low, got_low, mid_delta_ref, hidden_ref, gain_ref, out_ref):
    grad = jnp.concatenate(
        [keep_top[...] + got_top[...].astype(F32), keep_low[...] + got_low[...].astype(F32)], axis=0
    )
    normed, spread = normalise(hidden_ref[...].astype(F32))
    out_ref[...] = (mid_delta_ref[...] + norm_back(grad, normed, spread, gain_ref[...])).astype(BF)


def outs_kernel(table, mid_ref, lay_ref, got_lay, part_ref, got_part, lay_out, *outs, wide):
    lay_out[...] = (mid_ref[...] + lay_ref[...] + got_lay[...].astype(F32)).astype(BF)
    highs, rows, _ = outs[0].shape
    place = Place(table)
    for side, out in enumerate(outs):
        for at in range(highs):
            x, high = (place.x ^ side, place.zh ^ at) if wide == 2 else (side, at)
            first = (x * highs + high) * rows
            if wide == 2:
                first = pl.multiple_of(first, rows)
            out[at] = (part_ref[pl.ds(first, rows), :] + got_part[pl.ds(first, rows), :].astype(F32)).astype(BF)


def after(array, *others):
    return lax.optimization_barrier((array, *others))[0]


def apart(count, mask):
    return [(at, at ^ mask) for at in range(count)]


def stack(arrays):
    count = sum(array.shape[0] if array.ndim == 3 else 1 for array in arrays)
    return call(stack_kernel, arrays, [((count,) + arrays[0].shape[-2:], arrays[0].dtype)], smem=0)[0]


def meet(*arrays):
    return lax.optimization_barrier(arrays)


def near(arrays):
    return [lax.ppermute(arrays[at], ("y", "c"), apart(4, at)) for at in range(1, 4)]


def far(arrays):
    return [lax.ppermute(arrays[at], ("zh", "zl"), apart(4, at)) for at in range(1, 4)]


def swap(array, axis):
    return lax.ppermute(array, axis, SWAP)


def mix(arrays):
    shape = arrays[0].shape
    return call(mix_kernel, arrays, [((len(arrays),) + shape[1:], arrays[0].dtype)] * shape[0], smem=0)


def stack_kernel(*refs):
    at = 0
    for ref in refs[:-1]:
        count = ref.shape[0] if len(ref.shape) == 3 else 1
        for part in range(count):
            refs[-1][at] = ref[part] if len(ref.shape) == 3 else ref[...]
            at += 1


def spread(table, keep, got):
    shape = (keep.shape[0] // 8, keep.shape[1])
    return call(spread_kernel, (table, keep, got), [((2, *shape), BF)] * 2 + [((2, *shape), F32)] * 2)


def narrow(table, top, got_z, low, got_y, micros=0):
    shape = top.shape[1:]
    return call(
        narrow_kernel, (table, top, got_z, low, got_y), [(shape, BF)] * 2 + [(shape, F32)] * 2, micros=micros
    )


def add(one, two, kind):
    return call(sum_kernel, (one, two), [(one.shape, kind)], smem=0)[0]


class Steps:
    def __init__(self, arrays, sizes):
        (
            self.hidden, self.start, self.qkv, self.out, self.up, self.down,
            gain1, bias1, gain2, bias2, self.grad,
        ) = arrays
        self.hidden, self.grad = self.hidden[0], self.grad[0]
        self.gain1, self.bias1, self.gain2, self.bias2 = (a[None] for a in (gain1, bias1, gain2, bias2))
        self.repeats, self.wide = sizes["r"], sizes["x"]
        self.rows, self.width = self.hidden.shape
        self.half = self.rows // 2
        self.shards = self.repeats * HEADS
        self.total = self.shards * self.rows
        self.wrows, self.ffn = self.qkv.shape[0], self.down.shape[0]
        self.highs = 2 * self.repeats
        self.cols = self.highs * self.wide * self.ffn
        self.many = TEAM * self.rows
        self.qkv_tall = self.wrows * 3 // 2 + TAIL
        self.up_tall = self.wrows + TAIL
        self.sides = self.wide * self.highs
        self.piece = ((4, self.half, 2 * HD), BF)
        self.table = jnp.stack([lax.axis_index(axis).astype(jnp.int32) for axis in ALL])

    def first(self):
        masters = (self.qkv, self.out, self.up, self.down)
        row = ((1, self.width), F32)
        outs = call(
            partial(first_kernel, runs=self.highs),
            (self.table, self.hidden, self.gain1, self.bias1, *masters, self.start),
            [
                ((self.rows, self.width), BF),
                *[((4, self.qkv_tall, 2 * HD), BF)] * 4,
                ((self.wrows, self.width), BF),
                *[((2, self.wrows, self.cols), BF)] * 4,
                ((2 * self.ffn, self.width // 2), BF),
            ],
            [
                ((self.rows, self.width), BF), row, row,
                *[(a.shape, F32) for a in masters],
                (self.start.shape, jnp.int32),
                ((HEADS, self.qkv_tall, 2 * HD), BF),
            ],
            far=8,
            sems=8,
            limit=58,
        )
        return outs[0], list(outs[1:5]), outs[5], list(outs[6:10]), outs[10]

    def forward(self, pieces, others, packs):
        tokens = ((self.total, HD), BF)
        tiles = (self.total // TILE, TILE)
        sent = self.width // 2 if self.repeats == 1 and self.wide == 2 else self.width
        outs = call(
            partial(forward_kernel, wrows=self.wrows, chips=len(pieces), others=len(others), wide=self.wide),
            (self.table, *pieces, *others, *packs),
            [
                *[self.piece] * 4,
                (tiles, F32), (tiles, jnp.int32),
                ((self.width, TRIPLE), BF), ((sent, TRIPLE), BF),
                tokens, tokens, tokens,
                ((HD, self.total), F32),
            ],
            [((HD, self.total), BF), ((self.shards, self.half, 2 * HD), BF)]
            + [((self.shards, self.qkv_tall, 2 * HD), BF)] * (2 if self.wide == 2 else 0),
            limit=20 * self.repeats * self.repeats,
            micros=7,
        )
        return list(outs[:4]), list(outs[6:8]), (*outs[8:], *outs[4:6])

    def middle(self, weights, heads):
        return call(
            partial(middle_kernel, count=len(weights)),
            (self.table, *weights, *heads, self.hidden, self.gain2, self.bias2),
            [
                ((self.rows, self.width), BF),
                ((self.rows, self.width), F32),
                ((self.rows, self.width), BF),
                ((self.width, self.width), BF),
            ],
            [((HEADS, self.half, 2 * HD), BF)],
        )

    def feed(self, grads, mids, weights):
        half, full = (self.many // 2, self.width), (self.many, self.width)
        inner = ((self.many, self.cols), BF)
        return call(
            partial(
                feed_kernel, grads=len(grads), mids=len(mids), wide=self.wide, groups=self.highs * self.wide
            ),
            (self.table, *grads, *mids, *weights),
            [(half, BF), (half, BF), (half, F32), (half, BF), (full, BF), inner, inner, (full, BF)],
            [((self.width, self.cols), BF), ((self.cols, self.width), BF)],
            micros=6,
        )

    def up_gradient(self, mids, delta):
        return call(
            partial(up_pack_kernel, wide=self.wide),
            (self.table, dot(mids, delta, TN), delta),
            [((self.width // (self.highs * self.wide) + TAIL, self.cols), BF)] * self.sides,
        )

    def down_gradient(self, acts, grads):
        return call(
            partial(down_pack_kernel, wide=self.wide),
            (self.table, dot(acts, grads, TN)),
            [((self.ffn, self.width), BF)] * self.sides,
        )

    def turn(self, mid, w_out, ends):
        outs = call(
            turn_kernel,
            (self.table, self.grad, mid, w_out, *ends, self.gain2),
            [((self.rows, self.width), F32), ((self.rows, self.width), BF), *[self.piece] * 4],
            [((HEADS, self.half, 2 * HD), BF)],
        )
        return outs[0], outs[1], list(outs[2:])

    def out_gradient(self, lay_keep, lay_send, attended, delta):
        return call(
            partial(out_grad_kernel, wide=self.wide, wrows=self.wrows),
            (self.table, lay_keep, lay_send, attended, delta),
            [((self.many, self.width), BF)] * 2,
            [((self.shards * self.wide, self.wrows, self.width), BF)],
        )

    def backward(self, kept, douts):
        query, keys, values, out_t, lse, begin = kept
        tall = self.rows + self.half
        total = ((self.total, HD), F32)
        return call(
            backward_kernel,
            (self.table, *douts, query, keys, values, out_t, lse, begin),
            [
                ((TEAM, tall, 2 * HD), BF),
                ((TEAM, tall, 2 * HD), BF),
                ((self.shards, self.rows, TRIPLE), BF),
                ((1, TRIPLE), F32),
            ],
            [
                ((self.shards, self.half, 2 * HD), BF),
                ((self.total, HD), BF),
                ((HD, self.total), BF),
                total, total, total,
                ((self.shards, tall, 2 * HD), BF),
            ],
            limit=14 * self.repeats * self.repeats,
            micros=8,
        )

    def qkv_gradient(self, pieces, others, by_shard, sums):
        return call(
            partial(
                qkv_grad_kernel,
                repeats=self.repeats, chips=len(pieces), others=len(others), wide=self.wide,
            ),
            (self.table, *pieces, *others, by_shard, sums),
            [((HEADS, self.qkv_tall, 2 * HD), BF)] * self.wide,
            [((self.width, TRIPLE), F32)],
        )

    def up_share(self, own, got):
        return list(
            call(
                up_share_kernel,
                (self.table, own, got),
                [((2, self.up_tall, self.cols), BF)] * 4,
                [((TEAM, self.wrows, self.cols), BF)],
            )
        )

    def qkv_share(self, own, got):
        return list(call(qkv_add_kernel, (self.table, own, got), [((4, self.qkv_tall, 2 * HD), BF)] * 4))

    def outputs(self, mid, ends):
        return call(
            partial(outs_kernel, wide=self.wide),
            (self.table, mid, *ends),
            [((self.rows, self.width), BF)] + [((self.highs, self.wrows, self.width), BF)] * self.wide,
        )

    def inputs(self, to_own, from_mate, weights, mates):
        return call(
            input_kernel,
            (self.table, to_own, from_mate, weights, *mates),
            [((self.many // 2, self.width), F32), ((self.many // 2, self.width), BF)],
            [((self.many, 2 * TRIPLE), BF), ((self.width, 2 * TRIPLE), BF)],
        )

    def last(self, ends, mid_delta):
        return call(
            last_kernel,
            (self.table, *ends, mid_delta, self.hidden, self.gain1),
            [((self.rows, self.width), BF)],
        )[0]

    def up_end(self, ends):
        line = ((1, self.wrows), F32)
        return call(
            partial(up_end_kernel, runs=self.highs, wide=self.wide),
            (self.table, *ends, self.up, self.gain2, self.bias2),
            [(self.up.shape, F32), line, line],
            [((1, self.up.shape[1]), F32)],
        )

    def qkv_end(self, ends):
        line = ((1, self.wrows), F32)
        return call(
            partial(qkv_end_kernel, wide=self.wide),
            (self.table, *ends, self.qkv, self.gain1, self.bias1),
            [(self.qkv.shape, F32), line, line],
            [((HEADS, self.qkv_tall, 2 * HD), BF)],
        )


def ring_moves(long):
    count = 2 * long
    order = [2 * at for at in range(long)] + [2 * at + 1 for at in reversed(range(long))]
    right = [(order[at], order[(at + 1) % count]) for at in range(count)]
    return right, [(two, one) for one, two in right]


def results(layer_out, grad_in, qkv, out, up, down):
    return (
        layer_out[None], grad_in[None], qkv[0], out, up[0], down,
        qkv[1][0], qkv[2][0], up[1][0], up[2][0],
    )


def local(*arrays, sizes):
    s = Steps(arrays, sizes)
    right, left = ring_moves(4)

    def ahead(array):
        return lax.ppermute(array, CHIPS, right)

    def behind(array):
        return lax.ppermute(array, CHIPS, left)

    norm_in, by_head, out_b, up_b, down_b = s.first()
    a1, b1, *got = meet(ahead(norm_in), behind(norm_in), *near(by_head))
    packs = mix([by_head[0], *got])
    a2, b2, *got = meet(ahead(a1), behind(b1), *far(packs))
    (packed,) = call(settle_kernel, (s.table, packs[0], *got), [((HEADS, s.qkv_tall, 2 * HD), BF)])
    first = stack([norm_in, a1, b1, a2, b2])
    ups = [after(up, a2) for up in up_b]
    a3, b3, packed_x, *got = meet(ahead(a2), behind(b2), swap(packed, "x"), *near(ups))
    ups = mix([ups[0], *got])
    half = s.half
    one, two, up_z, first, down_x = meet(
        ahead(a3[:half]),
        behind(b3[half:]),
        swap(ups[1], "zl"),
        swap(after(first, a3), "c"),
        swap(after(down_b, a3), "x"),
    )
    a4 = stack([one, two]).reshape(s.rows, s.width)
    second = stack([a3, b3])
    (up_t,) = call(join_kernel, (s.table, ups[0], up_z, down_b), [((TEAM * s.wrows, s.cols), BF)])
    pieces = [norm_in, a1, b1, a2, b2, a3, b3, a4]
    others = [first, *meet(swap(second, "c"), swap(a4[None], "c"))]

    out = after(out_b, a4)
    out_z = [lax.ppermute(out, ("zh", "zl"), apart(4, at)) for at in range(1, 4)]
    grad = after(s.grad, a4)
    grad_z = swap(grad, "zl")
    att, w_head, kept = s.forward(pieces, others, [packed, packed_x])
    *att, grad_z, o1, o2, o3 = meet(*att, grad_z, *out_z)
    out_4 = stack([out, o1, o2, o3])
    *got, out_x, up_z, grad_y = meet(
        *near(att), swap(out_4, "x"), swap(after(up_t, att[0]), "zh"), swap(after(grad, att[0]), "y")
    )
    att = mix([att[0], *got])
    out_8 = stack([out_4, out_x])
    *got, out_8y, up_x, out_8c = meet(
        *far(att), swap(out_8, "y"), swap(after(up_t, att[0]), "x"), swap(out_8, "c")
    )
    attended, mid, norm_mid, w_out = s.middle([out_8, out_8y, out_8c, swap(out_8y, "c")], [att[0], *got])

    half = s.half
    grad_3 = stack([after(grad, norm_mid), grad_z, grad_y])
    by_z, by_y, up_zx, down_z, grad_3c = meet(
        swap(norm_mid, "zl"),
        swap(norm_mid, "y"),
        swap(after(up_z, norm_mid), "x"),
        swap(after(down_b, norm_mid), "zh"),
        swap(grad_3, "c"),
    )
    three = stack([norm_mid, by_z, by_y])
    both_one, both_two, three, down_zx, grad_one, grad_two = meet(
        swap(by_y[:half], "zl"),
        swap(by_z[half:], "y"),
        swap(three, "c"),
        swap(after(down_z, by_z), "x"),
        swap(after(grad_y[:half], by_z), "zl"),
        swap(after(grad_z[half:], by_z), "y"),
    )
    both = stack([both_one, both_two])
    grad_both = stack([grad_one, grad_two])
    mids = [norm_mid, by_z, by_y, both_one, both_two, three, swap(both, "c")]
    grads = [grad, grad_z, grad_y, grad_one, grad_two, grad_3c, swap(grad_both, "c")]
    lay_keep, lay_send, keep, send, mids, acts, delta, grads = s.feed(
        grads, mids, [up_t, up_z, up_x, up_zx, down_b, down_z, down_x, down_zx]
    )
    send_z, send_y, top, low = spread(s.table, keep, swap(send, "c"))
    up_parts = s.up_gradient(mids, after(delta, send_z))
    got_z, got_y, *up_parts = meet(swap(send_z, "zl"), swap(send_y, "y"), *up_parts)
    send_y, send_z, top, low = narrow(s.table, top, got_z, low, got_y)
    down_parts = s.down_gradient(after(acts, send_y), grads)
    end_top, end_low, *down_parts = meet(swap(send_y, "y"), swap(send_z, "zl"), *down_parts)
    mid_delta, mid_delta_b, by_head = s.turn(mid, w_out, (top, end_top, low, end_low))
    keep, send = s.out_gradient(after(lay_keep, mid_delta), lay_send, attended, mid_delta_b)
    *got, up_far, mate_1, keep, send = meet(
        *near(by_head),
        swap(after(up_parts[3], mid_delta), "x"),
        swap(after(w_head[1], mid_delta), "zh"),
        keep,
        send,
    )
    by_head = mix([by_head[0], *got])
    up_shape = up_parts[0].shape
    (up_send,) = call(up_add_kernel, (up_parts[1], after(up_far, by_head[0])), [(up_shape, BF)], smem=0)
    *got, send, down_far, up_send = meet(
        *far(by_head), swap(after(send, by_head[0]), "c"), swap(after(down_parts[3], by_head[0]), "x"), up_send
    )

    douts = [array[None] for array in (by_head[0], *got)]
    send_z, send_y, top, low = spread(s.table, keep, send)
    got_z, got_y = swap(send_z, "zl"), swap(send_y, "y")
    up_got = swap(after(up_send, send_z), "zh")
    up_near = swap(after(up_parts[2], send_z), "x")
    mate_2 = swap(after(mate_1, send_z), "x")
    kept = (after(kept[0], send_z), *kept[1:])
    to_own, to_mate, by_shard, sums = s.backward(kept, douts)
    from_mate = swap(to_mate, "zh")
    qkv_own, qkv_send = s.qkv_gradient(pieces, others, by_shard, sums)
    to_own, got_z, got_y, up_near, mate_2, up_got, qkv_send = meet(
        to_own, got_z, got_y, up_near, mate_2, up_got, qkv_send
    )
    send_y, send_z, top, low = narrow(s.table, top, got_z, low, got_y)
    down_send = add(down_parts[1], after(down_far, send_y), BF)
    (up_keep,) = call(up_add_kernel, (up_parts[0], after(up_near, send_y)), [(up_shape, BF)], smem=0)
    end_top, end_low, qkv_got, down_send, up_keep = meet(
        swap(send_y, "y"), swap(send_z, "zl"), swap(qkv_send, "x"), down_send, up_keep
    )
    qkv = s.qkv_share(qkv_own, qkv_got)
    ups = s.up_share(after(up_keep, qkv_got), up_got)
    layer_out, *outs = s.outputs(mid, (top, end_top, low, end_low))
    from_mate, *ups = meet(from_mate, *ups)
    keep, send = s.inputs(to_own, from_mate, w_head[0], [mate_1, mate_2])
    send, qkv_c, *got = meet(
        swap(send, "c"), lax.ppermute(after(qkv[1], send), ("y", "c"), apart(4, 1)), *near([after(a, send) for a in ups])
    )

    lines = 2 * HD
    half = (s.many // 8, s.width)
    quarter = s.half * s.width // (4 * lines)
    piece = ((4, s.qkv_tall, lines), BF)
    send_z, both, top, low = call(
        spread_both_kernel,
        (s.table, keep, send, qkv[2]),
        [
            ((2, s.half, s.width), BF),
            ((4, s.qkv_tall + 2 * quarter, lines), BF),
            ((2, s.half, s.width), F32),
            ((2, s.half, s.width), F32),
        ],
        [((2, s.half, s.width), BF)],
    )
    got_z, both, down_got, out_got, qkv_yc = meet(
        swap(send_z, "zl"),
        swap(both, "y"),
        swap(after(down_send, send_z), "zh"),
        swap(after(outs[1], send_z), "x"),
        lax.ppermute(after(qkv[3], send_z), ("y", "c"), apart(4, 3)),
    )
    send_y, top, low, up_keep, *qkv = call(
        blend_kernel,
        (s.table, top, got_z, low, both, *ups[:1], *got, qkv[0], qkv_c, qkv_yc, outs[0], out_got),
        [
            ((s.half, s.width), BF),
            ((s.half, s.width), F32),
            ((s.half, s.width), F32),
            ((4, s.up_tall, s.cols), BF),
            piece,
            ((4, s.qkv_tall + s.up_tall * s.cols // lines + quarter, lines), BF),
            ((4, s.qkv_tall + s.wrows * s.width // (4 * lines), lines), BF),
            piece,
        ],
    )
    end_top, down_near, *more = meet(
        swap(send_y, "y"), swap(after(down_parts[2], send_y), "x"), *far(qkv)
    )
    line = ((1, s.wrows), F32)
    outs = call(
        end_kernel,
        (
            s.table, top, end_top, low, mid_delta, s.hidden, s.gain1, s.bias1, s.gain2, s.bias2,
            qkv[0], *more, s.qkv, up_keep, s.up, down_parts[0], down_near, down_got, outs[0], out_got,
        ),
        [
            ((s.rows, s.width), BF),
            (s.qkv.shape, F32), line, line,
            (s.up.shape, F32), line, line,
            (s.down.shape, F32),
            (s.out.shape, F32),
        ],
        [
            ((HEADS, s.qkv_tall, 2 * HD), BF),
            ((4, s.up_tall, s.cols), BF),
            ((1, s.up.shape[1]), F32),
            ((s.half, s.width), BF),
        ],
    )
    return results(layer_out, outs[0], outs[1:4], outs[8], outs[4:7], outs[7])


def local_any(*arrays, sizes):
    s = Steps(arrays, sizes)
    repeats, wide = s.repeats, s.wide
    long = 4 * repeats
    right, left = ring_moves(long)
    norm_in, by_head, out_b, up_b, down_b = s.first()
    one = two = norm_in
    pieces = [norm_in]
    for hop in range(1, long + 1):
        one = lax.ppermute(one, CHIPS, right)
        pieces.append(one)
        if hop < long:
            two = lax.ppermute(two, CHIPS, left)
            pieces.append(two)
    others = [swap(piece[None], "c") for piece in pieces]

    def by_parts(arrays):
        return [lax.all_gather(array, "r", axis=0, tiled=False) for array in arrays]

    def share(arrays):
        got = mix([arrays[0], *near(arrays)])
        return [got[0], *far(got)]

    def team_gather(array):
        half = array.shape[0] // 2
        by_z, by_y = swap(array, "zl"), swap(array, "y")
        chip = [array, by_z, by_y, swap(by_y[:half], "zl"), swap(by_z[half:], "y")]
        return chip + [swap(piece, "c") for piece in chip]

    def team_scatter(keep, send):
        send_z, send_y, top, low = spread(s.table, keep, swap(send, "c"))
        send_y, send_z, top, low = narrow(s.table, top, swap(send_z, "zl"), low, swap(send_y, "y"))
        return top, swap(send_y, "y"), low, swap(send_z, "zl")

    def to_owners(parts):
        array = jnp.stack(parts).reshape((wide, s.highs) + parts[0].shape).swapaxes(0, 1)
        array = array.reshape((wide * s.highs,) + parts[0].shape)
        return jnp.sum(lax.all_to_all(array, GROUP, 0, 0, tiled=True).astype(F32), axis=0)

    packs = share(by_head)
    (packed,) = call(settle_kernel, (s.table, *packs), [((HEADS, s.qkv_tall, 2 * HD), BF)])
    packed = lax.all_gather(packed, "r", axis=0, tiled=True)
    packs = [packed, *lax.all_gather(packed, "x", axis=0, tiled=False)]
    if wide == 2:
        packs = [packed, swap(packed, "x")]
    ups = mix([up_b[0], *near(up_b)])
    up_t = call(
        join_kernel, (s.table, ups[0], swap(ups[1], "zl"), down_b), [((TEAM * s.wrows, s.cols), BF)]
    )[0]
    weights = [lax.all_gather(array, GROUP, axis=0, tiled=False) for array in (up_t, down_b)]
    att, w_head, kept = s.forward(pieces, others, packs)

    def mine(arrays):
        return share(arrays)

    w_out = lax.all_gather(out_b, ALL, axis=0, tiled=True)
    attended, mid, norm_mid, w_out = s.middle([w_out], mine(att))
    lay_keep, lay_send, keep, send, mids, acts, delta, grads = s.feed(
        team_gather(s.grad), team_gather(norm_mid), weights
    )
    mid_delta, mid_delta_b, by_head = s.turn(mid, w_out, team_scatter(keep, send))
    up = to_owners(s.up_gradient(mids, delta)).astype(BF)
    down = to_owners(s.down_gradient(acts, grads))
    to_own, to_mate, by_shard, sums = s.backward(kept, by_parts(share(by_head)))
    layer_out, *outs = s.outputs(
        mid, team_scatter(*s.out_gradient(lay_keep, lay_send, attended, mid_delta_b))
    )
    keep, send = s.inputs(to_own, swap(to_mate, "zh"), w_head[0], [swap(w_head[0], "zh")])
    grad_in = s.last(team_scatter(keep, send), mid_delta)
    parts = s.qkv_gradient(pieces, others, by_shard, sums)
    own, *got = list(lax.all_to_all(jnp.stack(parts), "x", 0, 0, tiled=True))
    while len(got) > 1:
        own, got = own.astype(F32) + got[0].astype(F32), got[1:]
    ups = s.up_share(up, jnp.zeros_like(up))
    ups = mix([ups[0], *near(ups)])
    return results(
        layer_out,
        grad_in,
        s.qkv_end(share(s.qkv_share(own, got[0]))),
        to_owners([part[at] for part in outs for at in range(s.highs)]),
        s.up_end((ups[0], swap(ups[1], "zl"))),
        down,
    )


def solution(mesh):
    ctx, wide = mesh.shape["ctx"], mesh.shape["wt"]
    sizes = {"r": ctx // HEADS, "zh": 2, "zl": 2, "y": 2, "c": 2, "x": wide}
    grid = Mesh(mesh.devices.reshape(tuple(sizes.values())), ALL)
    tokens, weights = P("x", CTX, None), P(ALL, None)
    return jax.shard_map(
        partial(local if sizes["r"] == 1 and wide == 2 else local_any, sizes=sizes),
        mesh=grid,
        in_specs=(tokens, P("x", CTX)) + (weights,) * 4 + (P(),) * 4 + (tokens,),
        out_specs=(tokens, tokens) + (weights,) * 4 + (P(ALL),) * 4,
        check_vma=False,
    )
```

```python
from functools import partial

import jax
import jax.numpy as jnp
from jax import lax
from jax.experimental import pallas as pl
from jax.experimental.pallas import tpu as pltpu
from jax.sharding import Mesh
from jax.sharding import PartitionSpec as P

HEADS = 16
HD = 64
TRIPLE = 3 * HD
EPS = 1e-05
FAR = -1e30
TILE = 256
TEAM = 8
TAIL = 8
BF = jnp.bfloat16
F32 = jnp.float32
ALL = ("r", "zh", "zl", "y", "c", "x")
CTX = ("r", "zh", "zl", "y", "c")
PART = ("zh", "zl", "y", "c")
CHIPS = ("r", "zh", "zl", "y")
TP = ("zl", "y", "c")
GROUP = ("r", "zh", "x")
SWAP = [(0, 1), (1, 0)]
MASKS = [
    z * 8 + y * 4 + c * 2 + x for c in range(2) for y in range(2) for x in range(2) for z in range(4)
]
NN = ((1,), (0,))
NT = ((1,), (1,))
TN = ((0,), (0,))


def dot(one, two, dims):
    return lax.dot_general(one, two, (dims, ((), ())), preferred_element_type=F32)


def normalise(rows):
    centred = rows - jnp.mean(rows, axis=-1, keepdims=True)
    spread = lax.rsqrt(jnp.mean(centred * centred, axis=-1, keepdims=True) + EPS)
    return centred * spread, spread


def norm_back(grad, normed, spread, gain):
    scaled = grad * gain
    inner = (
        scaled
        - jnp.mean(scaled, axis=-1, keepdims=True)
        - normed * jnp.mean(scaled * normed, axis=-1, keepdims=True)
    )
    return inner * spread


def gelu_both(up):
    root = 0.7978845608028654
    square = up * up
    inner = jnp.tanh(root * up * (1.0 + 0.044715 * square))
    plus = 0.5 * (1.0 + inner)
    slope = plus + 0.5 * up * (1.0 - inner * inner) * root * (1.0 + 3.0 * 0.044715 * square)
    return up * plus, slope


def block_home(block, shards):
    return (block, 0) if block < shards else (2 * shards - 1 - block, 1)


def split_two(values):
    high = values.astype(BF)
    return high, (values - high.astype(F32)).astype(BF)


def after(array, *others):
    return lax.optimization_barrier((array, *others))[0]


class Place:
    def __init__(self, table):
        self.r, self.zh, self.zl, self.y, self.c, self.x = (table[at] for at in range(6))
        self.mate = self.zl * 4 + self.y * 2 + self.c
        self.ctx = self.zh * TEAM + self.mate

    def flat(self, wide):
        return (self.r * HEADS + self.ctx) * wide + self.x


def call(body, arrays, outs, scratch=(), smem=1, smem_outs=(), far=0, sems=0, limit=12, micros=0):
    vector = pl.BlockSpec(memory_space=pltpu.VMEM)
    scalar = pl.BlockSpec(memory_space=pltpu.SMEM)
    there = pl.BlockSpec(memory_space=pl.ANY)
    scratch = [pltpu.VMEM(shape, kind) for shape, kind in scratch]
    if sems:
        scratch.append(pltpu.SemaphoreType.DMA((sems,)))
    return pl.pallas_call(
        body,
        out_shape=[jax.ShapeDtypeStruct(shape, kind) for shape, kind in outs],
        in_specs=[scalar] * smem + [there] * far + [vector] * (len(arrays) - smem - far),
        out_specs=[scalar if at in smem_outs else vector for at in range(len(outs))],
        scratch_shapes=scratch,
        compiler_params=pltpu.CompilerParams(vmem_limit_bytes=limit << 20),
        cost_estimate=pl.CostEstimate(flops=micros * 10**9 + 1000, bytes_accessed=1 << 10, transcendentals=0),
    )(*arrays)


def start_copies(pairs, sems):
    copies = [pltpu.make_async_copy(source, target, sems.at[at]) for at, (source, target) in enumerate(pairs)]
    for copy in copies:
        copy.start()
    return copies


def first_kernel(table, hidden_ref, gain_ref, bias_ref, qkv_ref, out_ref, up_ref, down_ref, start_ref, *refs, runs):
    (
        norm_out, *heads, out_b, one_ref, two_ref, three_ref, four_ref, down_b,
        hidden_at, gain_at, bias_at, qkv_at, out_at, up_at, down_at, start_at, made_ref, sems,
    ) = refs
    ups = one_ref, two_ref, three_ref, four_ref
    place = Place(table)
    copies = start_copies(
        (
            (hidden_ref, hidden_at), (gain_ref, gain_at), (bias_ref, bias_at), (start_ref, start_at), (qkv_ref, qkv_at),
            (out_ref, out_at), (up_ref, up_at), (down_ref, down_at),
        ),
        sems,
    )
    for copy in copies[:3]:
        copy.wait()
    normed, _ = normalise(hidden_at[...].astype(F32))
    norm_out[...] = (normed * gain_at[...] + bias_at[...]).astype(BF)
    for copy in copies[3:]:
        copy.wait()
    rows = qkv_at.shape[0]
    half = rows // 2
    width = HEADS * HD
    starts = start_at[...].astype(F32).astype(BF)
    for head in range(HEADS):
        part = [qkv_at[:, at * width + head * HD : at * width + (head + 1) * HD].astype(BF) for at in range(3)]
        made_ref[head, :rows] = jnp.concatenate(part[:2], axis=1)
        made_ref[head, rows : rows + half] = jnp.concatenate([part[2][:half], part[2][half:]], axis=1)
        made_ref[head, rows + half :] = jnp.broadcast_to(starts, (TAIL, 2 * HD))
    for near in range(4):
        for far in range(4):
            heads[near][far] = made_ref[place.ctx ^ (far * 4 + near)]
    out_b[...] = out_at[...].astype(BF)
    piece = ups[0].shape[2] // runs
    for near in range(4):
        for high in range(2):
            mate = place.mate ^ (high * 4 + near)
            for at in range(runs):
                first = pl.multiple_of((at * TEAM + mate) * piece, piece)
                ups[near][high, :, at * piece : (at + 1) * piece] = up_at[:, pl.ds(first, piece)].astype(BF)
    rows, half = down_at.shape[0], down_at.shape[1] // 2
    down_b[:rows] = down_at[:, :half].astype(BF)
    down_b[rows:] = down_at[:, half:].astype(BF)


def settle_kernel(table, *refs):
    place = Place(table)
    for far in range(4):
        for near in range(4):
            refs[4][place.ctx ^ (far * 4 + near)] = refs[far][near]


def head_weights(packs, w_ref, wrows, wide):
    whalf = wrows // 2
    for x in range(wide):
        for at in range(packs[x].shape[0]):
            first = (at * wide + x) * wrows
            w_ref[first : first + wrows, : 2 * HD] = packs[x][at, :wrows]
            pair = packs[x][at, wrows : wrows + whalf]
            w_ref[first : first + whalf, 2 * HD :] = pair[:, :HD]
            w_ref[first + whalf : first + wrows, 2 * HD :] = pair[:, HD:]


def unstacked(refs):
    return [ref.at[at] for ref in refs for at in range(ref.shape[0])]


def in_order(place, packs, one_ref, two_ref):
    for at in range(packs[0].shape[0]):
        one_ref[at] = jnp.where(place.x == 0, packs[0][at], packs[1][at])
        two_ref[at] = jnp.where(place.x == 0, packs[1][at], packs[0][at])


def join_kernel(table, one_ref, two_ref, _, out_ref):
    place = Place(table)
    rows = one_ref.shape[1]
    for at in range(TEAM):
        mate = place.mate ^ at
        part = (one_ref if at < 4 else two_ref)[at % 4]
        if rows % 16 == 0:
            out_ref[pl.ds(pl.multiple_of(mate * rows, rows), rows), :] = part
        else:
            for to in range(TEAM):

                @pl.when(mate == to)
                def _(to=to, part=part):
                    out_ref[to * rows : (to + 1) * rows, :] = part


def mix_kernel(*refs):
    count = len(refs) - refs[0].shape[0]
    for near in range(count):
        for far, out in enumerate(refs[count:]):
            out[near] = refs[near][far]


def ring_shifts(chips):
    shifts = [0]
    for hop in range(1, chips // 2 + 1):
        shifts += [-hop, hop] if hop < chips // 2 else [-hop]
    return shifts


def ring_order(chips, place):
    long = chips // 2
    along = (place.r * 2 + place.zh) * 2 + place.zl
    spot = jnp.where(place.y == 0, along, chips - 1 - along)
    order = []
    for shift in ring_shifts(chips):
        at = lax.rem(spot + shift + chips, chips)
        order.append(jnp.where(at < long, 2 * at, 2 * (chips - 1 - at) + 1))
    return order


def forward_kernel(table, *refs, wrows, chips, others, wide):
    pieces, others, refs = refs[:chips], refs[chips : chips + others], refs[chips + others :]
    pieces = list(pieces) + unstacked(others)
    own_ref, *refs = refs
    packs, refs = ([own_ref, refs[0]], refs[1:]) if wide == 2 else (refs[:wide], refs[wide:])
    outs, seconds = refs[:4], refs[14:]
    lse_ref, begin_ref, w_ref, w_send, q_ref, k_ref, v_ref, ot_ref, vt_ref, att_ref = refs[4:14]
    place = Place(table)
    if wide == 2:
        in_order(place, packs, *seconds)
        packs = seconds
    head_weights(packs, w_ref, wrows, wide)
    count = w_send.shape[0]
    if count < w_ref.shape[0]:
        w_send[...] = w_ref[pl.ds(pl.multiple_of(place.x * count, count), count), :]
    else:
        w_send[...] = w_ref[...]
    shards, half, _ = att_ref.shape
    rows = 2 * half
    total = shards * rows
    blocks = 2 * shards
    order = ring_order(chips, place)
    whalf = wrows // 2
    flags = []
    for block in range(blocks):
        shard, side = block_home(block, shards)
        row = own_ref[shard, wrows + whalf : wrows + whalf + 1].astype(F32)
        flags.append(row[:, side * half : (side + 1) * half])
    flags = jnp.concatenate(flags, axis=0)
    spots = half * lax.broadcasted_iota(jnp.int32, flags.shape, 0) + lax.broadcasted_iota(
        jnp.int32, flags.shape, 1
    )
    marks = jnp.where(flags > 0.5, spots.astype(F32), -1.0)
    lane = lax.broadcasted_iota(jnp.int32, marks.shape, 1)
    hop = 1
    while hop < half:
        moved = jnp.concatenate([marks[:, half - hop :], marks[:, : half - hop]], axis=1)
        marks = jnp.maximum(marks, jnp.where(lane >= hop, moved, -1.0))
        hop *= 2
    last = jnp.broadcast_to(marks[:, half - 1 :], marks.shape)
    line = lax.broadcasted_iota(jnp.int32, marks.shape, 0)
    hop = 1
    while hop < blocks:
        moved = jnp.concatenate([last[blocks - hop :], last[: blocks - hop]], axis=0)
        last = jnp.maximum(last, jnp.where(line >= hop, moved, -1.0))
        hop *= 2
    moved = jnp.concatenate([last[blocks - 1 :], last[: blocks - 1]], axis=0)
    begins = jnp.maximum(marks, jnp.where(line >= 1, moved, -1.0))
    group = TILE // half
    for tile in range(total // TILE):
        row = jnp.concatenate([begins[tile * group + at : tile * group + at + 1] for at in range(group)], axis=1)
        begin_ref[tile : tile + 1, :] = row.astype(jnp.int32)
    for which in range(2):
        for at in range(chips):
            made = dot(pieces[which * chips + at][...], w_ref[...], NN).astype(BF)
            shard = 2 * order[at] + (place.c if which == 0 else 1 - place.c)
            one = pl.multiple_of(shard * half, half)
            two = pl.multiple_of((blocks - 1 - shard) * half, half)
            scaled = made[:, :HD] * BF(HD**-0.5)
            for first, part in ((one, slice(0, half)), (two, slice(half, rows))):
                q_ref[pl.ds(first, half), :] = scaled[part]
                k_ref[pl.ds(first, half), :] = made[part, HD : 2 * HD]
                v_ref[pl.ds(first, half), :] = made[part, 2 * HD :]
    for at in range(0, total, 128):
        vt_ref[:, at : at + 128] = v_ref[at : at + 128, :].astype(F32).T.astype(BF)
    wide_tile = 2 * TILE
    for tile in range(total // wide_tile):
        low = max(0, tile - total // 2 // wide_tile) * wide_tile
        high = (tile + 1) * wide_tile
        query = q_ref[high - wide_tile : high, :]
        begin = jnp.concatenate([begin_ref[2 * tile : 2 * tile + 1, :], begin_ref[2 * tile + 1 : 2 * tile + 2, :]], axis=1)
        query_pos = high - wide_tile + lax.broadcasted_iota(jnp.int32, (1, wide_tile), 1)
        scores = dot(k_ref[low:high, :], query, NT)
        key_pos = low + lax.broadcasted_iota(jnp.int32, scores.shape, 0)
        scores = jnp.where((key_pos >= begin) & (key_pos <= query_pos), scores, FAR)
        top = jnp.max(scores, axis=0, keepdims=True)
        weights = jnp.exp(scores - top)
        sums = jnp.sum(weights, axis=0, keepdims=True)
        out = dot(vt_ref[:, low:high], weights.astype(BF), NN) / sums
        ot_ref[:, high - wide_tile : high] = out
        lse = top + jnp.log(sums)
        lse_ref[2 * tile : 2 * tile + 1, :] = lse[:, :TILE]
        lse_ref[2 * tile + 1 : 2 * tile + 2, :] = lse[:, TILE:]
        turned = out.T.astype(BF)
        for piece in range(2 * group):
            shard, side = block_home(tile * 2 * group + piece, shards)
            att_ref[shard, :, side * HD : (side + 1) * HD] = turned[piece * half : (piece + 1) * half]
    for near in range(4):
        for far in range(4):
            outs[near][far] = att_ref[place.r * HEADS + (place.ctx ^ (far * 4 + near))]


def middle_kernel(table, *refs, count):
    weights, atts, refs = refs[:count], refs[count : count + 4], refs[count + 4 :]
    hidden_ref, gain_ref, bias_ref, att_out, mid_out, norm_out, w_ref, heads_ref = refs
    place = Place(table)
    if count > 1:
        for at, ref in enumerate(unstacked(weights)):
            rows = ref.shape[0]
            first = (place.flat(2) ^ MASKS[at]) * rows
            w_ref[pl.ds(pl.multiple_of(first, rows), rows), :] = ref[...]
    else:
        w_ref[...] = weights[0][...]
    for far in range(4):
        for near in range(4):
            heads_ref[place.ctx ^ (far * 4 + near)] = atts[far][near]
    half = heads_ref.shape[1]
    for head in range(0, HEADS, 2):
        for side in range(2):
            lanes = slice(side * HD, (side + 1) * HD)
            att_out[side * half : (side + 1) * half, head * HD : (head + 2) * HD] = jnp.concatenate(
                [heads_ref[head, :, lanes], heads_ref[head + 1, :, lanes]], axis=1
            )
    mid = hidden_ref[...].astype(F32) + dot(att_out[...], w_ref[...], NN)
    mid_out[...] = mid
    normed, _ = normalise(mid)
    norm_out[...] = (normed * gain_ref[...] + bias_ref[...]).astype(BF)


def pair_kernel(mid_ref, mid_z, mid_y, grad_z, grad_y, three, send_z, send_y):
    half = send_z.shape[1]
    for at, ref in enumerate((mid_ref, mid_z, mid_y)):
        three[at] = ref[...]
    send_z[0], send_z[1] = mid_y[:half, :], grad_y[:half, :]
    send_y[0], send_y[1] = mid_z[half:, :], grad_z[half:, :]


def feed_kernel(table, *refs, grads, mids, wide, groups, paired):
    grads, mids, refs = refs[:grads], refs[grads : grads + mids], refs[grads + mids :]
    *weights, lay_keep, lay_send, mnd_keep, mnd_send, mid_out, act_out, delta_out, grad_out, up_ref, down_ref = refs
    place = Place(table)
    if paired:
        pairs = [mids[at] for at in (3, 4, 6, 7)]
        grads = [*grads[:3], *[ref.at[1] for ref in pairs[:2]], grads[3], *[ref.at[1] for ref in pairs[2:]]]
        mids = [*mids[:3], *[ref.at[0] for ref in pairs[:2]], mids[5], *[ref.at[0] for ref in pairs[2:]]]
    for out, arrays in ((grad_out, grads), (mid_out, mids)):
        first = 0
        for ref in arrays:
            for part in unstacked([ref]) if len(ref.shape) == 3 else [ref]:
                out[first : first + part.shape[0], :] = part[...]
                first += part.shape[0]
    width = mid_out.shape[1]
    own = width // (TEAM * groups)
    ffn = down_ref.shape[0] // groups
    moving = len(weights) > 2
    count = len(weights) // 2
    ups, downs = weights[:count], weights[count:]
    if not moving:
        ups, downs = unstacked(ups), unstacked(downs)
    for at in range(groups):
        if moving:
            high, x = place.zh ^ (at & 1), place.x ^ (at >> 1)
        else:
            high, x = at // wide, at % wide
        for mate in range(TEAM):
            first = ((high * TEAM + mate) * wide + x) * own
            if moving:
                first = pl.multiple_of(first, own)
            up_ref[pl.ds(first, own), :] = ups[at][mate * own : (mate + 1) * own, :]
        first = (high * wide + x) * ffn
        if moving:
            first = pl.multiple_of(first, ffn)
        down_ref[pl.ds(first, ffn), : width // 2] = downs[at][:ffn, :]
        down_ref[pl.ds(first, ffn), width // 2 :] = downs[at][ffn:, :]
    total = mid_out.shape[0]
    run = 256
    half = total // 2
    for first in list(range(half, total, run)) + list(range(0, half, run)):
        here = slice(first, first + run)
        up = dot(mid_out[here, :], up_ref[...], NN)
        value, slope = gelu_both(up)
        act = value.astype(BF)
        act_out[here, :] = act
        delta = (dot(grad_out[here, :], down_ref[...], NT) * slope).astype(BF)
        delta_out[here, :] = delta
        back = dot(delta, up_ref[...], NT)
        fore = dot(act, down_ref[...], NN)
        if first < half:
            mnd_keep[here, :] = back
            lay_keep[here, :] = fore.astype(BF)
        else:
            there = slice(first - half, first - half + run)
            mnd_send[there, :] = back.astype(BF)
            lay_send[there, :] = fore.astype(BF)


def turn_kernel(
    table, grad_ref, mid_ref, w_ref, keep_top, got_top, keep_low, got_low, gain_ref, delta_out, bf_out, *refs
):
    *outs, made_ref = refs
    mnd = jnp.concatenate(
        [keep_top[...] + got_top[...].astype(F32), keep_low[...] + got_low[...].astype(F32)], axis=0
    )
    normed, spread = normalise(mid_ref[...])
    delta = grad_ref[...].astype(F32) + norm_back(mnd, normed, spread, gain_ref[...])
    delta_out[...] = delta
    narrow = delta.astype(BF)
    bf_out[...] = narrow
    back = dot(narrow, w_ref[...], NT).astype(BF)
    half = made_ref.shape[1]
    for head in range(HEADS):
        cols = slice(head * HD, (head + 1) * HD)
        made_ref[head] = jnp.concatenate([back[:half, cols], back[half:, cols]], axis=1)
    place = Place(table)
    for near in range(4):
        for far in range(4):
            outs[near][far] = made_ref[place.ctx ^ (far * 4 + near)]


TEAM_ORDER = (0, 4, 2, 6, 1, 5, 3, 7)


def out_grad_kernel(table, lay_keep, lay_send, att_ref, delta_ref, keep_out, send_out, part_ref, *, wide, wrows):
    turned = att_ref[...].astype(F32).T.astype(BF)
    part_ref[...] = dot(turned, delta_ref[...], NN).astype(BF).reshape(part_ref.shape)
    place = Place(table)
    rows = lay_keep.shape[0] // 4
    highs = part_ref.shape[0] // (TEAM * wide)
    for at in range(TEAM):
        mate = place.mate ^ TEAM_ORDER[at]
        out, lay = (keep_out, lay_keep) if at < 4 else (send_out, lay_send)
        first = (at % 4) * 2 * rows
        out[first : first + rows, :] = lay[(at % 4) * rows : (at % 4 + 1) * rows, :]
        first += rows
        for x in range(wide):
            for high in range(highs):
                out[first : first + wrows, :] = part_ref[(high * TEAM + mate) * wide + x]
                first += wrows


def up_pack_kernel(table, part_ref, delta_ref, *outs, wide):
    rows = (outs[0].shape[0] - TAIL) // TEAM
    tail = sum_lines(jnp.sum(delta_ref[...].astype(F32), axis=0, keepdims=True))
    place = Place(table)
    highs = len(outs) // wide
    for at, out in enumerate(outs):
        if wide == 2:
            x, high = place.x ^ (at >> 1), place.zh ^ (at & 1)
        else:
            x, high = at // highs, at % highs
        for mate in range(TEAM):
            first = ((high * TEAM + mate) * wide + x) * rows
            if wide == 2:
                first = pl.multiple_of(first, rows)
            out[mate * rows : (mate + 1) * rows] = part_ref[pl.ds(first, rows), :].astype(BF)
        out[TEAM * rows :] = tail


def down_pack_kernel(table, part_ref, *outs, wide):
    rows = outs[0].shape[0]
    place = Place(table)
    highs = len(outs) // wide
    for at, out in enumerate(outs):
        if wide == 2:
            x, high = place.x ^ (at >> 1), place.zh ^ (at & 1)
        else:
            x, high = at // highs, at % highs
        first = (high * wide + x) * rows
        if wide == 2:
            first = pl.multiple_of(first, rows)
        out[...] = part_ref[pl.ds(first, rows), :].astype(BF)


def up_add_kernel(own_ref, got_ref, out_ref):
    body, tail = add_lines(own_ref[...], got_ref[...])
    out_ref[: body.shape[0]] = body
    out_ref[body.shape[0] :] = tail


def sum_kernel(own_ref, got_ref, out_ref):
    out_ref[...] = (own_ref[...].astype(F32) + got_ref[...].astype(F32)).astype(out_ref.dtype)


def up_share_kernel(table, own_ref, got_ref, *refs):
    *outs, all_ref = refs
    place = Place(table)
    rows = outs[0].shape[1] - TAIL
    body, tail = add_lines(own_ref[...], got_ref[...])
    for mate in range(TEAM):
        all_ref[mate] = body[mate * rows : (mate + 1) * rows]
    for near in range(4):
        for high in range(2):
            out = outs[near]
            out[high, :rows] = all_ref[place.mate ^ (high * 4 + near)]
            out[high, rows:] = tail


def sum_lines(sums):
    high, low = split_two(sums)
    line = lax.broadcasted_iota(jnp.int32, (8, sums.shape[1]), 0)
    return jnp.where(line == 0, high.astype(F32), jnp.where(line == 1, low.astype(F32), 0.0)).astype(BF)


def add_lines(own, got):
    rows = own.shape[0] - TAIL
    total = own.astype(F32) + got.astype(F32)
    return total[:rows].astype(BF), sum_lines(total[rows : rows + 1] + total[rows + 1 : rows + 2])


def owner_column(row_ref, first, rows):
    shape = (rows, row_ref.shape[1])
    hit = lax.broadcasted_iota(jnp.int32, shape, 1) == first + lax.broadcasted_iota(jnp.int32, shape, 0)
    return jnp.sum(jnp.where(hit, row_ref[...], 0.0), axis=1, keepdims=True)


def as_row(column):
    shape = (column.shape[0],) * 2
    hit = lax.broadcasted_iota(jnp.int32, shape, 0) == lax.broadcasted_iota(jnp.int32, shape, 1)
    return jnp.sum(jnp.where(hit, column, 0.0), axis=0, keepdims=True)


def norm_grads(place, master_ref, grad_ref, sums, gain_ref, bias_ref, gain_out, bias_out, wide):
    rows = master_ref.shape[0]
    first = place.flat(wide) * rows
    own = master_ref[...].astype(BF).astype(F32)
    bias_grad = jnp.sum(own * sums, axis=1, keepdims=True)
    bias_out[...] = as_row(bias_grad)
    gain_grad = jnp.sum(own * grad_ref[...], axis=1, keepdims=True) - owner_column(bias_ref, first, rows) * bias_grad
    gain_out[...] = as_row(gain_grad / owner_column(gain_ref, first, rows))


def up_end_kernel(table, one_ref, two_ref, own_ref, gain_ref, bias_ref, grad_out, gain_out, bias_out, sum_ref, *, runs, wide):
    place = Place(table)
    rows = own_ref.shape[0]
    piece = one_ref.shape[2] // runs
    for high, ref in ((0, one_ref), (1, two_ref)):
        for near in range(4):
            mate = place.mate ^ (high * 4 + near)
            for at in range(runs):
                there = pl.ds(pl.multiple_of((at * TEAM + mate) * piece, piece), piece)
                part = ref[near, :, at * piece : (at + 1) * piece].astype(F32)
                grad_out[:, there] = part[:rows]
                sum_ref[:, there] = part[rows : rows + 1] + part[rows + 1 : rows + 2]
    norm_grads(place, own_ref, grad_out, sum_ref[...], gain_ref, bias_ref, gain_out, bias_out, wide)


def qkv_end_kernel(table, *refs, wide):
    parts, (own_ref, gain_ref, bias_ref, grad_out, gain_out, bias_out, all_ref) = refs[:4], refs[4:]
    place = Place(table)
    for far in range(4):
        for near in range(4):
            all_ref[place.ctx ^ (far * 4 + near)] = parts[far][near, : all_ref.shape[1]]
    rows = own_ref.shape[0]
    half = rows // 2
    width = HEADS * HD
    body = rows + half
    for head in range(0, HEADS, 2):
        for at in range(2):
            lanes = slice(at * HD, (at + 1) * HD)
            grad_out[:, at * width + head * HD : at * width + (head + 2) * HD] = jnp.concatenate(
                [all_ref[head, :rows, lanes], all_ref[head + 1, :rows, lanes]], axis=1
            ).astype(F32)
        for side in range(2):
            lanes = slice(side * HD, (side + 1) * HD)
            grad_out[side * half : (side + 1) * half, 2 * width + head * HD : 2 * width + (head + 2) * HD] = (
                jnp.concatenate([all_ref[head, rows:body, lanes], all_ref[head + 1, rows:body, lanes]], axis=1).astype(
                    F32
                )
            )
    lines = [[], [], []]
    for head in range(HEADS):
        tail = all_ref[head, body:, :].astype(F32)
        pair = tail[0:1] + tail[1:2]
        lines[0].append(pair[:, :HD])
        lines[1].append(pair[:, HD:])
        lines[2].append(tail[2:3, :HD] + tail[2:3, HD:])
    sums = jnp.concatenate(lines[0] + lines[1] + lines[2], axis=1)
    norm_grads(place, own_ref, grad_out, sums, gain_ref, bias_ref, gain_out, bias_out, wide)


def backward_kernel(table, *refs):
    douts, refs = refs[:4], refs[4:]
    (
        q_ref, k_ref, v_ref, ot_ref, lse_ref, begin_ref, own_out, mate_out, dn_ref, sum_ref,
        do_ref, dop_ref, kt_ref, dq_ref, dk_ref, dv_ref, da_ref,
    ) = refs
    place = Place(table)
    for part in range(douts[0].shape[0]):
        for far in range(4):
            for near in range(4):
                do_ref[part * HEADS + (place.ctx ^ (far * 4 + near))] = douts[far][part, near]
    shards, half, _ = do_ref.shape
    rows = 2 * half
    total = shards * rows
    for block in range(2 * shards):
        shard, side = block_home(block, shards)
        dop_ref[block * half : (block + 1) * half, :] = do_ref[shard, :, side * HD : (side + 1) * HD]
    for at in range(0, total, 128):
        kt_ref[:, at : at + 128] = k_ref[at : at + 128, :].astype(F32).T.astype(BF)
    dk_ref[...] = jnp.zeros_like(dk_ref)
    dv_ref[...] = jnp.zeros_like(dv_ref)
    for tile in range(total // TILE):
        here = slice(tile * TILE, (tile + 1) * TILE)
        query = q_ref[here, :]
        dout = dop_ref[here, :]
        begin = begin_ref[tile : tile + 1, :]
        lse = lse_ref[tile : tile + 1, :]
        row_dot = jnp.sum(dout.astype(F32).T * ot_ref[:, here], axis=0, keepdims=True)
        query_pos = tile * TILE + lax.broadcasted_iota(jnp.int32, (1, TILE), 1)
        low = max(0, tile - total // 2 // TILE) * TILE
        there = slice(low, (tile + 1) * TILE)
        scores = dot(k_ref[there, :], query, NT)
        key_pos = low + lax.broadcasted_iota(jnp.int32, scores.shape, 0)
        allowed = (key_pos >= begin) & (key_pos <= query_pos)
        probs = jnp.where(allowed, jnp.exp(scores - lse), 0.0)
        dprobs = dot(v_ref[there, :], dout, NT)
        delta = (probs * (dprobs - row_dot)).astype(BF)
        dv_ref[there, :] += dot(probs.astype(BF), dout, NN)
        dk_ref[there, :] += dot(delta, query, NN)
        accum = dot(kt_ref[:, there], delta, NN)
        dq_ref[here, :] = (accum * HD**-0.5).T
    sums = jnp.zeros((1, TRIPLE), F32)
    for block in range(2 * shards):
        shard, side = block_home(block, shards)
        at = slice(block * half, (block + 1) * half)
        pair = jnp.concatenate([dq_ref[at, :], dk_ref[at, :]], axis=1).astype(BF)
        last = dv_ref[at, :].astype(BF)
        da_ref[shard, side * half : (side + 1) * half, :] = pair
        da_ref[shard, rows : rows + half, side * HD : (side + 1) * HD] = last
        to = slice(side * half, (side + 1) * half)
        joined = jnp.concatenate([pair, last], axis=1)
        dn_ref[shard, to, :] = joined
        sums = sums + jnp.sum(joined.astype(F32), axis=0, keepdims=True)
    sum_ref[...] = sums
    base = place.r * HEADS
    for at in range(TEAM):
        own_out[at] = da_ref[base + place.zh * TEAM + at]
        mate_out[at] = da_ref[base + (1 - place.zh) * TEAM + at]


def qkv_lines(pair, last):
    line = lax.broadcasted_iota(jnp.int32, (8, 2 * HD), 0)
    high, low = split_two(pair)
    both = jnp.concatenate(split_two(last), axis=1)
    lines = jnp.where(line == 0, high.astype(F32), jnp.where(line == 1, low.astype(F32), both.astype(F32)))
    return lines.astype(BF)


def qkv_grad_kernel(table, *refs, repeats, chips, others, wide):
    pieces, stacks, (dn_ref, sum_ref, *outs, acc_ref) = refs[:chips], refs[chips : chips + others], refs[chips + others :]
    pieces = list(pieces) + unstacked(stacks)
    place = Place(table)
    order = ring_order(chips, place)
    total = None
    for which in range(2):
        for at in range(chips):
            shard = 2 * order[at] + (place.c if which == 0 else 1 - place.c)
            turned = dn_ref[shard].astype(F32).T.astype(BF)
            step = dot(turned, pieces[which * chips + at][...], NN)
            total = step if total is None else total + step
    acc_ref[...] = total.T
    owners, tall, _ = outs[0].shape
    rows = (tall - TAIL) * 2 // 3
    half = rows // 2
    sums = sum_ref[...]
    lines = qkv_lines(sums[:, : 2 * HD], sums[:, 2 * HD :])

    def write(base):
        for at, out in enumerate(outs):
            x = place.x ^ at if wide == 2 else at
            for owner in range(owners):
                first = base + (owner * wide + x) * rows
                if wide == 2:
                    first = pl.multiple_of(first, rows)
                grad = acc_ref[pl.ds(first, rows), :]
                out[owner, :rows] = grad[:, : 2 * HD].astype(BF)
                out[owner, rows : rows + half] = jnp.concatenate(
                    [grad[:half, 2 * HD :], grad[half:, 2 * HD :]], axis=1
                ).astype(BF)
                out[owner, rows + half :] = lines

    if repeats == 1:
        write(0)
    else:
        for at in range(repeats):
            pl.when(place.r == at)(partial(write, at * owners * wide * rows))


def qkv_add_kernel(table, own_ref, got_ref, *outs):
    place = Place(table)
    body = own_ref.shape[1] - TAIL
    for near in range(4):
        for far in range(4):
            at = place.ctx ^ (far * 4 + near)
            total = own_ref[at].astype(F32) + got_ref[at].astype(F32)
            outs[near][far, :body] = total[:body].astype(BF)
            tail = total[body:]
            outs[near][far, body:] = qkv_lines(tail[0:1] + tail[1:2], tail[2:3, :HD] + tail[2:3, HD:])


def spread_kernel(_, keep_ref, got_ref, send_z, send_y, top_out, low_out):
    rows = keep_ref.shape[0] // 4
    half = rows // 2
    for at in range(4):
        for side in range(2):
            here = slice(at * rows + side * half, at * rows + (side + 1) * half)
            total = keep_ref[here, :].astype(F32) + got_ref[here, :].astype(F32)
            if side == 0:
                if at % 2 == 0:
                    top_out[at // 2] = total
                else:
                    send_z[at // 2] = total.astype(BF)
            elif at < 2:
                low_out[at] = total
            else:
                send_y[at - 2] = total.astype(BF)


def narrow_kernel(_, top_ref, got_z, low_ref, got_y, send_y, send_z, top_out, low_out):
    top_out[...] = top_ref[0] + got_z[0].astype(F32)
    low_out[...] = low_ref[0] + got_y[0].astype(F32)
    send_y[...] = (top_ref[1] + got_z[1].astype(F32)).astype(BF)
    send_z[...] = (low_ref[1] + got_y[1].astype(F32)).astype(BF)


def input_kernel(table, own_ref, got_ref, *refs):
    tall = own_ref.shape[1]
    rows = tall * 2 // 3
    half = rows // 2
    place = Place(table)
    w_own, *mates, keep_out, send_out, lhs_ref, rhs_ref = refs
    rhs_ref[:, : 2 * HD] = w_own[:, : 2 * HD]
    rhs_ref[:, 2 * HD : 3 * HD] = w_own[:, 2 * HD :]
    for at, w_got in enumerate(mates):
        count = w_got.shape[0]
        here = slice(0, count)
        if len(mates) == 2:
            here = pl.ds(pl.multiple_of((place.x ^ at) * count, count), count)
        rhs_ref[here, 3 * HD : 4 * HD] = w_got[:, 2 * HD :]
        rhs_ref[here, 4 * HD :] = w_got[:, : 2 * HD]
    for at in range(TEAM):
        mate = place.mate ^ TEAM_ORDER[at]
        first = at * rows
        one, two = own_ref[mate], got_ref[mate]
        lhs_ref[first : first + rows, : 2 * HD] = one[:rows]
        lhs_ref[first : first + rows, 4 * HD :] = two[:rows]
        for side in range(2):
            lanes = slice(side * HD, (side + 1) * HD)
            lhs_ref[first + side * half : first + (side + 1) * half, 2 * HD : 4 * HD] = jnp.concatenate(
                [one[rows:, lanes], two[rows:, lanes]], axis=1
            )
    middle = TEAM * rows // 2
    send_out[...] = dot(lhs_ref[middle:, :], rhs_ref[...], NT).astype(BF)
    keep_out[...] = dot(lhs_ref[:middle, :], rhs_ref[...], NT)


def blocks(count):
    return [(slice(at * 2 * HD, (at + 1) * 2 * HD), at * 4 // count, at % (count // 4)) for at in range(count)]


def spread_both_kernel(table, keep_ref, got_ref, share_ref, send_z, both_ref, top_out, low_out, send_y):
    spread_kernel(table, keep_ref, got_ref, send_z, send_y, top_out, low_out)
    tall, rows = share_ref.shape[1], send_y.shape[1]
    both_ref[:, :tall] = share_ref[...]
    for lanes, run, at in blocks(send_y.shape[2] // (2 * HD)):
        for high in range(2):
            first = tall + (2 * at + high) * rows
            both_ref[run, first : first + rows] = send_y[high, :, lanes]


def blend_kernel(_, top_ref, got_z, low_ref, both_ref, *refs):
    ups, qkvs, own_ref, got_ref = refs[:4], (refs[4], refs[5], both_ref, refs[6]), refs[7], refs[8]
    send_y, top_out, low_out, up_keep, *outs = refs[9:]
    tall, rows, part = refs[4].shape[1], ups[0].shape[1], own_ref.shape[1] // 4
    half = top_out.shape[0]
    top_out[...] = top_ref[0] + got_z[0].astype(F32)
    send_y[...] = (top_ref[1] + got_z[1].astype(F32)).astype(BF)
    after_ups = tall + rows * (ups[0].shape[2] // (2 * HD))
    for lanes, run, at in blocks(low_out.shape[1] // (2 * HD)):
        first = tall + 2 * at * half
        low_out[:, lanes] = low_ref[0, :, lanes] + both_ref[run, first : first + half].astype(F32)
        got = both_ref[run, first + half : first + 2 * half].astype(F32)
        to = after_ups + at * half
        outs[1][run, to : to + half] = (low_ref[1, :, lanes] + got).astype(BF)
    for near in range(4):
        up_keep[near] = ups[near][0]
        for far, out in enumerate(outs):
            out[near, :tall] = qkvs[near][far, :tall]
        for at in range(ups[0].shape[2] // (2 * HD)):
            first = tall + at * rows
            outs[1][near, first : first + rows] = ups[near][1, :, at * 2 * HD : (at + 1) * 2 * HD]
        here = slice(near * part, (near + 1) * part)
        total = (own_ref[1, here].astype(F32) + got_ref[1, here].astype(F32)).astype(BF)
        for at in range(own_ref.shape[2] // (2 * HD)):
            first = tall + at * part
            outs[2][near, first : first + part] = total[:, at * 2 * HD : (at + 1) * 2 * HD]


def end_kernel(
    table, keep_top, got_top, keep_low, mid_delta_ref, hidden_ref, gain1_ref, bias1_ref, gain2_ref, bias2_ref,
    q0_ref, q1_ref, q2_ref, q3_ref, qkv_ref, up_one, up_ref, down_ref, down_near, down_got, out_own, out_got,
    grad_out, qkv_out, qkv_gain, qkv_bias, up_out, up_gain, up_bias, down_out, out_out,
    all_ref, up_two, sum_ref, got_low,
):
    tall, rows, half = q0_ref.shape[1], up_one.shape[1], got_low.shape[0]
    after_ups = tall + rows * (up_one.shape[2] // (2 * HD))
    for lanes, run, at in blocks(got_low.shape[1] // (2 * HD)):
        first = after_ups + at * half
        got_low[:, lanes] = q1_ref[run, first : first + half]
    last_kernel(table, keep_top, got_top, keep_low, got_low, mid_delta_ref, hidden_ref, gain1_ref, grad_out)
    for near in range(4):
        for at in range(up_one.shape[2] // (2 * HD)):
            first = tall + at * rows
            up_two[near, :, at * 2 * HD : (at + 1) * 2 * HD] = q1_ref[near, first : first + rows]
    qkv_end_kernel(
        table, q0_ref, q1_ref, q2_ref, q3_ref, qkv_ref, gain1_ref, bias1_ref, qkv_out, qkv_gain, qkv_bias, all_ref, wide=2
    )
    up_end_kernel(
        table, up_one, up_two, up_ref, gain2_ref, bias2_ref, up_out, up_gain, up_bias, sum_ref, runs=2, wide=2
    )
    down_out[...] = down_ref[...].astype(F32) + down_near[...].astype(F32) + down_got[...].astype(F32)
    part = out_own.shape[1] // 4
    for near in range(4):
        rows = slice(near * part, (near + 1) * part)
        keep = out_own[0, rows].astype(F32) + out_got[0, rows].astype(F32)
        for at in range(out_own.shape[2] // (2 * HD)):
            first = tall + at * part
            lanes = slice(at * 2 * HD, (at + 1) * 2 * HD)
            out_out[rows, lanes] = keep[:, lanes] + q2_ref[near, first : first + part].astype(F32)


def last_kernel(_, keep_top, got_top, keep_low, got_low, mid_delta_ref, hidden_ref, gain_ref, out_ref):
    grad = jnp.concatenate(
        [keep_top[...] + got_top[...].astype(F32), keep_low[...] + got_low[...].astype(F32)], axis=0
    )
    normed, spread = normalise(hidden_ref[...].astype(F32))
    out_ref[...] = (mid_delta_ref[...] + norm_back(grad, normed, spread, gain_ref[...])).astype(BF)


def outs_kernel(table, mid_ref, lay_ref, got_lay, part_ref, got_part, lay_out, *outs, wide):
    lay_out[...] = (mid_ref[...] + lay_ref[...] + got_lay[...].astype(F32)).astype(BF)
    highs, rows, _ = outs[0].shape
    place = Place(table)
    for side, out in enumerate(outs):
        for at in range(highs):
            x, high = (place.x ^ side, place.zh ^ at) if wide == 2 else (side, at)
            first = (x * highs + high) * rows
            if wide == 2:
                first = pl.multiple_of(first, rows)
            out[at] = (part_ref[pl.ds(first, rows), :] + got_part[pl.ds(first, rows), :].astype(F32)).astype(BF)


def after(array, *others):
    return lax.optimization_barrier((array, *others))[0]


def apart(count, mask):
    return [(at, at ^ mask) for at in range(count)]


def stack(arrays):
    count = sum(array.shape[0] if array.ndim == 3 else 1 for array in arrays)
    return call(stack_kernel, arrays, [((count,) + arrays[0].shape[-2:], arrays[0].dtype)], smem=0)[0]


def meet(*arrays):
    return lax.optimization_barrier(arrays)


def near(arrays):
    return [lax.ppermute(arrays[at], ("y", "c"), apart(4, at)) for at in range(1, 4)]


def far(arrays):
    return [lax.ppermute(arrays[at], ("zh", "zl"), apart(4, at)) for at in range(1, 4)]


def swap(array, axis):
    return lax.ppermute(array, axis, SWAP)


def mix(arrays):
    shape = arrays[0].shape
    return call(mix_kernel, arrays, [((len(arrays),) + shape[1:], arrays[0].dtype)] * shape[0], smem=0)


def stack_kernel(*refs):
    at = 0
    for ref in refs[:-1]:
        count = ref.shape[0] if len(ref.shape) == 3 else 1
        for part in range(count):
            refs[-1][at] = ref[part] if len(ref.shape) == 3 else ref[...]
            at += 1


def spread(table, keep, got):
    shape = (keep.shape[0] // 8, keep.shape[1])
    return call(spread_kernel, (table, keep, got), [((2, *shape), BF)] * 2 + [((2, *shape), F32)] * 2)


def narrow(table, top, got_z, low, got_y, micros=0):
    shape = top.shape[1:]
    return call(
        narrow_kernel, (table, top, got_z, low, got_y), [(shape, BF)] * 2 + [(shape, F32)] * 2, micros=micros
    )


def add(one, two, kind):
    return call(sum_kernel, (one, two), [(one.shape, kind)], smem=0)[0]


class Steps:
    def __init__(self, arrays, sizes):
        (
            self.hidden, self.start, self.qkv, self.out, self.up, self.down,
            gain1, bias1, gain2, bias2, self.grad,
        ) = arrays
        self.hidden, self.grad = self.hidden[0], self.grad[0]
        self.gain1, self.bias1, self.gain2, self.bias2 = (a[None] for a in (gain1, bias1, gain2, bias2))
        self.repeats, self.wide = sizes["r"], sizes["x"]
        self.rows, self.width = self.hidden.shape
        self.half = self.rows // 2
        self.shards = self.repeats * HEADS
        self.total = self.shards * self.rows
        self.wrows, self.ffn = self.qkv.shape[0], self.down.shape[0]
        self.highs = 2 * self.repeats
        self.cols = self.highs * self.wide * self.ffn
        self.many = TEAM * self.rows
        self.qkv_tall = self.wrows * 3 // 2 + TAIL
        self.up_tall = self.wrows + TAIL
        self.sides = self.wide * self.highs
        self.piece = ((4, self.half, 2 * HD), BF)
        self.table = jnp.stack([lax.axis_index(axis).astype(jnp.int32) for axis in ALL])

    def first(self):
        masters = (self.qkv, self.out, self.up, self.down)
        row = ((1, self.width), F32)
        outs = call(
            partial(first_kernel, runs=self.highs),
            (self.table, self.hidden, self.gain1, self.bias1, *masters, self.start),
            [
                ((self.rows, self.width), BF),
                *[((4, self.qkv_tall, 2 * HD), BF)] * 4,
                ((self.wrows, self.width), BF),
                *[((2, self.wrows, self.cols), BF)] * 4,
                ((2 * self.ffn, self.width // 2), BF),
            ],
            [
                ((self.rows, self.width), BF), row, row,
                *[(a.shape, F32) for a in masters],
                (self.start.shape, jnp.int32),
                ((HEADS, self.qkv_tall, 2 * HD), BF),
            ],
            far=8,
            sems=8,
            limit=58,
        )
        return outs[0], list(outs[1:5]), outs[5], list(outs[6:10]), outs[10]

    def forward(self, pieces, others, packs):
        tokens = ((self.total, HD), BF)
        tiles = (self.total // TILE, TILE)
        sent = self.width // 2 if self.repeats == 1 and self.wide == 2 else self.width
        outs = call(
            partial(forward_kernel, wrows=self.wrows, chips=len(pieces), others=len(others), wide=self.wide),
            (self.table, *pieces, *others, *packs),
            [
                *[self.piece] * 4,
                (tiles, F32), (tiles, jnp.int32),
                ((self.width, TRIPLE), BF), ((sent, TRIPLE), BF),
                tokens, tokens, tokens,
                ((HD, self.total), F32),
            ],
            [((HD, self.total), BF), ((self.shards, self.half, 2 * HD), BF)]
            + [((self.shards, self.qkv_tall, 2 * HD), BF)] * (2 if self.wide == 2 else 0),
            limit=20 * self.repeats * self.repeats,
            micros=7,
        )
        return list(outs[:4]), list(outs[6:8]), (*outs[8:], *outs[4:6])

    def middle(self, weights, heads):
        return call(
            partial(middle_kernel, count=len(weights)),
            (self.table, *weights, *heads, self.hidden, self.gain2, self.bias2),
            [
                ((self.rows, self.width), BF),
                ((self.rows, self.width), F32),
                ((self.rows, self.width), BF),
                ((self.width, self.width), BF),
            ],
            [((HEADS, self.half, 2 * HD), BF)],
        )

    def feed(self, grads, mids, weights):
        half, full = (self.many // 2, self.width), (self.many, self.width)
        inner = ((self.many, self.cols), BF)
        return call(
            partial(
                feed_kernel, grads=len(grads), mids=len(mids), wide=self.wide, groups=self.highs * self.wide,
                paired=len(mids) > len(grads),
            ),
            (self.table, *grads, *mids, *weights),
            [(half, BF), (half, BF), (half, F32), (half, BF), (full, BF), inner, inner, (full, BF)],
            [((self.width, self.cols), BF), ((self.cols, self.width), BF)],
            micros=6,
        )

    def up_gradient(self, mids, delta):
        return call(
            partial(up_pack_kernel, wide=self.wide),
            (self.table, dot(mids, delta, TN), delta),
            [((self.width // (self.highs * self.wide) + TAIL, self.cols), BF)] * self.sides,
        )

    def down_gradient(self, acts, grads):
        return call(
            partial(down_pack_kernel, wide=self.wide),
            (self.table, dot(acts, grads, TN)),
            [((self.ffn, self.width), BF)] * self.sides,
        )

    def turn(self, mid, w_out, ends):
        outs = call(
            turn_kernel,
            (self.table, self.grad, mid, w_out, *ends, self.gain2),
            [((self.rows, self.width), F32), ((self.rows, self.width), BF), *[self.piece] * 4],
            [((HEADS, self.half, 2 * HD), BF)],
        )
        return outs[0], outs[1], list(outs[2:])

    def out_gradient(self, lay_keep, lay_send, attended, delta):
        return call(
            partial(out_grad_kernel, wide=self.wide, wrows=self.wrows),
            (self.table, lay_keep, lay_send, attended, delta),
            [((self.many, self.width), BF)] * 2,
            [((self.shards * self.wide, self.wrows, self.width), BF)],
        )

    def backward(self, kept, douts):
        query, keys, values, out_t, lse, begin = kept
        tall = self.rows + self.half
        total = ((self.total, HD), F32)
        return call(
            backward_kernel,
            (self.table, *douts, query, keys, values, out_t, lse, begin),
            [
                ((TEAM, tall, 2 * HD), BF),
                ((TEAM, tall, 2 * HD), BF),
                ((self.shards, self.rows, TRIPLE), BF),
                ((1, TRIPLE), F32),
            ],
            [
                ((self.shards, self.half, 2 * HD), BF),
                ((self.total, HD), BF),
                ((HD, self.total), BF),
                total, total, total,
                ((self.shards, tall, 2 * HD), BF),
            ],
            limit=14 * self.repeats * self.repeats,
            micros=8,
        )

    def qkv_gradient(self, pieces, others, by_shard, sums):
        return call(
            partial(
                qkv_grad_kernel,
                repeats=self.repeats, chips=len(pieces), others=len(others), wide=self.wide,
            ),
            (self.table, *pieces, *others, by_shard, sums),
            [((HEADS, self.qkv_tall, 2 * HD), BF)] * self.wide,
            [((self.width, TRIPLE), F32)],
        )

    def up_share(self, own, got):
        return list(
            call(
                up_share_kernel,
                (self.table, own, got),
                [((2, self.up_tall, self.cols), BF)] * 4,
                [((TEAM, self.wrows, self.cols), BF)],
            )
        )

    def qkv_share(self, own, got):
        return list(call(qkv_add_kernel, (self.table, own, got), [((4, self.qkv_tall, 2 * HD), BF)] * 4))

    def outputs(self, mid, ends):
        return call(
            partial(outs_kernel, wide=self.wide),
            (self.table, mid, *ends),
            [((self.rows, self.width), BF)] + [((self.highs, self.wrows, self.width), BF)] * self.wide,
        )

    def inputs(self, to_own, from_mate, weights, mates):
        return call(
            input_kernel,
            (self.table, to_own, from_mate, weights, *mates),
            [((self.many // 2, self.width), F32), ((self.many // 2, self.width), BF)],
            [((self.many, 2 * TRIPLE), BF), ((self.width, 2 * TRIPLE), BF)],
        )

    def last(self, ends, mid_delta):
        return call(
            last_kernel,
            (self.table, *ends, mid_delta, self.hidden, self.gain1),
            [((self.rows, self.width), BF)],
        )[0]

    def up_end(self, ends):
        line = ((1, self.wrows), F32)
        return call(
            partial(up_end_kernel, runs=self.highs, wide=self.wide),
            (self.table, *ends, self.up, self.gain2, self.bias2),
            [(self.up.shape, F32), line, line],
            [((1, self.up.shape[1]), F32)],
        )

    def qkv_end(self, ends):
        line = ((1, self.wrows), F32)
        return call(
            partial(qkv_end_kernel, wide=self.wide),
            (self.table, *ends, self.qkv, self.gain1, self.bias1),
            [(self.qkv.shape, F32), line, line],
            [((HEADS, self.qkv_tall, 2 * HD), BF)],
        )


def ring_moves(long):
    count = 2 * long
    order = [2 * at for at in range(long)] + [2 * at + 1 for at in reversed(range(long))]
    right = [(order[at], order[(at + 1) % count]) for at in range(count)]
    return right, [(two, one) for one, two in right]


def results(layer_out, grad_in, qkv, out, up, down):
    return (
        layer_out[None], grad_in[None], qkv[0], out, up[0], down,
        qkv[1][0], qkv[2][0], up[1][0], up[2][0],
    )


def local(*arrays, sizes):
    s = Steps(arrays, sizes)
    right, left = ring_moves(4)

    def ahead(array):
        return lax.ppermute(array, CHIPS, right)

    def behind(array):
        return lax.ppermute(array, CHIPS, left)

    norm_in, by_head, out_b, up_b, down_b = s.first()
    a1, b1, *got = meet(ahead(norm_in), behind(norm_in), *near(by_head))
    packs = mix([by_head[0], *got])
    a2, b2, *got = meet(ahead(a1), behind(b1), *far(packs))
    (packed,) = call(settle_kernel, (s.table, packs[0], *got), [((HEADS, s.qkv_tall, 2 * HD), BF)])
    first = stack([norm_in, a1, b1, a2, b2])
    ups = [after(up, a2) for up in up_b]
    a3, b3, packed_x, *got = meet(ahead(a2), behind(b2), swap(packed, "x"), *near(ups))
    ups = mix([ups[0], *got])
    half = s.half
    one, two, up_z, first, down_x = meet(
        ahead(a3[:half]),
        behind(b3[half:]),
        swap(ups[1], "zl"),
        swap(after(first, a3), "c"),
        swap(after(down_b, a3), "x"),
    )
    a4 = stack([one, two]).reshape(s.rows, s.width)
    second = stack([a3, b3])
    (up_t,) = call(join_kernel, (s.table, ups[0], up_z, down_b), [((TEAM * s.wrows, s.cols), BF)])
    pieces = [norm_in, a1, b1, a2, b2, a3, b3, a4]
    others = [first, *meet(swap(second, "c"), swap(a4[None], "c"))]

    out = after(out_b, a4)
    out_z = [lax.ppermute(out, ("zh", "zl"), apart(4, at)) for at in range(1, 4)]
    grad = after(s.grad, a4)
    grad_z = swap(grad, "zl")
    att, w_head, kept = s.forward(pieces, others, [packed, packed_x])
    *att, grad_z, o1, o2, o3 = meet(*att, grad_z, *out_z)
    out_4 = stack([out, o1, o2, o3])
    *got, out_x, up_z, grad_y = meet(
        *near(att), swap(out_4, "x"), swap(after(up_t, att[0]), "zh"), swap(after(grad, att[0]), "y")
    )
    att = mix([att[0], *got])
    out_8 = stack([out_4, out_x])
    *got, out_8y, up_x, out_8c = meet(
        *far(att), swap(out_8, "y"), swap(after(up_t, att[0]), "x"), swap(out_8, "c")
    )
    attended, mid, norm_mid, w_out = s.middle([out_8, out_8y, out_8c, swap(out_8y, "c")], [att[0], *got])

    half = s.half
    grad_3 = stack([after(grad, norm_mid), grad_z, grad_y])
    by_z, by_y, up_zx, down_z, grad_3c = meet(
        swap(norm_mid, "zl"),
        swap(norm_mid, "y"),
        swap(after(up_z, norm_mid), "x"),
        swap(after(down_b, norm_mid), "zh"),
        swap(grad_3, "c"),
    )
    three, send_z, send_y = call(
        pair_kernel,
        (norm_mid, by_z, by_y, grad_z, grad_y),
        [((3, s.rows, s.width), BF)] + [((2, s.half, s.width), BF)] * 2,
        smem=0,
    )
    pair_z, pair_y, three, down_zx = meet(
        swap(send_z, "zl"), swap(send_y, "y"), swap(three, "c"), swap(after(down_z, send_z), "x")
    )
    mids = [norm_mid, by_z, by_y, pair_z, pair_y, three, swap(pair_z, "c"), swap(pair_y, "c")]
    grads = [grad, grad_z, grad_y, grad_3c]
    lay_keep, lay_send, keep, send, mids, acts, delta, grads = s.feed(
        grads, mids, [up_t, up_z, up_x, up_zx, down_b, down_z, down_x, down_zx]
    )
    send_z, send_y, top, low = spread(s.table, keep, swap(send, "c"))
    up_parts = s.up_gradient(mids, after(delta, send_z))
    got_z, got_y, *up_parts = meet(swap(send_z, "zl"), swap(send_y, "y"), *up_parts)
    send_y, send_z, top, low = narrow(s.table, top, got_z, low, got_y)
    down_parts = s.down_gradient(after(acts, send_y), grads)
    end_top, end_low, *down_parts = meet(swap(send_y, "y"), swap(send_z, "zl"), *down_parts)
    mid_delta, mid_delta_b, by_head = s.turn(mid, w_out, (top, end_top, low, end_low))
    keep, send = s.out_gradient(after(lay_keep, mid_delta), lay_send, attended, mid_delta_b)
    *got, up_far, mate_1, keep, send = meet(
        *near(by_head),
        swap(after(up_parts[3], mid_delta), "x"),
        swap(after(w_head[1], mid_delta), "zh"),
        keep,
        send,
    )
    by_head = mix([by_head[0], *got])
    up_shape = up_parts[0].shape
    (up_send,) = call(up_add_kernel, (up_parts[1], after(up_far, by_head[0])), [(up_shape, BF)], smem=0)
    *got, send, down_far, up_send = meet(
        *far(by_head), swap(after(send, by_head[0]), "c"), swap(after(down_parts[3], by_head[0]), "x"), up_send
    )

    douts = [array[None] for array in (by_head[0], *got)]
    send_z, send_y, top, low = spread(s.table, keep, send)
    got_z, got_y = swap(send_z, "zl"), swap(send_y, "y")
    up_got = swap(after(up_send, send_z), "zh")
    up_near = swap(after(up_parts[2], send_z), "x")
    mate_2 = swap(after(mate_1, send_z), "x")
    kept = (after(kept[0], send_z), *kept[1:])
    to_own, to_mate, by_shard, sums = s.backward(kept, douts)
    from_mate = swap(to_mate, "zh")
    qkv_own, qkv_send = s.qkv_gradient(pieces, others, by_shard, sums)
    to_own, got_z, got_y, up_near, mate_2, up_got, qkv_send = meet(
        to_own, got_z, got_y, up_near, mate_2, up_got, qkv_send
    )
    send_y, send_z, top, low = narrow(s.table, top, got_z, low, got_y)
    down_send = add(down_parts[1], after(down_far, send_y), BF)
    (up_keep,) = call(up_add_kernel, (up_parts[0], after(up_near, send_y)), [(up_shape, BF)], smem=0)
    end_top, end_low, qkv_got, down_send, up_keep = meet(
        swap(send_y, "y"), swap(send_z, "zl"), swap(qkv_send, "x"), down_send, up_keep
    )
    qkv = s.qkv_share(qkv_own, qkv_got)
    ups = s.up_share(after(up_keep, qkv_got), up_got)
    layer_out, *outs = s.outputs(mid, (top, end_top, low, end_low))
    from_mate, *ups = meet(from_mate, *ups)
    keep, send = s.inputs(to_own, from_mate, w_head[0], [mate_1, mate_2])
    send, qkv_c, *got = meet(
        swap(send, "c"), lax.ppermute(after(qkv[1], send), ("y", "c"), apart(4, 1)), *near([after(a, send) for a in ups])
    )

    lines = 2 * HD
    half = (s.many // 8, s.width)
    quarter = s.half * s.width // (4 * lines)
    piece = ((4, s.qkv_tall, lines), BF)
    send_z, both, top, low = call(
        spread_both_kernel,
        (s.table, keep, send, qkv[2]),
        [
            ((2, s.half, s.width), BF),
            ((4, s.qkv_tall + 2 * quarter, lines), BF),
            ((2, s.half, s.width), F32),
            ((2, s.half, s.width), F32),
        ],
        [((2, s.half, s.width), BF)],
    )
    got_z, both, down_got, out_got, qkv_yc = meet(
        swap(send_z, "zl"),
        swap(both, "y"),
        swap(after(down_send, send_z), "zh"),
        swap(after(outs[1], send_z), "x"),
        lax.ppermute(after(qkv[3], send_z), ("y", "c"), apart(4, 3)),
    )
    send_y, top, low, up_keep, *qkv = call(
        blend_kernel,
        (s.table, top, got_z, low, both, *ups[:1], *got, qkv[0], qkv_c, qkv_yc, outs[0], out_got),
        [
            ((s.half, s.width), BF),
            ((s.half, s.width), F32),
            ((s.half, s.width), F32),
            ((4, s.up_tall, s.cols), BF),
            piece,
            ((4, s.qkv_tall + s.up_tall * s.cols // lines + quarter, lines), BF),
            ((4, s.qkv_tall + s.wrows * s.width // (4 * lines), lines), BF),
            piece,
        ],
    )
    end_top, down_near, *more = meet(
        swap(send_y, "y"), swap(after(down_parts[2], send_y), "x"), *far(qkv)
    )
    line = ((1, s.wrows), F32)
    outs = call(
        end_kernel,
        (
            s.table, top, end_top, low, mid_delta, s.hidden, s.gain1, s.bias1, s.gain2, s.bias2,
            qkv[0], *more, s.qkv, up_keep, s.up, down_parts[0], down_near, down_got, outs[0], out_got,
        ),
        [
            ((s.rows, s.width), BF),
            (s.qkv.shape, F32), line, line,
            (s.up.shape, F32), line, line,
            (s.down.shape, F32),
            (s.out.shape, F32),
        ],
        [
            ((HEADS, s.qkv_tall, 2 * HD), BF),
            ((4, s.up_tall, s.cols), BF),
            ((1, s.up.shape[1]), F32),
            ((s.half, s.width), BF),
        ],
    )
    return results(layer_out, outs[0], outs[1:4], outs[8], outs[4:7], outs[7])


def local_any(*arrays, sizes):
    s = Steps(arrays, sizes)
    repeats, wide = s.repeats, s.wide
    long = 4 * repeats
    right, left = ring_moves(long)
    norm_in, by_head, out_b, up_b, down_b = s.first()
    one = two = norm_in
    pieces = [norm_in]
    for hop in range(1, long + 1):
        one = lax.ppermute(one, CHIPS, right)
        pieces.append(one)
        if hop < long:
            two = lax.ppermute(two, CHIPS, left)
            pieces.append(two)
    others = [swap(piece[None], "c") for piece in pieces]

    def by_parts(arrays):
        return [lax.all_gather(array, "r", axis=0, tiled=False) for array in arrays]

    def share(arrays):
        got = mix([arrays[0], *near(arrays)])
        return [got[0], *far(got)]

    def team_gather(array):
        half = array.shape[0] // 2
        by_z, by_y = swap(array, "zl"), swap(array, "y")
        chip = [array, by_z, by_y, swap(by_y[:half], "zl"), swap(by_z[half:], "y")]
        return chip + [swap(piece, "c") for piece in chip]

    def team_scatter(keep, send):
        send_z, send_y, top, low = spread(s.table, keep, swap(send, "c"))
        send_y, send_z, top, low = narrow(s.table, top, swap(send_z, "zl"), low, swap(send_y, "y"))
        return top, swap(send_y, "y"), low, swap(send_z, "zl")

    def to_owners(parts):
        array = jnp.stack(parts).reshape((wide, s.highs) + parts[0].shape).swapaxes(0, 1)
        array = array.reshape((wide * s.highs,) + parts[0].shape)
        return jnp.sum(lax.all_to_all(array, GROUP, 0, 0, tiled=True).astype(F32), axis=0)

    packs = share(by_head)
    (packed,) = call(settle_kernel, (s.table, *packs), [((HEADS, s.qkv_tall, 2 * HD), BF)])
    packed = lax.all_gather(packed, "r", axis=0, tiled=True)
    packs = [packed, *lax.all_gather(packed, "x", axis=0, tiled=False)]
    if wide == 2:
        packs = [packed, swap(packed, "x")]
    ups = mix([up_b[0], *near(up_b)])
    up_t = call(
        join_kernel, (s.table, ups[0], swap(ups[1], "zl"), down_b), [((TEAM * s.wrows, s.cols), BF)]
    )[0]
    weights = [lax.all_gather(array, GROUP, axis=0, tiled=False) for array in (up_t, down_b)]
    att, w_head, kept = s.forward(pieces, others, packs)

    def mine(arrays):
        return share(arrays)

    w_out = lax.all_gather(out_b, ALL, axis=0, tiled=True)
    attended, mid, norm_mid, w_out = s.middle([w_out], mine(att))
    lay_keep, lay_send, keep, send, mids, acts, delta, grads = s.feed(
        team_gather(s.grad), team_gather(norm_mid), weights
    )
    mid_delta, mid_delta_b, by_head = s.turn(mid, w_out, team_scatter(keep, send))
    up = to_owners(s.up_gradient(mids, delta)).astype(BF)
    down = to_owners(s.down_gradient(acts, grads))
    to_own, to_mate, by_shard, sums = s.backward(kept, by_parts(share(by_head)))
    layer_out, *outs = s.outputs(
        mid, team_scatter(*s.out_gradient(lay_keep, lay_send, attended, mid_delta_b))
    )
    keep, send = s.inputs(to_own, swap(to_mate, "zh"), w_head[0], [swap(w_head[0], "zh")])
    grad_in = s.last(team_scatter(keep, send), mid_delta)
    parts = s.qkv_gradient(pieces, others, by_shard, sums)
    own, *got = list(lax.all_to_all(jnp.stack(parts), "x", 0, 0, tiled=True))
    while len(got) > 1:
        own, got = own.astype(F32) + got[0].astype(F32), got[1:]
    ups = s.up_share(up, jnp.zeros_like(up))
    ups = mix([ups[0], *near(ups)])
    return results(
        layer_out,
        grad_in,
        s.qkv_end(share(s.qkv_share(own, got[0]))),
        to_owners([part[at] for part in outs for at in range(s.highs)]),
        s.up_end((ups[0], swap(ups[1], "zl"))),
        down,
    )


def solution(mesh):
    ctx, wide = mesh.shape["ctx"], mesh.shape["wt"]
    sizes = {"r": ctx // HEADS, "zh": 2, "zl": 2, "y": 2, "c": 2, "x": wide}
    grid = Mesh(mesh.devices.reshape(tuple(sizes.values())), ALL)
    tokens, weights = P("x", CTX, None), P(ALL, None)
    return jax.shard_map(
        partial(local if sizes["r"] == 1 and wide == 2 else local_any, sizes=sizes),
        mesh=grid,
        in_specs=(tokens, P("x", CTX)) + (weights,) * 4 + (P(),) * 4 + (tokens,),
        out_specs=(tokens, tokens) + (weights,) * 4 + (P(ALL),) * 4,
        check_vma=False,
    )
```

```python
from functools import partial

import jax
import jax.numpy as jnp
from jax import lax
from jax.experimental import pallas as pl
from jax.experimental.pallas import tpu as pltpu
from jax.sharding import Mesh
from jax.sharding import PartitionSpec as P

HEADS = 16
HD = 64
TRIPLE = 3 * HD
EPS = 1e-05
FAR = -1e30
TILE = 256
TEAM = 8
TAIL = 8
BF = jnp.bfloat16
F32 = jnp.float32
ALL = ("r", "zh", "zl", "y", "c", "x")
CTX = ("r", "zh", "zl", "y", "c")
PART = ("zh", "zl", "y", "c")
CHIPS = ("r", "zh", "zl", "y")
TP = ("zl", "y", "c")
GROUP = ("r", "zh", "x")
SWAP = [(0, 1), (1, 0)]
MASKS = [
    z * 8 + y * 4 + c * 2 + x for c in range(2) for y in range(2) for x in range(2) for z in range(4)
]
NN = ((1,), (0,))
NT = ((1,), (1,))
TN = ((0,), (0,))


def dot(one, two, dims):
    return lax.dot_general(one, two, (dims, ((), ())), preferred_element_type=F32)


def normalise(rows):
    centred = rows - jnp.mean(rows, axis=-1, keepdims=True)
    spread = lax.rsqrt(jnp.mean(centred * centred, axis=-1, keepdims=True) + EPS)
    return centred * spread, spread


def norm_back(grad, normed, spread, gain):
    scaled = grad * gain
    inner = (
        scaled
        - jnp.mean(scaled, axis=-1, keepdims=True)
        - normed * jnp.mean(scaled * normed, axis=-1, keepdims=True)
    )
    return inner * spread


def gelu_both(up):
    root = 0.7978845608028654
    square = up * up
    inner = jnp.tanh(root * up * (1.0 + 0.044715 * square))
    plus = 0.5 * (1.0 + inner)
    slope = plus + 0.5 * up * (1.0 - inner * inner) * root * (1.0 + 3.0 * 0.044715 * square)
    return up * plus, slope


def block_home(block, shards):
    return (block, 0) if block < shards else (2 * shards - 1 - block, 1)


def split_two(values):
    high = values.astype(BF)
    return high, (values - high.astype(F32)).astype(BF)


def after(array, *others):
    return lax.optimization_barrier((array, *others))[0]


class Place:
    def __init__(self, table):
        self.r, self.zh, self.zl, self.y, self.c, self.x = (table[at] for at in range(6))
        self.mate = self.zl * 4 + self.y * 2 + self.c
        self.ctx = self.zh * TEAM + self.mate

    def flat(self, wide):
        return (self.r * HEADS + self.ctx) * wide + self.x


def call(body, arrays, outs, scratch=(), smem=1, smem_outs=(), far=0, sems=0, limit=12, micros=0):
    vector = pl.BlockSpec(memory_space=pltpu.VMEM)
    scalar = pl.BlockSpec(memory_space=pltpu.SMEM)
    there = pl.BlockSpec(memory_space=pl.ANY)
    scratch = [pltpu.VMEM(shape, kind) for shape, kind in scratch]
    if sems:
        scratch.append(pltpu.SemaphoreType.DMA((sems,)))
    return pl.pallas_call(
        body,
        out_shape=[jax.ShapeDtypeStruct(shape, kind) for shape, kind in outs],
        in_specs=[scalar] * smem + [there] * far + [vector] * (len(arrays) - smem - far),
        out_specs=[scalar if at in smem_outs else vector for at in range(len(outs))],
        scratch_shapes=scratch,
        compiler_params=pltpu.CompilerParams(vmem_limit_bytes=limit << 20),
        cost_estimate=pl.CostEstimate(flops=micros * 10**9 + 1000, bytes_accessed=1 << 10, transcendentals=0),
    )(*arrays)


def start_copies(pairs, sems):
    copies = [pltpu.make_async_copy(source, target, sems.at[at]) for at, (source, target) in enumerate(pairs)]
    for copy in copies:
        copy.start()
    return copies


def first_kernel(table, hidden_ref, gain_ref, bias_ref, qkv_ref, out_ref, up_ref, down_ref, start_ref, *refs, runs):
    (
        norm_out, *heads, out_b, one_ref, two_ref, three_ref, four_ref, down_b,
        hidden_at, gain_at, bias_at, qkv_at, out_at, up_at, down_at, start_at, made_ref, sems,
    ) = refs
    ups = one_ref, two_ref, three_ref, four_ref
    place = Place(table)
    copies = start_copies(
        (
            (hidden_ref, hidden_at), (gain_ref, gain_at), (bias_ref, bias_at), (start_ref, start_at), (qkv_ref, qkv_at),
            (out_ref, out_at), (up_ref, up_at), (down_ref, down_at),
        ),
        sems,
    )
    for copy in copies[:3]:
        copy.wait()
    normed, _ = normalise(hidden_at[...].astype(F32))
    norm_out[...] = (normed * gain_at[...] + bias_at[...]).astype(BF)
    for copy in copies[3:]:
        copy.wait()
    rows = qkv_at.shape[0]
    half = rows // 2
    width = HEADS * HD
    starts = start_at[...].astype(F32).astype(BF)
    for head in range(HEADS):
        part = [qkv_at[:, at * width + head * HD : at * width + (head + 1) * HD].astype(BF) for at in range(3)]
        made_ref[head, :rows] = jnp.concatenate(part[:2], axis=1)
        made_ref[head, rows : rows + half] = jnp.concatenate([part[2][:half], part[2][half:]], axis=1)
        made_ref[head, rows + half :] = jnp.broadcast_to(starts, (TAIL, 2 * HD))
    for near in range(4):
        for far in range(4):
            heads[near][far] = made_ref[place.ctx ^ (far * 4 + near)]
    out_b[...] = out_at[...].astype(BF)
    piece = ups[0].shape[2] // runs
    for near in range(4):
        for high in range(2):
            mate = place.mate ^ (high * 4 + near)
            for at in range(runs):
                first = pl.multiple_of((at * TEAM + mate) * piece, piece)
                ups[near][high, :, at * piece : (at + 1) * piece] = up_at[:, pl.ds(first, piece)].astype(BF)
    rows, half = down_at.shape[0], down_at.shape[1] // 2
    down_b[:rows] = down_at[:, :half].astype(BF)
    down_b[rows:] = down_at[:, half:].astype(BF)


def settle_kernel(table, *refs):
    place = Place(table)
    for far in range(4):
        for near in range(4):
            refs[4][place.ctx ^ (far * 4 + near)] = refs[far][near]


def head_weights(packs, w_ref, wrows, wide):
    whalf = wrows // 2
    for x in range(wide):
        for at in range(packs[x].shape[0]):
            first = (at * wide + x) * wrows
            w_ref[first : first + wrows, : 2 * HD] = packs[x][at, :wrows]
            pair = packs[x][at, wrows : wrows + whalf]
            w_ref[first : first + whalf, 2 * HD :] = pair[:, :HD]
            w_ref[first + whalf : first + wrows, 2 * HD :] = pair[:, HD:]


def unstacked(refs):
    return [ref.at[at] for ref in refs for at in range(ref.shape[0])]


def in_order(place, packs, one_ref, two_ref):
    for at in range(packs[0].shape[0]):
        one_ref[at] = jnp.where(place.x == 0, packs[0][at], packs[1][at])
        two_ref[at] = jnp.where(place.x == 0, packs[1][at], packs[0][at])


def join_kernel(table, one_ref, two_ref, _, out_ref):
    place = Place(table)
    rows = one_ref.shape[1]
    for at in range(TEAM):
        mate = place.mate ^ at
        part = (one_ref if at < 4 else two_ref)[at % 4]
        if rows % 16 == 0:
            out_ref[pl.ds(pl.multiple_of(mate * rows, rows), rows), :] = part
        else:
            for to in range(TEAM):

                @pl.when(mate == to)
                def _(to=to, part=part):
                    out_ref[to * rows : (to + 1) * rows, :] = part


def mix_kernel(*refs):
    count = len(refs) - refs[0].shape[0]
    for near in range(count):
        for far, out in enumerate(refs[count:]):
            out[near] = refs[near][far]


def ring_shifts(chips):
    shifts = [0]
    for hop in range(1, chips // 2 + 1):
        shifts += [-hop, hop] if hop < chips // 2 else [-hop]
    return shifts


def ring_order(chips, place):
    long = chips // 2
    along = (place.r * 2 + place.zh) * 2 + place.zl
    spot = jnp.where(place.y == 0, along, chips - 1 - along)
    order = []
    for shift in ring_shifts(chips):
        at = lax.rem(spot + shift + chips, chips)
        order.append(jnp.where(at < long, 2 * at, 2 * (chips - 1 - at) + 1))
    return order


def forward_kernel(table, *refs, wrows, chips, others, wide):
    pieces, others, refs = refs[:chips], refs[chips : chips + others], refs[chips + others :]
    pieces = list(pieces) + unstacked(others)
    own_ref, *refs = refs
    packs, refs = ([own_ref, refs[0]], refs[1:]) if wide == 2 else (refs[:wide], refs[wide:])
    outs, seconds = refs[:4], refs[14:]
    lse_ref, begin_ref, w_ref, w_send, q_ref, k_ref, v_ref, ot_ref, vt_ref, att_ref = refs[4:14]
    place = Place(table)
    if wide == 2:
        in_order(place, packs, *seconds)
        packs = seconds
    head_weights(packs, w_ref, wrows, wide)
    count = w_send.shape[0]
    if count < w_ref.shape[0]:
        w_send[...] = w_ref[pl.ds(pl.multiple_of(place.x * count, count), count), :]
    else:
        w_send[...] = w_ref[...]
    shards, half, _ = att_ref.shape
    rows = 2 * half
    total = shards * rows
    blocks = 2 * shards
    order = ring_order(chips, place)
    whalf = wrows // 2
    flags = []
    for block in range(blocks):
        shard, side = block_home(block, shards)
        row = own_ref[shard, wrows + whalf : wrows + whalf + 1].astype(F32)
        flags.append(row[:, side * half : (side + 1) * half])
    flags = jnp.concatenate(flags, axis=0)
    spots = half * lax.broadcasted_iota(jnp.int32, flags.shape, 0) + lax.broadcasted_iota(
        jnp.int32, flags.shape, 1
    )
    marks = jnp.where(flags > 0.5, spots.astype(F32), -1.0)
    lane = lax.broadcasted_iota(jnp.int32, marks.shape, 1)
    hop = 1
    while hop < half:
        moved = jnp.concatenate([marks[:, half - hop :], marks[:, : half - hop]], axis=1)
        marks = jnp.maximum(marks, jnp.where(lane >= hop, moved, -1.0))
        hop *= 2
    last = jnp.broadcast_to(marks[:, half - 1 :], marks.shape)
    line = lax.broadcasted_iota(jnp.int32, marks.shape, 0)
    hop = 1
    while hop < blocks:
        moved = jnp.concatenate([last[blocks - hop :], last[: blocks - hop]], axis=0)
        last = jnp.maximum(last, jnp.where(line >= hop, moved, -1.0))
        hop *= 2
    moved = jnp.concatenate([last[blocks - 1 :], last[: blocks - 1]], axis=0)
    begins = jnp.maximum(marks, jnp.where(line >= 1, moved, -1.0))
    group = TILE // half
    for tile in range(total // TILE):
        row = jnp.concatenate([begins[tile * group + at : tile * group + at + 1] for at in range(group)], axis=1)
        begin_ref[tile : tile + 1, :] = row.astype(jnp.int32)
    for which in range(2):
        for at in range(chips):
            made = dot(pieces[which * chips + at][...], w_ref[...], NN).astype(BF)
            shard = 2 * order[at] + (place.c if which == 0 else 1 - place.c)
            one = pl.multiple_of(shard * half, half)
            two = pl.multiple_of((blocks - 1 - shard) * half, half)
            scaled = made[:, :HD] * BF(HD**-0.5)
            for first, part in ((one, slice(0, half)), (two, slice(half, rows))):
                q_ref[pl.ds(first, half), :] = scaled[part]
                k_ref[pl.ds(first, half), :] = made[part, HD : 2 * HD]
                v_ref[pl.ds(first, half), :] = made[part, 2 * HD :]
    for at in range(0, total, 128):
        vt_ref[:, at : at + 128] = v_ref[at : at + 128, :].astype(F32).T.astype(BF)
    wide_tile = 2 * TILE
    for tile in range(total // wide_tile):
        low = max(0, tile - total // 2 // wide_tile) * wide_tile
        high = (tile + 1) * wide_tile
        query = q_ref[high - wide_tile : high, :]
        begin = jnp.concatenate([begin_ref[2 * tile : 2 * tile + 1, :], begin_ref[2 * tile + 1 : 2 * tile + 2, :]], axis=1)
        query_pos = high - wide_tile + lax.broadcasted_iota(jnp.int32, (1, wide_tile), 1)
        scores = dot(k_ref[low:high, :], query, NT)
        key_pos = low + lax.broadcasted_iota(jnp.int32, scores.shape, 0)
        scores = jnp.where((key_pos >= begin) & (key_pos <= query_pos), scores, FAR)
        top = jnp.max(scores, axis=0, keepdims=True)
        weights = jnp.exp(scores - top)
        sums = jnp.sum(weights, axis=0, keepdims=True)
        out = dot(vt_ref[:, low:high], weights.astype(BF), NN) / sums
        ot_ref[:, high - wide_tile : high] = out
        lse = top + jnp.log(sums)
        lse_ref[2 * tile : 2 * tile + 1, :] = lse[:, :TILE]
        lse_ref[2 * tile + 1 : 2 * tile + 2, :] = lse[:, TILE:]
        turned = out.T.astype(BF)
        for piece in range(2 * group):
            shard, side = block_home(tile * 2 * group + piece, shards)
            att_ref[shard, :, side * HD : (side + 1) * HD] = turned[piece * half : (piece + 1) * half]
    for near in range(4):
        for far in range(4):
            outs[near][far] = att_ref[place.r * HEADS + (place.ctx ^ (far * 4 + near))]


def middle_kernel(table, *refs, count):
    weights, atts, refs = refs[:count], refs[count : count + 4], refs[count + 4 :]
    hidden_ref, gain_ref, bias_ref, att_out, mid_out, norm_out, w_ref, heads_ref = refs
    place = Place(table)
    if count > 1:
        for at, ref in enumerate(unstacked(weights)):
            rows = ref.shape[0]
            first = (place.flat(2) ^ MASKS[at]) * rows
            w_ref[pl.ds(pl.multiple_of(first, rows), rows), :] = ref[...]
    else:
        w_ref[...] = weights[0][...]
    for far in range(4):
        for near in range(4):
            heads_ref[place.ctx ^ (far * 4 + near)] = atts[far][near]
    half = heads_ref.shape[1]
    for head in range(0, HEADS, 2):
        for side in range(2):
            lanes = slice(side * HD, (side + 1) * HD)
            att_out[side * half : (side + 1) * half, head * HD : (head + 2) * HD] = jnp.concatenate(
                [heads_ref[head, :, lanes], heads_ref[head + 1, :, lanes]], axis=1
            )
    mid = hidden_ref[...].astype(F32) + dot(att_out[...], w_ref[...], NN)
    mid_out[...] = mid
    normed, _ = normalise(mid)
    norm_out[...] = (normed * gain_ref[...] + bias_ref[...]).astype(BF)


def pair_kernel(mid_ref, mid_z, mid_y, grad_z, grad_y, three, send_z, send_y):
    half = send_z.shape[1]
    for at, ref in enumerate((mid_ref, mid_z, mid_y)):
        three[at] = ref[...]
    send_z[0], send_z[1] = mid_y[:half, :], grad_y[:half, :]
    send_y[0], send_y[1] = mid_z[half:, :], grad_z[half:, :]


def feed_kernel(table, *refs, grads, mids, wide, groups, paired):
    grads, mids, refs = refs[:grads], refs[grads : grads + mids], refs[grads + mids :]
    *weights, lay_keep, lay_send, mnd_keep, mnd_send, mid_out, act_out, delta_out, grad_out, up_ref, down_ref = refs
    place = Place(table)
    if paired:
        pairs = [mids[at] for at in (3, 4, 6, 7)]
        grads = [*grads[:3], *[ref.at[1] for ref in pairs[:2]], grads[3], *[ref.at[1] for ref in pairs[2:]]]
        mids = [*mids[:3], *[ref.at[0] for ref in pairs[:2]], mids[5], *[ref.at[0] for ref in pairs[2:]]]
    for out, arrays in ((grad_out, grads), (mid_out, mids)):
        first = 0
        for ref in arrays:
            for part in unstacked([ref]) if len(ref.shape) == 3 else [ref]:
                out[first : first + part.shape[0], :] = part[...]
                first += part.shape[0]
    width = mid_out.shape[1]
    own = width // (TEAM * groups)
    ffn = down_ref.shape[0] // groups
    moving = len(weights) > 2
    count = len(weights) // 2
    ups, downs = weights[:count], weights[count:]
    if not moving:
        ups, downs = unstacked(ups), unstacked(downs)
    for at in range(groups):
        if moving:
            high, x = place.zh ^ (at & 1), place.x ^ (at >> 1)
        else:
            high, x = at // wide, at % wide
        for mate in range(TEAM):
            first = ((high * TEAM + mate) * wide + x) * own
            if moving:
                first = pl.multiple_of(first, own)
            up_ref[pl.ds(first, own), :] = ups[at][mate * own : (mate + 1) * own, :]
        first = (high * wide + x) * ffn
        if moving:
            first = pl.multiple_of(first, ffn)
        down_ref[pl.ds(first, ffn), : width // 2] = downs[at][:ffn, :]
        down_ref[pl.ds(first, ffn), width // 2 :] = downs[at][ffn:, :]
    total = mid_out.shape[0]
    run = 256
    half = total // 2
    for first in list(range(half, total, run)) + list(range(0, half, run)):
        here = slice(first, first + run)
        up = dot(mid_out[here, :], up_ref[...], NN)
        value, slope = gelu_both(up)
        act = value.astype(BF)
        act_out[here, :] = act
        delta = (dot(grad_out[here, :], down_ref[...], NT) * slope).astype(BF)
        delta_out[here, :] = delta
        back = dot(delta, up_ref[...], NT)
        fore = dot(act, down_ref[...], NN)
        if first < half:
            mnd_keep[here, :] = back
            lay_keep[here, :] = fore.astype(BF)
        else:
            there = slice(first - half, first - half + run)
            mnd_send[there, :] = back.astype(BF)
            lay_send[there, :] = fore.astype(BF)


def turn_kernel(
    table, grad_ref, mid_ref, w_ref, keep_top, got_top, keep_low, got_low, gain_ref, delta_out, bf_out, *refs
):
    *outs, made_ref = refs
    mnd = jnp.concatenate(
        [keep_top[...] + got_top[...].astype(F32), keep_low[...] + got_low[...].astype(F32)], axis=0
    )
    normed, spread = normalise(mid_ref[...])
    delta = grad_ref[...].astype(F32) + norm_back(mnd, normed, spread, gain_ref[...])
    delta_out[...] = delta
    narrow = delta.astype(BF)
    bf_out[...] = narrow
    back = dot(narrow, w_ref[...], NT).astype(BF)
    half = made_ref.shape[1]
    for head in range(HEADS):
        cols = slice(head * HD, (head + 1) * HD)
        made_ref[head] = jnp.concatenate([back[:half, cols], back[half:, cols]], axis=1)
    place = Place(table)
    for near in range(4):
        for far in range(4):
            outs[near][far] = made_ref[place.ctx ^ (far * 4 + near)]


TEAM_ORDER = (0, 4, 2, 6, 1, 5, 3, 7)


def out_grad_kernel(table, lay_keep, lay_send, att_ref, delta_ref, keep_out, send_out, part_ref, *, wide, wrows):
    turned = att_ref[...].astype(F32).T.astype(BF)
    part_ref[...] = dot(turned, delta_ref[...], NN).astype(BF).reshape(part_ref.shape)
    place = Place(table)
    rows = lay_keep.shape[0] // 4
    highs = part_ref.shape[0] // (TEAM * wide)
    for at in range(TEAM):
        mate = place.mate ^ TEAM_ORDER[at]
        out, lay = (keep_out, lay_keep) if at < 4 else (send_out, lay_send)
        first = (at % 4) * 2 * rows
        out[first : first + rows, :] = lay[(at % 4) * rows : (at % 4 + 1) * rows, :]
        first += rows
        for x in range(wide):
            for high in range(highs):
                out[first : first + wrows, :] = part_ref[(high * TEAM + mate) * wide + x]
                first += wrows


def up_pack_kernel(table, part_ref, delta_ref, *outs, wide):
    rows = (outs[0].shape[0] - TAIL) // TEAM
    tail = sum_lines(jnp.sum(delta_ref[...].astype(F32), axis=0, keepdims=True))
    place = Place(table)
    highs = len(outs) // wide
    for at, out in enumerate(outs):
        if wide == 2:
            x, high = place.x ^ (at >> 1), place.zh ^ (at & 1)
        else:
            x, high = at // highs, at % highs
        for mate in range(TEAM):
            first = ((high * TEAM + mate) * wide + x) * rows
            if wide == 2:
                first = pl.multiple_of(first, rows)
            out[mate * rows : (mate + 1) * rows] = part_ref[pl.ds(first, rows), :].astype(BF)
        out[TEAM * rows :] = tail


def down_pack_kernel(table, part_ref, *outs, wide):
    rows = outs[0].shape[0]
    place = Place(table)
    highs = len(outs) // wide
    for at, out in enumerate(outs):
        if wide == 2:
            x, high = place.x ^ (at >> 1), place.zh ^ (at & 1)
        else:
            x, high = at // highs, at % highs
        first = (high * wide + x) * rows
        if wide == 2:
            first = pl.multiple_of(first, rows)
        out[...] = part_ref[pl.ds(first, rows), :].astype(BF)


def up_add_kernel(own_ref, got_ref, out_ref):
    body, tail = add_lines(own_ref[...], got_ref[...])
    out_ref[: body.shape[0]] = body
    out_ref[body.shape[0] :] = tail


def sum_kernel(own_ref, got_ref, out_ref):
    out_ref[...] = (own_ref[...].astype(F32) + got_ref[...].astype(F32)).astype(out_ref.dtype)


def up_share_kernel(table, own_ref, got_ref, *refs):
    *outs, all_ref = refs
    place = Place(table)
    rows = outs[0].shape[1] - TAIL
    body, tail = add_lines(own_ref[...], got_ref[...])
    for mate in range(TEAM):
        all_ref[mate] = body[mate * rows : (mate + 1) * rows]
    for near in range(4):
        for high in range(2):
            out = outs[near]
            out[high, :rows] = all_ref[place.mate ^ (high * 4 + near)]
            out[high, rows:] = tail


def sum_lines(sums):
    high, low = split_two(sums)
    line = lax.broadcasted_iota(jnp.int32, (8, sums.shape[1]), 0)
    return jnp.where(line == 0, high.astype(F32), jnp.where(line == 1, low.astype(F32), 0.0)).astype(BF)


def add_lines(own, got):
    rows = own.shape[0] - TAIL
    total = own.astype(F32) + got.astype(F32)
    return total[:rows].astype(BF), sum_lines(total[rows : rows + 1] + total[rows + 1 : rows + 2])


def owner_column(row_ref, first, rows):
    shape = (rows, row_ref.shape[1])
    hit = lax.broadcasted_iota(jnp.int32, shape, 1) == first + lax.broadcasted_iota(jnp.int32, shape, 0)
    return jnp.sum(jnp.where(hit, row_ref[...], 0.0), axis=1, keepdims=True)


def as_row(column):
    shape = (column.shape[0],) * 2
    hit = lax.broadcasted_iota(jnp.int32, shape, 0) == lax.broadcasted_iota(jnp.int32, shape, 1)
    return jnp.sum(jnp.where(hit, column, 0.0), axis=0, keepdims=True)


def norm_grads(place, master_ref, grad_ref, sums, gain_ref, bias_ref, gain_out, bias_out, wide):
    rows = master_ref.shape[0]
    first = place.flat(wide) * rows
    own = master_ref[...].astype(BF).astype(F32)
    bias_grad = jnp.sum(own * sums, axis=1, keepdims=True)
    bias_out[...] = as_row(bias_grad)
    gain_grad = jnp.sum(own * grad_ref[...], axis=1, keepdims=True) - owner_column(bias_ref, first, rows) * bias_grad
    gain_out[...] = as_row(gain_grad / owner_column(gain_ref, first, rows))


def up_end_kernel(table, one_ref, two_ref, own_ref, gain_ref, bias_ref, grad_out, gain_out, bias_out, sum_ref, *, runs, wide):
    place = Place(table)
    rows = own_ref.shape[0]
    piece = one_ref.shape[2] // runs
    for high, ref in ((0, one_ref), (1, two_ref)):
        for near in range(4):
            mate = place.mate ^ (high * 4 + near)
            for at in range(runs):
                there = pl.ds(pl.multiple_of((at * TEAM + mate) * piece, piece), piece)
                part = ref[near, :, at * piece : (at + 1) * piece].astype(F32)
                grad_out[:, there] = part[:rows]
                sum_ref[:, there] = part[rows : rows + 1] + part[rows + 1 : rows + 2]
    norm_grads(place, own_ref, grad_out, sum_ref[...], gain_ref, bias_ref, gain_out, bias_out, wide)


def qkv_end_kernel(table, *refs, wide):
    parts, (own_ref, gain_ref, bias_ref, grad_out, gain_out, bias_out, all_ref) = refs[:4], refs[4:]
    place = Place(table)
    for far in range(4):
        for near in range(4):
            all_ref[place.ctx ^ (far * 4 + near)] = parts[far][near, : all_ref.shape[1]]
    rows = own_ref.shape[0]
    half = rows // 2
    width = HEADS * HD
    body = rows + half
    for head in range(0, HEADS, 2):
        for at in range(2):
            lanes = slice(at * HD, (at + 1) * HD)
            grad_out[:, at * width + head * HD : at * width + (head + 2) * HD] = jnp.concatenate(
                [all_ref[head, :rows, lanes], all_ref[head + 1, :rows, lanes]], axis=1
            ).astype(F32)
        for side in range(2):
            lanes = slice(side * HD, (side + 1) * HD)
            grad_out[side * half : (side + 1) * half, 2 * width + head * HD : 2 * width + (head + 2) * HD] = (
                jnp.concatenate([all_ref[head, rows:body, lanes], all_ref[head + 1, rows:body, lanes]], axis=1).astype(
                    F32
                )
            )
    lines = [[], [], []]
    for head in range(HEADS):
        tail = all_ref[head, body:, :].astype(F32)
        pair = tail[0:1] + tail[1:2]
        lines[0].append(pair[:, :HD])
        lines[1].append(pair[:, HD:])
        lines[2].append(tail[2:3, :HD] + tail[2:3, HD:])
    sums = jnp.concatenate(lines[0] + lines[1] + lines[2], axis=1)
    norm_grads(place, own_ref, grad_out, sums, gain_ref, bias_ref, gain_out, bias_out, wide)


def backward_kernel(table, *refs):
    douts, refs = refs[:4], refs[4:]
    (
        q_ref, k_ref, v_ref, ot_ref, lse_ref, begin_ref, own_out, mate_out, dn_ref, sum_ref,
        do_ref, dop_ref, kt_ref, dq_ref, dk_ref, dv_ref, da_ref,
    ) = refs
    place = Place(table)
    for part in range(douts[0].shape[0]):
        for far in range(4):
            for near in range(4):
                do_ref[part * HEADS + (place.ctx ^ (far * 4 + near))] = douts[far][part, near]
    shards, half, _ = do_ref.shape
    rows = 2 * half
    total = shards * rows
    for block in range(2 * shards):
        shard, side = block_home(block, shards)
        dop_ref[block * half : (block + 1) * half, :] = do_ref[shard, :, side * HD : (side + 1) * HD]
    for at in range(0, total, 128):
        kt_ref[:, at : at + 128] = k_ref[at : at + 128, :].astype(F32).T.astype(BF)
    dk_ref[...] = jnp.zeros_like(dk_ref)
    dv_ref[...] = jnp.zeros_like(dv_ref)
    for tile in range(total // TILE):
        here = slice(tile * TILE, (tile + 1) * TILE)
        query = q_ref[here, :]
        dout = dop_ref[here, :]
        begin = begin_ref[tile : tile + 1, :]
        lse = lse_ref[tile : tile + 1, :]
        row_dot = jnp.sum(dout.astype(F32).T * ot_ref[:, here], axis=0, keepdims=True)
        query_pos = tile * TILE + lax.broadcasted_iota(jnp.int32, (1, TILE), 1)
        low = max(0, tile - total // 2 // TILE) * TILE
        there = slice(low, (tile + 1) * TILE)
        scores = dot(k_ref[there, :], query, NT)
        key_pos = low + lax.broadcasted_iota(jnp.int32, scores.shape, 0)
        allowed = (key_pos >= begin) & (key_pos <= query_pos)
        probs = jnp.where(allowed, jnp.exp(scores - lse), 0.0)
        dprobs = dot(v_ref[there, :], dout, NT)
        delta = (probs * (dprobs - row_dot)).astype(BF)
        dv_ref[there, :] += dot(probs.astype(BF), dout, NN)
        dk_ref[there, :] += dot(delta, query, NN)
        accum = dot(kt_ref[:, there], delta, NN)
        dq_ref[here, :] = (accum * HD**-0.5).T
    sums = jnp.zeros((1, TRIPLE), F32)
    for block in range(2 * shards):
        shard, side = block_home(block, shards)
        at = slice(block * half, (block + 1) * half)
        pair = jnp.concatenate([dq_ref[at, :], dk_ref[at, :]], axis=1).astype(BF)
        last = dv_ref[at, :].astype(BF)
        da_ref[shard, side * half : (side + 1) * half, :] = pair
        da_ref[shard, rows : rows + half, side * HD : (side + 1) * HD] = last
        to = slice(side * half, (side + 1) * half)
        joined = jnp.concatenate([pair, last], axis=1)
        dn_ref[shard, to, :] = joined
        sums = sums + jnp.sum(joined.astype(F32), axis=0, keepdims=True)
    sum_ref[...] = sums
    base = place.r * HEADS
    for at in range(TEAM):
        own_out[at] = da_ref[base + place.zh * TEAM + at]
        mate_out[at] = da_ref[base + (1 - place.zh) * TEAM + at]


def qkv_lines(pair, last):
    line = lax.broadcasted_iota(jnp.int32, (8, 2 * HD), 0)
    high, low = split_two(pair)
    both = jnp.concatenate(split_two(last), axis=1)
    lines = jnp.where(line == 0, high.astype(F32), jnp.where(line == 1, low.astype(F32), both.astype(F32)))
    return lines.astype(BF)


def qkv_grad_kernel(table, *refs, repeats, chips, others, wide):
    pieces, stacks, (dn_ref, sum_ref, *outs, acc_ref) = refs[:chips], refs[chips : chips + others], refs[chips + others :]
    pieces = list(pieces) + unstacked(stacks)
    place = Place(table)
    order = ring_order(chips, place)
    total = None
    for which in range(2):
        for at in range(chips):
            shard = 2 * order[at] + (place.c if which == 0 else 1 - place.c)
            turned = dn_ref[shard].astype(F32).T.astype(BF)
            step = dot(turned, pieces[which * chips + at][...], NN)
            total = step if total is None else total + step
    acc_ref[...] = total.T
    owners, tall, _ = outs[0].shape
    rows = (tall - TAIL) * 2 // 3
    half = rows // 2
    sums = sum_ref[...]
    lines = qkv_lines(sums[:, : 2 * HD], sums[:, 2 * HD :])

    def write(base):
        for at, out in enumerate(outs):
            x = place.x ^ at if wide == 2 else at
            for owner in range(owners):
                first = base + (owner * wide + x) * rows
                if wide == 2:
                    first = pl.multiple_of(first, rows)
                grad = acc_ref[pl.ds(first, rows), :]
                out[owner, :rows] = grad[:, : 2 * HD].astype(BF)
                out[owner, rows : rows + half] = jnp.concatenate(
                    [grad[:half, 2 * HD :], grad[half:, 2 * HD :]], axis=1
                ).astype(BF)
                out[owner, rows + half :] = lines

    if repeats == 1:
        write(0)
    else:
        for at in range(repeats):
            pl.when(place.r == at)(partial(write, at * owners * wide * rows))


def qkv_add_kernel(table, own_ref, got_ref, *outs):
    place = Place(table)
    body = own_ref.shape[1] - TAIL
    for near in range(4):
        for far in range(4):
            at = place.ctx ^ (far * 4 + near)
            total = own_ref[at].astype(F32) + got_ref[at].astype(F32)
            outs[near][far, :body] = total[:body].astype(BF)
            tail = total[body:]
            outs[near][far, body:] = qkv_lines(tail[0:1] + tail[1:2], tail[2:3, :HD] + tail[2:3, HD:])


def spread_kernel(_, keep_ref, got_ref, send_z, send_y, top_out, low_out):
    rows = keep_ref.shape[0] // 4
    half = rows // 2
    for at in range(4):
        for side in range(2):
            here = slice(at * rows + side * half, at * rows + (side + 1) * half)
            total = keep_ref[here, :].astype(F32) + got_ref[here, :].astype(F32)
            if side == 0:
                if at % 2 == 0:
                    top_out[at // 2] = total
                else:
                    send_z[at // 2] = total.astype(BF)
            elif at < 2:
                low_out[at] = total
            else:
                send_y[at - 2] = total.astype(BF)


def narrow_kernel(_, top_ref, got_z, low_ref, got_y, send_y, send_z, top_out, low_out):
    top_out[...] = top_ref[0] + got_z[0].astype(F32)
    low_out[...] = low_ref[0] + got_y[0].astype(F32)
    send_y[...] = (top_ref[1] + got_z[1].astype(F32)).astype(BF)
    send_z[...] = (low_ref[1] + got_y[1].astype(F32)).astype(BF)


def input_kernel(table, own_ref, got_ref, *refs):
    tall = own_ref.shape[1]
    rows = tall * 2 // 3
    half = rows // 2
    place = Place(table)
    w_own, *mates, keep_out, send_out, lhs_ref, rhs_ref = refs
    rhs_ref[:, : 2 * HD] = w_own[:, : 2 * HD]
    rhs_ref[:, 2 * HD : 3 * HD] = w_own[:, 2 * HD :]
    for at, w_got in enumerate(mates):
        count = w_got.shape[0]
        here = slice(0, count)
        if len(mates) == 2:
            here = pl.ds(pl.multiple_of((place.x ^ at) * count, count), count)
        rhs_ref[here, 3 * HD : 4 * HD] = w_got[:, 2 * HD :]
        rhs_ref[here, 4 * HD :] = w_got[:, : 2 * HD]
    for at in range(TEAM):
        mate = place.mate ^ TEAM_ORDER[at]
        first = at * rows
        one, two = own_ref[mate], got_ref[mate]
        lhs_ref[first : first + rows, : 2 * HD] = one[:rows]
        lhs_ref[first : first + rows, 4 * HD :] = two[:rows]
        for side in range(2):
            lanes = slice(side * HD, (side + 1) * HD)
            lhs_ref[first + side * half : first + (side + 1) * half, 2 * HD : 4 * HD] = jnp.concatenate(
                [one[rows:, lanes], two[rows:, lanes]], axis=1
            )
    middle = TEAM * rows // 2
    send_out[...] = dot(lhs_ref[middle:, :], rhs_ref[...], NT).astype(BF)
    keep_out[...] = dot(lhs_ref[:middle, :], rhs_ref[...], NT)


def blocks(count):
    return [(slice(at * 2 * HD, (at + 1) * 2 * HD), at * 4 // count, at % (count // 4)) for at in range(count)]


def spread_both_kernel(table, keep_ref, got_ref, share_ref, send_z, both_ref, top_out, low_out, send_y):
    spread_kernel(table, keep_ref, got_ref, send_z, send_y, top_out, low_out)
    tall, rows = share_ref.shape[1], send_y.shape[1]
    both_ref[:, :tall] = share_ref[...]
    for lanes, run, at in blocks(send_y.shape[2] // (2 * HD)):
        for high in range(2):
            first = tall + (2 * at + high) * rows
            both_ref[run, first : first + rows] = send_y[high, :, lanes]


def blend_kernel(_, top_ref, got_z, low_ref, both_ref, *refs):
    ups, qkvs, own_ref, got_ref = refs[:4], (refs[4], refs[5], both_ref, refs[6]), refs[7], refs[8]
    send_y, top_out, low_out, up_keep, *outs = refs[9:]
    tall, rows, part = refs[4].shape[1], ups[0].shape[1], own_ref.shape[1] // 4
    half = top_out.shape[0]
    top_out[...] = top_ref[0] + got_z[0].astype(F32)
    send_y[...] = (top_ref[1] + got_z[1].astype(F32)).astype(BF)
    after_ups = tall + rows * (ups[0].shape[2] // (2 * HD))
    for lanes, run, at in blocks(low_out.shape[1] // (2 * HD)):
        first = tall + 2 * at * half
        low_out[:, lanes] = low_ref[0, :, lanes] + both_ref[run, first : first + half].astype(F32)
        got = both_ref[run, first + half : first + 2 * half].astype(F32)
        to = after_ups + at * half
        outs[1][run, to : to + half] = (low_ref[1, :, lanes] + got).astype(BF)
    for near in range(4):
        up_keep[near] = ups[near][0]
        for far, out in enumerate(outs):
            out[near, :tall] = qkvs[near][far, :tall]
        for at in range(ups[0].shape[2] // (2 * HD)):
            first = tall + at * rows
            outs[1][near, first : first + rows] = ups[near][1, :, at * 2 * HD : (at + 1) * 2 * HD]
        here = slice(near * part, (near + 1) * part)
        total = (own_ref[1, here].astype(F32) + got_ref[1, here].astype(F32)).astype(BF)
        for at in range(own_ref.shape[2] // (2 * HD)):
            first = tall + at * part
            outs[2][near, first : first + part] = total[:, at * 2 * HD : (at + 1) * 2 * HD]


def end_kernel(
    table, keep_top, got_top, keep_low, mid_delta_ref, hidden_ref, gain1_ref, bias1_ref, gain2_ref, bias2_ref,
    q0_ref, q1_ref, q2_ref, q3_ref, qkv_ref, up_one, up_ref, down_ref, down_near, down_got, out_own, out_got,
    grad_out, qkv_out, qkv_gain, qkv_bias, up_out, up_gain, up_bias, down_out, out_out,
    all_ref, up_two, sum_ref, got_low,
):
    tall, rows, half = q0_ref.shape[1], up_one.shape[1], got_low.shape[0]
    after_ups = tall + rows * (up_one.shape[2] // (2 * HD))
    for lanes, run, at in blocks(got_low.shape[1] // (2 * HD)):
        first = after_ups + at * half
        got_low[:, lanes] = q1_ref[run, first : first + half]
    last_kernel(table, keep_top, got_top, keep_low, got_low, mid_delta_ref, hidden_ref, gain1_ref, grad_out)
    for near in range(4):
        for at in range(up_one.shape[2] // (2 * HD)):
            first = tall + at * rows
            up_two[near, :, at * 2 * HD : (at + 1) * 2 * HD] = q1_ref[near, first : first + rows]
    qkv_end_kernel(
        table, q0_ref, q1_ref, q2_ref, q3_ref, qkv_ref, gain1_ref, bias1_ref, qkv_out, qkv_gain, qkv_bias, all_ref, wide=2
    )
    up_end_kernel(
        table, up_one, up_two, up_ref, gain2_ref, bias2_ref, up_out, up_gain, up_bias, sum_ref, runs=2, wide=2
    )
    down_out[...] = down_ref[...].astype(F32) + down_near[...].astype(F32) + down_got[...].astype(F32)
    part = out_own.shape[1] // 4
    for near in range(4):
        rows = slice(near * part, (near + 1) * part)
        keep = out_own[0, rows].astype(F32) + out_got[0, rows].astype(F32)
        for at in range(out_own.shape[2] // (2 * HD)):
            first = tall + at * part
            lanes = slice(at * 2 * HD, (at + 1) * 2 * HD)
            out_out[rows, lanes] = keep[:, lanes] + q2_ref[near, first : first + part].astype(F32)


def last_kernel(_, keep_top, got_top, keep_low, got_low, mid_delta_ref, hidden_ref, gain_ref, out_ref):
    grad = jnp.concatenate(
        [keep_top[...] + got_top[...].astype(F32), keep_low[...] + got_low[...].astype(F32)], axis=0
    )
    normed, spread = normalise(hidden_ref[...].astype(F32))
    out_ref[...] = (mid_delta_ref[...] + norm_back(grad, normed, spread, gain_ref[...])).astype(BF)


def outs_kernel(table, mid_ref, lay_ref, got_lay, part_ref, got_part, lay_out, *outs, wide):
    lay_out[...] = (mid_ref[...] + lay_ref[...] + got_lay[...].astype(F32)).astype(BF)
    highs, rows, _ = outs[0].shape
    place = Place(table)
    for side, out in enumerate(outs):
        for at in range(highs):
            x, high = (place.x ^ side, place.zh ^ at) if wide == 2 else (side, at)
            first = (x * highs + high) * rows
            if wide == 2:
                first = pl.multiple_of(first, rows)
            out[at] = (part_ref[pl.ds(first, rows), :] + got_part[pl.ds(first, rows), :].astype(F32)).astype(BF)


def after(array, *others):
    return lax.optimization_barrier((array, *others))[0]


def apart(count, mask):
    return [(at, at ^ mask) for at in range(count)]


def stack(arrays):
    count = sum(array.shape[0] if array.ndim == 3 else 1 for array in arrays)
    return call(stack_kernel, arrays, [((count,) + arrays[0].shape[-2:], arrays[0].dtype)], smem=0)[0]


def meet(*arrays):
    return lax.optimization_barrier(arrays)


def near(arrays):
    return [lax.ppermute(arrays[at], ("y", "c"), apart(4, at)) for at in range(1, 4)]


def far(arrays):
    return [lax.ppermute(arrays[at], ("zh", "zl"), apart(4, at)) for at in range(1, 4)]


def swap(array, axis):
    return lax.ppermute(array, axis, SWAP)


def mix(arrays):
    shape = arrays[0].shape
    return call(mix_kernel, arrays, [((len(arrays),) + shape[1:], arrays[0].dtype)] * shape[0], smem=0)


def stack_kernel(*refs):
    at = 0
    for ref in refs[:-1]:
        count = ref.shape[0] if len(ref.shape) == 3 else 1
        for part in range(count):
            refs[-1][at] = ref[part] if len(ref.shape) == 3 else ref[...]
            at += 1


def spread(table, keep, got):
    shape = (keep.shape[0] // 8, keep.shape[1])
    return call(spread_kernel, (table, keep, got), [((2, *shape), BF)] * 2 + [((2, *shape), F32)] * 2)


def narrow(table, top, got_z, low, got_y, micros=0):
    shape = top.shape[1:]
    return call(
        narrow_kernel, (table, top, got_z, low, got_y), [(shape, BF)] * 2 + [(shape, F32)] * 2, micros=micros
    )


def add(one, two, kind):
    return call(sum_kernel, (one, two), [(one.shape, kind)], smem=0)[0]


class Steps:
    def __init__(self, arrays, sizes):
        (
            self.hidden, self.start, self.qkv, self.out, self.up, self.down,
            gain1, bias1, gain2, bias2, self.grad,
        ) = arrays
        self.hidden, self.grad = self.hidden[0], self.grad[0]
        self.gain1, self.bias1, self.gain2, self.bias2 = (a[None] for a in (gain1, bias1, gain2, bias2))
        self.repeats, self.wide = sizes["r"], sizes["x"]
        self.rows, self.width = self.hidden.shape
        self.half = self.rows // 2
        self.shards = self.repeats * HEADS
        self.total = self.shards * self.rows
        self.wrows, self.ffn = self.qkv.shape[0], self.down.shape[0]
        self.highs = 2 * self.repeats
        self.cols = self.highs * self.wide * self.ffn
        self.many = TEAM * self.rows
        self.qkv_tall = self.wrows * 3 // 2 + TAIL
        self.up_tall = self.wrows + TAIL
        self.sides = self.wide * self.highs
        self.piece = ((4, self.half, 2 * HD), BF)
        self.table = jnp.stack([lax.axis_index(axis).astype(jnp.int32) for axis in ALL])

    def first(self):
        masters = (self.qkv, self.out, self.up, self.down)
        row = ((1, self.width), F32)
        outs = call(
            partial(first_kernel, runs=self.highs),
            (self.table, self.hidden, self.gain1, self.bias1, *masters, self.start),
            [
                ((self.rows, self.width), BF),
                *[((4, self.qkv_tall, 2 * HD), BF)] * 4,
                ((self.wrows, self.width), BF),
                *[((2, self.wrows, self.cols), BF)] * 4,
                ((2 * self.ffn, self.width // 2), BF),
            ],
            [
                ((self.rows, self.width), BF), row, row,
                *[(a.shape, F32) for a in masters],
                (self.start.shape, jnp.int32),
                ((HEADS, self.qkv_tall, 2 * HD), BF),
            ],
            far=8,
            sems=8,
            limit=58,
        )
        return outs[0], list(outs[1:5]), outs[5], list(outs[6:10]), outs[10]

    def forward(self, pieces, others, packs):
        tokens = ((self.total, HD), BF)
        tiles = (self.total // TILE, TILE)
        sent = self.width // 2 if self.repeats == 1 and self.wide == 2 else self.width
        outs = call(
            partial(forward_kernel, wrows=self.wrows, chips=len(pieces), others=len(others), wide=self.wide),
            (self.table, *pieces, *others, *packs),
            [
                *[self.piece] * 4,
                (tiles, F32), (tiles, jnp.int32),
                ((self.width, TRIPLE), BF), ((sent, TRIPLE), BF),
                tokens, tokens, tokens,
                ((HD, self.total), F32),
            ],
            [((HD, self.total), BF), ((self.shards, self.half, 2 * HD), BF)]
            + [((self.shards, self.qkv_tall, 2 * HD), BF)] * (2 if self.wide == 2 else 0),
            limit=20 * self.repeats * self.repeats,
            micros=7,
        )
        return list(outs[:4]), list(outs[6:8]), (*outs[8:], *outs[4:6])

    def middle(self, weights, heads):
        return call(
            partial(middle_kernel, count=len(weights)),
            (self.table, *weights, *heads, self.hidden, self.gain2, self.bias2),
            [
                ((self.rows, self.width), BF),
                ((self.rows, self.width), F32),
                ((self.rows, self.width), BF),
                ((self.width, self.width), BF),
            ],
            [((HEADS, self.half, 2 * HD), BF)],
        )

    def feed(self, grads, mids, weights):
        half, full = (self.many // 2, self.width), (self.many, self.width)
        inner = ((self.many, self.cols), BF)
        return call(
            partial(
                feed_kernel, grads=len(grads), mids=len(mids), wide=self.wide, groups=self.highs * self.wide,
                paired=len(mids) > len(grads),
            ),
            (self.table, *grads, *mids, *weights),
            [(half, BF), (half, BF), (half, F32), (half, BF), (full, BF), inner, inner, (full, BF)],
            [((self.width, self.cols), BF), ((self.cols, self.width), BF)],
            micros=6,
        )

    def up_gradient(self, mids, delta):
        return call(
            partial(up_pack_kernel, wide=self.wide),
            (self.table, dot(mids, delta, TN), delta),
            [((self.width // (self.highs * self.wide) + TAIL, self.cols), BF)] * self.sides,
        )

    def down_gradient(self, acts, grads):
        return call(
            partial(down_pack_kernel, wide=self.wide),
            (self.table, dot(acts, grads, TN)),
            [((self.ffn, self.width), BF)] * self.sides,
        )

    def turn(self, mid, w_out, ends):
        outs = call(
            turn_kernel,
            (self.table, self.grad, mid, w_out, *ends, self.gain2),
            [((self.rows, self.width), F32), ((self.rows, self.width), BF), *[self.piece] * 4],
            [((HEADS, self.half, 2 * HD), BF)],
        )
        return outs[0], outs[1], list(outs[2:])

    def out_gradient(self, lay_keep, lay_send, attended, delta):
        return call(
            partial(out_grad_kernel, wide=self.wide, wrows=self.wrows),
            (self.table, lay_keep, lay_send, attended, delta),
            [((self.many, self.width), BF)] * 2,
            [((self.shards * self.wide, self.wrows, self.width), BF)],
        )

    def backward(self, kept, douts):
        query, keys, values, out_t, lse, begin = kept
        tall = self.rows + self.half
        total = ((self.total, HD), F32)
        return call(
            backward_kernel,
            (self.table, *douts, query, keys, values, out_t, lse, begin),
            [
                ((TEAM, tall, 2 * HD), BF),
                ((TEAM, tall, 2 * HD), BF),
                ((self.shards, self.rows, TRIPLE), BF),
                ((1, TRIPLE), F32),
            ],
            [
                ((self.shards, self.half, 2 * HD), BF),
                ((self.total, HD), BF),
                ((HD, self.total), BF),
                total, total, total,
                ((self.shards, tall, 2 * HD), BF),
            ],
            limit=14 * self.repeats * self.repeats,
            micros=8,
        )

    def qkv_gradient(self, pieces, others, by_shard, sums):
        return call(
            partial(
                qkv_grad_kernel,
                repeats=self.repeats, chips=len(pieces), others=len(others), wide=self.wide,
            ),
            (self.table, *pieces, *others, by_shard, sums),
            [((HEADS, self.qkv_tall, 2 * HD), BF)] * self.wide,
            [((self.width, TRIPLE), F32)],
        )

    def up_share(self, own, got):
        return list(
            call(
                up_share_kernel,
                (self.table, own, got),
                [((2, self.up_tall, self.cols), BF)] * 4,
                [((TEAM, self.wrows, self.cols), BF)],
            )
        )

    def qkv_share(self, own, got):
        return list(call(qkv_add_kernel, (self.table, own, got), [((4, self.qkv_tall, 2 * HD), BF)] * 4))

    def outputs(self, mid, ends):
        return call(
            partial(outs_kernel, wide=self.wide),
            (self.table, mid, *ends),
            [((self.rows, self.width), BF)] + [((self.highs, self.wrows, self.width), BF)] * self.wide,
        )

    def inputs(self, to_own, from_mate, weights, mates):
        return call(
            input_kernel,
            (self.table, to_own, from_mate, weights, *mates),
            [((self.many // 2, self.width), F32), ((self.many // 2, self.width), BF)],
            [((self.many, 2 * TRIPLE), BF), ((self.width, 2 * TRIPLE), BF)],
        )

    def last(self, ends, mid_delta):
        return call(
            last_kernel,
            (self.table, *ends, mid_delta, self.hidden, self.gain1),
            [((self.rows, self.width), BF)],
        )[0]

    def up_end(self, ends):
        line = ((1, self.wrows), F32)
        return call(
            partial(up_end_kernel, runs=self.highs, wide=self.wide),
            (self.table, *ends, self.up, self.gain2, self.bias2),
            [(self.up.shape, F32), line, line],
            [((1, self.up.shape[1]), F32)],
        )

    def qkv_end(self, ends):
        line = ((1, self.wrows), F32)
        return call(
            partial(qkv_end_kernel, wide=self.wide),
            (self.table, *ends, self.qkv, self.gain1, self.bias1),
            [(self.qkv.shape, F32), line, line],
            [((HEADS, self.qkv_tall, 2 * HD), BF)],
        )


def ring_moves(long):
    count = 2 * long
    order = [2 * at for at in range(long)] + [2 * at + 1 for at in reversed(range(long))]
    right = [(order[at], order[(at + 1) % count]) for at in range(count)]
    return right, [(two, one) for one, two in right]


def results(layer_out, grad_in, qkv, out, up, down):
    return (
        layer_out[None], grad_in[None], qkv[0], out, up[0], down,
        qkv[1][0], qkv[2][0], up[1][0], up[2][0],
    )


def local(*arrays, sizes):
    s = Steps(arrays, sizes)
    right, left = ring_moves(4)

    def ahead(array):
        return lax.ppermute(array, CHIPS, right)

    def behind(array):
        return lax.ppermute(array, CHIPS, left)

    norm_in, by_head, out_b, up_b, down_b = s.first()
    a1, b1, *got = meet(ahead(norm_in), behind(norm_in), *near(by_head))
    packs = mix([by_head[0], *got])
    a2, b2, *got = meet(ahead(a1), behind(b1), *far(packs))
    (packed,) = call(settle_kernel, (s.table, packs[0], *got), [((HEADS, s.qkv_tall, 2 * HD), BF)])
    first = stack([norm_in, a1, b1, a2, b2])
    ups = [after(up, a2) for up in up_b]
    a3, b3, packed_x, *got = meet(ahead(a2), behind(b2), swap(packed, "x"), *near(ups))
    ups = mix([ups[0], *got])
    half = s.half
    one, two, up_z, first, down_x = meet(
        ahead(a3[:half]),
        behind(b3[half:]),
        swap(ups[1], "zl"),
        swap(after(first, a3), "c"),
        swap(after(down_b, a3), "x"),
    )
    a4 = stack([one, two]).reshape(s.rows, s.width)
    second = stack([a3, b3])
    (up_t,) = call(join_kernel, (s.table, ups[0], up_z, down_b), [((TEAM * s.wrows, s.cols), BF)])
    pieces = [norm_in, a1, b1, a2, b2, a3, b3, a4]
    others = [first, *meet(swap(second, "c"), swap(a4[None], "c"))]

    out = after(out_b, a4)
    out_z = [lax.ppermute(out, ("zh", "zl"), apart(4, at)) for at in range(1, 4)]
    grad = after(s.grad, a4)
    grad_z = swap(grad, "zl")
    att, w_head, kept = s.forward(pieces, others, [packed, packed_x])
    *att, grad_z, o1, o2, o3 = meet(*att, grad_z, *out_z)
    out_4 = stack([out, o1, o2, o3])
    *got, out_x, up_z, grad_y = meet(
        *near(att), swap(out_4, "x"), swap(after(up_t, att[0]), "zh"), swap(after(grad, att[0]), "y")
    )
    att = mix([att[0], *got])
    out_8 = stack([out_4, out_x])
    *got, out_8y, up_x, out_8c = meet(
        *far(att), swap(out_8, "y"), swap(after(up_t, att[0]), "x"), swap(out_8, "c")
    )
    attended, mid, norm_mid, w_out = s.middle([out_8, out_8y, out_8c, swap(out_8y, "c")], [att[0], *got])

    half = s.half
    grad_3 = stack([after(grad, norm_mid), grad_z, grad_y])
    by_z, by_y, up_zx, down_z, grad_3c = meet(
        swap(norm_mid, "zl"),
        swap(norm_mid, "y"),
        swap(after(up_z, norm_mid), "x"),
        swap(after(down_b, norm_mid), "zh"),
        swap(grad_3, "c"),
    )
    three, send_z, send_y = call(
        pair_kernel,
        (norm_mid, by_z, by_y, grad_z, grad_y),
        [((3, s.rows, s.width), BF)] + [((2, s.half, s.width), BF)] * 2,
        smem=0,
    )
    pair_z, pair_y, three, down_zx = meet(
        swap(send_z, "zl"), swap(send_y, "y"), swap(three, "c"), swap(after(down_z, send_z), "x")
    )
    mids = [norm_mid, by_z, by_y, pair_z, pair_y, three, swap(pair_z, "c"), swap(pair_y, "c")]
    grads = [grad, grad_z, grad_y, grad_3c]
    lay_keep, lay_send, keep, send, mids, acts, delta, grads = s.feed(
        grads, mids, [up_t, up_z, up_x, up_zx, down_b, down_z, down_x, down_zx]
    )
    send_z, send_y, top, low = spread(s.table, keep, swap(send, "c"))
    up_parts = s.up_gradient(mids, after(delta, send_z))
    got_z, got_y, *up_parts = meet(swap(send_z, "zl"), swap(send_y, "y"), *up_parts)
    send_y, send_z, top, low = narrow(s.table, top, got_z, low, got_y)
    down_parts = s.down_gradient(after(acts, send_y), grads)
    end_top, end_low, *down_parts = meet(swap(send_y, "y"), swap(send_z, "zl"), *down_parts)
    mid_delta, mid_delta_b, by_head = s.turn(mid, w_out, (top, end_top, low, end_low))
    keep, send = s.out_gradient(after(lay_keep, mid_delta), lay_send, attended, mid_delta_b)
    *got, up_far, mate_1, keep, send = meet(
        *near(by_head),
        swap(after(up_parts[3], mid_delta), "x"),
        swap(after(w_head[1], mid_delta), "zh"),
        keep,
        send,
    )
    by_head = mix([by_head[0], *got])
    up_shape = up_parts[0].shape
    (up_send,) = call(up_add_kernel, (up_parts[1], after(up_far, by_head[0])), [(up_shape, BF)], smem=0)
    *got, send, down_far, up_send = meet(
        *far(by_head), swap(after(send, by_head[0]), "c"), swap(after(down_parts[3], by_head[0]), "x"), up_send
    )

    douts = [array[None] for array in (by_head[0], *got)]
    send_z, send_y, top, low = spread(s.table, keep, send)
    got_z, got_y = swap(send_z, "zl"), swap(send_y, "y")
    up_got = swap(up_send, "zh")
    up_near = swap(after(up_parts[2], send_z), "x")
    mate_2 = swap(after(mate_1, send_z), "x")
    kept = (after(kept[0], send_z), *kept[1:])
    to_own, to_mate, by_shard, sums = s.backward(kept, douts)
    from_mate = swap(to_mate, "zh")
    qkv_own, qkv_send = s.qkv_gradient(pieces, others, by_shard, sums)
    to_own, got_z, got_y, up_near, mate_2, up_got, qkv_send = meet(
        to_own, got_z, got_y, up_near, mate_2, up_got, qkv_send
    )
    send_y, send_z, top, low = narrow(s.table, top, got_z, low, got_y)
    down_send = add(down_parts[1], after(down_far, send_y), BF)
    (up_keep,) = call(up_add_kernel, (up_parts[0], after(up_near, send_y)), [(up_shape, BF)], smem=0)
    end_top, end_low, qkv_got, down_send, up_keep = meet(
        swap(send_y, "y"), swap(send_z, "zl"), swap(qkv_send, "x"), down_send, up_keep
    )
    qkv = s.qkv_share(qkv_own, qkv_got)
    ups = s.up_share(after(up_keep, qkv_got), up_got)
    layer_out, *outs = s.outputs(mid, (top, end_top, low, end_low))
    from_mate, *ups = meet(from_mate, *ups)
    keep, send = s.inputs(to_own, from_mate, w_head[0], [mate_1, mate_2])
    send, qkv_c, *got = meet(
        swap(send, "c"), lax.ppermute(after(qkv[1], send), ("y", "c"), apart(4, 1)), *near([after(a, send) for a in ups])
    )

    lines = 2 * HD
    half = (s.many // 8, s.width)
    quarter = s.half * s.width // (4 * lines)
    piece = ((4, s.qkv_tall, lines), BF)
    send_z, both, top, low = call(
        spread_both_kernel,
        (s.table, keep, send, qkv[2]),
        [
            ((2, s.half, s.width), BF),
            ((4, s.qkv_tall + 2 * quarter, lines), BF),
            ((2, s.half, s.width), F32),
            ((2, s.half, s.width), F32),
        ],
        [((2, s.half, s.width), BF)],
    )
    got_z, both, down_got, out_got, qkv_yc = meet(
        swap(send_z, "zl"),
        swap(both, "y"),
        swap(after(down_send, send_z), "zh"),
        swap(after(outs[1], send_z), "x"),
        lax.ppermute(after(qkv[3], send_z), ("y", "c"), apart(4, 3)),
    )
    send_y, top, low, up_keep, *qkv = call(
        blend_kernel,
        (s.table, top, got_z, low, both, *ups[:1], *got, qkv[0], qkv_c, qkv_yc, outs[0], out_got),
        [
            ((s.half, s.width), BF),
            ((s.half, s.width), F32),
            ((s.half, s.width), F32),
            ((4, s.up_tall, s.cols), BF),
            piece,
            ((4, s.qkv_tall + s.up_tall * s.cols // lines + quarter, lines), BF),
            ((4, s.qkv_tall + s.wrows * s.width // (4 * lines), lines), BF),
            piece,
        ],
    )
    end_top, down_near, *more = meet(
        swap(send_y, "y"), swap(after(down_parts[2], send_y), "x"), *far(qkv)
    )
    line = ((1, s.wrows), F32)
    outs = call(
        end_kernel,
        (
            s.table, top, end_top, low, mid_delta, s.hidden, s.gain1, s.bias1, s.gain2, s.bias2,
            qkv[0], *more, s.qkv, up_keep, s.up, down_parts[0], down_near, down_got, outs[0], out_got,
        ),
        [
            ((s.rows, s.width), BF),
            (s.qkv.shape, F32), line, line,
            (s.up.shape, F32), line, line,
            (s.down.shape, F32),
            (s.out.shape, F32),
        ],
        [
            ((HEADS, s.qkv_tall, 2 * HD), BF),
            ((4, s.up_tall, s.cols), BF),
            ((1, s.up.shape[1]), F32),
            ((s.half, s.width), BF),
        ],
    )
    return results(layer_out, outs[0], outs[1:4], outs[8], outs[4:7], outs[7])


def local_any(*arrays, sizes):
    s = Steps(arrays, sizes)
    repeats, wide = s.repeats, s.wide
    long = 4 * repeats
    right, left = ring_moves(long)
    norm_in, by_head, out_b, up_b, down_b = s.first()
    one = two = norm_in
    pieces = [norm_in]
    for hop in range(1, long + 1):
        one = lax.ppermute(one, CHIPS, right)
        pieces.append(one)
        if hop < long:
            two = lax.ppermute(two, CHIPS, left)
            pieces.append(two)
    others = [swap(piece[None], "c") for piece in pieces]

    def by_parts(arrays):
        return [lax.all_gather(array, "r", axis=0, tiled=False) for array in arrays]

    def share(arrays):
        got = mix([arrays[0], *near(arrays)])
        return [got[0], *far(got)]

    def team_gather(array):
        half = array.shape[0] // 2
        by_z, by_y = swap(array, "zl"), swap(array, "y")
        chip = [array, by_z, by_y, swap(by_y[:half], "zl"), swap(by_z[half:], "y")]
        return chip + [swap(piece, "c") for piece in chip]

    def team_scatter(keep, send):
        send_z, send_y, top, low = spread(s.table, keep, swap(send, "c"))
        send_y, send_z, top, low = narrow(s.table, top, swap(send_z, "zl"), low, swap(send_y, "y"))
        return top, swap(send_y, "y"), low, swap(send_z, "zl")

    def to_owners(parts):
        array = jnp.stack(parts).reshape((wide, s.highs) + parts[0].shape).swapaxes(0, 1)
        array = array.reshape((wide * s.highs,) + parts[0].shape)
        return jnp.sum(lax.all_to_all(array, GROUP, 0, 0, tiled=True).astype(F32), axis=0)

    packs = share(by_head)
    (packed,) = call(settle_kernel, (s.table, *packs), [((HEADS, s.qkv_tall, 2 * HD), BF)])
    packed = lax.all_gather(packed, "r", axis=0, tiled=True)
    packs = [packed, *lax.all_gather(packed, "x", axis=0, tiled=False)]
    if wide == 2:
        packs = [packed, swap(packed, "x")]
    ups = mix([up_b[0], *near(up_b)])
    up_t = call(
        join_kernel, (s.table, ups[0], swap(ups[1], "zl"), down_b), [((TEAM * s.wrows, s.cols), BF)]
    )[0]
    weights = [lax.all_gather(array, GROUP, axis=0, tiled=False) for array in (up_t, down_b)]
    att, w_head, kept = s.forward(pieces, others, packs)

    def mine(arrays):
        return share(arrays)

    w_out = lax.all_gather(out_b, ALL, axis=0, tiled=True)
    attended, mid, norm_mid, w_out = s.middle([w_out], mine(att))
    lay_keep, lay_send, keep, send, mids, acts, delta, grads = s.feed(
        team_gather(s.grad), team_gather(norm_mid), weights
    )
    mid_delta, mid_delta_b, by_head = s.turn(mid, w_out, team_scatter(keep, send))
    up = to_owners(s.up_gradient(mids, delta)).astype(BF)
    down = to_owners(s.down_gradient(acts, grads))
    to_own, to_mate, by_shard, sums = s.backward(kept, by_parts(share(by_head)))
    layer_out, *outs = s.outputs(
        mid, team_scatter(*s.out_gradient(lay_keep, lay_send, attended, mid_delta_b))
    )
    keep, send = s.inputs(to_own, swap(to_mate, "zh"), w_head[0], [swap(w_head[0], "zh")])
    grad_in = s.last(team_scatter(keep, send), mid_delta)
    parts = s.qkv_gradient(pieces, others, by_shard, sums)
    own, *got = list(lax.all_to_all(jnp.stack(parts), "x", 0, 0, tiled=True))
    while len(got) > 1:
        own, got = own.astype(F32) + got[0].astype(F32), got[1:]
    ups = s.up_share(up, jnp.zeros_like(up))
    ups = mix([ups[0], *near(ups)])
    return results(
        layer_out,
        grad_in,
        s.qkv_end(share(s.qkv_share(own, got[0]))),
        to_owners([part[at] for part in outs for at in range(s.highs)]),
        s.up_end((ups[0], swap(ups[1], "zl"))),
        down,
    )


def solution(mesh):
    ctx, wide = mesh.shape["ctx"], mesh.shape["wt"]
    sizes = {"r": ctx // HEADS, "zh": 2, "zl": 2, "y": 2, "c": 2, "x": wide}
    grid = Mesh(mesh.devices.reshape(tuple(sizes.values())), ALL)
    tokens, weights = P("x", CTX, None), P(ALL, None)
    return jax.shard_map(
        partial(local if sizes["r"] == 1 and wide == 2 else local_any, sizes=sizes),
        mesh=grid,
        in_specs=(tokens, P("x", CTX)) + (weights,) * 4 + (P(),) * 4 + (tokens,),
        out_specs=(tokens, tokens) + (weights,) * 4 + (P(ALL),) * 4,
        check_vma=False,
    )
```
